32 devices in a mesh: group: 4 (over x, core), ctx: 8 (over z, y).
Axes of the slice: x: 2, y: 2, z: 4, core: 2. Of those that a mesh axis runs over, the one named last changes fastest.
Arguments:
- tokens_in: bfloat16 [16, 2048, 768], P('group', 'ctx'), may hold values from -6 to 6
- seq_lengths: int32 [16], P('group'), may hold values from 512 to 2048, as said below
- norm_gain: float32 [768], replicated, may hold values from 0.5 to 1.5
- w_zx: bfloat16 [768, 3328], P('group'), may hold values from -0.21875 to 0.21875
- w_delta: bfloat16 [768, 24], P('group'), may hold values from -0.21875 to 0.21875
- w_out: bfloat16 [1536, 768], P('group'), may hold values from -0.15625 to 0.15625
- conv_weight: float32 [4, 1792], replicated, may hold values from -3 to 3
- conv_bias: float32 [1792], replicated, may hold values from -1.8 to 1.8
- delta_bias: float32 [24], replicated, may hold values from -2 to 0
- decay_log: float32 [24], replicated, may hold values from -11 to -2
- skip_gain: float32 [24], replicated, may hold values from 0.5 to 1.5
- gated_gain: float32 [1536], replicated, may hold values from 0.5 to 1.5
- cotangent: bfloat16 [16, 2048, 768], P('group', 'ctx'), may hold values from -6 to 6
Outputs:
- mixed_out: bfloat16 [16, 2048, 768], P('group', 'ctx')
- grad_tokens: bfloat16 [16, 2048, 768], P('group', 'ctx')
- grad_norm_gain: float32 [768], replicated
- grad_w_zx: float32 [768, 3328], P('group')
- grad_w_delta: float32 [768, 24], P('group')
- grad_w_out: float32 [1536, 768], P('group')
- grad_conv_weight: float32 [4, 1792], replicated
- grad_conv_bias: float32 [1792], replicated
- grad_delta_bias: float32 [24], replicated
- grad_decay_log: float32 [24], replicated
- grad_skip_gain: float32 [24], replicated
- grad_gated_gain: float32 [1536], replicated
The draws below stay inside these ranges and needn't reach their ends.
Inputs may be any that keep to these rules, and one draw needn't show every extreme that they name: `seq_lengths`: valid slots of each sequence, counted from its start; some sequence is full and some has 512.
All inputs are finite; a program needn't handle non-finite values.
Results may differ from the reference program's by a relative error of at most 0.015.
Values may be sent and summed in bfloat16 or wider, within the bound.
A program may use at most 192 MiB of HBM per device.

```python
import math
import jax
import jax.numpy as jnp
from jax import lax

D = 768
HEADS = 24
HEADDIM = 64
NSTATE = 128
KCONV = 4
SPAN = 256
DIN = 1536
CONVW = 1792
ZXW = 3328
LENGTH = 2048
SEQS = 16
N_CTX = 8


def draw_seq_lengths(key, part):
    key_rest = jax.random.fold_in(key, 11)
    key_order = jax.random.fold_in(key, 12)
    values = jax.random.randint(key_rest, (SEQS,), LENGTH // 4, LENGTH + 1).astype(jnp.int32)
    extremes = jnp.array([LENGTH, LENGTH // 4], jnp.int32)
    values = values.at[:2].set(extremes)
    ordering = jax.random.permutation(key_order, SEQS)
    return values[ordering]


def draw_decay_log(key, part):
    low_end = math.log(1.0 / LENGTH)
    high_end = math.log(0.1)
    return jax.random.uniform(jax.random.fold_in(key, 21), (HEADS,), jnp.float32, low_end, high_end)


def block_scale(key, shape, cuts, least, high):
    gain = 1.0
    for dim, blocks in cuts:
        heights = jax.random.uniform(jax.random.fold_in(jax.random.fold_in(key, 6), dim), (blocks,), jnp.float32, least / len(cuts), high / len(cuts))
        gain = gain * jnp.repeat(jnp.exp(heights), shape[dim] // blocks).reshape((-1,) + (1,) * (len(shape) - 1 - dim))
    return gain


def scatter_about(own_key, dims, width, reach, split=(), held_as=jnp.bfloat16):
    entries = jax.random.normal(own_key, dims, jnp.float32) * width
    if len(split) > 0:
        entries = block_scale(own_key, dims, split, -0.22, 0.18) * entries
    return jnp.clip(entries, min=-reach, max=reach).astype(held_as)


def setup_inputs(seed: int = 0) -> dict:
    streams_of = jax.random.split(jax.random.key(seed), 14)
    return {
        "tokens_in": scatter_about(streams_of[0], (SEQS, LENGTH, D), 1.0, 6.0, ((0, 4), (1, 8))),
        "seq_lengths": draw_seq_lengths(jax.random.fold_in(streams_of[13], 71), 0),
        "norm_gain": jnp.clip(1.0 + 0.1 * jax.random.normal(streams_of[2], (D,), jnp.float32), 0.5, 1.5),
        "w_zx": scatter_about(streams_of[3], (D, ZXW), D ** -0.5, 0.21875, ((0, 4),)),
        "w_delta": scatter_about(streams_of[4], (D, HEADS), D ** -0.5, 0.21875, ((0, 4),)),
        "w_out": scatter_about(streams_of[5], (DIN, D), DIN ** -0.5, 0.15625, ((0, 4),)),
        "conv_weight": scatter_about(streams_of[6], (KCONV, CONVW), KCONV ** -0.5, 3.0, (), jnp.float32),
        "conv_bias": scatter_about(streams_of[7], (CONVW,), 0.3, 1.8, (), jnp.float32),
        "delta_bias": jnp.clip(jax.random.uniform(streams_of[8], (HEADS,), jnp.float32, -2.0, 0.0), -2.0, 0.0),
        "decay_log": draw_decay_log(jax.random.fold_in(streams_of[13], 71), 0),
        "skip_gain": jnp.clip(jax.random.uniform(streams_of[10], (HEADS,), jnp.float32, 0.5, 1.5), 0.5, 1.5),
        "gated_gain": jnp.clip(1.0 + 0.1 * jax.random.normal(streams_of[11], (DIN,), jnp.float32), 0.5, 1.5),
        "cotangent": scatter_about(streams_of[12], (SEQS, LENGTH, D), 1.0, 6.0, ((0, 4), (1, 8))),
    }


@jax.custom_vjp
def low(v):
    return lax.optimization_barrier(v.astype(jnp.bfloat16)).astype(jnp.float32)

@jax.custom_vjp
def low_back(v):
    return v

def low_keep(v):
    return (low(v), None)

def low_pass(kept, grad):
    return (grad,)

def back_keep(v):
    return (v, None)

def back_low(kept, grad):
    return (low(grad),)
low.defvjp(low_keep, low_pass)
low_back.defvjp(back_keep, back_low)
epsilon = 1e-05

def input_norm(values, scale_row):
    return values * lax.rsqrt(lax.optimization_barrier(jnp.mean(values * values, axis=-1, keepdims=True)) + epsilon) * scale_row

def prepare(conv_rows, delta_raw, before_rows, conv_weight, conv_bias, delta_bias, decay_log):
    row_count = conv_rows.shape[0]
    extended = jnp.concatenate([before_rows, conv_rows], axis=0)
    conv_out = conv_bias[None, :]
    for offset in range(KCONV):
        conv_out = conv_out + conv_weight[offset][None, :] * extended[offset:offset + row_count]
    activated = jax.nn.silu(conv_out)
    seq_inputs = activated[:, :DIN].reshape(row_count, HEADS, HEADDIM)
    write_b = activated[:, DIN:DIN + NSTATE]
    read_c = activated[:, DIN + NSTATE:]
    step_size = jax.nn.softplus(delta_raw + delta_bias[None, :])
    log_decay = -jnp.exp(decay_log)[None, :] * step_size
    cumulative = jnp.cumsum(log_decay, axis=0)
    return (seq_inputs, write_b, read_c, step_size, cumulative)

def block_states(seq_inputs, write_b, step_size, cumulative):
    to_end = jnp.exp(cumulative[-1][None, :] - cumulative)
    weighted = seq_inputs * (step_size * to_end)[:, :, None]
    local_state = jnp.einsum('qhp,qn->hpn', weighted, write_b, precision=lax.Precision.HIGHEST)
    return (local_state, jnp.exp(cumulative[-1]))

def finish(gate_part, seq_inputs, write_b, read_c, step_size, cumulative, state_in, skip_gain, gated_gain):
    row_count = gate_part.shape[0]
    scores = jnp.dot(read_c, write_b.T, precision=lax.Precision.HIGHEST)
    causal = jnp.arange(row_count)[:, None] >= jnp.arange(row_count)[None, :]
    log_gaps = cumulative.T[:, :, None] - cumulative.T[:, None, :]
    decays = jnp.exp(jnp.where(causal[None], log_gaps, -jnp.inf))
    scaled = seq_inputs * step_size[:, :, None]
    within = jnp.einsum('hts,shp->thp', decays * scores[None], scaled, precision=lax.Precision.HIGHEST)
    carried = jnp.einsum('tn,hpn->thp', read_c, state_in, precision=lax.Precision.HIGHEST) * jnp.exp(cumulative)[:, :, None]
    outputs = within + carried + skip_gain[None, :, None] * seq_inputs
    flat_rows = outputs.reshape(row_count, HEADS * HEADDIM)
    gated_rows = flat_rows * jax.nn.silu(gate_part)
    return input_norm(gated_rows, gated_gain)

def reference(tokens_in, seq_lengths, norm_gain, w_zx, w_delta, w_out, conv_weight, conv_bias, delta_bias, decay_log, skip_gain, gated_gain, cotangent):
    live_mask = (jnp.arange(LENGTH)[None, :] < seq_lengths[:, None]).astype(jnp.float32)[:, :, None]

    def forward(tokens32, norm_gain, w_zx, w_delta, w_out, conv_weight, conv_bias, delta_bias, decay_log, skip_gain, gated_gain):
        normed_low = low(input_norm(tokens32, norm_gain)).reshape(SEQS * LENGTH, D)
        proj_zx = low_back(jnp.dot(normed_low, w_zx, precision=lax.Precision.HIGHEST)).reshape(SEQS, N_CTX, SPAN, ZXW)
        proj_delta = low_back(jnp.dot(normed_low, w_delta, precision=lax.Precision.HIGHEST)).reshape(SEQS, N_CTX, SPAN, HEADS)

        def block_step(carried_in, block_rows):
            state_in, before_rows = carried_in
            zx_rows, delta_rows = block_rows
            gate_rows = zx_rows[:, :DIN]
            conv_rows = zx_rows[:, DIN:]
            pieces = prepare(conv_rows, delta_rows, before_rows, conv_weight, conv_bias, delta_bias, decay_log)
            local_state, total_decay = block_states(pieces[0], pieces[1], pieces[3], pieces[4])
            mixer_rows = finish(gate_rows, pieces[0], pieces[1], pieces[2], pieces[3], pieces[4], state_in, skip_gain, gated_gain)
            following = (total_decay[:, None, None] * state_in + local_state, conv_rows[SPAN - KCONV + 1:])
            return (following, mixer_rows)

        def one_sequence(members):
            initial = (jnp.zeros((HEADS, HEADDIM, NSTATE), jnp.float32), jnp.zeros((KCONV - 1, CONVW), jnp.float32))
            final_carry, mixer_blocks = lax.scan(jax.checkpoint(block_step), initial, members)
            return mixer_blocks.reshape(LENGTH, DIN)
        mixers = lax.map(one_sequence, (proj_zx, proj_delta))
        out_proj = jnp.dot(low(mixers).reshape(SEQS * LENGTH, DIN), w_out, precision=lax.Precision.HIGHEST).reshape(SEQS, LENGTH, D)
        return live_mask * (tokens32 + out_proj)
    primals = (tokens_in.astype(jnp.float32), norm_gain, w_zx.astype(jnp.float32), w_delta.astype(jnp.float32), w_out.astype(jnp.float32), conv_weight, conv_bias, delta_bias, decay_log, skip_gain, gated_gain)
    mixed_out, pullback = jax.vjp(forward, *primals)
    gradients = pullback(cotangent.astype(jnp.float32))
    return (mixed_out.astype(jnp.bfloat16), gradients[0].astype(jnp.bfloat16), gradients[1], gradients[2], gradients[3], gradients[4], gradients[5], gradients[6], gradients[7], gradients[8], gradients[9], gradients[10])
```

```python
import jax
import jax.numpy as jnp
from jax import lax
from jax.experimental import pallas as pl
from jax.experimental.pallas import tpu as pltpu
from jax.sharding import PartitionSpec as P

D = 768
HEADS = 24
HEADDIM = 64
NSTATE = 128
KCONV = 4
SPAN = 256
DIN = 1536
CONVW = 1792
ZXW = 3328
RIM = 16
HALF = 128
TILE = 256
PAIRS = 12
EPS = 1e-05

f32 = jnp.float32
bf16 = jnp.bfloat16
NT = (((1,), (1,)), ((), ()))
TN = (((0,), (0,)), ((), ()))
VMEM_LIMIT = 62 * 1024 * 1024


def mm(a, b):
    return jnp.dot(a, b, preferred_element_type=f32)


def mm_nt(a, b):
    return lax.dot_general(a, b, NT, preferred_element_type=f32)


def mm_tn(a, b):
    return lax.dot_general(a, b, TN, preferred_element_type=f32)


def halves(v):
    high = v.astype(bf16)
    return high, (v - high.astype(f32)).astype(bf16)


def head_map():
    rows = lax.broadcasted_iota(jnp.int32, (2 * HALF, DIN), 0) % HALF
    cols = lax.broadcasted_iota(jnp.int32, (2 * HALF, DIN), 1) // HEADDIM
    return jnp.where(rows == cols, 1.0, 0.0).astype(bf16)


def spread(v, sel):
    return mm(jnp.concatenate(halves(v), axis=1), sel[...])


def gather_heads(v, sel_part):
    high, low = halves(v)
    return mm_nt(high, sel_part) + mm_nt(low, sel_part)


def triangle(size, lower):
    rows = lax.broadcasted_iota(jnp.int32, (size, size), 0)
    cols = lax.broadcasted_iota(jnp.int32, (size, size), 1)
    keep = rows >= cols if lower else rows <= cols
    return jnp.where(keep, 1.0, 0.0).astype(f32)


def exact_mm(a, b):
    return jnp.dot(a, b, precision=lax.Precision.HIGHEST, preferred_element_type=f32)


def softplus(v):
    return jnp.maximum(v, 0.0) + jnp.log1p(jnp.exp(-jnp.abs(v)))


def sigmoid(v):
    return 1.0 / (1.0 + jnp.exp(-v))


def local_decays(cum):
    mid, end = cum[HALF - 1 : HALF], cum[SPAN - 1 : SPAN]
    rows = lax.broadcasted_iota(jnp.int32, (SPAN, 1), 0)
    first = rows < HALF
    start = jnp.where(first, 0.0, mid)
    stop = jnp.where(first, mid, end)
    return jnp.exp(cum - start), jnp.exp(stop - cum), jnp.exp(mid), jnp.exp(end - mid), jnp.exp(end)


def rows_of(v):
    return jnp.broadcast_to(v, (8, v.shape[1]))


def normalized(rows, gain):
    rows = rows.astype(f32)
    inv = lax.rsqrt(jnp.mean(rows * rows, axis=-1, keepdims=True) + EPS)
    return rows, inv, (rows * inv * gain).astype(bf16)


def first_kernel(
    tok, halo, gain, wzx, wdl, cw, cb, db, dl,
    normed, nhalo, cin, act, gate, vout, cumout, st0, loc, tdec,
    sel, ext, fexp,
):
    @pl.when(pl.program_id(0) == 0)
    def _():
        sel[...] = head_map()

    nh = normalized(halo[0], gain[...])[2]
    nm = normalized(tok[0], gain[...])[2]
    ext[0:RIM] = nh
    ext[RIM:] = nm
    nhalo[0] = nh
    normed[0] = nm
    v = mm(nm, wdl[...]) + db[...]
    vout[0] = v
    dt = softplus(v)
    cum = exact_mm(triangle(SPAN, True), -jnp.exp(dl[...]) * dt)
    cumout[0] = cum
    e_in, e_out, tot0, tot1, total = local_decays(cum)
    fexp[...] = spread(dt * e_out, sel)
    tot1x = spread(rows_of(tot1), sel)[0:1]
    tdec[0] = spread(rows_of(total), sel)[0:1]

    def conv_tile(c):
        cols = pl.ds(c, TILE)
        cin[0, :, cols] = mm(ext[...], wzx[:, pl.ds(DIN + c, TILE)])
        o = cb[:, cols]
        for k in range(KCONV):
            o = o + cw[k : k + 1, cols] * cin[0, RIM - KCONV + 1 + k : RIM - KCONV + 1 + k + SPAN, cols]
        a = o * sigmoid(o)
        act[0, :, cols] = a
        return a

    bc = conv_tile(DIN)
    bt = jnp.transpose(bc[:, :NSTATE]).astype(bf16)

    for j in range(DIN // TILE):
        c = j * TILE
        cols = pl.ds(c, TILE)
        a = conv_tile(c)
        xw = (a * fexp[:, cols]).astype(bf16)
        s0 = mm(bt[:, :HALF], xw[:HALF])
        s1 = mm(bt[:, HALF:], xw[HALF:])
        st0[0, :, cols] = s0
        loc[0, :, cols] = (tot1x[:, c : c + TILE] * s0 + s1).astype(bf16)
    for j in range(DIN // TILE):
        gate[0, :, j * TILE : (j + 1) * TILE] = mm(ext[RIM:], wzx[:, j * TILE : (j + 1) * TILE])


def pair_decays(cum, cum_t, p, causal):
    rolled = pltpu.roll(cum, lax.rem(HALF - 2 * p, HALF), 1)
    out = []
    for q in range(2):
        rows = slice(q * HALF, (q + 1) * HALF)
        for a in range(2):
            gaps = rolled[rows, a : a + 1] - cum_t[q, pl.ds(2 * p + a, 1), :]
            out.append(jnp.exp(jnp.where(causal, gaps, -jnp.inf)))
    return out


def second_kernel(
    rel, tok, cot, act, gate, vin, cumin, st0, sin, wout, skip, ggain,
    mixed, mlow, dyout, ggate, wred, dirout, dir1, dcs, gskip, gggain, sin1out,
    sel, cum_t, dtx, einx, ys, gs, ss, s_in, dcacc,
):
    s = pl.program_id(0)

    @pl.when(s == 0)
    def _():
        sel[...] = head_map()
        gskip[...] = jnp.zeros_like(gskip)
        gggain[...] = jnp.zeros_like(gggain)

    causal = lax.broadcasted_iota(jnp.int32, (HALF, HALF), 0) >= lax.broadcasted_iota(jnp.int32, (HALF, HALF), 1)
    low_lanes = lax.broadcasted_iota(jnp.int32, (HALF, HALF), 1) < HEADDIM
    cum = cumin[0]
    dt = softplus(vin[0])
    e_in, e_out, tot0, tot1, total = local_decays(cum)
    cum_t[0] = jnp.transpose(cum[:HALF])
    cum_t[1] = jnp.transpose(cum[HALF:])
    dtx[...] = spread(dt, sel)
    einx[...] = spread(e_in, sel)
    tot0x = spread(rows_of(tot0), sel)[0:1]
    s_in[0] = sin[0]
    s_in[1] = (tot0x * sin[0].astype(f32) + st0[0]).astype(bf16)
    sin1out[0] = s_in[1]
    bb = act[0, :, DIN : DIN + NSTATE].astype(bf16)
    cc = act[0, :, DIN + NSTATE :].astype(bf16)
    scores = [mm_nt(cc[q * HALF : (q + 1) * HALF], bb[q * HALF : (q + 1) * HALF]) for q in range(2)]

    def pair_step(p, _):
        cols = pl.ds(pl.multiple_of(p * HALF, HALF), HALF)
        decays = pair_decays(cum, cum_t, p, causal)
        for q in range(2):
            rows = slice(q * HALF, (q + 1) * HALF)
            m = jnp.concatenate([(decays[2 * q + a] * scores[q]).astype(bf16) for a in range(2)], axis=1)
            x = act[0, rows, cols]
            xs = x * dtx[rows, cols]
            xs = jnp.concatenate([jnp.where(low_lanes, xs, 0.0), jnp.where(low_lanes, 0.0, xs)], axis=0)
            yn = mm(m, xs.astype(bf16)) + einx[rows, cols] * mm(cc[rows], s_in[q, :, cols])
            ys[rows, cols] = yn + skip[:, cols] * x
        return 0

    lax.fori_loop(0, PAIRS, pair_step, 0)

    def gate_step(j, total_sq):
        cols = pl.ds(pl.multiple_of(j * HALF, HALF), HALF)
        g = gate[0, :, cols]
        gated = ys[:, cols] * (g * sigmoid(g))
        gs[:, cols] = gated
        return total_sq + gated * gated

    sq = lax.fori_loop(0, PAIRS, gate_step, jnp.zeros((SPAN, HALF), f32))
    inv = lax.rsqrt(jnp.sum(sq, axis=1, keepdims=True) * (1.0 / DIN) + EPS)

    def low_step(j, _):
        cols = pl.ds(pl.multiple_of(j * HALF, HALF), HALF)
        mlow[0, :, cols] = (gs[:, cols] * inv * ggain[:, cols]).astype(bf16)
        return 0

    lax.fori_loop(0, PAIRS, low_step, 0)
    live = (lax.broadcasted_iota(jnp.int32, (SPAN, 1), 0) < rel[s]).astype(f32)
    for j in range(D // TILE):
        cols = slice(j * TILE, (j + 1) * TILE)
        mixed[0, :, cols] = (live * (tok[0, :, cols].astype(f32) + mm(mlow[0], wout[:, cols]))).astype(bf16)
    drive = (live * cot[0].astype(f32)).astype(bf16)

    def back_step(j, acc):
        cols = pl.ds(pl.multiple_of(j * TILE, TILE), TILE)
        gm = mm_nt(drive, wout[cols, :])
        gated = gs[:, cols]
        gggain[:, cols] += jnp.sum(gm * (gated * inv), axis=0, keepdims=True)
        scaled = gm * ggain[:, cols]
        ss[:, cols] = scaled
        prod = scaled * gated
        return acc + prod[:, :HALF] + prod[:, HALF:]

    dots = lax.fori_loop(0, DIN // TILE, back_step, jnp.zeros((SPAN, HALF), f32))
    dots = jnp.sum(dots, axis=1, keepdims=True) * (1.0 / DIN)
    corr = inv * inv * inv * dots
    cct = jnp.transpose(act[0, :, DIN + NSTATE :]).astype(bf16)
    tot0_rows = tot0x
    dcacc[...] = jnp.zeros_like(dcacc)
    wred[0] = jnp.zeros((SPAN, HALF), f32)
    for j in range(DIN // TILE):
        cols = slice(j * TILE, (j + 1) * TILE)
        g = gate[0, :, cols]
        sg = sigmoid(g)
        sl = g * sg
        grad_gated = inv * ss[:, cols] - gs[:, cols] * corr
        dy = grad_gated * sl
        y = ys[:, cols]
        ggate[0, :, cols] = (grad_gated * y * (sg + sl * (1.0 - sg))).astype(bf16)
        dyout[0, :, cols] = dy.astype(bf16)
        x = act[0, :, cols]
        gskip[:, cols] += jnp.sum(dy * x, axis=0, keepdims=True)
        wred[0] += gather_heads(dy * (y - skip[:, cols] * x), sel[:HALF, cols])
        dye = (dy * einx[:, cols]).astype(bf16)
        d0 = mm(cct[:, :HALF], dye[:HALF])
        d1 = mm(cct[:, HALF:], dye[HALF:])
        dir1[0, :, cols] = d1
        dirout[0, :, cols] = (d0 + tot0_rows[:, cols] * d1).astype(bf16)
        dcacc[:HALF] += mm_nt(dye[:HALF], s_in[0, :, cols])
        dcacc[HALF:] += mm_nt(dye[HALF:], s_in[1, :, cols])
    dcs[0] = dcacc[...]


def third_kernel(
    cin, vin, cumin, dyin, wred, dcs, dir1, later, sin, loc, cw, cb, dl, skip, skip_rows,
    gz, gzh, gdelta, gcw, gcb, gdb, gdl,
    sel, cum_t, dtx, eoutx, xx, sp, dact, xwb, g_s, dg_s, dout, qacc, gp,
):
    s = pl.program_id(0)

    @pl.when(s == 0)
    def _():
        sel[...] = head_map()
        gcw[...] = jnp.zeros_like(gcw)
        gcb[...] = jnp.zeros_like(gcb)
        gdb[...] = jnp.zeros_like(gdb)
        gdl[...] = jnp.zeros_like(gdl)
        gp[0:RIM] = jnp.zeros((RIM, CONVW), f32)
        gp[RIM + SPAN :] = jnp.zeros((8, CONVW), f32)

    causal = lax.broadcasted_iota(jnp.int32, (HALF, HALF), 0) >= lax.broadcasted_iota(jnp.int32, (HALF, HALF), 1)
    low_lanes = lax.broadcasted_iota(jnp.int32, (HALF, HALF), 1) < HEADDIM
    cum = cumin[0]
    v = vin[0]
    dt = softplus(v)
    e_in, e_out, tot0, tot1, total = local_decays(cum)
    cum_t[0] = jnp.transpose(cum[:HALF])
    cum_t[1] = jnp.transpose(cum[HALF:])
    dtx[...] = spread(dt, sel)
    eoutx[...] = spread(e_out, sel)
    tot1x = spread(rows_of(tot1), sel)[0:1]
    totalx = spread(rows_of(total), sel)[0:1]

    def conv_step(j, _):
        cols = pl.ds(pl.multiple_of(j * HALF, HALF), HALF)
        o = cb[:, cols]
        for k in range(KCONV):
            o = o + cw[k : k + 1, cols] * cin[0, RIM - KCONV + 1 + k : RIM - KCONV + 1 + k + SPAN, cols]
        sg = sigmoid(o)
        a = o * sg
        xx[:, cols] = a
        sp[:, cols] = sg + a * (1.0 - sg)
        return 0

    lax.fori_loop(0, CONVW // HALF, conv_step, 0)
    bb = xx[:, DIN : DIN + NSTATE].astype(bf16)
    cc = xx[:, DIN + NSTATE :].astype(bf16)
    for q in range(2):
        rows = slice(q * HALF, (q + 1) * HALF)
        g_s[q] = mm_nt(cc[rows], bb[rows])
    dg_s[...] = jnp.zeros_like(dg_s)
    qacc[...] = jnp.zeros_like(qacc)
    dout[1] = later[0]
    dout[0] = (dir1[0] + tot1x * later[0].astype(f32)).astype(bf16)

    def pair_step(p, _):
        cols = pl.ds(pl.multiple_of(p * HALF, HALF), HALF)
        decays = pair_decays(cum, cum_t, p, causal)
        for q in range(2):
            rows = slice(q * HALF, (q + 1) * HALF)
            x = xx[rows, cols]
            dte = dtx[rows, cols]
            eo = eoutx[rows, cols]
            xs = x * dte
            xsb = xs.astype(bf16)
            dyb = dyin[0, rows, cols]
            dyf = dyb.astype(f32)
            dxs = []
            for a in range(2):
                m = (decays[2 * q + a] * g_s[q]).astype(bf16)
                dxs.append(mm_tn(m, dyb))
                mine = low_lanes if a == 0 else jnp.logical_not(low_lanes)
                dm = mm_nt(jnp.where(mine, dyf, 0.0).astype(bf16), xsb)
                dg_s[q] += dm * decays[2 * q + a]
            dx_s = jnp.where(low_lanes, dxs[0], dxs[1]) + eo * mm(bb[rows], dout[q, :, cols])
            dact[rows, cols] = dte * dx_s + skip[:, cols] * dyf
            qacc[rows] += gather_heads(x * dx_s, sel[:HALF, cols])
            xwb[rows, cols] = (xs * eo).astype(bf16)
        return 0

    lax.fori_loop(0, PAIRS, pair_step, 0)
    for q in range(2):
        rows = slice(q * HALF, (q + 1) * HALF)
        dg = dg_s[q].astype(bf16)
        dact[rows, DIN : DIN + NSTATE] = mm_tn(dg, cc[rows]) + mm_nt(xwb[rows, :], dout[q])
        dact[rows, DIN + NSTATE :] = mm(dg, bb[rows]) + dcs[0, rows]

    ends = jnp.sum(later[0].astype(f32) * (totalx * sin[0].astype(f32) + loc[0].astype(f32)), axis=0, keepdims=True)
    ends = gather_heads(rows_of(ends), sel[:HALF])[0:1]
    at_end = lax.broadcasted_iota(jnp.int32, (SPAN, 1), 0) == SPAN - 1
    dcum = wred[0] - dt * qacc[...] + jnp.where(at_end, ends, 0.0)
    glog = exact_mm(triangle(SPAN, False), dcum)
    rate = jnp.exp(dl[...])
    gpd = (qacc[...] - rate * glog) * sigmoid(v)
    lanes = lax.broadcasted_iota(jnp.int32, (SPAN, HALF), 1) < HEADS
    gpd = jnp.where(lanes, gpd, 0.0)
    gdelta[0] = gpd.astype(bf16)
    gdb[...] += jnp.sum(gpd, axis=0, keepdims=True)
    gdl[...] += -rate * jnp.sum(dt * glog, axis=0, keepdims=True)

    def out_step(j, _):
        cols = pl.ds(pl.multiple_of(j * HALF, HALF), HALF)
        gco = dact[:, cols] * sp[:, cols]
        gp[RIM : RIM + SPAN, cols] = gco
        gcb[:, cols] += jnp.sum(gco, axis=0, keepdims=True)
        for k in range(KCONV):
            gcw[k : k + 1, cols] += jnp.sum(
                gco * cin[0, RIM - KCONV + 1 + k : RIM - KCONV + 1 + k + SPAN, cols], axis=0, keepdims=True
            )
        main = jnp.zeros((SPAN, HALF), f32)
        rim = jnp.zeros((RIM, HALF), f32)
        for k in range(KCONV):
            ahead = KCONV - 1 - k
            main = main + cw[k : k + 1, cols] * gp[RIM + ahead : RIM + ahead + SPAN, cols]
            rim = rim + cw[k : k + 1, cols] * gp[ahead : ahead + RIM, cols]
        gz[0, :, cols] = main.astype(bf16)
        gzh[0, :, cols] = rim.astype(bf16)
        return 0

    lax.fori_loop(0, CONVW // HALF, out_step, 0)


def fourth_kernel(
    rel, tok, halo, cot, gain, ggate, gz, gzh, gdelta, wzx, wdl,
    gtok, gtail, grim, ggain,
):
    s = pl.program_id(0)

    @pl.when(s == 0)
    def _():
        ggain[...] = jnp.zeros_like(ggain)

    def back(rows, grad):
        rows, inv, _ = normalized(rows, gain[...])
        ggain[...] += jnp.sum(grad * rows * inv, axis=0, keepdims=True)
        gained = gain[...] * grad
        mean = jnp.mean(gained * rows, axis=-1, keepdims=True)
        return inv * gained - rows * (inv * inv * inv * mean)

    grad = mm_nt(ggate[0], wzx[:, :DIN]) + mm_nt(gz[0], wzx[:, DIN:]) + mm_nt(gdelta[0], wdl[...])
    live = (lax.broadcasted_iota(jnp.int32, (SPAN, 1), 0) < rel[s]).astype(f32)
    out = live * cot[0].astype(f32) + back(tok[0], grad)
    gtok[0] = out.astype(bf16)
    gtail[0] = out[SPAN - RIM :]
    grim[0] = back(halo[0], mm_nt(gzh[0], wzx[:, DIN:])).astype(bf16)


def whole(shape):
    zeros = (0,) * len(shape)
    return pl.BlockSpec(shape, lambda s: zeros, pipeline_mode=pl.Buffered(1))


def summed(shape):
    zeros = (0,) * len(shape)
    return pl.BlockSpec(shape, lambda s: zeros)


def per_seq(*shape):
    zeros = (0,) * len(shape)
    return pl.BlockSpec((1,) + shape, lambda s: (s,) + zeros)


SMEM = pl.BlockSpec(memory_space=pltpu.SMEM)


def call(kernel, seqs, in_specs, outs, scratch, name, flops=0):
    params = pltpu.CompilerParams(vmem_limit_bytes=VMEM_LIMIT)
    return pl.pallas_call(
        kernel,
        grid=(seqs,),
        in_specs=in_specs,
        out_specs=[o[0] for o in outs],
        out_shape=[jax.ShapeDtypeStruct(o[1], o[2]) for o in outs],
        scratch_shapes=[pltpu.VMEM(*sc) for sc in scratch],
        compiler_params=params,
        name=name,
    )


def state_scan(local, decay, count, reverse):
    seqs = local.shape[0]
    part = NSTATE // count
    moved = local.reshape(seqs, count, part, DIN).transpose(1, 0, 2, 3)
    moved = lax.all_to_all(moved, "ctx", 0, 0, tiled=True)
    decays = lax.all_gather(decay, "ctx", axis=0)
    order = range(count - 1, -1, -1) if reverse else range(count)
    carry = jnp.zeros((seqs, part, DIN), f32)
    found = [None] * count
    for b in order:
        found[b] = carry
        carry = decays[b] * carry + moved[b].astype(f32)
    back = jnp.stack(found).astype(bf16)
    back = lax.all_to_all(back, "ctx", 0, 0, tiled=True)
    return back.transpose(1, 0, 2, 3).reshape(seqs, NSTATE, DIN)


def passed_along(value, axis, steps):
    count = lax.axis_size(axis)
    leading, last = (max(0, -steps), min(count, count - steps))
    return lax.ppermute(value, axis, [(source, source + steps) for source in range(leading, last)])


def lanes_of(v):
    return jnp.pad(v[None, :], ((0, 0), (0, HALF - v.shape[0])))


def local(
    tokens_in, seq_lengths, norm_gain, w_zx, w_delta, w_out, conv_weight, conv_bias,
    delta_bias, decay_log, skip_gain, gated_gain, cotangent,
):
    seqs = tokens_in.shape[0]
    count = lax.axis_size("ctx")
    full_zx = lax.all_gather(w_zx, "group", axis=0, tiled=True)
    full_delta = lax.all_gather(w_delta, "group", axis=0, tiled=True)
    full_out = lax.all_gather(w_out, "group", axis=0, tiled=True)
    full_delta = jnp.pad(full_delta, ((0, 0), (0, HALF - HEADS)))
    rel = seq_lengths - lax.axis_index("ctx") * SPAN
    halo = passed_along(tokens_in[:, SPAN - RIM :, :], "ctx", 1)
    gain = norm_gain[None, :]
    cb = conv_bias[None, :]
    db = lanes_of(delta_bias)
    dl = lanes_of(decay_log)
    skip = jnp.repeat(skip_gain, HEADDIM)[None, :]
    ggain = gated_gain[None, :]

    normed, nhalo, cin, act, gate, vraw, cum, st0, loc, tdec = call(
        first_kernel,
        seqs,
        [per_seq(SPAN, D), per_seq(RIM, D), whole((1, D)), whole((D, ZXW)), whole((D, HALF)), whole((KCONV, CONVW)),
         whole((1, CONVW)), whole((1, HALF)), whole((1, HALF))],
        [
            (per_seq(SPAN, D), (seqs, SPAN, D), bf16),
            (per_seq(RIM, D), (seqs, RIM, D), bf16),
            (per_seq(RIM + SPAN, CONVW), (seqs, RIM + SPAN, CONVW), f32),
            (per_seq(SPAN, CONVW), (seqs, SPAN, CONVW), f32),
            (per_seq(SPAN, DIN), (seqs, SPAN, DIN), f32),
            (per_seq(SPAN, HALF), (seqs, SPAN, HALF), f32),
            (per_seq(SPAN, HALF), (seqs, SPAN, HALF), f32),
            (per_seq(NSTATE, DIN), (seqs, NSTATE, DIN), f32),
            (per_seq(NSTATE, DIN), (seqs, NSTATE, DIN), bf16),
            (per_seq(1, DIN), (seqs, 1, DIN), f32),
        ],
        [((2 * HALF, DIN), bf16), ((RIM + SPAN, D), bf16), ((SPAN, DIN), f32)],
        "first",
    )(tokens_in, halo, gain, full_zx, full_delta, conv_weight, cb, db, dl)

    state_in = state_scan(loc, tdec, count, False)

    mixed_out, mlow, dy, ggate, wred, direct, dir1, dcs, gskip, gggain, sin1 = call(
        second_kernel,
        seqs,
        [SMEM, per_seq(SPAN, D), per_seq(SPAN, D), per_seq(SPAN, CONVW), per_seq(SPAN, DIN), per_seq(SPAN, HALF),
         per_seq(SPAN, HALF), per_seq(NSTATE, DIN), per_seq(NSTATE, DIN), whole((DIN, D)), whole((1, DIN)), whole((1, DIN))],
        [
            (per_seq(SPAN, D), (seqs, SPAN, D), bf16),
            (per_seq(SPAN, DIN), (seqs, SPAN, DIN), bf16),
            (per_seq(SPAN, DIN), (seqs, SPAN, DIN), bf16),
            (per_seq(SPAN, DIN), (seqs, SPAN, DIN), bf16),
            (per_seq(SPAN, HALF), (seqs, SPAN, HALF), f32),
            (per_seq(NSTATE, DIN), (seqs, NSTATE, DIN), bf16),
            (per_seq(NSTATE, DIN), (seqs, NSTATE, DIN), f32),
            (per_seq(SPAN, HALF), (seqs, SPAN, HALF), f32),
            (summed((1, DIN)), (1, DIN), f32),
            (summed((1, DIN)), (1, DIN), f32),
            (per_seq(NSTATE, DIN), (seqs, NSTATE, DIN), bf16),
        ],
        [((2 * HALF, DIN), bf16), ((2, HALF, HALF), f32), ((SPAN, DIN), f32), ((SPAN, DIN), f32), ((SPAN, DIN), f32),
         ((SPAN, DIN), f32), ((SPAN, DIN), f32), ((2, NSTATE, DIN), bf16), ((SPAN, HALF), f32)],
        "second",
    )(rel, tokens_in, cotangent, act, gate, vraw, cum, st0, state_in, full_out, skip, ggain)

    later = state_scan(direct, tdec, count, True)

    gz, gzh, gdelta, gcw, gcb, gdb, gdl = call(
        third_kernel,
        seqs,
        [per_seq(RIM + SPAN, CONVW), per_seq(SPAN, HALF), per_seq(SPAN, HALF), per_seq(SPAN, DIN), per_seq(SPAN, HALF),
         per_seq(SPAN, HALF), per_seq(NSTATE, DIN), per_seq(NSTATE, DIN), per_seq(NSTATE, DIN), per_seq(NSTATE, DIN),
         whole((KCONV, CONVW)), whole((1, CONVW)), whole((1, HALF)), whole((1, DIN)), whole((1, HALF))],
        [
            (per_seq(SPAN, CONVW), (seqs, SPAN, CONVW), bf16),
            (per_seq(RIM, CONVW), (seqs, RIM, CONVW), bf16),
            (per_seq(SPAN, HALF), (seqs, SPAN, HALF), bf16),
            (summed((KCONV, CONVW)), (KCONV, CONVW), f32),
            (summed((1, CONVW)), (1, CONVW), f32),
            (summed((1, HALF)), (1, HALF), f32),
            (summed((1, HALF)), (1, HALF), f32),
        ],
        [((2 * HALF, DIN), bf16), ((2, HALF, HALF), f32), ((SPAN, DIN), f32), ((SPAN, DIN), f32), ((SPAN, CONVW), f32),
         ((SPAN, CONVW), f32), ((SPAN, CONVW), f32), ((SPAN, DIN), bf16), ((2, HALF, HALF), f32), ((2, HALF, HALF), f32),
         ((2, NSTATE, DIN), bf16), ((SPAN, HALF), f32), ((RIM + SPAN + 8, CONVW), f32)],
        "third",
    )(cin, vraw, cum, dy, wred, dcs, dir1, later, state_in, loc, conv_weight, cb, dl, skip, db)

    live = (jnp.arange(SPAN, dtype=jnp.int32)[None, :] < rel[:, None]).astype(f32)[:, :, None]
    drive = (live * cotangent.astype(f32)).astype(bf16)
    flat = lambda v: v.reshape(-1, v.shape[-1])
    g_out = mm_tn(flat(mlow), flat(drive))
    g_gate = mm_tn(flat(normed), flat(ggate))
    g_conv = mm_tn(flat(normed), flat(gz)) + mm_tn(flat(nhalo), flat(gzh))
    g_delta = mm_tn(flat(normed), flat(gdelta))

    gtok, gtail, grim, g_gain = call(
        fourth_kernel,
        seqs,
        [SMEM, per_seq(SPAN, D), per_seq(RIM, D), per_seq(SPAN, D), whole((1, D)), per_seq(SPAN, DIN), per_seq(SPAN, CONVW),
         per_seq(RIM, CONVW), per_seq(SPAN, HALF), whole((D, ZXW)), whole((D, HALF))],
        [
            (per_seq(SPAN, D), (seqs, SPAN, D), bf16),
            (per_seq(RIM, D), (seqs, RIM, D), f32),
            (per_seq(RIM, D), (seqs, RIM, D), bf16),
            (summed((1, D)), (1, D), f32),
        ],
        [],
        "fourth",
    )(rel, tokens_in, halo, cotangent, gain, ggate, gz, gzh, gdelta, full_zx, full_delta)
    grim = passed_along(grim, "ctx", -1)
    gtok = lax.dynamic_update_slice(gtok, (gtail + grim.astype(f32)).astype(bf16), (0, SPAN - RIM, 0))

    def reduced(g):
        part = lax.psum_scatter(g.astype(bf16), "group", scatter_dimension=0, tiled=True)
        return lax.psum(part, "ctx").astype(f32)

    g_zx = jnp.concatenate([reduced(g_gate), reduced(g_conv)], axis=1)
    g_out = reduced(g_out)
    g_delta = reduced(g_delta)[:, :HEADS]
    small = jnp.concatenate(
        [g_gain.reshape(-1), gcw.reshape(-1), gcb.reshape(-1), gdb[0], gdl[0],
         gskip.reshape(-1), gggain.reshape(-1)]
    )
    small = lax.psum(small, ("group", "ctx"))
    at = 0
    pieces = []
    for size in (D, KCONV * CONVW, CONVW, HALF, HALF, DIN, DIN):
        pieces.append(small[at : at + size])
        at += size
    return (
        mixed_out, gtok, pieces[0], g_zx, g_delta, g_out, pieces[1].reshape(KCONV, CONVW), pieces[2],
        pieces[3][:HEADS], pieces[4][:HEADS], pieces[5].reshape(HEADS, HEADDIM).sum(1), pieces[6],
    )


def solution(mesh):
    rows = P("group", "ctx", None)
    own = P("group", None)
    in_specs = (rows, P("group"), P(), own, own, own, P(), P(), P(), P(), P(), P(), rows)
    out_specs = (rows, rows, P(), own, own, own, P(), P(), P(), P(), P(), P())
    return jax.shard_map(local, mesh=mesh, in_specs=in_specs, out_specs=out_specs, check_vma=False)
```

```python
import jax
import jax.numpy as jnp
from jax import lax
from jax.experimental import pallas as pl
from jax.experimental.pallas import tpu as pltpu
from jax.sharding import PartitionSpec as P

D = 768
HEADS = 24
HEADDIM = 64
NSTATE = 128
KCONV = 4
SPAN = 256
DIN = 1536
CONVW = 1792
ZXW = 3328
RIM = 16
HALF = 128
TILE = 256
PAIRS = 12
EPS = 1e-05

f32 = jnp.float32
bf16 = jnp.bfloat16
NT = (((1,), (1,)), ((), ()))
TN = (((0,), (0,)), ((), ()))
VMEM_LIMIT = 62 * 1024 * 1024


def mm(a, b):
    return jnp.dot(a, b, preferred_element_type=f32)


def mm_nt(a, b):
    return lax.dot_general(a, b, NT, preferred_element_type=f32)


def mm_tn(a, b):
    return lax.dot_general(a, b, TN, preferred_element_type=f32)


def halves(v):
    high = v.astype(bf16)
    return high, (v - high.astype(f32)).astype(bf16)


def head_map():
    rows = lax.broadcasted_iota(jnp.int32, (2 * HALF, DIN), 0) % HALF
    cols = lax.broadcasted_iota(jnp.int32, (2 * HALF, DIN), 1) // HEADDIM
    return jnp.where(rows == cols, 1.0, 0.0).astype(bf16)


def spread(v, sel):
    return mm(jnp.concatenate(halves(v), axis=1), sel[...])


def gather_heads(v, sel_part):
    high, low = halves(v)
    return mm_nt(high, sel_part) + mm_nt(low, sel_part)


def triangle(size, lower):
    rows = lax.broadcasted_iota(jnp.int32, (size, size), 0)
    cols = lax.broadcasted_iota(jnp.int32, (size, size), 1)
    keep = rows >= cols if lower else rows <= cols
    return jnp.where(keep, 1.0, 0.0).astype(f32)


def exact_mm(a, b):
    return jnp.dot(a, b, precision=lax.Precision.HIGHEST, preferred_element_type=f32)


def softplus(v):
    return jnp.maximum(v, 0.0) + jnp.log1p(jnp.exp(-jnp.abs(v)))


def sigmoid(v):
    return 1.0 / (1.0 + jnp.exp(-v))


def local_decays(cum):
    mid, end = cum[HALF - 1 : HALF], cum[SPAN - 1 : SPAN]
    rows = lax.broadcasted_iota(jnp.int32, (SPAN, 1), 0)
    first = rows < HALF
    start = jnp.where(first, 0.0, mid)
    stop = jnp.where(first, mid, end)
    return jnp.exp(cum - start), jnp.exp(stop - cum), jnp.exp(mid), jnp.exp(end - mid), jnp.exp(end)


def rows_of(v):
    return jnp.broadcast_to(v, (8, v.shape[1]))


def normalized(rows, gain):
    rows = rows.astype(f32)
    inv = lax.rsqrt(jnp.mean(rows * rows, axis=-1, keepdims=True) + EPS)
    return rows, inv, (rows * inv * gain).astype(bf16)


def remote(src, dst, send_sem, recv_sem, **where):
    return pltpu.make_async_remote_copy(
        src_ref=src, dst_ref=dst, send_sem=send_sem, recv_sem=recv_sem,
        device_id=where, device_id_type=pl.DeviceIdType.MESH,
    )


def loop(start, stop, body):
    def step(i, c):
        body(i)
        return c

    lax.fori_loop(start, stop, step, 0)


def meet(axes):
    barrier = pltpu.get_barrier_semaphore()
    total = 0
    for axis in axes:
        size = lax.axis_size(axis)
        me = lax.axis_index(axis)

        def greet(d):
            pl.semaphore_signal(
                barrier, inc=1, device_id={axis: lax.rem(me + d, size)}, device_id_type=pl.DeviceIdType.MESH
            )

        loop(1, size, greet)
        total += size - 1
    pl.semaphore_wait(barrier, total)


class Exchange:
    def __init__(self, count, buf, recv, back, out, sends, recvs, back_sends, back_recvs, own_sem):
        self.count = count
        self.parts = min(count, 8)
        self.stride = count // self.parts
        self.rows = NSTATE // self.parts
        self.me = lax.axis_index("ctx")
        self.mine = self.me // self.stride
        self.buf, self.recv, self.back, self.out = buf, recv, back, out
        self.sends, self.recvs, self.back_sends, self.back_recvs, self.own_sem = (
            sends, recvs, back_sends, back_recvs, own_sem,
        )

    def part(self, j):
        return pl.ds(pl.multiple_of(j * self.rows, self.rows), self.rows)

    def owners(self, body):
        if self.stride == 1:
            loop(1, self.parts, lambda d: body(lax.rem(self.mine + d, self.parts)))
        else:
            def step(d):
                j = lax.rem(self.mine + d, self.parts)
                pl.when(j * self.stride != self.me)(lambda: body(j))

            loop(0, self.parts, step)

    def if_owner(self, body):
        if self.stride == 1:
            body()
        else:
            pl.when(self.mine * self.stride == self.me)(body)

    def others(self, body):
        loop(1, self.count, lambda d: body(lax.rem(self.me + d, self.count)))

    def to_owner(self, s, j, sender):
        return remote(
            self.buf.at[s, self.part(j)], self.recv.at[s, sender], self.sends.at[s, j], self.recvs.at[s, sender],
            ctx=j * self.stride,
        )

    def to_block(self, s, b, j):
        return remote(
            self.back.at[s, b], self.out.at[s, self.part(j)], self.back_sends.at[s, b], self.back_recvs.at[s, j], ctx=b
        )

    def keep(self, s):
        return pltpu.make_async_copy(self.back.at[s, self.me], self.out.at[s, self.part(self.mine)], self.own_sem.at[s])

    def start(self, s):
        self.owners(lambda j: self.to_owner(s, j, self.me).start())

        def own():
            self.recv[s, self.me] = self.buf[s, self.part(self.mine), :]

        self.if_owner(own)

    def scan(self, s, decx, reverse):
        def run():
            self.others(lambda b: self.to_owner(s, self.mine, b).wait_recv())

            def block(k, carry):
                b = self.count - 1 - k if reverse else k
                self.back[s, b] = carry.astype(bf16)
                return decx[pl.ds(pl.multiple_of(b * 8, 8), 8), :][0:1] * carry + self.recv[s, b].astype(f32)

            lax.fori_loop(0, self.count, block, jnp.zeros((self.rows, DIN), f32))
            self.others(lambda b: self.to_block(s, b, self.mine).start())
            self.keep(s).start()

        self.if_owner(run)

    def finish(self, s):
        self.owners(lambda j: self.to_block(s, self.me, j).wait_recv())
        self.owners(lambda j: self.to_owner(s, j, self.me).wait_send())

        def own():
            self.others(lambda b: self.to_block(s, b, self.mine).wait_send())
            self.keep(s).wait()

        self.if_owner(own)


class Spread:
    def __init__(self, index, shard, full, cols, sems):
        self.index, self.shard, self.full, self.cols = index, shard, full, cols
        self.x_send, self.x_recv, self.m_send, self.m_recv, self.own = sems
        self.size = lax.axis_size("group")
        self.cores = 2 if self.size % 2 == 0 else 1
        self.chips = self.size // self.cores
        self.me = lax.axis_index("group")
        self.core = lax.rem(self.me, self.cores)
        self.chip = self.me // self.cores
        self.rows = shard.shape[0]

    def place(self, member):
        return self.full.at[pl.ds(pl.multiple_of(member * self.rows, 64), self.rows), self.cols]

    def source(self):
        return self.shard.at[:, self.cols]

    def across(self, d):
        peer = lax.rem(self.chip + d, self.chips) * self.cores + self.core
        return remote(
            self.source(), self.place(self.me), self.x_send.at[self.index, d], self.x_recv.at[self.index, d], group=peer
        )

    def mate(self, d):
        member = lax.rem(self.chip + self.chips - d, self.chips) * self.cores + self.core
        src = self.source() if d == 0 else self.place(member)
        return remote(
            src, self.place(member), self.m_send.at[self.index, d], self.m_recv.at[self.index, d],
            group=self.me + 1 - 2 * self.core,
        )

    def keep(self):
        return pltpu.make_async_copy(self.source(), self.place(self.me), self.own.at[self.index])

    def start(self):
        for d in range(1, self.chips):
            self.across(d).start()
        if self.cores == 2:
            self.mate(0).start()
        self.keep().start()

    def forward(self):
        for d in range(1, self.chips):
            self.across(d).wait_recv()
            if self.cores == 2:
                self.mate(d).start()

    def finish(self):
        self.keep().wait()
        if self.cores == 2:
            for d in range(self.chips):
                self.mate(d).wait_recv()

    def drain(self):
        for d in range(1, self.chips):
            self.across(d).wait_send()
        if self.cores == 2:
            for d in range(self.chips):
                self.mate(d).wait_send()


def masks():
    rows = lax.broadcasted_iota(jnp.int32, (HALF, HALF), 0)
    cols = lax.broadcasted_iota(jnp.int32, (HALF, HALF), 1)
    return rows >= cols, cols < HEADDIM


def both(q):
    return slice(q * HALF, (q + 1) * HALF)


def pair_decays(cum, cum_t, p, causal):
    rolled = pltpu.roll(cum, lax.rem(HALF - 2 * p, HALF), 1)
    out = []
    for q in range(2):
        for a in range(2):
            gaps = rolled[both(q), a : a + 1] - cum_t[q, pl.ds(2 * p + a, 1), :]
            out.append(jnp.exp(jnp.where(causal, gaps, -jnp.inf)))
    return out


def front_kernel(
    tok, tok_all, wcat, wout, gain, cw, cb, db, dl,
    normed, nhalo, cin, xb, vout, cumout, st0, loc, ylocal, gate, decs_out, wfull, wofull, sin,
    sel, halo, ext, ns, xs_s, cum_s, dt_s, cum_t, wv, wg, fexp, decs, decx, buf, recv, back,
    halo_sem, x_send, x_recv, m_send, m_recv, w_own, w_load, sends, recvs, back_sends, back_recvs, own_sem,
    dec_send, dec_recv,
):
    i = pl.program_id(0)
    seqs = tok_all.shape[0]
    count = lax.axis_size("ctx")
    me = lax.axis_index("ctx")
    ex = Exchange(count, buf, recv, back, sin, sends, recvs, back_sends, back_recvs, own_sem)
    sems = (x_send, x_recv, m_send, m_recv, w_own)
    conv_cols, gate_cols = pl.ds(DIN, CONVW + HALF), pl.ds(0, DIN)
    spreads = [
        Spread(0, wcat, wfull, conv_cols, sems),
        Spread(1, wcat, wfull, gate_cols, sems),
        Spread(2, wout, wofull, pl.ds(0, D), sems),
    ]
    halo_copy = remote(
        tok_all.at[:, pl.ds(SPAN - RIM, RIM), :], halo, halo_sem.at[0], halo_sem.at[1], ctx=lax.rem(me + 1, count)
    )
    load_v = pltpu.make_async_copy(wfull.at[:, conv_cols], wv, w_load.at[0])
    load_g = pltpu.make_async_copy(wfull.at[:, gate_cols], wg, w_load.at[1])

    def dec_copy(s, j, sender):
        rows = pl.ds(pl.multiple_of(sender * 8, 8), 8)
        return remote(
            decs.at[s, rows, :], decs.at[s, rows, :], dec_send.at[s, j], dec_recv.at[s, sender], ctx=j * ex.stride
        )

    @pl.when(i == 0)
    def _():
        meet(("ctx", "group"))
        pl.when(me < count - 1)(lambda: halo_copy.start())
        for sp in spreads:
            sp.start()
        sel[...] = head_map()

        @pl.when(me == 0)
        def _():
            halo[...] = jnp.zeros_like(halo)

        @pl.when(me > 0)
        def _():
            halo_copy.wait_recv()

        spreads[0].forward()
        spreads[0].finish()
        load_v.start()
        load_v.wait()

    @pl.when(i == 1)
    def _():
        spreads[1].forward()
        spreads[2].forward()

    @pl.when(i == seqs - 1)
    def _():
        spreads[1].finish()
        load_g.start()

    @pl.when(i < seqs)
    def _():
        s = i
        nh = normalized(halo[s], gain[...])[2]
        nm = normalized(tok[0], gain[...])[2]
        ext[0:RIM] = nh
        ext[RIM:] = nm
        ns[s] = nm
        nhalo[0] = nh
        normed[0] = nm
        v = mm(nm, wv[:, CONVW:]) + db[...]
        vout[0] = v
        dt = softplus(v)
        cum = exact_mm(triangle(SPAN, True), -jnp.exp(dl[...]) * dt)
        cumout[0] = cum
        cum_s[s] = cum
        dt_s[s] = dt
        e_in, e_out, tot0, tot1, total = local_decays(cum)
        decs[s, pl.ds(pl.multiple_of(me * 8, 8), 8), :] = rows_of(total)
        ex.owners(lambda j: dec_copy(s, j, me).start())
        fexp[...] = spread(dt * e_out, sel)
        tot1x = spread(rows_of(tot1), sel)[0:1]

        def conv_tile(c):
            cols = slice(c, c + TILE)
            cin[0, :, cols] = mm(ext[...], wv[:, cols])
            o = cb[:, cols]
            for k in range(KCONV):
                o = o + cw[k : k + 1, cols] * cin[0, RIM - KCONV + 1 + k : RIM - KCONV + 1 + k + SPAN, cols]
            a = o * sigmoid(o)
            low = a.astype(bf16)
            xb[0, :, cols] = low
            xs_s[s, :, cols] = low
            return a

        bc = conv_tile(DIN)
        bt = jnp.transpose(bc[:, :NSTATE]).astype(bf16)
        for j in range(DIN // TILE):
            c = j * TILE
            cols = slice(c, c + TILE)
            a = conv_tile(c)
            xw = (a * fexp[:, cols]).astype(bf16)
            s0 = mm(bt[:, :HALF], xw[:HALF])
            s1 = mm(bt[:, HALF:], xw[HALF:])
            st0[0, :, cols] = s0
            low = (tot1x[:, cols] * s0 + s1).astype(bf16)
            loc[0, :, cols] = low
            buf[s, :, cols] = low
        ex.start(s)

    def scan(s):
        ex.if_owner(lambda: ex.others(lambda b: dec_copy(s, ex.mine, b).wait_recv()))
        decx[...] = spread(decs[s], sel)
        ex.scan(s, decx, False)

    @pl.when(i == seqs)
    def _():
        load_g.wait()
        for s in range(seqs - 1):
            scan(s)

    @pl.when(i == seqs + 1)
    def _():
        scan(seqs - 1)

    @pl.when(i >= seqs)
    def _():
        s = i - seqs
        causal, low_lanes = masks()
        cum = cum_s[s]
        for q in range(2):
            cum_t[q] = jnp.transpose(cum[both(q)])
        fexp[...] = spread(dt_s[s], sel)
        bb = xs_s[s, :, DIN : DIN + NSTATE]
        cc = xs_s[s, :, DIN + NSTATE :]
        scores = [mm_nt(cc[both(q)], bb[both(q)]) for q in range(2)]

        def pair_step(p):
            cols = pl.ds(pl.multiple_of(p * HALF, HALF), HALF)
            decays = pair_decays(cum, cum_t, p, causal)
            for q in range(2):
                rows = both(q)
                m = jnp.concatenate([(decays[2 * q + a] * scores[q]).astype(bf16) for a in range(2)], axis=1)
                x = xs_s[s, rows, cols].astype(f32) * fexp[rows, cols]
                x = jnp.concatenate([jnp.where(low_lanes, x, 0.0), jnp.where(low_lanes, 0.0, x)], axis=0)
                ylocal[0, rows, cols] = mm(m, x.astype(bf16))

        loop(0, PAIRS, pair_step)
        for j in range(DIN // TILE):
            cols = slice(j * TILE, (j + 1) * TILE)
            gate[0, :, cols] = mm(ns[s], wg[:, cols])

    @pl.when(i == 2 * seqs - 1)
    def _():
        decs_out[...] = decs[...]
        for s in range(seqs):
            ex.finish(s)
            ex.owners(lambda j: dec_copy(s, j, me).wait_send())
        for sp in spreads[1:]:
            if sp.index == 2:
                sp.finish()
        for sp in spreads:
            sp.drain()
        pl.when(me < count - 1)(lambda: halo_copy.wait_send())


def middle_kernel(
    rel, tok, cot, ylocal, gate, xb, vin, cumin, st0, sin, decs, wout, skip, ggain,
    mixed, mlow, dyout, ggate, wred, dir1, gskip, gggain, dxs, dbc, later,
    sel, cum_t, einx, ys, gs, ss, s_in, dcs, dy_s, ml_s, g_s, dg_s, decx, buf, recv, back,
    sends, recvs, back_sends, back_recvs, own_sem,
):
    i = pl.program_id(0)
    seqs = dy_s.shape[0]
    count = lax.axis_size("ctx")
    ex = Exchange(count, buf, recv, back, later, sends, recvs, back_sends, back_recvs, own_sem)

    @pl.when(i == 0)
    def _():
        meet(("ctx",))
        sel[...] = head_map()
        gskip[...] = jnp.zeros_like(gskip)
        gggain[...] = jnp.zeros_like(gggain)

    @pl.when(i < seqs)
    def _():
        s = i
        cum = cumin[0]
        e_in, e_out, tot0, tot1, total = local_decays(cum)
        einx[...] = spread(e_in, sel)
        tot0x = spread(rows_of(tot0), sel)[0:1]
        s_in[0] = sin[0]
        s_in[1] = (tot0x * sin[0].astype(f32) + st0[0]).astype(bf16)
        cc = xb[0, :, DIN + NSTATE :]

        def gate_step(j, total_sq):
            cols = pl.ds(pl.multiple_of(j * TILE, TILE), TILE)
            for q in range(2):
                rows = both(q)
                ys[rows, cols] = ylocal[0, rows, cols] + einx[rows, cols] * mm(cc[rows], s_in[q, :, cols])
            y = ys[:, cols] + skip[:, cols] * xb[0, :, cols].astype(f32)
            g = gate[0, :, cols]
            gated = y * (g * sigmoid(g))
            gs[:, cols] = gated
            sq = gated * gated
            return total_sq + sq[:, :HALF] + sq[:, HALF:]

        sq = lax.fori_loop(0, DIN // TILE, gate_step, jnp.zeros((SPAN, HALF), f32))
        inv = lax.rsqrt(jnp.sum(sq, axis=1, keepdims=True) * (1.0 / DIN) + EPS)
        live = (lax.broadcasted_iota(jnp.int32, (SPAN, 1), 0) < rel[s]).astype(f32)
        drive = (live * cot[0].astype(f32)).astype(bf16)

        def back_step(j, acc):
            cols = pl.ds(pl.multiple_of(j * TILE, TILE), TILE)
            gm = mm_nt(drive, wout[cols, :])
            gated = gs[:, cols]
            unit = gated * inv
            low = (unit * ggain[:, cols]).astype(bf16)
            mlow[0, :, cols] = low
            ml_s[s, :, cols] = low
            gggain[:, cols] += jnp.sum(gm * unit, axis=0, keepdims=True)
            scaled = gm * ggain[:, cols]
            ss[:, cols] = scaled
            prod = scaled * gated
            return acc + prod[:, :HALF] + prod[:, HALF:]

        dots = lax.fori_loop(0, DIN // TILE, back_step, jnp.zeros((SPAN, HALF), f32))
        dots = jnp.sum(dots, axis=1, keepdims=True) * (1.0 / DIN)
        corr = inv * inv * inv * dots
        cct = jnp.transpose(cc.astype(f32)).astype(bf16)
        acc = jnp.zeros((SPAN, HALF), f32)
        dc = [jnp.zeros((HALF, HALF), f32) for _ in range(2)]
        for j in range(DIN // TILE):
            cols = slice(j * TILE, (j + 1) * TILE)
            g = gate[0, :, cols]
            sg = sigmoid(g)
            sl = g * sg
            grad_gated = inv * ss[:, cols] - gs[:, cols] * corr
            dy = grad_gated * sl
            yn = ys[:, cols]
            x = xb[0, :, cols].astype(f32)
            y = yn + skip[:, cols] * x
            ggate[0, :, cols] = (grad_gated * y * (sg + sl * (1.0 - sg))).astype(bf16)
            dyb = dy.astype(bf16)
            dyout[0, :, cols] = dyb
            dy_s[s, :, cols] = dyb
            gskip[:, cols] += jnp.sum(dy * x, axis=0, keepdims=True)
            acc = acc + gather_heads(dy * yn, sel[:HALF, cols])
            dye = (dy * einx[:, cols]).astype(bf16)
            d0 = mm(cct[:, :HALF], dye[:HALF])
            d1 = mm(cct[:, HALF:], dye[HALF:])
            dir1[0, :, cols] = d1
            buf[s, :, cols] = (d0 + tot0x[:, cols] * d1).astype(bf16)
            for q in range(2):
                dc[q] = dc[q] + mm_nt(dye[both(q)], s_in[q, :, cols])
        wred[0] = acc
        for q in range(2):
            dcs[s, both(q)] = dc[q]
        ex.start(s)

    def scan(s):
        decx[...] = spread(decs[s], sel)
        ex.scan(s, decx, True)

    @pl.when(i == seqs)
    def _():
        for s in range(seqs - 1):
            scan(s)

    @pl.when(i == seqs + 1)
    def _():
        scan(seqs - 1)

    @pl.when(i >= seqs)
    def _():
        s = i - seqs
        causal, low_lanes = masks()
        cum = cumin[0]
        for q in range(2):
            cum_t[q] = jnp.transpose(cum[both(q)])
        einx[...] = spread(softplus(vin[0]), sel)
        bb = xb[0, :, DIN : DIN + NSTATE]
        cc = xb[0, :, DIN + NSTATE :]
        for q in range(2):
            g_s[q] = mm_nt(cc[both(q)], bb[both(q)])
        dg_s[...] = jnp.zeros_like(dg_s)

        def pair_step(p):
            cols = pl.ds(pl.multiple_of(p * HALF, HALF), HALF)
            decays = pair_decays(cum, cum_t, p, causal)
            for q in range(2):
                rows = both(q)
                xsb = (xb[0, rows, cols].astype(f32) * einx[rows, cols]).astype(bf16)
                dyb = dy_s[s, rows, cols]
                dyf = dyb.astype(f32)
                grads = []
                for a in range(2):
                    m = (decays[2 * q + a] * g_s[q]).astype(bf16)
                    grads.append(mm_tn(m, dyb))
                    mine = low_lanes if a == 0 else jnp.logical_not(low_lanes)
                    dm = mm_nt(jnp.where(mine, dyf, 0.0).astype(bf16), xsb)
                    dg_s[q] += dm * decays[2 * q + a]
                dxs[0, rows, cols] = jnp.where(low_lanes, grads[0], grads[1])

        loop(0, PAIRS, pair_step)
        for q in range(2):
            rows = both(q)
            dg = dg_s[q].astype(bf16)
            dbc[0, rows, :NSTATE] = mm_tn(dg, cc[rows])
            dbc[0, rows, NSTATE:] = mm(dg, bb[rows]) + dcs[s, rows]
        live = (lax.broadcasted_iota(jnp.int32, (SPAN, 1), 0) < rel[s]).astype(f32)
        for j in range(D // TILE):
            cols = slice(j * TILE, (j + 1) * TILE)
            mixed[0, :, cols] = (live * (tok[0, :, cols].astype(f32) + mm(ml_s[s], wout[:, cols]))).astype(bf16)

    @pl.when(i == 2 * seqs - 1)
    def _():
        for s in range(seqs):
            ex.finish(s)


def third_kernel(
    cin, vin, cumin, dyin, wred, dxs, dbc, dir1, later, sin, loc, cw, cb, dl, skip,
    gz, gzh, gdelta, gcw, gcb, gdb, gdl,
    sel, dtx, eoutx, xx, sp, dact, xwb, dout, qacc, gp,
):
    s = pl.program_id(0)

    @pl.when(s == 0)
    def _():
        sel[...] = head_map()
        gcw[...] = jnp.zeros_like(gcw)
        gcb[...] = jnp.zeros_like(gcb)
        gdb[...] = jnp.zeros_like(gdb)
        gdl[...] = jnp.zeros_like(gdl)
        gp[0:RIM] = jnp.zeros((RIM, CONVW), f32)
        gp[RIM + SPAN :] = jnp.zeros((8, CONVW), f32)

    cum = cumin[0]
    v = vin[0]
    dt = softplus(v)
    e_in, e_out, tot0, tot1, total = local_decays(cum)
    dtx[...] = spread(dt, sel)
    eoutx[...] = spread(e_out, sel)
    tot1x = spread(rows_of(tot1), sel)[0:1]
    totalx = spread(rows_of(total), sel)[0:1]

    def conv_step(j):
        cols = pl.ds(pl.multiple_of(j * HALF, HALF), HALF)
        o = cb[:, cols]
        for k in range(KCONV):
            o = o + cw[k : k + 1, cols] * cin[0, RIM - KCONV + 1 + k : RIM - KCONV + 1 + k + SPAN, cols]
        sg = sigmoid(o)
        a = o * sg
        xx[:, cols] = a
        sp[:, cols] = sg + a * (1.0 - sg)

    loop(0, CONVW // HALF, conv_step)
    bb = xx[:, DIN : DIN + NSTATE].astype(bf16)
    qacc[...] = jnp.zeros_like(qacc)
    dout[1] = later[0]
    dout[0] = (dir1[0] + tot1x * later[0].astype(f32)).astype(bf16)

    def state_step(j):
        cols = pl.ds(pl.multiple_of(j * TILE, TILE), TILE)
        for q in range(2):
            rows = both(q)
            x = xx[rows, cols]
            dte = dtx[rows, cols]
            eo = eoutx[rows, cols]
            dx_s = dxs[0, rows, cols] + eo * mm(bb[rows], dout[q, :, cols])
            dact[rows, cols] = dte * dx_s + skip[:, cols] * dyin[0, rows, cols].astype(f32)
            qacc[rows] += gather_heads(x * dx_s, sel[:HALF, cols])
            xwb[rows, cols] = (x * dte * eo).astype(bf16)

    loop(0, DIN // TILE, state_step)
    for q in range(2):
        rows = both(q)
        dact[rows, DIN : DIN + NSTATE] = dbc[0, rows, :NSTATE] + mm_nt(xwb[rows, :], dout[q])
        dact[rows, DIN + NSTATE :] = dbc[0, rows, NSTATE:]

    ends = jnp.sum(later[0].astype(f32) * (totalx * sin[0].astype(f32) + loc[0].astype(f32)), axis=0, keepdims=True)
    ends = gather_heads(rows_of(ends), sel[:HALF])[0:1]
    at_end = lax.broadcasted_iota(jnp.int32, (SPAN, 1), 0) == SPAN - 1
    dcum = wred[0] - dt * qacc[...] + jnp.where(at_end, ends, 0.0)
    glog = exact_mm(triangle(SPAN, False), dcum)
    rate = jnp.exp(dl[...])
    gpd = (qacc[...] - rate * glog) * sigmoid(v)
    lanes = lax.broadcasted_iota(jnp.int32, (SPAN, HALF), 1) < HEADS
    gpd = jnp.where(lanes, gpd, 0.0)
    gdelta[0] = gpd.astype(bf16)
    gdb[...] += jnp.sum(gpd, axis=0, keepdims=True)
    gdl[...] += -rate * jnp.sum(dt * glog, axis=0, keepdims=True)

    def out_step(j):
        cols = pl.ds(pl.multiple_of(j * HALF, HALF), HALF)
        gco = dact[:, cols] * sp[:, cols]
        gp[RIM : RIM + SPAN, cols] = gco
        gcb[:, cols] += jnp.sum(gco, axis=0, keepdims=True)
        for k in range(KCONV):
            gcw[k : k + 1, cols] += jnp.sum(
                gco * cin[0, RIM - KCONV + 1 + k : RIM - KCONV + 1 + k + SPAN, cols], axis=0, keepdims=True
            )
        main = jnp.zeros((SPAN, HALF), f32)
        rim = jnp.zeros((RIM, HALF), f32)
        for k in range(KCONV):
            ahead = KCONV - 1 - k
            main = main + cw[k : k + 1, cols] * gp[RIM + ahead : RIM + ahead + SPAN, cols]
            rim = rim + cw[k : k + 1, cols] * gp[ahead : ahead + RIM, cols]
        gz[0, :, cols] = main.astype(bf16)
        gzh[0, :, cols] = rim.astype(bf16)

    loop(0, CONVW // HALF, out_step)


def fourth_kernel(
    rel, tok, halo, cot, gain, ggate, gz, gzh, gdelta, wfull,
    gtok, gtail, grim, ggain,
):
    s = pl.program_id(0)

    @pl.when(s == 0)
    def _():
        ggain[...] = jnp.zeros_like(ggain)

    def back(rows, grad):
        rows, inv, _ = normalized(rows, gain[...])
        ggain[...] += jnp.sum(grad * rows * inv, axis=0, keepdims=True)
        gained = gain[...] * grad
        mean = jnp.mean(gained * rows, axis=-1, keepdims=True)
        return inv * gained - rows * (inv * inv * inv * mean)

    grad = mm_nt(ggate[0], wfull[:, :DIN]) + mm_nt(gz[0], wfull[:, DIN:ZXW]) + mm_nt(gdelta[0], wfull[:, ZXW:])
    live = (lax.broadcasted_iota(jnp.int32, (SPAN, 1), 0) < rel[s]).astype(f32)
    out = live * cot[0].astype(f32) + back(tok[0], grad)
    gtok[0] = out.astype(bf16)
    gtail[0] = out[SPAN - RIM :]
    grim[0] = back(halo[0], mm_nt(gzh[0], wfull[:, DIN:ZXW])).astype(bf16)


def whole(shape):
    zeros = (0,) * len(shape)
    return pl.BlockSpec(shape, lambda s: zeros, pipeline_mode=pl.Buffered(1))


def summed(shape):
    zeros = (0,) * len(shape)
    return pl.BlockSpec(shape, lambda s: zeros)


def per_seq(*shape):
    zeros = (0,) * len(shape)
    return pl.BlockSpec((1,) + shape, lambda s: (s,) + zeros)


SMEM = pl.BlockSpec(memory_space=pltpu.SMEM)
ANY = pl.BlockSpec(memory_space=pl.ANY)


def staged(seqs, phase, *shape):
    zeros = (0,) * len(shape)
    if phase == 0:
        return pl.BlockSpec((1,) + shape, lambda i: (jnp.minimum(i, seqs - 1),) + zeros)
    if phase == 1:
        return pl.BlockSpec((1,) + shape, lambda i: (jnp.maximum(i - seqs, 0),) + zeros)
    return pl.BlockSpec((1,) + shape, lambda i: (lax.rem(i, seqs),) + zeros)


def call(kernel, steps, in_specs, outs, scratch, name, collective=None):
    params = dict(vmem_limit_bytes=VMEM_LIMIT)
    if collective is not None:
        params.update(collective_id=collective, has_side_effects=True)
    return pl.pallas_call(
        kernel,
        grid=(steps,),
        in_specs=in_specs,
        out_specs=[o[0] for o in outs],
        out_shape=[jax.ShapeDtypeStruct(o[1], o[2]) for o in outs],
        scratch_shapes=[pltpu.VMEM(*sc) if isinstance(sc, tuple) else sc for sc in scratch],
        compiler_params=pltpu.CompilerParams(**params),
        name=name,
    )


def exchange_scratch(seqs, count):
    parts = min(count, 8)
    rows = NSTATE // parts
    dma = pltpu.SemaphoreType.DMA
    buffers = [((count * 8, DIN), f32), ((seqs, NSTATE, DIN), bf16), ((seqs, count, rows, DIN), bf16),
               ((seqs, count, rows, DIN), bf16)]
    sems = [dma((seqs, parts)), dma((seqs, count)), dma((seqs, count)), dma((seqs, parts)), dma((seqs,))]
    return buffers, sems


def passed_along(value, axis, steps):
    count = lax.axis_size(axis)
    leading, last = (max(0, -steps), min(count, count - steps))
    return lax.ppermute(value, axis, [(source, source + steps) for source in range(leading, last)])


def lanes_of(v):
    return jnp.pad(v[None, :], ((0, 0), (0, HALF - v.shape[0])))


def local(
    tokens_in, seq_lengths, norm_gain, w_zx, w_delta, w_out, conv_weight, conv_bias,
    delta_bias, decay_log, skip_gain, gated_gain, cotangent,
):
    seqs = tokens_in.shape[0]
    count = lax.axis_size("ctx")
    group = lax.axis_size("group")
    chips = max(group // 2, 1)
    rel = seq_lengths - lax.axis_index("ctx") * SPAN
    gain = norm_gain[None, :]
    cb = conv_bias[None, :]
    db = lanes_of(delta_bias)
    dl = lanes_of(decay_log)
    skip = jnp.repeat(skip_gain, HEADDIM)[None, :]
    ggain = gated_gain[None, :]
    wcat = jnp.concatenate([w_zx, jnp.pad(w_delta, ((0, 0), (0, HALF - HEADS)))], axis=1)
    buffers, sems = exchange_scratch(seqs, count)
    dma = pltpu.SemaphoreType.DMA
    at0 = lambda *shape: staged(seqs, 0, *shape)
    at1 = lambda *shape: staged(seqs, 1, *shape)
    at01 = lambda *shape: staged(seqs, 2, *shape)

    normed, nhalo, cin, xb, vraw, cum, st0, loc, ylocal, gate, decs, wfull, wofull, state_in = call(
        front_kernel,
        2 * seqs,
        [at0(SPAN, D), ANY, ANY, ANY, whole((1, D)), whole((KCONV, CONVW)), whole((1, CONVW)), whole((1, HALF)),
         whole((1, HALF))],
        [
            (at0(SPAN, D), (seqs, SPAN, D), bf16),
            (at0(RIM, D), (seqs, RIM, D), bf16),
            (at0(RIM + SPAN, CONVW), (seqs, RIM + SPAN, CONVW), f32),
            (at0(SPAN, CONVW), (seqs, SPAN, CONVW), bf16),
            (at0(SPAN, HALF), (seqs, SPAN, HALF), f32),
            (at0(SPAN, HALF), (seqs, SPAN, HALF), f32),
            (at0(NSTATE, DIN), (seqs, NSTATE, DIN), f32),
            (at0(NSTATE, DIN), (seqs, NSTATE, DIN), bf16),
            (at1(SPAN, DIN), (seqs, SPAN, DIN), f32),
            (at1(SPAN, DIN), (seqs, SPAN, DIN), f32),
            (summed((seqs, count * 8, HALF)), (seqs, count * 8, HALF), f32),
            (ANY, (D, ZXW + HALF), bf16),
            (ANY, (DIN, D), bf16),
            (ANY, (seqs, NSTATE, DIN), bf16),
        ],
        [((2 * HALF, DIN), bf16), ((seqs, RIM, D), bf16), ((RIM + SPAN, D), bf16), ((seqs, SPAN, D), bf16),
         ((seqs, SPAN, CONVW), bf16), ((seqs, SPAN, HALF), f32), ((seqs, SPAN, HALF), f32), ((2, HALF, HALF), f32),
         ((D, CONVW + HALF), bf16), ((D, DIN), bf16), ((SPAN, DIN), f32), ((seqs, count * 8, HALF), f32)]
        + buffers
        + [dma((2,)), dma((3, chips)), dma((3, chips)), dma((3, chips)), dma((3, chips)), dma((3,)), dma((2,))]
        + sems
        + [dma((seqs, min(count, 8))), dma((seqs, count))],
        "front",
        0,
    )(tokens_in, tokens_in, wcat, w_out, gain, conv_weight, cb, db, dl)

    mixed_out, mlow, dy, ggate, wred, dir1, gskip, gggain, dxs, dbc, later = call(
        middle_kernel,
        2 * seqs,
        [SMEM, at1(SPAN, D), at0(SPAN, D), at0(SPAN, DIN), at0(SPAN, DIN), at01(SPAN, CONVW), at01(SPAN, HALF),
         at01(SPAN, HALF), at0(NSTATE, DIN), at0(NSTATE, DIN), whole((seqs, count * 8, HALF)), whole((DIN, D)),
         whole((1, DIN)), whole((1, DIN))],
        [
            (at1(SPAN, D), (seqs, SPAN, D), bf16),
            (at0(SPAN, DIN), (seqs, SPAN, DIN), bf16),
            (at0(SPAN, DIN), (seqs, SPAN, DIN), bf16),
            (at0(SPAN, DIN), (seqs, SPAN, DIN), bf16),
            (at0(SPAN, HALF), (seqs, SPAN, HALF), f32),
            (at0(NSTATE, DIN), (seqs, NSTATE, DIN), f32),
            (summed((1, DIN)), (1, DIN), f32),
            (summed((1, DIN)), (1, DIN), f32),
            (at1(SPAN, DIN), (seqs, SPAN, DIN), f32),
            (at1(SPAN, 2 * NSTATE), (seqs, SPAN, 2 * NSTATE), f32),
            (ANY, (seqs, NSTATE, DIN), bf16),
        ],
        [((2 * HALF, DIN), bf16), ((2, HALF, HALF), f32), ((SPAN, DIN), f32), ((SPAN, DIN), f32), ((SPAN, DIN), f32),
         ((SPAN, DIN), f32), ((2, NSTATE, DIN), bf16), ((seqs, SPAN, HALF), f32), ((seqs, SPAN, DIN), bf16),
         ((seqs, SPAN, DIN), bf16), ((2, HALF, HALF), f32), ((2, HALF, HALF), f32)]
        + buffers
        + sems,
        "middle",
        1,
    )(rel, tokens_in, cotangent, ylocal, gate, xb, vraw, cum, st0, state_in, decs, wofull, skip, ggain)

    gz, gzh, gdelta, gcw, gcb, gdb, gdl = call(
        third_kernel,
        seqs,
        [per_seq(RIM + SPAN, CONVW), per_seq(SPAN, HALF), per_seq(SPAN, HALF), per_seq(SPAN, DIN), per_seq(SPAN, HALF),
         per_seq(SPAN, DIN), per_seq(SPAN, 2 * NSTATE), per_seq(NSTATE, DIN), per_seq(NSTATE, DIN), per_seq(NSTATE, DIN),
         per_seq(NSTATE, DIN), whole((KCONV, CONVW)), whole((1, CONVW)), whole((1, HALF)), whole((1, DIN))],
        [
            (per_seq(SPAN, CONVW), (seqs, SPAN, CONVW), bf16),
            (per_seq(RIM, CONVW), (seqs, RIM, CONVW), bf16),
            (per_seq(SPAN, HALF), (seqs, SPAN, HALF), bf16),
            (summed((KCONV, CONVW)), (KCONV, CONVW), f32),
            (summed((1, CONVW)), (1, CONVW), f32),
            (summed((1, HALF)), (1, HALF), f32),
            (summed((1, HALF)), (1, HALF), f32),
        ],
        [((2 * HALF, DIN), bf16), ((SPAN, DIN), f32), ((SPAN, DIN), f32), ((SPAN, CONVW), f32), ((SPAN, CONVW), f32),
         ((SPAN, CONVW), f32), ((SPAN, DIN), bf16), ((2, NSTATE, DIN), bf16), ((SPAN, HALF), f32),
         ((RIM + SPAN + 8, CONVW), f32)],
        "third",
    )(cin, vraw, cum, dy, wred, dxs, dbc, dir1, later, state_in, loc, conv_weight, cb, dl, skip)

    live = (jnp.arange(SPAN, dtype=jnp.int32)[None, :] < rel[:, None]).astype(f32)[:, :, None]
    drive = (live * cotangent.astype(f32)).astype(bf16)
    flat = lambda v: v.reshape(-1, v.shape[-1])
    g_out = mm_tn(flat(mlow), flat(drive))
    g_gate = mm_tn(flat(normed), flat(ggate))
    g_conv = mm_tn(flat(normed), flat(gz)) + mm_tn(flat(nhalo), flat(gzh))
    g_delta = mm_tn(flat(normed), flat(gdelta))

    halo = passed_along(tokens_in[:, SPAN - RIM :, :], "ctx", 1)
    gtok, gtail, grim, g_gain = call(
        fourth_kernel,
        seqs,
        [SMEM, per_seq(SPAN, D), per_seq(RIM, D), per_seq(SPAN, D), whole((1, D)), per_seq(SPAN, DIN), per_seq(SPAN, CONVW),
         per_seq(RIM, CONVW), per_seq(SPAN, HALF), whole((D, ZXW + HALF))],
        [
            (per_seq(SPAN, D), (seqs, SPAN, D), bf16),
            (per_seq(RIM, D), (seqs, RIM, D), f32),
            (per_seq(RIM, D), (seqs, RIM, D), bf16),
            (summed((1, D)), (1, D), f32),
        ],
        [],
        "fourth",
    )(rel, tokens_in, halo, cotangent, gain, ggate, gz, gzh, gdelta, wfull)
    grim = passed_along(grim, "ctx", -1)
    gtok = lax.dynamic_update_slice(gtok, (gtail + grim.astype(f32)).astype(bf16), (0, SPAN - RIM, 0))

    def reduced(g):
        part = lax.psum_scatter(g.astype(bf16), "group", scatter_dimension=0, tiled=True)
        return lax.psum(part, "ctx").astype(f32)

    g_zx = jnp.concatenate([reduced(g_gate), reduced(g_conv)], axis=1)
    g_out = reduced(g_out)
    g_delta = reduced(g_delta)[:, :HEADS]
    small = jnp.concatenate(
        [g_gain.reshape(-1), gcw.reshape(-1), gcb.reshape(-1), gdb[0], gdl[0],
         gskip.reshape(-1), gggain.reshape(-1)]
    )
    small = lax.psum(small, ("group", "ctx"))
    at = 0
    pieces = []
    for size in (D, KCONV * CONVW, CONVW, HALF, HALF, DIN, DIN):
        pieces.append(small[at : at + size])
        at += size
    return (
        mixed_out, gtok, pieces[0], g_zx, g_delta, g_out, pieces[1].reshape(KCONV, CONVW), pieces[2],
        pieces[3][:HEADS], pieces[4][:HEADS], pieces[5].reshape(HEADS, HEADDIM).sum(1), pieces[6],
    )


def solution(mesh):
    rows = P("group", "ctx", None)
    own = P("group", None)
    in_specs = (rows, P("group"), P(), own, own, own, P(), P(), P(), P(), P(), P(), rows)
    out_specs = (rows, rows, P(), own, own, own, P(), P(), P(), P(), P(), P())
    return jax.shard_map(local, mesh=mesh, in_specs=in_specs, out_specs=out_specs, check_vma=False)
```

```python
import jax
import jax.numpy as jnp
from jax import lax
from jax.experimental import pallas as pl
from jax.experimental.pallas import tpu as pltpu
from jax.sharding import PartitionSpec as P

D = 768
HEADS = 24
HEADDIM = 64
NSTATE = 128
KCONV = 4
SPAN = 256
DIN = 1536
CONVW = 1792
ZXW = 3328
RIM = 16
HALF = 128
TILE = 256
PAIRS = 12
EPS = 1e-05

f32 = jnp.float32
bf16 = jnp.bfloat16
NT = (((1,), (1,)), ((), ()))
TN = (((0,), (0,)), ((), ()))
VMEM_LIMIT = 62 * 1024 * 1024
GATE_CHUNK = 512
OUT_CHUNK = 256
CONV_CHUNK = 512
GZW = 2048


def mm(a, b):
    return jnp.dot(a, b, preferred_element_type=f32)


def mm_nt(a, b):
    return lax.dot_general(a, b, NT, preferred_element_type=f32)


def mm_tn(a, b):
    return lax.dot_general(a, b, TN, preferred_element_type=f32)


def halves(v):
    high = v.astype(bf16)
    return high, (v - high.astype(f32)).astype(bf16)


def head_map():
    rows = lax.broadcasted_iota(jnp.int32, (2 * HALF, DIN), 0) % HALF
    cols = lax.broadcasted_iota(jnp.int32, (2 * HALF, DIN), 1) // HEADDIM
    return jnp.where(rows == cols, 1.0, 0.0).astype(bf16)


def spread(v, sel):
    return mm(jnp.concatenate(halves(v), axis=1), sel[...])


def gather_heads(v, sel_part):
    high, low = halves(v)
    return mm_nt(high, sel_part) + mm_nt(low, sel_part)


def triangle(size, lower):
    rows = lax.broadcasted_iota(jnp.int32, (size, size), 0)
    cols = lax.broadcasted_iota(jnp.int32, (size, size), 1)
    keep = rows >= cols if lower else rows <= cols
    return jnp.where(keep, 1.0, 0.0).astype(f32)


def exact_mm(a, b):
    return jnp.dot(a, b, precision=lax.Precision.HIGHEST, preferred_element_type=f32)


def softplus(v):
    return jnp.maximum(v, 0.0) + jnp.log1p(jnp.exp(-jnp.abs(v)))


def sigmoid(v):
    return 1.0 / (1.0 + jnp.exp(-v))


def local_decays(cum):
    mid, end = cum[HALF - 1 : HALF], cum[SPAN - 1 : SPAN]
    rows = lax.broadcasted_iota(jnp.int32, (SPAN, 1), 0)
    first = rows < HALF
    start = jnp.where(first, 0.0, mid)
    stop = jnp.where(first, mid, end)
    return jnp.exp(cum - start), jnp.exp(stop - cum), jnp.exp(mid), jnp.exp(end - mid), jnp.exp(end)


def rows_of(v):
    return jnp.broadcast_to(v, (8, v.shape[1]))


def normalized(rows, gain):
    rows = rows.astype(f32)
    inv = lax.rsqrt(jnp.mean(rows * rows, axis=-1, keepdims=True) + EPS)
    return rows, inv, (rows * inv * gain).astype(bf16)


def remote(src, dst, send_sem, recv_sem, **where):
    return pltpu.make_async_remote_copy(
        src_ref=src, dst_ref=dst, send_sem=send_sem, recv_sem=recv_sem,
        device_id=where, device_id_type=pl.DeviceIdType.MESH,
    )


def loop(start, stop, body):
    def step(i, c):
        body(i)
        return c

    lax.fori_loop(start, stop, step, 0)


def meet(axes):
    barrier = pltpu.get_barrier_semaphore()
    total = 0
    for axis in axes:
        size = lax.axis_size(axis)
        me = lax.axis_index(axis)

        def greet(d):
            pl.semaphore_signal(
                barrier, inc=1, device_id={axis: lax.rem(me + d, size)}, device_id_type=pl.DeviceIdType.MESH
            )

        loop(1, size, greet)
        total += size - 1
    pl.semaphore_wait(barrier, total)


class Exchange:
    def __init__(self, count, buf, recv, back, out, sends, recvs, back_sends, back_recvs, own_sem):
        self.count = count
        self.parts = min(count, 8)
        self.stride = count // self.parts
        self.rows = NSTATE // self.parts
        self.me = lax.axis_index("ctx")
        self.mine = self.me // self.stride
        self.buf, self.recv, self.back, self.out = buf, recv, back, out
        self.sends, self.recvs, self.back_sends, self.back_recvs, self.own_sem = (
            sends, recvs, back_sends, back_recvs, own_sem,
        )

    def part(self, j):
        return pl.ds(pl.multiple_of(j * self.rows, self.rows), self.rows)

    def owners(self, body):
        if self.stride == 1:
            loop(1, self.parts, lambda d: body(lax.rem(self.mine + d, self.parts)))
        else:
            def step(d):
                j = lax.rem(self.mine + d, self.parts)
                pl.when(j * self.stride != self.me)(lambda: body(j))

            loop(0, self.parts, step)

    def if_owner(self, body):
        if self.stride == 1:
            body()
        else:
            pl.when(self.mine * self.stride == self.me)(body)

    def others(self, body):
        loop(1, self.count, lambda d: body(lax.rem(self.me + d, self.count)))

    def to_owner(self, s, j, sender):
        return remote(
            self.buf.at[s, self.part(j)], self.recv.at[s, sender], self.sends.at[s, j], self.recvs.at[s, sender],
            ctx=j * self.stride,
        )

    def to_block(self, s, b, j):
        return remote(
            self.back.at[s, b], self.out.at[s, self.part(j)], self.back_sends.at[s, b], self.back_recvs.at[s, j], ctx=b
        )

    def keep(self, s):
        return pltpu.make_async_copy(self.back.at[s, self.me], self.out.at[s, self.part(self.mine)], self.own_sem.at[s])

    def start(self, s):
        self.owners(lambda j: self.to_owner(s, j, self.me).start())

        def own():
            self.recv[s, self.me] = self.buf[s, self.part(self.mine), :]

        self.if_owner(own)

    def scan(self, s, decx, reverse):
        def run():
            self.others(lambda b: self.to_owner(s, self.mine, b).wait_recv())

            def block(k, carry):
                b = self.count - 1 - k if reverse else k
                self.back[s, b] = carry.astype(bf16)
                return decx[pl.ds(pl.multiple_of(b * 8, 8), 8), :][0:1] * carry + self.recv[s, b].astype(f32)

            lax.fori_loop(0, self.count, block, jnp.zeros((self.rows, DIN), f32))
            self.others(lambda b: self.to_block(s, b, self.mine).start())
            self.keep(s).start()

        self.if_owner(run)

    def finish(self, s):
        self.owners(lambda j: self.to_block(s, self.me, j).wait_recv())
        self.owners(lambda j: self.to_owner(s, j, self.me).wait_send())

        def own():
            self.others(lambda b: self.to_block(s, b, self.mine).wait_send())
            self.keep(s).wait()

        self.if_owner(own)


class Spread:
    def __init__(self, index, shard, full, cols, sems):
        self.index, self.shard, self.full, self.cols = index, shard, full, cols
        self.x_send, self.x_recv, self.m_send, self.m_recv, self.own = sems
        self.size = lax.axis_size("group")
        self.cores = 2 if self.size % 2 == 0 else 1
        self.chips = self.size // self.cores
        self.me = lax.axis_index("group")
        self.core = lax.rem(self.me, self.cores)
        self.chip = self.me // self.cores
        self.rows = shard.shape[0]

    def place(self, member):
        return self.full.at[pl.ds(pl.multiple_of(member * self.rows, 64), self.rows), self.cols]

    def source(self):
        return self.shard.at[:, self.cols]

    def across(self, d):
        peer = lax.rem(self.chip + d, self.chips) * self.cores + self.core
        return remote(
            self.source(), self.place(self.me), self.x_send.at[self.index, d], self.x_recv.at[self.index, d], group=peer
        )

    def mate(self, d):
        member = lax.rem(self.chip + self.chips - d, self.chips) * self.cores + self.core
        src = self.source() if d == 0 else self.place(member)
        return remote(
            src, self.place(member), self.m_send.at[self.index, d], self.m_recv.at[self.index, d],
            group=self.me + 1 - 2 * self.core,
        )

    def keep(self):
        return pltpu.make_async_copy(self.source(), self.place(self.me), self.own.at[self.index])

    def start(self):
        for d in range(1, self.chips):
            self.across(d).start()
        if self.cores == 2:
            self.mate(0).start()
        self.keep().start()

    def forward(self):
        for d in range(1, self.chips):
            self.across(d).wait_recv()
            if self.cores == 2:
                self.mate(d).start()

    def finish(self):
        self.keep().wait()
        if self.cores == 2:
            for d in range(self.chips):
                self.mate(d).wait_recv()

    def drain(self):
        for d in range(1, self.chips):
            self.across(d).wait_send()
        if self.cores == 2:
            for d in range(self.chips):
                self.mate(d).wait_send()


def owner_count(rows, width, by_rows, outer):
    fits = lambda n: (rows // 2) % (16 * n) == 0 if by_rows else width % (128 * n) == 0
    return max(n for n in (1, 2, 4) if outer % n == 0 and fits(n))


class Reducer:
    def __init__(self, part, out, rows, width, by_rows, bufs, sems):
        self.part, self.out, self.rows, self.width, self.by_rows = part, out, rows, width, by_rows
        self.m_buf, self.x_src, self.x_buf, self.y_src, self.y_buf, self.z_src, self.z_buf, self.full = bufs
        self.sems = sems
        self.chunks = part.shape[1] // width
        self.group = lax.axis_index("group")
        self.cores = 2
        self.chips = lax.axis_size("group") // 2
        self.core = lax.rem(self.group, 2)
        self.chip = self.group // 2
        self.ctx = lax.axis_index("ctx")
        self.outer = lax.axis_size("ctx") // 2
        self.owners = owner_count(rows, width, by_rows, self.outer)
        self.stride = self.outer // self.owners
        self.inner = lax.rem(self.ctx, 2)
        self.line = self.ctx // 2
        self.mine = self.line // self.stride
        self.half = rows // 2

    def cols(self, k):
        return pl.ds(pl.multiple_of(k * self.width, self.width), self.width)

    def member(self, chip, core):
        return pl.ds(pl.multiple_of((chip * 2 + core) * self.rows, 64), self.rows)

    def half_rows(self, inner):
        return pl.ds(pl.multiple_of(inner * self.half, 16), self.half)

    def piece(self, j, base):
        if self.by_rows:
            n = self.half // self.owners
            return pl.ds(pl.multiple_of(base + j * n, 16), n), pl.ds(0, self.width)
        n = self.width // self.owners
        return pl.ds(pl.multiple_of(base, 16), self.half), pl.ds(pl.multiple_of(j * n, 128), n)

    def m_copy(self, k, chip):
        return remote(
            self.part.at[self.member(chip, 1 - self.core), self.cols(k)], self.m_buf.at[k, chip],
            self.sems.at[0, k, chip], self.sems.at[1, k, chip], group=self.group + 1 - 2 * self.core,
        )

    def x_copy(self, k, chip, sender):
        return remote(
            self.x_src.at[k, chip], self.x_buf.at[k, sender], self.sems.at[2, k, chip], self.sems.at[3, k, sender],
            group=chip * 2 + self.core,
        )

    def y_copy(self, k):
        return remote(
            self.y_src.at[k, self.half_rows(1 - self.inner)], self.y_buf.at[k], self.sems.at[4, k, 0], self.sems.at[5, k, 0],
            ctx=self.ctx + 1 - 2 * self.inner,
        )

    def z_copy(self, k, j, sender):
        rows, cols = self.piece(j, 0)
        return remote(
            self.z_src.at[k, rows, cols], self.z_buf.at[k, sender], self.sems.at[6, k, j], self.sems.at[7, k, sender],
            ctx=j * self.stride * 2 + self.inner,
        )

    def b_copy(self, k, line, j):
        rows, cols = self.piece(j, self.inner * self.half)
        return remote(
            self.full.at[k, rows, cols], self.full.at[k, rows, cols], self.sems.at[8, k, line], self.sems.at[9, k, j],
            ctx=line * 2 + self.inner,
        )

    def f_copy(self, k, inner):
        rows = self.half_rows(inner)
        return remote(
            self.full.at[k, rows], self.full.at[k, rows], self.sems.at[10, k, 0], self.sems.at[11, k, 0],
            ctx=self.ctx + 1 - 2 * self.inner,
        )

    def other_chips(self, body):
        for d in range(1, self.chips):
            body(lax.rem(self.chip + d, self.chips))

    def other_owners(self, body):
        if self.stride == 1:
            for d in range(1, self.owners):
                body(lax.rem(self.mine + d, self.owners))
        else:
            for j in range(self.owners):
                pl.when(j * self.stride != self.line)(lambda j=j: body(j))

    def other_lines(self, body):
        loop(1, self.outer, lambda d: body(lax.rem(self.line + d, self.outer)))

    def if_owner(self, body):
        if self.stride == 1:
            body()
        else:
            pl.when(self.mine * self.stride == self.line)(body)

    def m_start(self, k):
        for chip in range(self.chips):
            self.m_copy(k, chip).start()

    def m_done(self, k):
        for chip in range(self.chips):
            self.m_copy(k, chip).wait_recv()
            own = self.part[self.member(chip, self.core), self.cols(k)].astype(f32)
            self.x_src[k, chip] = (own + self.m_buf[k, chip].astype(f32)).astype(bf16)
        self.other_chips(lambda chip: self.x_copy(k, chip, self.chip).start())

    def x_done(self, k):
        total = self.x_src[k, self.chip].astype(f32)
        for d in range(1, self.chips):
            chip = lax.rem(self.chip + d, self.chips)
            self.x_copy(k, chip, chip).wait_recv()
            total = total + self.x_buf[k, chip].astype(f32)
        self.y_src[k] = total.astype(bf16)
        self.y_copy(k).start()

    def y_done(self, k):
        self.y_copy(k).wait_recv()
        own = self.y_src[k, self.half_rows(self.inner), :].astype(f32)
        self.z_src[k] = (own + self.y_buf[k].astype(f32)).astype(bf16)
        self.other_owners(lambda j: self.z_copy(k, j, self.line).start())

    def z_done(self, k):
        def run():
            rows, cols = self.piece(self.mine, 0)
            self.other_lines(lambda line: self.z_copy(k, self.mine, line).wait_recv())
            self.z_buf[k, self.line] = self.z_src[k, rows, cols]
            total = self.z_buf[k, 0].astype(f32)
            for line in range(1, self.outer):
                total = total + self.z_buf[k, line].astype(f32)
            rows, cols = self.piece(self.mine, self.inner * self.half)
            self.full[k, rows, cols] = total.astype(bf16)
            self.other_lines(lambda line: self.b_copy(k, line, self.mine).start())

        self.if_owner(run)

    def b_done(self, k):
        self.other_owners(lambda j: self.b_copy(k, self.line, j).wait_recv())
        self.f_copy(k, self.inner).start()

    def f_done(self, k):
        self.f_copy(k, 1 - self.inner).wait_recv()
        self.out[:, self.cols(k)] = self.full[k]

    def drain(self, k):
        for chip in range(self.chips):
            self.m_copy(k, chip).wait_send()
        self.other_chips(lambda chip: self.x_copy(k, chip, self.chip).wait_send())
        self.y_copy(k).wait_send()
        self.other_owners(lambda j: self.z_copy(k, j, self.line).wait_send())
        self.if_owner(lambda: self.other_lines(lambda line: self.b_copy(k, line, self.mine).wait_send()))
        self.f_copy(k, self.inner).wait_send()

    def wave(self, t):
        for lag, act in ((4, self.f_done), (3, self.b_done), (2, self.z_done), (1, self.y_done), (0, self.x_done)):
            k = t - lag
            pl.when(jnp.logical_and(k >= 0, k < self.chunks))(lambda k=k, act=act: act(k))

    @staticmethod
    def scratch(chunks, rows, width, by_rows, group, count):
        chips, outer = group // 2, count // 2
        owners = owner_count(rows, width, by_rows, outer)
        half = rows // 2
        piece = (half // owners, width) if by_rows else (half, width // owners)
        bufs = [(chunks, chips, rows, width), (chunks, chips, rows, width), (chunks, chips, rows, width), (chunks, rows, width),
                (chunks, half, width), (chunks, half, width), (chunks, outer) + piece, (chunks, rows, width)]
        return [(b, bf16) for b in bufs] + [pltpu.SemaphoreType.DMA((12, chunks, max(chips, outer, 2)))]


class Small:
    def __init__(self, held, got, sends, recvs):
        self.held, self.got, self.sends, self.recvs = held, got, sends, recvs
        group, ctx = lax.axis_index("group"), lax.axis_index("ctx")
        core, chip, inner, line = lax.rem(group, 2), group // 2, lax.rem(ctx, 2), ctx // 2
        self.hops = [
            (2, core, lambda j: dict(group=chip * 2 + j)),
            (lax.axis_size("group") // 2, chip, lambda j: dict(group=j * 2 + core)),
            (2, inner, lambda j: dict(ctx=line * 2 + j)),
            (lax.axis_size("ctx") // 2, line, lambda j: dict(ctx=j * 2 + inner)),
        ]

    def copy(self, h, j, sender):
        return remote(
            self.held.at[h], self.got.at[h, sender], self.sends.at[h, j], self.recvs.at[h, sender], **self.hops[h][2](j)
        )

    def others(self, h, body):
        size, mine, _ = self.hops[h]
        loop(1, size, lambda d: body(lax.rem(mine + d, size)))

    def start(self, h):
        self.others(h, lambda j: self.copy(h, j, self.hops[h][1]).start())

    def done(self, h):
        size, mine, _ = self.hops[h]
        self.others(h, lambda j: self.copy(h, j, j).wait_recv())
        self.got[h, mine] = self.held[h]
        total = self.got[h, 0]
        for j in range(1, size):
            total = total + self.got[h, j]
        self.held[h + 1] = total

    def drain(self):
        for h in range(4):
            self.others(h, lambda j: self.copy(h, j, self.hops[h][1]).wait_send())


def masks():
    rows = lax.broadcasted_iota(jnp.int32, (HALF, HALF), 0)
    cols = lax.broadcasted_iota(jnp.int32, (HALF, HALF), 1)
    return rows >= cols, cols < HEADDIM


def both(q):
    return slice(q * HALF, (q + 1) * HALF)


def pair_decays(cum, cum_t, p, causal):
    rolled = pltpu.roll(cum, lax.rem(HALF - 2 * p, HALF), 1)
    out = []
    for q in range(2):
        for a in range(2):
            gaps = rolled[both(q), a : a + 1] - cum_t[q, pl.ds(2 * p + a, 1), :]
            out.append(jnp.exp(jnp.where(causal, gaps, -jnp.inf)))
    return out


def front_kernel(
    tok, tok_all, wcat, wout, gain, cw, cb, db, dl,
    normed, nhalo, rhalo, cin, xb, vout, cumout, st0, loc, ylocal, gate, decs_out, wfull, wofull, sin,
    sel, halo, ext, ns, xs_s, cum_s, dt_s, cum_t, wv, wg, fexp, decs, decx, buf, recv, back,
    halo_sem, x_send, x_recv, m_send, m_recv, w_own, w_load, sends, recvs, back_sends, back_recvs, own_sem,
    dec_send, dec_recv,
):
    i = pl.program_id(0)
    seqs = tok_all.shape[0]
    count = lax.axis_size("ctx")
    me = lax.axis_index("ctx")
    ex = Exchange(count, buf, recv, back, sin, sends, recvs, back_sends, back_recvs, own_sem)
    sems = (x_send, x_recv, m_send, m_recv, w_own)
    conv_cols, gate_cols = pl.ds(DIN, CONVW + HALF), pl.ds(0, DIN)
    spreads = [
        Spread(0, wcat, wfull, conv_cols, sems),
        Spread(1, wcat, wfull, gate_cols, sems),
        Spread(2, wout, wofull, pl.ds(0, D), sems),
    ]
    halo_copy = remote(
        tok_all.at[:, pl.ds(SPAN - RIM, RIM), :], halo, halo_sem.at[0], halo_sem.at[1], ctx=lax.rem(me + 1, count)
    )
    load_v = pltpu.make_async_copy(wfull.at[:, conv_cols], wv, w_load.at[0])
    load_g = pltpu.make_async_copy(wfull.at[:, gate_cols], wg, w_load.at[1])

    def dec_copy(s, j, sender):
        rows = pl.ds(pl.multiple_of(sender * 8, 8), 8)
        return remote(
            decs.at[s, rows, :], decs.at[s, rows, :], dec_send.at[s, j], dec_recv.at[s, sender], ctx=j * ex.stride
        )

    @pl.when(i == 0)
    def _():
        meet(("ctx", "group"))
        pl.when(me < count - 1)(lambda: halo_copy.start())
        spreads[0].start()
        sel[...] = head_map()

        @pl.when(me == 0)
        def _():
            halo[...] = jnp.zeros_like(halo)

        @pl.when(me > 0)
        def _():
            halo_copy.wait_recv()

        spreads[0].forward()
        spreads[0].finish()
        load_v.start()
        spreads[1].start()
        spreads[2].start()
        load_v.wait()

    @pl.when(i == seqs - 1)
    def _():
        spreads[1].forward()
        spreads[1].finish()
        load_g.start()

    @pl.when(i < seqs)
    def _():
        s = i
        nh = normalized(halo[s], gain[...])[2]
        nm = normalized(tok[0], gain[...])[2]
        ext[0:RIM] = nh
        ext[RIM:] = nm
        ns[s] = nm
        nhalo[0] = nh
        rhalo[0] = halo[s]
        normed[0] = nm
        v = mm(nm, wv[:, CONVW:]) + db[...]
        vout[0] = v
        dt = softplus(v)
        cum = exact_mm(triangle(SPAN, True), -jnp.exp(dl[...]) * dt)
        cumout[0] = cum
        cum_s[s] = cum
        dt_s[s] = dt
        e_in, e_out, tot0, tot1, total = local_decays(cum)
        decs[s, pl.ds(pl.multiple_of(me * 8, 8), 8), :] = rows_of(total)
        ex.owners(lambda j: dec_copy(s, j, me).start())
        fexp[...] = spread(dt * e_out, sel)
        tot1x = spread(rows_of(tot1), sel)[0:1]

        def conv_tile(c):
            cols = slice(c, c + TILE)
            cin[0, :, cols] = mm(ext[...], wv[:, cols])
            o = cb[:, cols]
            for k in range(KCONV):
                o = o + cw[k : k + 1, cols] * cin[0, RIM - KCONV + 1 + k : RIM - KCONV + 1 + k + SPAN, cols]
            a = o * sigmoid(o)
            low = a.astype(bf16)
            xb[0, :, cols] = low
            xs_s[s, :, cols] = low
            return a

        bc = conv_tile(DIN)
        bt = jnp.transpose(bc[:, :NSTATE]).astype(bf16)
        for j in range(DIN // TILE):
            c = j * TILE
            cols = slice(c, c + TILE)
            a = conv_tile(c)
            xw = (a * fexp[:, cols]).astype(bf16)
            s0 = mm(bt[:, :HALF], xw[:HALF])
            s1 = mm(bt[:, HALF:], xw[HALF:])
            st0[0, :, cols] = s0
            low = (tot1x[:, cols] * s0 + s1).astype(bf16)
            loc[0, :, cols] = low
            buf[s, :, cols] = low
        ex.start(s)

    def scan(s):
        ex.if_owner(lambda: ex.others(lambda b: dec_copy(s, ex.mine, b).wait_recv()))
        decx[...] = spread(decs[s], sel)
        ex.scan(s, decx, False)

    @pl.when(i == seqs)
    def _():
        load_g.wait()
        spreads[2].forward()
        for s in range(seqs - 1):
            scan(s)

    @pl.when(i == seqs + 1)
    def _():
        scan(seqs - 1)

    @pl.when(i >= seqs)
    def _():
        s = i - seqs
        causal, low_lanes = masks()
        cum = cum_s[s]
        for q in range(2):
            cum_t[q] = jnp.transpose(cum[both(q)])
        fexp[...] = spread(dt_s[s], sel)
        bb = xs_s[s, :, DIN : DIN + NSTATE]
        cc = xs_s[s, :, DIN + NSTATE :]
        scores = [mm_nt(cc[both(q)], bb[both(q)]) for q in range(2)]

        def pair_step(p):
            cols = pl.ds(pl.multiple_of(p * HALF, HALF), HALF)
            decays = pair_decays(cum, cum_t, p, causal)
            for q in range(2):
                rows = both(q)
                m = jnp.concatenate([(decays[2 * q + a] * scores[q]).astype(bf16) for a in range(2)], axis=1)
                x = xs_s[s, rows, cols].astype(f32) * fexp[rows, cols]
                x = jnp.concatenate([jnp.where(low_lanes, x, 0.0), jnp.where(low_lanes, 0.0, x)], axis=0)
                ylocal[0, rows, cols] = mm(m, x.astype(bf16))

        loop(0, PAIRS, pair_step)
        for j in range(DIN // TILE):
            cols = slice(j * TILE, (j + 1) * TILE)
            gate[0, :, cols] = mm(ns[s], wg[:, cols])

    @pl.when(i == 2 * seqs - 1)
    def _():
        decs_out[...] = decs[...]
        for s in range(seqs):
            ex.finish(s)
            ex.owners(lambda j: dec_copy(s, j, me).wait_send())
        for sp in spreads[1:]:
            if sp.index == 2:
                sp.finish()
        for sp in spreads:
            sp.drain()
        pl.when(me < count - 1)(lambda: halo_copy.wait_send())


def middle_kernel(
    rel, tok, cot, ylocal, gate, xb, vin, cumin, st0, sin, decs, wout, skip, ggain,
    mixed, mlow, dyout, ggate, wred, dir1, gskip, gggain, dxs, dbc, later,
    sel, cum_t, einx, ys, gs, ss, s_in, dcs, dy_s, ml_s, g_s, dg_s, decx, buf, recv, back,
    sends, recvs, back_sends, back_recvs, own_sem,
):
    i = pl.program_id(0)
    seqs = dy_s.shape[0]
    count = lax.axis_size("ctx")
    ex = Exchange(count, buf, recv, back, later, sends, recvs, back_sends, back_recvs, own_sem)

    @pl.when(i == 0)
    def _():
        meet(("ctx",))
        sel[...] = head_map()
        gskip[...] = jnp.zeros_like(gskip)
        gggain[...] = jnp.zeros_like(gggain)

    @pl.when(i < seqs)
    def _():
        s = i
        cum = cumin[0]
        e_in, e_out, tot0, tot1, total = local_decays(cum)
        einx[...] = spread(e_in, sel)
        tot0x = spread(rows_of(tot0), sel)[0:1]
        s_in[0] = sin[0]
        s_in[1] = (tot0x * sin[0].astype(f32) + st0[0]).astype(bf16)
        cc = xb[0, :, DIN + NSTATE :]

        def gate_step(j, total_sq):
            cols = pl.ds(pl.multiple_of(j * TILE, TILE), TILE)
            for q in range(2):
                rows = both(q)
                ys[rows, cols] = ylocal[0, rows, cols] + einx[rows, cols] * mm(cc[rows], s_in[q, :, cols])
            y = ys[:, cols] + skip[:, cols] * xb[0, :, cols].astype(f32)
            g = gate[0, :, cols]
            gated = y * (g * sigmoid(g))
            gs[:, cols] = gated
            sq = gated * gated
            return total_sq + sq[:, :HALF] + sq[:, HALF:]

        sq = lax.fori_loop(0, DIN // TILE, gate_step, jnp.zeros((SPAN, HALF), f32))
        inv = lax.rsqrt(jnp.sum(sq, axis=1, keepdims=True) * (1.0 / DIN) + EPS)
        live = (lax.broadcasted_iota(jnp.int32, (SPAN, 1), 0) < rel[s]).astype(f32)
        drive = (live * cot[0].astype(f32)).astype(bf16)

        def back_step(j, acc):
            cols = pl.ds(pl.multiple_of(j * TILE, TILE), TILE)
            gm = mm_nt(drive, wout[cols, :])
            gated = gs[:, cols]
            unit = gated * inv
            low = (unit * ggain[:, cols]).astype(bf16)
            mlow[0, :, cols] = low
            ml_s[s, :, cols] = low
            gggain[:, cols] += jnp.sum(gm * unit, axis=0, keepdims=True)
            scaled = gm * ggain[:, cols]
            ss[:, cols] = scaled
            prod = scaled * gated
            return acc + prod[:, :HALF] + prod[:, HALF:]

        dots = lax.fori_loop(0, DIN // TILE, back_step, jnp.zeros((SPAN, HALF), f32))
        dots = jnp.sum(dots, axis=1, keepdims=True) * (1.0 / DIN)
        corr = inv * inv * inv * dots
        cct = jnp.transpose(cc.astype(f32)).astype(bf16)
        acc = jnp.zeros((SPAN, HALF), f32)
        dc = [jnp.zeros((HALF, HALF), f32) for _ in range(2)]
        for j in range(DIN // TILE):
            cols = slice(j * TILE, (j + 1) * TILE)
            g = gate[0, :, cols]
            sg = sigmoid(g)
            sl = g * sg
            grad_gated = inv * ss[:, cols] - gs[:, cols] * corr
            dy = grad_gated * sl
            yn = ys[:, cols]
            x = xb[0, :, cols].astype(f32)
            y = yn + skip[:, cols] * x
            ggate[0, :, cols] = (grad_gated * y * (sg + sl * (1.0 - sg))).astype(bf16)
            dyb = dy.astype(bf16)
            dyout[0, :, cols] = dyb
            dy_s[s, :, cols] = dyb
            gskip[:, cols] += jnp.sum(dy * x, axis=0, keepdims=True)
            acc = acc + gather_heads(dy * yn, sel[:HALF, cols])
            dye = (dy * einx[:, cols]).astype(bf16)
            d0 = mm(cct[:, :HALF], dye[:HALF])
            d1 = mm(cct[:, HALF:], dye[HALF:])
            dir1[0, :, cols] = d1
            buf[s, :, cols] = (d0 + tot0x[:, cols] * d1).astype(bf16)
            for q in range(2):
                dc[q] = dc[q] + mm_nt(dye[both(q)], s_in[q, :, cols])
        wred[0] = acc
        for q in range(2):
            dcs[s, both(q)] = dc[q]
        ex.start(s)

    def scan(s):
        decx[...] = spread(decs[s], sel)
        ex.scan(s, decx, True)

    @pl.when(i == seqs)
    def _():
        for s in range(seqs - 1):
            scan(s)

    @pl.when(i == seqs + 1)
    def _():
        scan(seqs - 1)

    @pl.when(i >= seqs)
    def _():
        s = i - seqs
        causal, low_lanes = masks()
        cum = cumin[0]
        for q in range(2):
            cum_t[q] = jnp.transpose(cum[both(q)])
        einx[...] = spread(softplus(vin[0]), sel)
        bb = xb[0, :, DIN : DIN + NSTATE]
        cc = xb[0, :, DIN + NSTATE :]
        for q in range(2):
            g_s[q] = mm_nt(cc[both(q)], bb[both(q)])
        dg_s[...] = jnp.zeros_like(dg_s)

        def pair_step(p):
            cols = pl.ds(pl.multiple_of(p * HALF, HALF), HALF)
            decays = pair_decays(cum, cum_t, p, causal)
            for q in range(2):
                rows = both(q)
                xsb = (xb[0, rows, cols].astype(f32) * einx[rows, cols]).astype(bf16)
                dyb = dy_s[s, rows, cols]
                dyf = dyb.astype(f32)
                grads = []
                for a in range(2):
                    m = (decays[2 * q + a] * g_s[q]).astype(bf16)
                    grads.append(mm_tn(m, dyb))
                    mine = low_lanes if a == 0 else jnp.logical_not(low_lanes)
                    dm = mm_nt(jnp.where(mine, dyf, 0.0).astype(bf16), xsb)
                    dg_s[q] += dm * decays[2 * q + a]
                dxs[0, rows, cols] = jnp.where(low_lanes, grads[0], grads[1])

        loop(0, PAIRS, pair_step)
        for q in range(2):
            rows = both(q)
            dg = dg_s[q].astype(bf16)
            dbc[0, rows, :NSTATE] = mm_tn(dg, cc[rows])
            dbc[0, rows, NSTATE:] = mm(dg, bb[rows]) + dcs[s, rows]
        live = (lax.broadcasted_iota(jnp.int32, (SPAN, 1), 0) < rel[s]).astype(f32)
        for j in range(D // TILE):
            cols = slice(j * TILE, (j + 1) * TILE)
            mixed[0, :, cols] = (live * (tok[0, :, cols].astype(f32) + mm(ml_s[s], wout[:, cols]))).astype(bf16)

    @pl.when(i == 2 * seqs - 1)
    def _():
        for s in range(seqs):
            ex.finish(s)


def third_kernel(
    cin, vin, cumin, dyin, wred, dxs, dbc, dir1, later, sin, loc, cw, cb, dl, skip, pgate, pout,
    gz, gzh, gcw, gcb, gdb, gdl, rgate, rout,
    sel, dtx, eoutx, xx, sp, dact, xwb, dout, qacc, gp, *comm,
):
    s = pl.program_id(0)
    seqs = pl.num_programs(0)
    reducers = [
        Reducer(pgate, rgate, D // lax.axis_size("group"), GATE_CHUNK, False, comm[:8], comm[8]),
        Reducer(pout, rout, DIN // lax.axis_size("group"), OUT_CHUNK, True, comm[9:17], comm[17]),
    ]

    def wave(t):
        reducers[1].wave(t - reducers[0].chunks)
        reducers[0].wave(t)

    @pl.when(s == 0)
    def _():
        meet(("ctx", "group"))
        for r in reducers:
            loop(0, r.chunks, r.m_start)
        sel[...] = head_map()
        gcw[...] = jnp.zeros_like(gcw)
        gcb[...] = jnp.zeros_like(gcb)
        gdb[...] = jnp.zeros_like(gdb)
        gdl[...] = jnp.zeros_like(gdl)
        gp[0:RIM] = jnp.zeros((RIM, CONVW), f32)
        gp[RIM + SPAN :] = jnp.zeros((8, CONVW), f32)

    cum = cumin[0]
    v = vin[0]
    dt = softplus(v)
    e_in, e_out, tot0, tot1, total = local_decays(cum)
    dtx[...] = spread(dt, sel)
    eoutx[...] = spread(e_out, sel)
    tot1x = spread(rows_of(tot1), sel)[0:1]
    totalx = spread(rows_of(total), sel)[0:1]

    def conv_step(j):
        cols = pl.ds(pl.multiple_of(j * HALF, HALF), HALF)
        o = cb[:, cols]
        for k in range(KCONV):
            o = o + cw[k : k + 1, cols] * cin[0, RIM - KCONV + 1 + k : RIM - KCONV + 1 + k + SPAN, cols]
        sg = sigmoid(o)
        a = o * sg
        xx[:, cols] = a
        sp[:, cols] = sg + a * (1.0 - sg)

    wave(3 * s - 2)
    loop(0, CONVW // HALF, conv_step)

    @pl.when(s == 0)
    def _():
        for r in reducers:
            loop(0, r.chunks, r.m_done)

    wave(3 * s - 1)
    bb = xx[:, DIN : DIN + NSTATE].astype(bf16)
    qacc[...] = jnp.zeros_like(qacc)
    dout[1] = later[0]
    dout[0] = (dir1[0] + tot1x * later[0].astype(f32)).astype(bf16)

    def state_step(j):
        cols = pl.ds(pl.multiple_of(j * TILE, TILE), TILE)
        for q in range(2):
            rows = both(q)
            x = xx[rows, cols]
            dte = dtx[rows, cols]
            eo = eoutx[rows, cols]
            dx_s = dxs[0, rows, cols] + eo * mm(bb[rows], dout[q, :, cols])
            dact[rows, cols] = dte * dx_s + skip[:, cols] * dyin[0, rows, cols].astype(f32)
            qacc[rows] += gather_heads(x * dx_s, sel[:HALF, cols])
            xwb[rows, cols] = (x * dte * eo).astype(bf16)

    loop(0, DIN // TILE, state_step)
    for q in range(2):
        rows = both(q)
        dact[rows, DIN : DIN + NSTATE] = dbc[0, rows, :NSTATE] + mm_nt(xwb[rows, :], dout[q])
        dact[rows, DIN + NSTATE :] = dbc[0, rows, NSTATE:]

    ends = jnp.sum(later[0].astype(f32) * (totalx * sin[0].astype(f32) + loc[0].astype(f32)), axis=0, keepdims=True)
    ends = gather_heads(rows_of(ends), sel[:HALF])[0:1]
    at_end = lax.broadcasted_iota(jnp.int32, (SPAN, 1), 0) == SPAN - 1
    dcum = wred[0] - dt * qacc[...] + jnp.where(at_end, ends, 0.0)
    glog = exact_mm(triangle(SPAN, False), dcum)
    rate = jnp.exp(dl[...])
    gpd = (qacc[...] - rate * glog) * sigmoid(v)
    lanes = lax.broadcasted_iota(jnp.int32, (SPAN, HALF), 1) < HEADS
    gpd = jnp.where(lanes, gpd, 0.0)
    gz[0, :, CONVW : CONVW + HALF] = gpd.astype(bf16)
    gz[0, :, CONVW + HALF :] = jnp.zeros((SPAN, HALF), bf16)
    gzh[0, :, CONVW:] = jnp.zeros((RIM, 2 * HALF), bf16)
    gdb[...] += jnp.sum(gpd, axis=0, keepdims=True)
    gdl[...] += -rate * jnp.sum(dt * glog, axis=0, keepdims=True)

    def out_step(j):
        cols = pl.ds(pl.multiple_of(j * HALF, HALF), HALF)
        gco = dact[:, cols] * sp[:, cols]
        gp[RIM : RIM + SPAN, cols] = gco
        gcb[:, cols] += jnp.sum(gco, axis=0, keepdims=True)
        for k in range(KCONV):
            gcw[k : k + 1, cols] += jnp.sum(
                gco * cin[0, RIM - KCONV + 1 + k : RIM - KCONV + 1 + k + SPAN, cols], axis=0, keepdims=True
            )
        main = jnp.zeros((SPAN, HALF), f32)
        rim = jnp.zeros((RIM, HALF), f32)
        for k in range(KCONV):
            ahead = KCONV - 1 - k
            main = main + cw[k : k + 1, cols] * gp[RIM + ahead : RIM + ahead + SPAN, cols]
            rim = rim + cw[k : k + 1, cols] * gp[ahead : ahead + RIM, cols]
        gz[0, :, cols] = main.astype(bf16)
        gzh[0, :, cols] = rim.astype(bf16)

    wave(3 * s)
    loop(0, CONVW // HALF, out_step)

    @pl.when(s == seqs - 1)
    def _():
        loop(3 * seqs - 2, reducers[0].chunks + reducers[1].chunks + 4, wave)
        for r in reducers:
            loop(0, r.chunks, r.drain)


def tail_kernel(
    rel, tok, halo, cot, gain, ggate, gz, gzh, wfull, pconv, small,
    gtok, rconv, small_out,
    ggain, rim_out, rim_in, rim_send, rim_recv, *comm,
):
    s = pl.program_id(0)
    seqs = pl.num_programs(0)
    count = lax.axis_size("ctx")
    me = lax.axis_index("ctx")
    reducer = Reducer(pconv, rconv, D // lax.axis_size("group"), CONV_CHUNK, False, comm[:8], comm[8])
    little = Small(*comm[9:13])

    def rim_copy(q):
        return remote(rim_out.at[q], rim_in.at[q], rim_send.at[q], rim_recv.at[q], ctx=lax.rem(me + count - 1, count))

    def back(rows, grad):
        rows, inv, _ = normalized(rows, gain[...])
        ggain[...] += jnp.sum(grad * rows * inv, axis=0, keepdims=True)
        gained = gain[...] * grad
        mean = jnp.mean(gained * rows, axis=-1, keepdims=True)
        return inv * gained - rows * (inv * inv * inv * mean)

    @pl.when(s == 0)
    def _():
        meet(("ctx", "group"))
        loop(0, reducer.chunks, reducer.m_start)
        ggain[...] = jnp.zeros_like(ggain)
        for q in range(halo.shape[0]):
            rim_out[q] = back(halo[q], mm_nt(gzh[q, :, :CONVW], wfull[:, DIN:ZXW])).astype(bf16)
            pl.when(me > 0)(lambda q=q: rim_copy(q).start())

        @pl.when(me == count - 1)
        def _():
            rim_in[...] = jnp.zeros_like(rim_in)

        loop(0, reducer.chunks, reducer.m_done)

    @pl.when(s > 0)
    def _():
        reducer.wave(s - 1)

    grad = mm_nt(ggate[0], wfull[:, :DIN]) + mm_nt(gz[0, :, : CONVW + HALF], wfull[:, DIN:])
    live = (lax.broadcasted_iota(jnp.int32, (SPAN, 1), 0) < rel[s]).astype(f32)
    out = live * cot[0].astype(f32) + back(tok[0], grad)
    gtok[0, : SPAN - RIM] = out[: SPAN - RIM].astype(bf16)
    pl.when(me < count - 1)(lambda: rim_copy(s).wait_recv())
    gtok[0, SPAN - RIM :] = (out[SPAN - RIM :] + rim_in[s].astype(f32)).astype(bf16)

    @pl.when(s == seqs - 1)
    def _():
        held = comm[9]
        held[0] = small[...]
        for j in range(D // HALF):
            held[0, j : j + 1, :] = ggain[:, j * HALF : (j + 1) * HALF]
        little.start(0)
        first = halo.shape[0] - 1
        for h in range(4):
            reducer.wave(first + h)
            little.done(h)
            if h < 3:
                little.start(h + 1)
        small_out[...] = held[4]
        loop(first + 4, reducer.chunks + 4, reducer.wave)
        loop(0, reducer.chunks, reducer.drain)
        little.drain()
        for q in range(halo.shape[0]):
            pl.when(me > 0)(lambda q=q: rim_copy(q).wait_send())


def whole(shape):
    zeros = (0,) * len(shape)
    return pl.BlockSpec(shape, lambda s: zeros, pipeline_mode=pl.Buffered(1))


def summed(shape):
    zeros = (0,) * len(shape)
    return pl.BlockSpec(shape, lambda s: zeros)


def per_seq(*shape):
    zeros = (0,) * len(shape)
    return pl.BlockSpec((1,) + shape, lambda s: (s,) + zeros)


SMEM = pl.BlockSpec(memory_space=pltpu.SMEM)
ANY = pl.BlockSpec(memory_space=pl.ANY)


def staged(seqs, phase, *shape):
    zeros = (0,) * len(shape)
    if phase == 0:
        return pl.BlockSpec((1,) + shape, lambda i: (jnp.minimum(i, seqs - 1),) + zeros)
    if phase == 1:
        return pl.BlockSpec((1,) + shape, lambda i: (jnp.maximum(i - seqs, 0),) + zeros)
    return pl.BlockSpec((1,) + shape, lambda i: (lax.rem(i, seqs),) + zeros)


def call(kernel, steps, in_specs, outs, scratch, name, collective=None):
    params = dict(vmem_limit_bytes=VMEM_LIMIT)
    if collective is not None:
        params.update(collective_id=collective, has_side_effects=True)
    return pl.pallas_call(
        kernel,
        grid=(steps,),
        in_specs=in_specs,
        out_specs=[o[0] for o in outs],
        out_shape=[jax.ShapeDtypeStruct(o[1], o[2]) for o in outs],
        scratch_shapes=[pltpu.VMEM(*sc) if isinstance(sc, tuple) else sc for sc in scratch],
        compiler_params=pltpu.CompilerParams(**params),
        name=name,
    )


def exchange_scratch(seqs, count):
    parts = min(count, 8)
    rows = NSTATE // parts
    dma = pltpu.SemaphoreType.DMA
    buffers = [((count * 8, DIN), f32), ((seqs, NSTATE, DIN), bf16), ((seqs, count, rows, DIN), bf16),
               ((seqs, count, rows, DIN), bf16)]
    sems = [dma((seqs, parts)), dma((seqs, count)), dma((seqs, count)), dma((seqs, parts)), dma((seqs,))]
    return buffers, sems


def lanes_of(v):
    return jnp.pad(v[None, :], ((0, 0), (0, HALF - v.shape[0])))


def local(
    tokens_in, seq_lengths, norm_gain, w_zx, w_delta, w_out, conv_weight, conv_bias,
    delta_bias, decay_log, skip_gain, gated_gain, cotangent,
):
    seqs = tokens_in.shape[0]
    count = lax.axis_size("ctx")
    group = lax.axis_size("group")
    chips = max(group // 2, 1)
    rel = seq_lengths - lax.axis_index("ctx") * SPAN
    gain = norm_gain[None, :]
    cb = conv_bias[None, :]
    db = lanes_of(delta_bias)
    dl = lanes_of(decay_log)
    skip = jnp.repeat(skip_gain, HEADDIM)[None, :]
    ggain = gated_gain[None, :]
    wcat = jnp.concatenate([w_zx, jnp.pad(w_delta, ((0, 0), (0, HALF - HEADS)))], axis=1)
    buffers, sems = exchange_scratch(seqs, count)
    dma = pltpu.SemaphoreType.DMA
    at0 = lambda *shape: staged(seqs, 0, *shape)
    at1 = lambda *shape: staged(seqs, 1, *shape)
    at01 = lambda *shape: staged(seqs, 2, *shape)

    normed, nhalo, rhalo, cin, xb, vraw, cum, st0, loc, ylocal, gate, decs, wfull, wofull, state_in = call(
        front_kernel,
        2 * seqs,
        [at0(SPAN, D), ANY, ANY, ANY, whole((1, D)), whole((KCONV, CONVW)), whole((1, CONVW)), whole((1, HALF)),
         whole((1, HALF))],
        [
            (at0(SPAN, D), (seqs, SPAN, D), bf16),
            (at0(RIM, D), (seqs, RIM, D), bf16),
            (at0(RIM, D), (seqs, RIM, D), bf16),
            (at0(RIM + SPAN, CONVW), (seqs, RIM + SPAN, CONVW), f32),
            (at0(SPAN, CONVW), (seqs, SPAN, CONVW), bf16),
            (at0(SPAN, HALF), (seqs, SPAN, HALF), f32),
            (at0(SPAN, HALF), (seqs, SPAN, HALF), f32),
            (at0(NSTATE, DIN), (seqs, NSTATE, DIN), f32),
            (at0(NSTATE, DIN), (seqs, NSTATE, DIN), bf16),
            (at1(SPAN, DIN), (seqs, SPAN, DIN), f32),
            (at1(SPAN, DIN), (seqs, SPAN, DIN), f32),
            (summed((seqs, count * 8, HALF)), (seqs, count * 8, HALF), f32),
            (ANY, (D, ZXW + HALF), bf16),
            (ANY, (DIN, D), bf16),
            (ANY, (seqs, NSTATE, DIN), bf16),
        ],
        [((2 * HALF, DIN), bf16), ((seqs, RIM, D), bf16), ((RIM + SPAN, D), bf16), ((seqs, SPAN, D), bf16),
         ((seqs, SPAN, CONVW), bf16), ((seqs, SPAN, HALF), f32), ((seqs, SPAN, HALF), f32), ((2, HALF, HALF), f32),
         ((D, CONVW + HALF), bf16), ((D, DIN), bf16), ((SPAN, DIN), f32), ((seqs, count * 8, HALF), f32)]
        + buffers
        + [dma((2,)), dma((3, chips)), dma((3, chips)), dma((3, chips)), dma((3, chips)), dma((3,)), dma((2,))]
        + sems
        + [dma((seqs, min(count, 8))), dma((seqs, count))],
        "front",
        0,
    )(tokens_in, tokens_in, wcat, w_out, gain, conv_weight, cb, db, dl)

    mixed_out, mlow, dy, ggate, wred, dir1, gskip, gggain, dxs, dbc, later = call(
        middle_kernel,
        2 * seqs,
        [SMEM, at1(SPAN, D), at0(SPAN, D), at0(SPAN, DIN), at0(SPAN, DIN), at01(SPAN, CONVW), at01(SPAN, HALF),
         at01(SPAN, HALF), at0(NSTATE, DIN), at0(NSTATE, DIN), whole((seqs, count * 8, HALF)), whole((DIN, D)),
         whole((1, DIN)), whole((1, DIN))],
        [
            (at1(SPAN, D), (seqs, SPAN, D), bf16),
            (at0(SPAN, DIN), (seqs, SPAN, DIN), bf16),
            (at0(SPAN, DIN), (seqs, SPAN, DIN), bf16),
            (at0(SPAN, DIN), (seqs, SPAN, DIN), bf16),
            (at0(SPAN, HALF), (seqs, SPAN, HALF), f32),
            (at0(NSTATE, DIN), (seqs, NSTATE, DIN), f32),
            (summed((1, DIN)), (1, DIN), f32),
            (summed((1, DIN)), (1, DIN), f32),
            (at1(SPAN, DIN), (seqs, SPAN, DIN), f32),
            (at1(SPAN, 2 * NSTATE), (seqs, SPAN, 2 * NSTATE), f32),
            (ANY, (seqs, NSTATE, DIN), bf16),
        ],
        [((2 * HALF, DIN), bf16), ((2, HALF, HALF), f32), ((SPAN, DIN), f32), ((SPAN, DIN), f32), ((SPAN, DIN), f32),
         ((SPAN, DIN), f32), ((2, NSTATE, DIN), bf16), ((seqs, SPAN, HALF), f32), ((seqs, SPAN, DIN), bf16),
         ((seqs, SPAN, DIN), bf16), ((2, HALF, HALF), f32), ((2, HALF, HALF), f32)]
        + buffers
        + sems,
        "middle",
        1,
    )(rel, tokens_in, cotangent, ylocal, gate, xb, vraw, cum, st0, state_in, decs, wofull, skip, ggain)

    live = (jnp.arange(SPAN, dtype=jnp.int32)[None, :] < rel[:, None]).astype(f32)[:, :, None]
    drive = (live * cotangent.astype(f32)).astype(bf16)
    flat = lambda v: v.reshape(-1, v.shape[-1])
    p_out = mm_tn(flat(mlow), flat(drive)).astype(bf16)
    p_gate = mm_tn(flat(normed), flat(ggate)).astype(bf16)

    gz, gzh, gcw, gcb, gdb, gdl, r_gate, r_out = call(
        third_kernel,
        seqs,
        [per_seq(RIM + SPAN, CONVW), per_seq(SPAN, HALF), per_seq(SPAN, HALF), per_seq(SPAN, DIN), per_seq(SPAN, HALF),
         per_seq(SPAN, DIN), per_seq(SPAN, 2 * NSTATE), per_seq(NSTATE, DIN), per_seq(NSTATE, DIN), per_seq(NSTATE, DIN),
         per_seq(NSTATE, DIN), whole((KCONV, CONVW)), whole((1, CONVW)), whole((1, HALF)), whole((1, DIN)),
         whole((D, DIN)), whole((DIN, D))],
        [
            (per_seq(SPAN, GZW), (seqs, SPAN, GZW), bf16),
            (per_seq(RIM, GZW), (seqs, RIM, GZW), bf16),
            (summed((KCONV, CONVW)), (KCONV, CONVW), f32),
            (summed((1, CONVW)), (1, CONVW), f32),
            (summed((1, HALF)), (1, HALF), f32),
            (summed((1, HALF)), (1, HALF), f32),
            (summed((D // group, DIN)), (D // group, DIN), bf16),
            (summed((DIN // group, D)), (DIN // group, D), bf16),
        ],
        [((2 * HALF, DIN), bf16), ((SPAN, DIN), f32), ((SPAN, DIN), f32), ((SPAN, CONVW), f32), ((SPAN, CONVW), f32),
         ((SPAN, CONVW), f32), ((SPAN, DIN), bf16), ((2, NSTATE, DIN), bf16), ((SPAN, HALF), f32),
         ((RIM + SPAN + 8, CONVW), f32)]
        + Reducer.scratch(DIN // GATE_CHUNK, D // group, GATE_CHUNK, False, group, count)
        + Reducer.scratch(D // OUT_CHUNK, DIN // group, OUT_CHUNK, True, group, count),
        "third",
        2,
    )(cin, vraw, cum, dy, wred, dxs, dbc, dir1, later, state_in, loc, conv_weight, cb, dl, skip, p_gate, p_out)

    p_conv = (mm_tn(flat(normed), flat(gz)) + mm_tn(flat(nhalo), flat(gzh))).astype(bf16)
    sizes = (D, KCONV * CONVW, CONVW, HALF, HALF, DIN, DIN)
    small = jnp.concatenate(
        [jnp.zeros((D,), f32), gcw.reshape(-1), gcb.reshape(-1), gdb[0], gdl[0], gskip.reshape(-1), gggain.reshape(-1)]
    ).reshape(-1, HALF)
    small = jnp.pad(small, ((0, -small.shape[0] % 8), (0, 0)))
    height = small.shape[0]
    widest = max(group // 2, count // 2, 2)

    gtok, r_conv, small = call(
        tail_kernel,
        seqs,
        [SMEM, per_seq(SPAN, D), whole((seqs, RIM, D)), per_seq(SPAN, D), whole((1, D)), per_seq(SPAN, DIN),
         per_seq(SPAN, GZW), whole((seqs, RIM, GZW)), whole((D, ZXW + HALF)), whole((D, GZW)), whole((height, HALF))],
        [
            (per_seq(SPAN, D), (seqs, SPAN, D), bf16),
            (summed((D // group, GZW)), (D // group, GZW), bf16),
            (summed((height, HALF)), (height, HALF), f32),
        ],
        [((1, D), f32), ((seqs, RIM, D), bf16), ((seqs, RIM, D), bf16), dma((seqs,)), dma((seqs,))]
        + Reducer.scratch(GZW // CONV_CHUNK, D // group, CONV_CHUNK, False, group, count)
        + [((5, height, HALF), f32), ((4, widest, height, HALF), f32), dma((4, widest)), dma((4, widest))],
        "tail",
        3,
    )(rel, tokens_in, rhalo, cotangent, gain, ggate, gz, gzh, wfull, p_conv, small)

    g_zx = jnp.concatenate([r_gate, r_conv[:, :CONVW]], axis=1).astype(f32)
    g_delta = r_conv[:, CONVW : CONVW + HEADS].astype(f32)
    small = small.reshape(-1)
    at = 0
    pieces = []
    for size in sizes:
        pieces.append(small[at : at + size])
        at += size
    return (
        mixed_out, gtok, pieces[0], g_zx, g_delta, r_out.astype(f32), pieces[1].reshape(KCONV, CONVW), pieces[2],
        pieces[3][:HEADS], pieces[4][:HEADS], pieces[5].reshape(HEADS, HEADDIM).sum(1), pieces[6],
    )


def solution(mesh):
    rows = P("group", "ctx", None)
    own = P("group", None)
    in_specs = (rows, P("group"), P(), own, own, own, P(), P(), P(), P(), P(), P(), rows)
    out_specs = (rows, rows, P(), own, own, own, P(), P(), P(), P(), P(), P())
    return jax.shard_map(local, mesh=mesh, in_specs=in_specs, out_specs=out_specs, check_vma=False)
```

```python
import jax
import jax.numpy as jnp
from jax import lax
from jax.experimental import pallas as pl
from jax.experimental.pallas import tpu as pltpu
from jax.sharding import PartitionSpec as P

D = 768
HEADS = 24
HEADDIM = 64
NSTATE = 128
KCONV = 4
SPAN = 256
DIN = 1536
CONVW = 1792
ZXW = 3328
RIM = 16
HALF = 128
TILE = 256
PAIRS = 12
EPS = 1e-05

f32 = jnp.float32
bf16 = jnp.bfloat16
NT = (((1,), (1,)), ((), ()))
TN = (((0,), (0,)), ((), ()))
VMEM_LIMIT = 62 * 1024 * 1024
GATE_CHUNK = 512
OUT_CHUNK = 256
CONV_CHUNK = 512
MIDDLE_LAG = 2
SCAN_LAG = 4
CLOSE_LAG = 6
GZW = 2048


def mm(a, b):
    return jnp.dot(a, b, preferred_element_type=f32)


def mm_nt(a, b):
    return lax.dot_general(a, b, NT, preferred_element_type=f32)


def mm_tn(a, b):
    return lax.dot_general(a, b, TN, preferred_element_type=f32)


def halves(v):
    high = v.astype(bf16)
    return high, (v - high.astype(f32)).astype(bf16)


def head_map():
    rows = lax.broadcasted_iota(jnp.int32, (2 * HALF, DIN), 0) % HALF
    cols = lax.broadcasted_iota(jnp.int32, (2 * HALF, DIN), 1) // HEADDIM
    return jnp.where(rows == cols, 1.0, 0.0).astype(bf16)


def spread(v, sel):
    return mm(jnp.concatenate(halves(v), axis=1), sel[...])


def gather_heads(v, sel_part):
    high, low = halves(v)
    return mm_nt(high, sel_part) + mm_nt(low, sel_part)


def triangle(size, lower):
    rows = lax.broadcasted_iota(jnp.int32, (size, size), 0)
    cols = lax.broadcasted_iota(jnp.int32, (size, size), 1)
    keep = rows >= cols if lower else rows <= cols
    return jnp.where(keep, 1.0, 0.0).astype(f32)


def exact_mm(a, b):
    return jnp.dot(a, b, precision=lax.Precision.HIGHEST, preferred_element_type=f32)


def softplus(v):
    return jnp.maximum(v, 0.0) + jnp.log1p(jnp.exp(-jnp.abs(v)))


def sigmoid(v):
    return 1.0 / (1.0 + jnp.exp(-v))


def gate_of(v):
    return 0.5 * jnp.tanh(0.5 * v) + 0.5


def local_decays(cum):
    mid, end = cum[HALF - 1 : HALF], cum[SPAN - 1 : SPAN]
    rows = lax.broadcasted_iota(jnp.int32, (SPAN, 1), 0)
    first = rows < HALF
    start = jnp.where(first, 0.0, mid)
    stop = jnp.where(first, mid, end)
    return jnp.exp(cum - start), jnp.exp(stop - cum), jnp.exp(mid), jnp.exp(end - mid), jnp.exp(end)


def rows_of(v):
    return jnp.broadcast_to(v, (8, v.shape[1]))


def normalized(rows, gain):
    rows = rows.astype(f32)
    inv = lax.rsqrt(jnp.mean(rows * rows, axis=-1, keepdims=True) + EPS)
    return rows, inv, (rows * inv * gain).astype(bf16)


def remote(src, dst, send_sem, recv_sem, **where):
    return pltpu.make_async_remote_copy(
        src_ref=src, dst_ref=dst, send_sem=send_sem, recv_sem=recv_sem,
        device_id=where, device_id_type=pl.DeviceIdType.MESH,
    )


def loop(start, stop, body):
    def step(i, c):
        body(i)
        return c

    lax.fori_loop(start, stop, step, 0)


def meet(axes):
    barrier = pltpu.get_barrier_semaphore()
    total = 0
    for axis in axes:
        size = lax.axis_size(axis)
        me = lax.axis_index(axis)

        def greet(d):
            pl.semaphore_signal(
                barrier, inc=1, device_id={axis: lax.rem(me + d, size)}, device_id_type=pl.DeviceIdType.MESH
            )

        loop(1, size, greet)
        total += size - 1
    pl.semaphore_wait(barrier, total)


class Exchange:
    def __init__(self, reverse, out_at, bufs, sems):
        self.reverse, self.out_at, self.sems = reverse, out_at, sems
        self.buf, self.y_buf, self.z_src, self.z_buf, self.z_back, self.p_buf, self.mine_buf, self.their_buf, self.decx = bufs
        self.depth = self.buf.shape[1]
        ctx = lax.axis_index("ctx")
        self.ctx = ctx
        self.outer = lax.axis_size("ctx") // 2
        self.owners = min(self.outer, 4)
        self.stride = self.outer // self.owners
        self.inner = lax.rem(ctx, 2)
        self.line = ctx // 2
        self.mine = self.line // self.stride
        self.half = NSTATE // 2
        self.rows = self.half // self.owners

    def half_rows(self, inner):
        return pl.ds(pl.multiple_of(inner * self.half, self.half), self.half)

    def part(self, j):
        return pl.ds(pl.multiple_of(j * self.rows, self.rows), self.rows)

    def other_owners(self, body):
        if self.stride == 1:
            loop(1, self.owners, lambda d: body(lax.rem(self.mine + d, self.owners)))
        else:
            loop(0, self.owners, lambda j: pl.when(j * self.stride != self.line)(lambda: body(j)))

    def other_lines(self, body):
        loop(1, self.outer, lambda d: body(lax.rem(self.line + d, self.outer)))

    def if_owner(self, body):
        if self.stride == 1:
            body()
        else:
            pl.when(self.mine * self.stride == self.line)(body)

    def y_copy(self, u):
        return remote(
            self.buf.at[u, :, self.half_rows(1 - self.inner)], self.y_buf.at[u], self.sems.at[0, u, 0], self.sems.at[1, u, 0],
            ctx=self.ctx + 1 - 2 * self.inner,
        )

    def z_copy(self, u, j, sender):
        return remote(
            self.z_src.at[u, :, self.part(j)], self.z_buf.at[u, sender], self.sems.at[2, u, j], self.sems.at[3, u, sender],
            ctx=j * self.stride * 2 + self.inner,
        )

    def b_copy(self, u, line, j):
        return remote(
            self.z_back.at[u, line], self.p_buf.at[u, :, self.part(j)], self.sems.at[4, u, line], self.sems.at[5, u, j],
            ctx=line * 2 + self.inner,
        )

    def f_copy(self, u, inner):
        return remote(
            self.their_buf.at[u], self.out_at(u, self.half_rows(inner)), self.sems.at[6, u, 0], self.sems.at[7, u, 0],
            ctx=self.ctx + 1 - 2 * self.inner,
        )

    def keep(self, u):
        return pltpu.make_async_copy(self.mine_buf.at[u], self.out_at(u, self.half_rows(self.inner)), self.sems.at[8, u, 0])

    def decay(self, a, block):
        return self.decx[a, pl.ds(pl.multiple_of(block * 8, 8), 8), :][0:1]

    def pair(self, u, a):
        own = self.buf[u, a, self.half_rows(self.inner), :].astype(f32)
        other = self.y_buf[u, a].astype(f32)
        first = self.inner == 0
        return jnp.where(first, own, other), jnp.where(first, other, own)

    def start(self, u):
        self.y_copy(u).start()

    def middle(self, u):
        self.y_copy(u).wait_recv()
        for a in range(self.depth):
            s0, s1 = self.pair(u, a)
            if self.reverse:
                total = s0 + self.decay(a, 2 * self.line) * s1
            else:
                total = self.decay(a, 2 * self.line + 1) * s0 + s1
            self.z_src[u, a] = total.astype(bf16)
        self.other_owners(lambda j: self.z_copy(u, j, self.line).start())

    def scan(self, u):
        def run():
            self.other_lines(lambda line: self.z_copy(u, self.mine, line).wait_recv())
            self.z_buf[u, self.line] = self.z_src[u, :, self.part(self.mine), :]
            for a in range(self.depth):

                def step(k, carry):
                    line = self.outer - 1 - k if self.reverse else k
                    self.z_back[u, line, a] = carry.astype(bf16)
                    both_decays = self.decay(a, 2 * line) * self.decay(a, 2 * line + 1)
                    return both_decays * carry + self.z_buf[u, line, a].astype(f32)

                lax.fori_loop(0, self.outer, step, jnp.zeros(self.z_buf.shape[3:], f32))
            self.other_lines(lambda line: self.b_copy(u, line, self.mine).start())
            self.p_buf[u, :, self.part(self.mine), :] = self.z_back[u, self.line]

        self.if_owner(run)

    def close(self, u):
        self.other_owners(lambda j: self.b_copy(u, self.line, j).wait_recv())
        for a in range(self.depth):
            s0, s1 = self.pair(u, a)
            near = self.p_buf[u, a].astype(f32)
            if self.reverse:
                far = s1 + self.decay(a, 2 * self.line + 1) * near
            else:
                far = s0 + self.decay(a, 2 * self.line) * near
            keeps_near = self.inner == (1 if self.reverse else 0)
            self.mine_buf[u, a] = jnp.where(keeps_near, near, far).astype(bf16)
            self.their_buf[u, a] = jnp.where(keeps_near, far, near).astype(bf16)
        self.f_copy(u, self.inner).start()
        self.keep(u).start()

    def finish(self, u):
        self.f_copy(u, 1 - self.inner).wait_recv()
        self.keep(u).wait()
        self.y_copy(u).wait_send()
        self.other_owners(lambda j: self.z_copy(u, j, self.line).wait_send())
        self.if_owner(lambda: self.other_lines(lambda line: self.b_copy(u, line, self.mine).wait_send()))
        self.f_copy(u, self.inner).wait_send()

    @staticmethod
    def scratch(units, depth, lanes, count):
        outer = count // 2
        half = NSTATE // 2
        rows = half // min(outer, 4)
        bufs = [(units, depth, NSTATE, lanes), (units, depth, half, lanes), (units, depth, half, lanes),
                (units, outer, depth, rows, lanes), (units, outer, depth, rows, lanes), (units, depth, half, lanes),
                (units, depth, half, lanes), (units, depth, half, lanes)]
        return (
            [(b, bf16) for b in bufs]
            + [((depth, count * 8, lanes), f32)]
            + [pltpu.SemaphoreType.DMA((9, units, max(outer, 4)))]
        )


class Spread:
    def __init__(self, shard, full, sems):
        self.shard, self.full = shard, full
        self.x_send, self.x_recv, self.m_send, self.m_recv, self.own = sems
        size = lax.axis_size("group")
        self.cores = 2 if size % 2 == 0 else 1
        self.chips = size // self.cores
        self.me = lax.axis_index("group")
        self.core = lax.rem(self.me, self.cores)
        self.chip = self.me // self.cores
        self.rows = shard.shape[0]

    def place(self, member, cols):
        return self.full.at[pl.ds(pl.multiple_of(member * self.rows, 32), self.rows), cols]

    def across(self, p, cols, d):
        peer = lax.rem(self.chip + d, self.chips) * self.cores + self.core
        return remote(
            self.shard.at[:, cols], self.place(self.me, cols), self.x_send.at[p, d], self.x_recv.at[p, d], group=peer
        )

    def mate(self, p, cols, d):
        member = lax.rem(self.chip + self.chips - d, self.chips) * self.cores + self.core
        src = self.shard.at[:, cols] if d == 0 else self.place(member, cols)
        return remote(
            src, self.place(member, cols), self.m_send.at[p, d], self.m_recv.at[p, d],
            group=self.me + 1 - 2 * self.core,
        )

    def keep(self, p):
        return pltpu.make_async_copy(self.shard, self.place(self.me, slice(None)), self.own.at[p])

    def start_chip(self, p):
        if self.cores == 2:
            self.mate(p, slice(None), 0).start()
        self.keep(p).start()

    def finish_chip(self, p):
        if self.cores == 2:
            self.mate(p, slice(None), 0).wait_recv()
        self.keep(p).wait()

    def start(self, p, cols):
        for d in range(1, self.chips):
            self.across(p, cols, d).start()

    def forward(self, p, cols):
        for d in range(1, self.chips):
            self.across(p, cols, d).wait_recv()
            if self.cores == 2:
                self.mate(p, cols, d).start()

    def finish(self, p, cols):
        if self.cores == 2:
            for d in range(1, self.chips):
                self.mate(p, cols, d).wait_recv()

    def drain(self, p, cols):
        for d in range(1, self.chips):
            self.across(p, cols, d).wait_send()
            if self.cores == 2:
                self.mate(p, cols, d).wait_send()

    def drain_chip(self, p):
        if self.cores == 2:
            self.mate(p, slice(None), 0).wait_send()


def owner_count(rows, width, by_rows, outer):
    fits = lambda n: (rows // 2) % (16 * n) == 0 if by_rows else width % (128 * n) == 0
    return max(n for n in (1, 2, 4) if outer % n == 0 and fits(n))


class Reducer:
    def __init__(self, part, out, rows, width, by_rows, bufs, sems):
        self.part, self.out, self.rows, self.width, self.by_rows = part, out, rows, width, by_rows
        self.m_buf, self.x_src, self.x_buf, self.y_src, self.y_buf, self.z_src, self.z_buf, self.full = bufs
        self.sems = sems
        self.chunks = part.shape[1] // width
        self.group = lax.axis_index("group")
        self.cores = 2
        self.chips = lax.axis_size("group") // 2
        self.core = lax.rem(self.group, 2)
        self.chip = self.group // 2
        self.ctx = lax.axis_index("ctx")
        self.outer = lax.axis_size("ctx") // 2
        self.owners = owner_count(rows, width, by_rows, self.outer)
        self.stride = self.outer // self.owners
        self.inner = lax.rem(self.ctx, 2)
        self.line = self.ctx // 2
        self.mine = self.line // self.stride
        self.half = rows // 2

    def cols(self, k):
        return pl.ds(pl.multiple_of(k * self.width, self.width), self.width)

    def member(self, chip, core):
        return pl.ds(pl.multiple_of((chip * 2 + core) * self.rows, 64), self.rows)

    def half_rows(self, inner):
        return pl.ds(pl.multiple_of(inner * self.half, 16), self.half)

    def piece(self, j, base):
        if self.by_rows:
            n = self.half // self.owners
            return pl.ds(pl.multiple_of(base + j * n, 16), n), pl.ds(0, self.width)
        n = self.width // self.owners
        return pl.ds(pl.multiple_of(base, 16), self.half), pl.ds(pl.multiple_of(j * n, 128), n)

    def m_copy(self, k, chip):
        return remote(
            self.part.at[self.member(chip, 1 - self.core), self.cols(k)], self.m_buf.at[k, chip],
            self.sems.at[0, k, chip], self.sems.at[1, k, chip], group=self.group + 1 - 2 * self.core,
        )

    def x_copy(self, k, chip, sender):
        return remote(
            self.x_src.at[k, chip], self.x_buf.at[k, sender], self.sems.at[2, k, chip], self.sems.at[3, k, sender],
            group=chip * 2 + self.core,
        )

    def y_copy(self, k):
        return remote(
            self.y_src.at[k, self.half_rows(1 - self.inner)], self.y_buf.at[k], self.sems.at[4, k, 0], self.sems.at[5, k, 0],
            ctx=self.ctx + 1 - 2 * self.inner,
        )

    def z_copy(self, k, j, sender):
        rows, cols = self.piece(j, 0)
        return remote(
            self.z_src.at[k, rows, cols], self.z_buf.at[k, sender], self.sems.at[6, k, j], self.sems.at[7, k, sender],
            ctx=j * self.stride * 2 + self.inner,
        )

    def b_copy(self, k, line, j):
        rows, cols = self.piece(j, self.inner * self.half)
        return remote(
            self.full.at[k, rows, cols], self.full.at[k, rows, cols], self.sems.at[8, k, line], self.sems.at[9, k, j],
            ctx=line * 2 + self.inner,
        )

    def f_copy(self, k, inner):
        rows = self.half_rows(inner)
        return remote(
            self.full.at[k, rows], self.full.at[k, rows], self.sems.at[10, k, 0], self.sems.at[11, k, 0],
            ctx=self.ctx + 1 - 2 * self.inner,
        )

    def other_chips(self, body):
        for d in range(1, self.chips):
            body(lax.rem(self.chip + d, self.chips))

    def other_owners(self, body):
        if self.stride == 1:
            for d in range(1, self.owners):
                body(lax.rem(self.mine + d, self.owners))
        else:
            for j in range(self.owners):
                pl.when(j * self.stride != self.line)(lambda j=j: body(j))

    def other_lines(self, body):
        loop(1, self.outer, lambda d: body(lax.rem(self.line + d, self.outer)))

    def if_owner(self, body):
        if self.stride == 1:
            body()
        else:
            pl.when(self.mine * self.stride == self.line)(body)

    def m_start(self, k):
        for chip in range(self.chips):
            self.m_copy(k, chip).start()

    def m_done(self, k):
        for chip in range(self.chips):
            self.m_copy(k, chip).wait_recv()
            own = self.part[self.member(chip, self.core), self.cols(k)].astype(f32)
            self.x_src[k, chip] = (own + self.m_buf[k, chip].astype(f32)).astype(bf16)
        self.other_chips(lambda chip: self.x_copy(k, chip, self.chip).start())

    def x_done(self, k):
        total = self.x_src[k, self.chip].astype(f32)
        for d in range(1, self.chips):
            chip = lax.rem(self.chip + d, self.chips)
            self.x_copy(k, chip, chip).wait_recv()
            total = total + self.x_buf[k, chip].astype(f32)
        self.y_src[k] = total.astype(bf16)
        self.y_copy(k).start()

    def y_done(self, k):
        self.y_copy(k).wait_recv()
        own = self.y_src[k, self.half_rows(self.inner), :].astype(f32)
        self.z_src[k] = (own + self.y_buf[k].astype(f32)).astype(bf16)
        self.other_owners(lambda j: self.z_copy(k, j, self.line).start())

    def z_done(self, k):
        def run():
            rows, cols = self.piece(self.mine, 0)
            self.other_lines(lambda line: self.z_copy(k, self.mine, line).wait_recv())
            self.z_buf[k, self.line] = self.z_src[k, rows, cols]
            total = self.z_buf[k, 0].astype(f32)
            for line in range(1, self.outer):
                total = total + self.z_buf[k, line].astype(f32)
            rows, cols = self.piece(self.mine, self.inner * self.half)
            self.full[k, rows, cols] = total.astype(bf16)
            self.other_lines(lambda line: self.b_copy(k, line, self.mine).start())

        self.if_owner(run)

    def b_done(self, k):
        self.other_owners(lambda j: self.b_copy(k, self.line, j).wait_recv())
        self.f_copy(k, self.inner).start()

    def f_done(self, k):
        self.f_copy(k, 1 - self.inner).wait_recv()
        self.out[:, self.cols(k)] = self.full[k]

    def drain(self, k):
        for chip in range(self.chips):
            self.m_copy(k, chip).wait_send()
        self.other_chips(lambda chip: self.x_copy(k, chip, self.chip).wait_send())
        self.y_copy(k).wait_send()
        self.other_owners(lambda j: self.z_copy(k, j, self.line).wait_send())
        self.if_owner(lambda: self.other_lines(lambda line: self.b_copy(k, line, self.mine).wait_send()))
        self.f_copy(k, self.inner).wait_send()

    def wave(self, t):
        for lag, act in ((4, self.f_done), (3, self.b_done), (2, self.z_done), (1, self.y_done), (0, self.x_done)):
            k = t - lag
            pl.when(jnp.logical_and(k >= 0, k < self.chunks))(lambda k=k, act=act: act(k))

    @staticmethod
    def scratch(chunks, rows, width, by_rows, group, count):
        chips, outer = group // 2, count // 2
        owners = owner_count(rows, width, by_rows, outer)
        half = rows // 2
        piece = (half // owners, width) if by_rows else (half, width // owners)
        bufs = [(chunks, chips, rows, width), (chunks, chips, rows, width), (chunks, chips, rows, width), (chunks, rows, width),
                (chunks, half, width), (chunks, half, width), (chunks, outer) + piece, (chunks, rows, width)]
        return [(b, bf16) for b in bufs] + [pltpu.SemaphoreType.DMA((12, chunks, max(chips, outer, 2)))]


class Small:
    def __init__(self, held, got, sends, recvs):
        self.held, self.got, self.sends, self.recvs = held, got, sends, recvs
        group, ctx = lax.axis_index("group"), lax.axis_index("ctx")
        core, chip, inner, line = lax.rem(group, 2), group // 2, lax.rem(ctx, 2), ctx // 2
        self.hops = [
            (2, core, lambda j: dict(group=chip * 2 + j)),
            (lax.axis_size("group") // 2, chip, lambda j: dict(group=j * 2 + core)),
            (2, inner, lambda j: dict(ctx=line * 2 + j)),
            (lax.axis_size("ctx") // 2, line, lambda j: dict(ctx=j * 2 + inner)),
        ]

    def copy(self, h, j, sender):
        return remote(
            self.held.at[h], self.got.at[h, sender], self.sends.at[h, j], self.recvs.at[h, sender], **self.hops[h][2](j)
        )

    def others(self, h, body):
        size, mine, _ = self.hops[h]
        loop(1, size, lambda d: body(lax.rem(mine + d, size)))

    def start(self, h):
        self.others(h, lambda j: self.copy(h, j, self.hops[h][1]).start())

    def done(self, h):
        size, mine, _ = self.hops[h]
        self.others(h, lambda j: self.copy(h, j, j).wait_recv())
        self.got[h, mine] = self.held[h]
        total = self.got[h, 0]
        for j in range(1, size):
            total = total + self.got[h, j]
        self.held[h + 1] = total

    def drain(self):
        for h in range(4):
            self.others(h, lambda j: self.copy(h, j, self.hops[h][1]).wait_send())


def masks():
    rows = lax.broadcasted_iota(jnp.int32, (HALF, HALF), 0)
    cols = lax.broadcasted_iota(jnp.int32, (HALF, HALF), 1)
    return rows >= cols, cols < HEADDIM


def both(q):
    return slice(q * HALF, (q + 1) * HALF)


def pair_decays(cum, cum_t, p, causal):
    rolled = pltpu.roll(cum, lax.rem(HALF - 2 * p, HALF), 1)
    out = []
    for q in range(2):
        for a in range(2):
            gaps = rolled[both(q), a : a + 1] - cum_t[q, pl.ds(2 * p + a, 1), :]
            out.append(jnp.exp(jnp.where(causal, gaps, -jnp.inf)))
    return out


TILES = DIN // TILE
PIECES = 2 * TILES + 1
DT0 = DIN + CONVW - 2 * NSTATE


def front_kernel(
    tok, tok_any, wcat, wout, gain, cw, cb, db, dl,
    normed, nhalo, rhalo, cin, xb, spb, vout, cumout, st0, loc, ylocal, gate, decs_out, wfull, wofull, sin,
    sel, halo, ext, w, cin_s, xs_s, bt, scores, out_cat, dt_cat, cum_t, tot1x, decs,
    halo_sem, x_send, x_recv, m_send, m_recv, w_own, w_store, dec_send, dec_recv, *exchange,
):
    i = pl.program_id(0)
    seqs = tok.shape[0]
    count = lax.axis_size("ctx")
    me = lax.axis_index("ctx")
    sems = (x_send, x_recv, m_send, m_recv, w_own)
    zx, wo = Spread(wcat, w, sems), Spread(wout, wofull, sems)
    last = PIECES

    def unit_cols(u):
        return pl.ds(pl.multiple_of(u * TILE, TILE), TILE)

    def piece(p):
        at = jnp.where(p <= TILES, DIN + (p - 1) * TILE, (p - 1 - TILES) * TILE)
        return pl.ds(pl.multiple_of(at, TILE), TILE)

    first_piece = pl.ds(DT0, 2 * NSTATE + HALF)
    ex = Exchange(False, lambda u, rows: sin.at[:, rows, unit_cols(u)], exchange[:9], exchange[9])
    halo_copy = remote(
        tok_any.at[:, pl.ds(SPAN - RIM, RIM), :], halo, halo_sem.at[0], halo_sem.at[1], ctx=lax.rem(me + 1, count)
    )
    keep_w = pltpu.make_async_copy(w, wfull, w_store.at[0])

    def dec_copy(block, sender):
        rows = pl.ds(pl.multiple_of(sender * 8, 8), 8)
        return remote(decs.at[:, rows, :], decs.at[:, rows, :], dec_send.at[block], dec_recv.at[sender], ctx=block)

    def other_blocks(body):
        loop(1, count, lambda d: body(lax.rem(me + d, count)))

    def conv_tile(s, cols_w, cols_c):
        cin_s[s] = mm(ext[s], w[:, cols_w])
        cin[s] = cin_s[s].astype(bf16)
        o = cb[:, cols_c]
        for k in range(KCONV):
            o = o + cw[k : k + 1, cols_c] * cin_s[s, RIM - KCONV + 1 + k : RIM - KCONV + 1 + k + SPAN, :]
        sg = gate_of(o)
        a = o * sg
        xb[s] = a.astype(bf16)
        spb[s] = (sg + a * (1.0 - sg)).astype(bf16)
        return a

    def unit_decays(u):
        for s in range(seqs):
            ex.decx[s] = spread(decs[s], sel.at[:, unit_cols(u)])

    @pl.when(i == 0)
    def _():
        meet(("ctx", "group"))
        pl.when(me < count - 1)(lambda: halo_copy.start())
        zx.start(0, first_piece)
        zx.start_chip(0)
        zx.start(1, piece(1))
        zx.start(2, piece(2))
        wo.start_chip(1)
        sel[...] = head_map()

        @pl.when(me == 0)
        def _():
            halo[...] = jnp.zeros_like(halo)

        def norm_main(s):
            nm = normalized(tok[s], gain[...])[2]
            ext[s, RIM:] = nm
            normed[s] = nm

        loop(0, seqs, norm_main)

        @pl.when(me > 0)
        def _():
            halo_copy.wait_recv()

        def norm_halo(s):
            nh = normalized(halo[s], gain[...])[2]
            ext[s, 0:RIM] = nh
            nhalo[s] = nh
            rhalo[s] = halo[s]

        loop(0, seqs, norm_halo)
        zx.forward(0, first_piece)
        zx.finish_chip(0)

    @pl.when(i + 1 < PIECES)
    def _():
        zx.forward(i + 1, piece(i + 1))

    @pl.when(i + 3 < PIECES)
    def _():
        zx.start(i + 3, piece(i + 3))

    @pl.when(i + 3 == PIECES)
    def _():
        wo.start(last, slice(None))

    @pl.when(i == 0)
    def _():
        zx.finish(0, first_piece)

        def delta(s):
            a = conv_tile(s, slice(DT0, DT0 + TILE), slice(DIN, DIN + TILE))
            bb, cc = a[:, :NSTATE].astype(bf16), a[:, NSTATE:].astype(bf16)
            bt[s] = jnp.transpose(a[:, :NSTATE]).astype(bf16)
            for q in range(2):
                scores[s, q] = mm_nt(cc[both(q)], bb[both(q)])
            v = mm(ext[s, RIM:], w[:, DT0 + TILE :]) + db[...]
            vout[s] = v
            dt = softplus(v)
            cum = exact_mm(triangle(SPAN, True), -jnp.exp(dl[...]) * dt)
            cumout[s] = cum
            for q in range(2):
                cum_t[s, q] = jnp.transpose(cum[both(q)])
            e_in, e_out, tot0, tot1, total = local_decays(cum)
            decs[s, pl.ds(pl.multiple_of(me * 8, 8), 8), :] = rows_of(total)
            out_cat[s] = jnp.concatenate(halves(dt * e_out), axis=1)
            dt_cat[s] = jnp.concatenate(halves(dt), axis=1)
            tot1x[s] = spread(rows_of(tot1), sel)

        loop(0, seqs, delta)
        other_blocks(lambda b: dec_copy(b, me).start())

    @pl.when(jnp.logical_and(i >= 1, i < PIECES))
    def _():
        zx.finish(i, piece(i))

    def act_at(lag, act):
        u = i - 1 - lag
        pl.when(jnp.logical_and(u >= 0, u < TILES))(lambda: act(u))

    def close(u):
        unit_decays(u)
        ex.close(u)

    def scan(u):
        unit_decays(u)
        ex.scan(u)

    def middle(u):
        unit_decays(u)
        ex.middle(u)

    @pl.when(i == 3)
    def _():
        other_blocks(lambda b: dec_copy(b, b).wait_recv())

    act_at(CLOSE_LAG, close)
    act_at(SCAN_LAG, scan)
    act_at(MIDDLE_LAG, middle)

    @pl.when(jnp.logical_and(i >= 1, i <= TILES))
    def _():
        u = i - 1
        cols = unit_cols(u)

        def x_tile(s):
            a = conv_tile(s, piece(i), cols)
            xs_s[s, :, cols] = a.astype(bf16)
            xw = (a * mm(out_cat[s], sel[:, cols])).astype(bf16)
            s0 = mm(bt[s, :, :HALF], xw[:HALF])
            s1 = mm(bt[s, :, HALF:], xw[HALF:])
            st0[s] = s0
            low = (tot1x[s, :, cols][0:1] * s0 + s1).astype(bf16)
            loc[s] = low
            ex.buf[u, s] = low

        loop(0, seqs, x_tile)
        ex.start(u)

    @pl.when(i > TILES)
    def _():
        u = i - 1 - TILES
        causal, low_lanes = masks()

        def intra(s):
            cum = cumout[s]
            dtx = mm(dt_cat[s], sel[:, unit_cols(u)])
            for h in range(2):
                p = 2 * u + h
                lanes = slice(h * HALF, (h + 1) * HALF)
                decays = pair_decays(cum, cum_t.at[s], p, causal)
                for q in range(2):
                    rows = both(q)
                    m = jnp.concatenate([(decays[2 * q + a] * scores[s, q]).astype(bf16) for a in range(2)], axis=1)
                    x = xs_s[s, rows, pl.ds(pl.multiple_of(p * HALF, HALF), HALF)].astype(f32) * dtx[rows, lanes]
                    x = jnp.concatenate([jnp.where(low_lanes, x, 0.0), jnp.where(low_lanes, 0.0, x)], axis=0)
                    ylocal[s, rows, lanes] = mm(m, x.astype(bf16))
            gate[s] = mm(ext[s, RIM:], w[:, piece(i)])

        loop(0, seqs, intra)

    @pl.when(i == PIECES - 1)
    def _():
        keep_w.start()
        decs_out[...] = decs[...]
        wo.forward(last, slice(None))
        loop(TILES + TILES - CLOSE_LAG, TILES, close)
        loop(0, TILES, ex.finish)
        wo.finish(last, slice(None))
        wo.finish_chip(1)
        zx.drain_chip(0)
        wo.drain_chip(1)
        zx.drain(0, first_piece)
        loop(1, PIECES, lambda p: zx.drain(p, piece(p)))
        wo.drain(last, slice(None))
        other_blocks(lambda b: dec_copy(b, me).wait_send())
        pl.when(me < count - 1)(lambda: halo_copy.wait_send())
        keep_w.wait()


def middle_kernel(
    rel, tok, cot, ylocal, gate, xb, vin, cumin, st0, sin, decs, wout, skip, ggain,
    mixed, mlow, dyout, ggate, wred, dir1, gskip, gggain, dxs, dbc, later,
    sel, cum_t, einx, ys, gs, ss, s_in, dcs, dy_s, ml_s, g_s, dg_s, *exchange,
):
    i = pl.program_id(0)
    seqs = dy_s.shape[0]
    ex = Exchange(True, lambda u, rows: later.at[pl.ds(u, 1), rows, :], exchange[:9], exchange[9])

    def wave(t):
        def act_at(lag, act):
            u = lax.div(t - lag, 2)

            def run():
                ex.decx[0] = spread(decs[u], sel)
                act(u)

            pl.when(jnp.logical_and(t >= lag, jnp.logical_and(2 * u + lag == t, u < seqs)))(run)

        act_at(6, ex.close)
        act_at(5, ex.scan)
        act_at(4, ex.middle)

    @pl.when(i == 0)
    def _():
        meet(("ctx",))
        sel[...] = head_map()
        gskip[...] = jnp.zeros_like(gskip)
        gggain[...] = jnp.zeros_like(gggain)

    wave(2 * i)

    @pl.when(i < seqs)
    def _():
        s = i
        cum = cumin[0]
        e_in, e_out, tot0, tot1, total = local_decays(cum)
        einx[...] = spread(e_in, sel)
        tot0x = spread(rows_of(tot0), sel)[0:1]
        s_in[0] = sin[0]
        s_in[1] = (tot0x * sin[0].astype(f32) + st0[0]).astype(bf16)
        cc = xb[0, :, DIN + NSTATE :]

        def gate_step(j, total_sq):
            cols = pl.ds(pl.multiple_of(j * TILE, TILE), TILE)
            for q in range(2):
                rows = both(q)
                ys[rows, cols] = ylocal[0, rows, cols] + einx[rows, cols] * mm(cc[rows], s_in[q, :, cols])
            y = ys[:, cols] + skip[:, cols] * xb[0, :, cols].astype(f32)
            g = gate[0, :, cols]
            gated = y * (g * gate_of(g))
            gs[:, cols] = gated
            sq = gated * gated
            return total_sq + sq[:, :HALF] + sq[:, HALF:]

        wave(2 * i + 1)
        sq = lax.fori_loop(0, DIN // TILE, gate_step, jnp.zeros((SPAN, HALF), f32))
        inv = lax.rsqrt(jnp.sum(sq, axis=1, keepdims=True) * (1.0 / DIN) + EPS)
        live = (lax.broadcasted_iota(jnp.int32, (SPAN, 1), 0) < rel[s]).astype(f32)
        drive = (live * cot[0].astype(f32)).astype(bf16)

        def back_step(j, acc):
            cols = pl.ds(pl.multiple_of(j * TILE, TILE), TILE)
            gm = mm_nt(drive, wout[cols, :])
            gated = gs[:, cols]
            unit = gated * inv
            low = (unit * ggain[:, cols]).astype(bf16)
            mlow[0, :, cols] = low
            ml_s[s, :, cols] = low
            gggain[:, cols] += jnp.sum(gm * unit, axis=0, keepdims=True)
            scaled = gm * ggain[:, cols]
            ss[:, cols] = scaled
            prod = scaled * gated
            return acc + prod[:, :HALF] + prod[:, HALF:]

        dots = lax.fori_loop(0, DIN // TILE, back_step, jnp.zeros((SPAN, HALF), f32))
        dots = jnp.sum(dots, axis=1, keepdims=True) * (1.0 / DIN)
        corr = inv * inv * inv * dots
        cct = jnp.transpose(cc.astype(f32)).astype(bf16)
        acc = jnp.zeros((SPAN, HALF), f32)
        dc = [jnp.zeros((HALF, HALF), f32) for _ in range(2)]
        for j in range(DIN // TILE):
            cols = slice(j * TILE, (j + 1) * TILE)
            g = gate[0, :, cols]
            sg = gate_of(g)
            sl = g * sg
            grad_gated = inv * ss[:, cols] - gs[:, cols] * corr
            dy = grad_gated * sl
            yn = ys[:, cols]
            x = xb[0, :, cols].astype(f32)
            y = yn + skip[:, cols] * x
            ggate[0, :, cols] = (grad_gated * y * (sg + sl * (1.0 - sg))).astype(bf16)
            dyb = dy.astype(bf16)
            dyout[0, :, cols] = dyb
            dy_s[s, :, cols] = dyb
            gskip[:, cols] += jnp.sum(dy * x, axis=0, keepdims=True)
            acc = acc + gather_heads(dy * yn, sel[:HALF, cols])
            dye = (dy * einx[:, cols]).astype(bf16)
            d0 = mm(cct[:, :HALF], dye[:HALF])
            d1 = mm(cct[:, HALF:], dye[HALF:])
            dir1[0, :, cols] = d1
            ex.buf[s, 0, :, cols] = (d0 + tot0x[:, cols] * d1).astype(bf16)
            for q in range(2):
                dc[q] = dc[q] + mm_nt(dye[both(q)], s_in[q, :, cols])
        wred[0] = acc
        for q in range(2):
            dcs[s, both(q)] = dc[q]
        ex.start(s)

    @pl.when(i >= seqs)
    def _():
        s = i - seqs
        causal, low_lanes = masks()
        cum = cumin[0]
        for q in range(2):
            cum_t[q] = jnp.transpose(cum[both(q)])
        einx[...] = spread(softplus(vin[0]), sel)
        bb = xb[0, :, DIN : DIN + NSTATE]
        cc = xb[0, :, DIN + NSTATE :]
        for q in range(2):
            g_s[q] = mm_nt(cc[both(q)], bb[both(q)])
        dg_s[...] = jnp.zeros_like(dg_s)

        def pair_step(p):
            cols = pl.ds(pl.multiple_of(p * HALF, HALF), HALF)
            decays = pair_decays(cum, cum_t, p, causal)
            for q in range(2):
                rows = both(q)
                xsb = (xb[0, rows, cols].astype(f32) * einx[rows, cols]).astype(bf16)
                dyb = dy_s[s, rows, cols]
                dyf = dyb.astype(f32)
                grads = []
                for a in range(2):
                    m = (decays[2 * q + a] * g_s[q]).astype(bf16)
                    grads.append(mm_tn(m, dyb))
                    mine = low_lanes if a == 0 else jnp.logical_not(low_lanes)
                    dm = mm_nt(jnp.where(mine, dyf, 0.0).astype(bf16), xsb)
                    dg_s[q] += dm * decays[2 * q + a]
                dxs[0, rows, cols] = jnp.where(low_lanes, grads[0], grads[1])

        loop(0, PAIRS // 2, pair_step)
        wave(2 * i + 1)
        loop(PAIRS // 2, PAIRS, pair_step)
        for q in range(2):
            rows = both(q)
            dg = dg_s[q].astype(bf16)
            dbc[0, rows, :NSTATE] = mm_tn(dg, cc[rows])
            dbc[0, rows, NSTATE:] = mm(dg, bb[rows]) + dcs[s, rows]
        live = (lax.broadcasted_iota(jnp.int32, (SPAN, 1), 0) < rel[s]).astype(f32)
        for j in range(D // TILE):
            cols = slice(j * TILE, (j + 1) * TILE)
            mixed[0, :, cols] = (live * (tok[0, :, cols].astype(f32) + mm(ml_s[s], wout[:, cols]))).astype(bf16)

    @pl.when(i == 2 * seqs - 1)
    def _():
        loop(4 * seqs, 2 * seqs + 5, wave)
        loop(0, seqs, ex.finish)


def third_kernel(
    cin, xb, spb, vin, cumin, dyin, wred, dxs, dbc, dir1, later, sin, loc, cw, dl, skip, pgate, pout,
    gz, gzh, gcw, gcb, gdb, gdl, rgate, rout,
    sel, dtx, eoutx, dact, xwb, dout, qacc, gp, *comm,
):
    s = pl.program_id(0)
    seqs = pl.num_programs(0)
    reducers = [
        Reducer(pgate, rgate, D // lax.axis_size("group"), GATE_CHUNK, False, comm[:8], comm[8]),
        Reducer(pout, rout, DIN // lax.axis_size("group"), OUT_CHUNK, True, comm[9:17], comm[17]),
    ]

    def wave(t):
        reducers[1].wave(t - reducers[0].chunks)
        reducers[0].wave(t)

    @pl.when(s == 0)
    def _():
        meet(("ctx", "group"))
        for r in reducers:
            loop(0, r.chunks, r.m_start)
        sel[...] = head_map()
        gcw[...] = jnp.zeros_like(gcw)
        gcb[...] = jnp.zeros_like(gcb)
        gdb[...] = jnp.zeros_like(gdb)
        gdl[...] = jnp.zeros_like(gdl)
        gp[0:RIM] = jnp.zeros((RIM, CONVW), f32)
        gp[RIM + SPAN :] = jnp.zeros((8, CONVW), f32)

    cum = cumin[0]
    v = vin[0]
    dt = softplus(v)
    e_in, e_out, tot0, tot1, total = local_decays(cum)
    dtx[...] = spread(dt, sel)
    eoutx[...] = spread(e_out, sel)
    tot1x = spread(rows_of(tot1), sel)[0:1]
    totalx = spread(rows_of(total), sel)[0:1]

    wave(3 * s - 2)

    @pl.when(s == 0)
    def _():
        for r in reducers:
            loop(0, r.chunks, r.m_done)

    wave(3 * s - 1)
    bb = xb[0, :, DIN : DIN + NSTATE]
    qacc[...] = jnp.zeros_like(qacc)
    dout[1] = later[0]
    dout[0] = (dir1[0] + tot1x * later[0].astype(f32)).astype(bf16)

    def state_step(j):
        cols = pl.ds(pl.multiple_of(j * TILE, TILE), TILE)
        for q in range(2):
            rows = both(q)
            x = xb[0, rows, cols].astype(f32)
            dte = dtx[rows, cols]
            eo = eoutx[rows, cols]
            dx_s = dxs[0, rows, cols] + eo * mm(bb[rows], dout[q, :, cols])
            dact[rows, cols] = dte * dx_s + skip[:, cols] * dyin[0, rows, cols].astype(f32)
            qacc[rows] += gather_heads(x * dx_s, sel[:HALF, cols])
            xwb[rows, cols] = (x * dte * eo).astype(bf16)

    loop(0, DIN // TILE, state_step)
    for q in range(2):
        rows = both(q)
        dact[rows, DIN : DIN + NSTATE] = dbc[0, rows, :NSTATE] + mm_nt(xwb[rows, :], dout[q])
        dact[rows, DIN + NSTATE :] = dbc[0, rows, NSTATE:]

    ends = jnp.sum(later[0].astype(f32) * (totalx * sin[0].astype(f32) + loc[0].astype(f32)), axis=0, keepdims=True)
    ends = gather_heads(rows_of(ends), sel[:HALF])[0:1]
    at_end = lax.broadcasted_iota(jnp.int32, (SPAN, 1), 0) == SPAN - 1
    dcum = wred[0] - dt * qacc[...] + jnp.where(at_end, ends, 0.0)
    glog = exact_mm(triangle(SPAN, False), dcum)
    rate = jnp.exp(dl[...])
    gpd = (qacc[...] - rate * glog) * sigmoid(v)
    lanes = lax.broadcasted_iota(jnp.int32, (SPAN, HALF), 1) < HEADS
    gpd = jnp.where(lanes, gpd, 0.0)
    gz[0, :, CONVW : CONVW + HALF] = gpd.astype(bf16)
    gz[0, :, CONVW + HALF :] = jnp.zeros((SPAN, HALF), bf16)
    gzh[0, :, CONVW:] = jnp.zeros((RIM, 2 * HALF), bf16)
    gdb[...] += jnp.sum(gpd, axis=0, keepdims=True)
    gdl[...] += -rate * jnp.sum(dt * glog, axis=0, keepdims=True)

    def out_step(j):
        cols = pl.ds(pl.multiple_of(j * HALF, HALF), HALF)
        gco = dact[:, cols] * spb[0, :, cols].astype(f32)
        gp[RIM : RIM + SPAN, cols] = gco
        gcb[:, cols] += jnp.sum(gco, axis=0, keepdims=True)
        own = cin[0, RIM:, cols].astype(f32)
        before = cin[0, :RIM, cols].astype(f32)
        main = jnp.zeros((SPAN, HALF), f32)
        rim = jnp.zeros((RIM, HALF), f32)
        for k in range(KCONV):
            ahead = KCONV - 1 - k
            moved = gp[RIM + ahead : RIM + ahead + SPAN, cols]
            early = gp[ahead : ahead + RIM, cols]
            main = main + cw[k : k + 1, cols] * moved
            rim = rim + cw[k : k + 1, cols] * early
            gcw[k : k + 1, cols] += jnp.sum(own * moved, axis=0, keepdims=True) + jnp.sum(
                before * early, axis=0, keepdims=True
            )
        gz[0, :, cols] = main.astype(bf16)
        gzh[0, :, cols] = rim.astype(bf16)

    wave(3 * s)
    loop(0, CONVW // HALF, out_step)

    @pl.when(s == seqs - 1)
    def _():
        loop(3 * seqs - 2, reducers[0].chunks + reducers[1].chunks + 4, wave)
        for r in reducers:
            loop(0, r.chunks, r.drain)


def tail_kernel(
    rel, tok, halo, cot, gain, ggate, gz, gzh, wfull, pconv, small,
    gtok, rconv, small_out,
    ggain, rim_out, rim_in, rim_send, rim_recv, *comm,
):
    s = pl.program_id(0)
    seqs = pl.num_programs(0)
    count = lax.axis_size("ctx")
    me = lax.axis_index("ctx")
    reducer = Reducer(pconv, rconv, D // lax.axis_size("group"), CONV_CHUNK, False, comm[:8], comm[8])
    little = Small(*comm[9:13])

    def rim_copy(q):
        return remote(rim_out.at[q], rim_in.at[q], rim_send.at[q], rim_recv.at[q], ctx=lax.rem(me + count - 1, count))

    def back(rows, grad):
        rows, inv, _ = normalized(rows, gain[...])
        ggain[...] += jnp.sum(grad * rows * inv, axis=0, keepdims=True)
        gained = gain[...] * grad
        mean = jnp.mean(gained * rows, axis=-1, keepdims=True)
        return inv * gained - rows * (inv * inv * inv * mean)

    @pl.when(s == 0)
    def _():
        meet(("ctx", "group"))
        loop(0, reducer.chunks, reducer.m_start)
        ggain[...] = jnp.zeros_like(ggain)
        for q in range(halo.shape[0]):
            rim_out[q] = back(halo[q], mm_nt(gzh[q, :, :CONVW], wfull[:, DIN:ZXW])).astype(bf16)
            pl.when(me > 0)(lambda q=q: rim_copy(q).start())

        @pl.when(me == count - 1)
        def _():
            rim_in[...] = jnp.zeros_like(rim_in)

        loop(0, reducer.chunks, reducer.m_done)

    @pl.when(s > 0)
    def _():
        reducer.wave(s - 1)

    grad = mm_nt(ggate[0], wfull[:, :DIN]) + mm_nt(gz[0, :, : CONVW + HALF], wfull[:, DIN:])
    live = (lax.broadcasted_iota(jnp.int32, (SPAN, 1), 0) < rel[s]).astype(f32)
    out = live * cot[0].astype(f32) + back(tok[0], grad)
    gtok[0, : SPAN - RIM] = out[: SPAN - RIM].astype(bf16)
    pl.when(me < count - 1)(lambda: rim_copy(s).wait_recv())
    gtok[0, SPAN - RIM :] = (out[SPAN - RIM :] + rim_in[s].astype(f32)).astype(bf16)

    @pl.when(s == seqs - 1)
    def _():
        held = comm[9]
        held[0] = small[...]
        for j in range(D // HALF):
            held[0, j : j + 1, :] = ggain[:, j * HALF : (j + 1) * HALF]
        little.start(0)
        first = halo.shape[0] - 1
        for h in range(4):
            reducer.wave(first + h)
            little.done(h)
            if h < 3:
                little.start(h + 1)
        small_out[...] = held[4]
        loop(first + 4, reducer.chunks + 4, reducer.wave)
        loop(0, reducer.chunks, reducer.drain)
        little.drain()
        for q in range(halo.shape[0]):
            pl.when(me > 0)(lambda q=q: rim_copy(q).wait_send())


def whole(shape):
    zeros = (0,) * len(shape)
    return pl.BlockSpec(shape, lambda s: zeros, pipeline_mode=pl.Buffered(1))


def summed(shape):
    zeros = (0,) * len(shape)
    return pl.BlockSpec(shape, lambda s: zeros)


def per_seq(*shape):
    zeros = (0,) * len(shape)
    return pl.BlockSpec((1,) + shape, lambda s: (s,) + zeros)


SMEM = pl.BlockSpec(memory_space=pltpu.SMEM)
ANY = pl.BlockSpec(memory_space=pl.ANY)


def staged(seqs, phase, *shape):
    zeros = (0,) * len(shape)
    if phase == 0:
        return pl.BlockSpec((1,) + shape, lambda i: (jnp.minimum(i, seqs - 1),) + zeros)
    if phase == 1:
        return pl.BlockSpec((1,) + shape, lambda i: (jnp.maximum(i - seqs, 0),) + zeros)
    return pl.BlockSpec((1,) + shape, lambda i: (lax.rem(i, seqs),) + zeros)


def call(kernel, steps, in_specs, outs, scratch, name, collective=None):
    params = dict(vmem_limit_bytes=VMEM_LIMIT)
    if collective is not None:
        params.update(collective_id=collective, has_side_effects=True)
    return pl.pallas_call(
        kernel,
        grid=(steps,),
        in_specs=in_specs,
        out_specs=[o[0] for o in outs],
        out_shape=[jax.ShapeDtypeStruct(o[1], o[2]) for o in outs],
        scratch_shapes=[pltpu.VMEM(*sc) if isinstance(sc, tuple) else sc for sc in scratch],
        compiler_params=pltpu.CompilerParams(**params),
        name=name,
    )


def lanes_of(v):
    return jnp.pad(v[None, :], ((0, 0), (0, HALF - v.shape[0])))


def local(
    tokens_in, seq_lengths, norm_gain, w_zx, w_delta, w_out, conv_weight, conv_bias,
    delta_bias, decay_log, skip_gain, gated_gain, cotangent,
):
    seqs = tokens_in.shape[0]
    count = lax.axis_size("ctx")
    group = lax.axis_size("group")
    chips = max(group // 2, 1)
    rel = seq_lengths - lax.axis_index("ctx") * SPAN
    gain = norm_gain[None, :]
    cb = conv_bias[None, :]
    db = lanes_of(delta_bias)
    dl = lanes_of(decay_log)
    skip = jnp.repeat(skip_gain, HEADDIM)[None, :]
    ggain = gated_gain[None, :]
    wcat = jnp.concatenate([w_zx, jnp.pad(w_delta, ((0, 0), (0, HALF - HEADS)))], axis=1)
    dma = pltpu.SemaphoreType.DMA
    at0 = lambda *shape: staged(seqs, 0, *shape)
    at1 = lambda *shape: staged(seqs, 1, *shape)
    at01 = lambda *shape: staged(seqs, 2, *shape)

    def tiled(rows, first, lead=None):
        def index(i):
            u = jnp.clip(i - first, 0, TILES - 1)
            return (0, 0, u if lead is None else jnp.where(i == 0, lead, u))

        return pl.BlockSpec((seqs, rows, TILE), index)

    state = (seqs, NSTATE, DIN)
    normed, nhalo, rhalo, cin, xb, spb, vraw, cum, st0, loc, ylocal, gate, decs, wfull, wofull, state_in = call(
        front_kernel,
        PIECES,
        [whole((seqs, SPAN, D)), ANY, ANY, ANY, whole((1, D)), whole((KCONV, CONVW)), whole((1, CONVW)), whole((1, HALF)),
         whole((1, HALF))],
        [
            (summed((seqs, SPAN, D)), (seqs, SPAN, D), bf16),
            (summed((seqs, RIM, D)), (seqs, RIM, D), bf16),
            (summed((seqs, RIM, D)), (seqs, RIM, D), bf16),
            (tiled(RIM + SPAN, 1, TILES), (seqs, RIM + SPAN, CONVW), bf16),
            (tiled(SPAN, 1, TILES), (seqs, SPAN, CONVW), bf16),
            (tiled(SPAN, 1, TILES), (seqs, SPAN, CONVW), bf16),
            (summed((seqs, SPAN, HALF)), (seqs, SPAN, HALF), f32),
            (summed((seqs, SPAN, HALF)), (seqs, SPAN, HALF), f32),
            (tiled(NSTATE, 1), state, f32),
            (tiled(NSTATE, 1), state, bf16),
            (tiled(SPAN, TILES + 1), (seqs, SPAN, DIN), f32),
            (tiled(SPAN, TILES + 1), (seqs, SPAN, DIN), f32),
            (summed((seqs, count * 8, HALF)), (seqs, count * 8, HALF), f32),
            (ANY, (D, ZXW + HALF), bf16),
            (ANY, (DIN, D), bf16),
            (ANY, state, bf16),
        ],
        [((2 * HALF, DIN), bf16), ((seqs, RIM, D), bf16), ((seqs, RIM + SPAN, D), bf16), ((D, ZXW + HALF), bf16),
         ((seqs, RIM + SPAN, TILE), f32), ((seqs, SPAN, DIN), bf16), ((seqs, NSTATE, SPAN), bf16),
         ((seqs, 2, HALF, HALF), f32), ((seqs, SPAN, 2 * HALF), bf16), ((seqs, SPAN, 2 * HALF), bf16),
         ((seqs, 2, HALF, HALF), f32), ((seqs, 8, DIN), f32), ((seqs, count * 8, HALF), f32)]
        + [dma((2,))] + [dma((PIECES + 1, chips))] * 4 + [dma((2,)), dma((1,)), dma((count,)), dma((count,))]
        + Exchange.scratch(TILES, seqs, TILE, count),
        "front",
        0,
    )(tokens_in, tokens_in, wcat, w_out, gain, conv_weight, cb, db, dl)

    mixed_out, mlow, dy, ggate, wred, dir1, gskip, gggain, dxs, dbc, later = call(
        middle_kernel,
        2 * seqs,
        [SMEM, at1(SPAN, D), at0(SPAN, D), at0(SPAN, DIN), at0(SPAN, DIN), at01(SPAN, CONVW), at01(SPAN, HALF),
         at01(SPAN, HALF), at0(NSTATE, DIN), at0(NSTATE, DIN), whole((seqs, count * 8, HALF)), whole((DIN, D)),
         whole((1, DIN)), whole((1, DIN))],
        [
            (at1(SPAN, D), (seqs, SPAN, D), bf16),
            (at0(SPAN, DIN), (seqs, SPAN, DIN), bf16),
            (at0(SPAN, DIN), (seqs, SPAN, DIN), bf16),
            (at0(SPAN, DIN), (seqs, SPAN, DIN), bf16),
            (at0(SPAN, HALF), (seqs, SPAN, HALF), f32),
            (at0(NSTATE, DIN), (seqs, NSTATE, DIN), f32),
            (summed((1, DIN)), (1, DIN), f32),
            (summed((1, DIN)), (1, DIN), f32),
            (at1(SPAN, DIN), (seqs, SPAN, DIN), f32),
            (at1(SPAN, 2 * NSTATE), (seqs, SPAN, 2 * NSTATE), f32),
            (ANY, (seqs, NSTATE, DIN), bf16),
        ],
        [((2 * HALF, DIN), bf16), ((2, HALF, HALF), f32), ((SPAN, DIN), f32), ((SPAN, DIN), f32), ((SPAN, DIN), f32),
         ((SPAN, DIN), f32), ((2, NSTATE, DIN), bf16), ((seqs, SPAN, HALF), f32), ((seqs, SPAN, DIN), bf16),
         ((seqs, SPAN, DIN), bf16), ((2, HALF, HALF), f32), ((2, HALF, HALF), f32)]
        + Exchange.scratch(seqs, 1, DIN, count),
        "middle",
        1,
    )(rel, tokens_in, cotangent, ylocal, gate, xb, vraw, cum, st0, state_in, decs, wofull, skip, ggain)

    live = (jnp.arange(SPAN, dtype=jnp.int32)[None, :] < rel[:, None]).astype(f32)[:, :, None]
    drive = (live * cotangent.astype(f32)).astype(bf16)
    flat = lambda v: v.reshape(-1, v.shape[-1])
    p_out = mm_tn(flat(mlow), flat(drive)).astype(bf16)
    p_gate = mm_tn(flat(normed), flat(ggate)).astype(bf16)

    gz, gzh, gcw, gcb, gdb, gdl, r_gate, r_out = call(
        third_kernel,
        seqs,
        [per_seq(RIM + SPAN, CONVW), per_seq(SPAN, CONVW), per_seq(SPAN, CONVW), per_seq(SPAN, HALF), per_seq(SPAN, HALF),
         per_seq(SPAN, DIN), per_seq(SPAN, HALF), per_seq(SPAN, DIN), per_seq(SPAN, 2 * NSTATE), per_seq(NSTATE, DIN),
         per_seq(NSTATE, DIN), per_seq(NSTATE, DIN), per_seq(NSTATE, DIN), whole((KCONV, CONVW)), whole((1, HALF)),
         whole((1, DIN)), whole((D, DIN)), whole((DIN, D))],
        [
            (per_seq(SPAN, GZW), (seqs, SPAN, GZW), bf16),
            (per_seq(RIM, GZW), (seqs, RIM, GZW), bf16),
            (summed((KCONV, CONVW)), (KCONV, CONVW), f32),
            (summed((1, CONVW)), (1, CONVW), f32),
            (summed((1, HALF)), (1, HALF), f32),
            (summed((1, HALF)), (1, HALF), f32),
            (summed((D // group, DIN)), (D // group, DIN), bf16),
            (summed((DIN // group, D)), (DIN // group, D), bf16),
        ],
        [((2 * HALF, DIN), bf16), ((SPAN, DIN), f32), ((SPAN, DIN), f32), ((SPAN, CONVW), f32), ((SPAN, DIN), bf16),
         ((2, NSTATE, DIN), bf16), ((SPAN, HALF), f32), ((RIM + SPAN + 8, CONVW), f32)]
        + Reducer.scratch(DIN // GATE_CHUNK, D // group, GATE_CHUNK, False, group, count)
        + Reducer.scratch(D // OUT_CHUNK, DIN // group, OUT_CHUNK, True, group, count),
        "third",
        2,
    )(cin, xb, spb, vraw, cum, dy, wred, dxs, dbc, dir1, later, state_in, loc, conv_weight, dl, skip, p_gate, p_out)

    p_conv = (mm_tn(flat(normed), flat(gz)) + mm_tn(flat(nhalo), flat(gzh))).astype(bf16)
    sizes = (D, KCONV * CONVW, CONVW, HALF, HALF, DIN, DIN)
    small = jnp.concatenate(
        [jnp.zeros((D,), f32), gcw.reshape(-1), gcb.reshape(-1), gdb[0], gdl[0], gskip.reshape(-1), gggain.reshape(-1)]
    ).reshape(-1, HALF)
    small = jnp.pad(small, ((0, -small.shape[0] % 8), (0, 0)))
    height = small.shape[0]
    widest = max(group // 2, count // 2, 2)

    gtok, r_conv, small = call(
        tail_kernel,
        seqs,
        [SMEM, per_seq(SPAN, D), whole((seqs, RIM, D)), per_seq(SPAN, D), whole((1, D)), per_seq(SPAN, DIN),
         per_seq(SPAN, GZW), whole((seqs, RIM, GZW)), whole((D, ZXW + HALF)), whole((D, GZW)), whole((height, HALF))],
        [
            (per_seq(SPAN, D), (seqs, SPAN, D), bf16),
            (summed((D // group, GZW)), (D // group, GZW), bf16),
            (summed((height, HALF)), (height, HALF), f32),
        ],
        [((1, D), f32), ((seqs, RIM, D), bf16), ((seqs, RIM, D), bf16), dma((seqs,)), dma((seqs,))]
        + Reducer.scratch(GZW // CONV_CHUNK, D // group, CONV_CHUNK, False, group, count)
        + [((5, height, HALF), f32), ((4, widest, height, HALF), f32), dma((4, widest)), dma((4, widest))],
        "tail",
        3,
    )(rel, tokens_in, rhalo, cotangent, gain, ggate, gz, gzh, wfull, p_conv, small)

    g_zx = jnp.concatenate([r_gate, r_conv[:, :CONVW]], axis=1).astype(f32)
    g_delta = r_conv[:, CONVW : CONVW + HEADS].astype(f32)
    small = small.reshape(-1)
    at = 0
    pieces = []
    for size in sizes:
        pieces.append(small[at : at + size])
        at += size
    return (
        mixed_out, gtok, pieces[0], g_zx, g_delta, r_out.astype(f32), pieces[1].reshape(KCONV, CONVW), pieces[2],
        pieces[3][:HEADS], pieces[4][:HEADS], pieces[5].reshape(HEADS, HEADDIM).sum(1), pieces[6],
    )


def solution(mesh):
    rows = P("group", "ctx", None)
    own = P("group", None)
    in_specs = (rows, P("group"), P(), own, own, own, P(), P(), P(), P(), P(), P(), rows)
    out_specs = (rows, rows, P(), own, own, own, P(), P(), P(), P(), P(), P())
    return jax.shard_map(local, mesh=mesh, in_specs=in_specs, out_specs=out_specs, check_vma=False)
```

```python
import jax
import jax.numpy as jnp
from jax import lax
from jax.experimental import pallas as pl
from jax.experimental.pallas import tpu as pltpu
from jax.sharding import PartitionSpec as P

D = 768
HEADS = 24
HEADDIM = 64
NSTATE = 128
KCONV = 4
SPAN = 256
DIN = 1536
CONVW = 1792
ZXW = 3328
RIM = 16
HALF = 128
TILE = 256
PAIRS = 12
EPS = 1e-05

f32 = jnp.float32
bf16 = jnp.bfloat16
NT = (((1,), (1,)), ((), ()))
TN = (((0,), (0,)), ((), ()))
VMEM_LIMIT = 62 * 1024 * 1024
GATE_CHUNK = 512
OUT_CHUNK = 256
CONV_CHUNK = 512
MIDDLE_LAG = 2
SCAN_LAG = 4
HOPS = ("group", "ctx")
CLOSE_LAG = 6
GZW = 2048


def mm(a, b):
    return jnp.dot(a, b, preferred_element_type=f32)


def mm_nt(a, b):
    return lax.dot_general(a, b, NT, preferred_element_type=f32)


def mm_tn(a, b):
    return lax.dot_general(a, b, TN, preferred_element_type=f32)


def halves(v):
    high = v.astype(bf16)
    return high, (v - high.astype(f32)).astype(bf16)


def head_map():
    rows = lax.broadcasted_iota(jnp.int32, (2 * HALF, DIN), 0) % HALF
    cols = lax.broadcasted_iota(jnp.int32, (2 * HALF, DIN), 1) // HEADDIM
    return jnp.where(rows == cols, 1.0, 0.0).astype(bf16)


def spread(v, sel):
    return mm(jnp.concatenate(halves(v), axis=1), sel[...])


def gather_heads(v, sel_part):
    high, low = halves(v)
    return mm_nt(high, sel_part) + mm_nt(low, sel_part)


def triangle(size, lower):
    rows = lax.broadcasted_iota(jnp.int32, (size, size), 0)
    cols = lax.broadcasted_iota(jnp.int32, (size, size), 1)
    keep = rows >= cols if lower else rows <= cols
    return jnp.where(keep, 1.0, 0.0).astype(f32)


def exact_mm(a, b):
    return jnp.dot(a, b, precision=lax.Precision.HIGHEST, preferred_element_type=f32)


def softplus(v):
    return jnp.maximum(v, 0.0) + jnp.log1p(jnp.exp(-jnp.abs(v)))


def sigmoid(v):
    return 1.0 / (1.0 + jnp.exp(-v))


def gate_of(v):
    return 0.5 * jnp.tanh(0.5 * v) + 0.5


def local_decays(cum):
    mid, end = cum[HALF - 1 : HALF], cum[SPAN - 1 : SPAN]
    rows = lax.broadcasted_iota(jnp.int32, (SPAN, 1), 0)
    first = rows < HALF
    start = jnp.where(first, 0.0, mid)
    stop = jnp.where(first, mid, end)
    return jnp.exp(cum - start), jnp.exp(stop - cum), jnp.exp(mid), jnp.exp(end - mid), jnp.exp(end)


def rows_of(v):
    return jnp.broadcast_to(v, (8, v.shape[1]))


def normalized(rows, gain):
    rows = rows.astype(f32)
    inv = lax.rsqrt(jnp.mean(rows * rows, axis=-1, keepdims=True) + EPS)
    return rows, inv, (rows * inv * gain).astype(bf16)


def remote(src, dst, send_sem, recv_sem, **where):
    return pltpu.make_async_remote_copy(
        src_ref=src, dst_ref=dst, send_sem=send_sem, recv_sem=recv_sem,
        device_id=where, device_id_type=pl.DeviceIdType.MESH,
    )


def loop(start, stop, body):
    def step(i, c):
        body(i)
        return c

    lax.fori_loop(start, stop, step, 0)


def meet(axes):
    barrier = pltpu.get_barrier_semaphore()
    total = 0
    for axis in axes:
        size = lax.axis_size(axis)
        me = lax.axis_index(axis)

        def greet(d):
            pl.semaphore_signal(
                barrier, inc=1, device_id={axis: lax.rem(me + d, size)}, device_id_type=pl.DeviceIdType.MESH
            )

        loop(1, size, greet)
        total += size - 1
    pl.semaphore_wait(barrier, total)


class Exchange:
    def __init__(self, reverse, out_at, bufs, sems):
        self.reverse, self.out_at, self.sems = reverse, out_at, sems
        self.buf, self.y_buf, self.z_src, self.z_buf, self.z_back, self.p_buf, self.mine_buf, self.their_buf, self.decx = bufs
        self.depth = self.buf.shape[1]
        ctx = lax.axis_index("ctx")
        self.ctx = ctx
        self.outer = lax.axis_size("ctx") // 2
        self.owners = min(self.outer, 4)
        self.stride = self.outer // self.owners
        self.inner = lax.rem(ctx, 2)
        self.line = ctx // 2
        self.mine = self.line // self.stride
        self.half = NSTATE // 2
        self.rows = self.half // self.owners

    def half_rows(self, inner):
        return pl.ds(pl.multiple_of(inner * self.half, self.half), self.half)

    def part(self, j):
        return pl.ds(pl.multiple_of(j * self.rows, self.rows), self.rows)

    def other_owners(self, body):
        if self.stride == 1:
            loop(1, self.owners, lambda d: body(lax.rem(self.mine + d, self.owners)))
        else:
            loop(0, self.owners, lambda j: pl.when(j * self.stride != self.line)(lambda: body(j)))

    def other_lines(self, body):
        loop(1, self.outer, lambda d: body(lax.rem(self.line + d, self.outer)))

    def if_owner(self, body):
        if self.stride == 1:
            body()
        else:
            pl.when(self.mine * self.stride == self.line)(body)

    def y_copy(self, u):
        return remote(
            self.buf.at[u, :, self.half_rows(1 - self.inner)], self.y_buf.at[u], self.sems.at[0, u, 0], self.sems.at[1, u, 0],
            ctx=self.ctx + 1 - 2 * self.inner,
        )

    def z_copy(self, u, j, sender):
        return remote(
            self.z_src.at[u, :, self.part(j)], self.z_buf.at[u, sender], self.sems.at[2, u, j], self.sems.at[3, u, sender],
            ctx=j * self.stride * 2 + self.inner,
        )

    def b_copy(self, u, line, j):
        return remote(
            self.z_back.at[u, line], self.p_buf.at[u, :, self.part(j)], self.sems.at[4, u, line], self.sems.at[5, u, j],
            ctx=line * 2 + self.inner,
        )

    def f_copy(self, u, inner):
        return remote(
            self.their_buf.at[u], self.out_at(u, self.half_rows(inner)), self.sems.at[6, u, 0], self.sems.at[7, u, 0],
            ctx=self.ctx + 1 - 2 * self.inner,
        )

    def keep(self, u):
        return pltpu.make_async_copy(self.mine_buf.at[u], self.out_at(u, self.half_rows(self.inner)), self.sems.at[8, u, 0])

    def decay(self, a, block):
        return self.decx[a, pl.ds(pl.multiple_of(block * 8, 8), 8), :][0:1]

    def pair(self, u, a):
        own = self.buf[u, a, self.half_rows(self.inner), :].astype(f32)
        other = self.y_buf[u, a].astype(f32)
        first = self.inner == 0
        return jnp.where(first, own, other), jnp.where(first, other, own)

    def start(self, u):
        self.y_copy(u).start()

    def middle(self, u):
        self.y_copy(u).wait_recv()
        for a in range(self.depth):
            s0, s1 = self.pair(u, a)
            if self.reverse:
                total = s0 + self.decay(a, 2 * self.line) * s1
            else:
                total = self.decay(a, 2 * self.line + 1) * s0 + s1
            self.z_src[u, a] = total.astype(bf16)
        self.other_owners(lambda j: self.z_copy(u, j, self.line).start())

    def scan(self, u):
        def run():
            self.other_lines(lambda line: self.z_copy(u, self.mine, line).wait_recv())
            self.z_buf[u, self.line] = self.z_src[u, :, self.part(self.mine), :]
            for a in range(self.depth):

                def step(k, carry):
                    line = self.outer - 1 - k if self.reverse else k
                    self.z_back[u, line, a] = carry.astype(bf16)
                    both_decays = self.decay(a, 2 * line) * self.decay(a, 2 * line + 1)
                    return both_decays * carry + self.z_buf[u, line, a].astype(f32)

                lax.fori_loop(0, self.outer, step, jnp.zeros(self.z_buf.shape[3:], f32))
            self.other_lines(lambda line: self.b_copy(u, line, self.mine).start())
            self.p_buf[u, :, self.part(self.mine), :] = self.z_back[u, self.line]

        self.if_owner(run)

    def close(self, u):
        self.other_owners(lambda j: self.b_copy(u, self.line, j).wait_recv())
        for a in range(self.depth):
            s0, s1 = self.pair(u, a)
            near = self.p_buf[u, a].astype(f32)
            if self.reverse:
                far = s1 + self.decay(a, 2 * self.line + 1) * near
            else:
                far = s0 + self.decay(a, 2 * self.line) * near
            keeps_near = self.inner == (1 if self.reverse else 0)
            self.mine_buf[u, a] = jnp.where(keeps_near, near, far).astype(bf16)
            self.their_buf[u, a] = jnp.where(keeps_near, far, near).astype(bf16)
        self.f_copy(u, self.inner).start()
        self.keep(u).start()

    def finish(self, u):
        self.f_copy(u, 1 - self.inner).wait_recv()
        self.keep(u).wait()
        self.y_copy(u).wait_send()
        self.other_owners(lambda j: self.z_copy(u, j, self.line).wait_send())
        self.if_owner(lambda: self.other_lines(lambda line: self.b_copy(u, line, self.mine).wait_send()))
        self.f_copy(u, self.inner).wait_send()

    @staticmethod
    def scratch(units, depth, lanes, count):
        outer = count // 2
        half = NSTATE // 2
        rows = half // min(outer, 4)
        bufs = [(units, depth, NSTATE, lanes), (units, depth, half, lanes), (units, depth, half, lanes),
                (units, outer, depth, rows, lanes), (units, outer, depth, rows, lanes), (units, depth, half, lanes),
                (units, depth, half, lanes), (units, depth, half, lanes)]
        return (
            [(b, bf16) for b in bufs]
            + [((depth, count * 8, lanes), f32)]
            + [pltpu.SemaphoreType.DMA((9, units, max(outer, 4)))]
        )


class Spread:
    def __init__(self, shard, full, sems):
        self.shard, self.full = shard, full
        self.x_send, self.x_recv, self.m_send, self.m_recv, self.own = sems
        size = lax.axis_size("group")
        self.cores = 2 if size % 2 == 0 else 1
        self.chips = size // self.cores
        self.me = lax.axis_index("group")
        self.core = lax.rem(self.me, self.cores)
        self.chip = self.me // self.cores
        self.rows = shard.shape[0]

    def place(self, member, cols):
        return self.full.at[pl.ds(pl.multiple_of(member * self.rows, 32), self.rows), cols]

    def across(self, p, cols, d):
        peer = lax.rem(self.chip + d, self.chips) * self.cores + self.core
        return remote(
            self.shard.at[:, cols], self.place(self.me, cols), self.x_send.at[p, d], self.x_recv.at[p, d], group=peer
        )

    def mate(self, p, cols, d):
        member = lax.rem(self.chip + self.chips - d, self.chips) * self.cores + self.core
        src = self.shard.at[:, cols] if d == 0 else self.place(member, cols)
        return remote(
            src, self.place(member, cols), self.m_send.at[p, d], self.m_recv.at[p, d],
            group=self.me + 1 - 2 * self.core,
        )

    def keep(self, p):
        return pltpu.make_async_copy(self.shard, self.place(self.me, slice(None)), self.own.at[p])

    def start_chip(self, p):
        if self.cores == 2:
            self.mate(p, slice(None), 0).start()
        self.keep(p).start()

    def finish_chip(self, p):
        if self.cores == 2:
            self.mate(p, slice(None), 0).wait_recv()
        self.keep(p).wait()

    def start(self, p, cols):
        for d in range(1, self.chips):
            self.across(p, cols, d).start()

    def forward(self, p, cols):
        for d in range(1, self.chips):
            self.across(p, cols, d).wait_recv()
            if self.cores == 2:
                self.mate(p, cols, d).start()

    def finish(self, p, cols):
        if self.cores == 2:
            for d in range(1, self.chips):
                self.mate(p, cols, d).wait_recv()

    def drain(self, p, cols):
        for d in range(1, self.chips):
            self.across(p, cols, d).wait_send()
            if self.cores == 2:
                self.mate(p, cols, d).wait_send()

    def drain_chip(self, p):
        if self.cores == 2:
            self.mate(p, slice(None), 0).wait_send()


def owner_count(rows, width, by_rows, outer):
    fits = lambda n: (rows // 2) % (16 * n) == 0 if by_rows else width % (128 * n) == 0
    return max(n for n in (1, 2, 4) if outer % n == 0 and fits(n))


class Reducer:
    def __init__(self, part, out, rows, width, by_rows, bufs, sems):
        self.part, self.out, self.rows, self.width, self.by_rows = part, out, rows, width, by_rows
        self.m_buf, self.x_buf, self.y_src, self.y_buf, self.z_src, self.z_buf, self.full = bufs
        self.x_src = self.m_buf
        self.sems = sems
        self.chunks = part.shape[1] // width
        self.group = lax.axis_index("group")
        self.cores = 2
        self.chips = lax.axis_size("group") // 2
        self.core = lax.rem(self.group, 2)
        self.chip = self.group // 2
        self.ctx = lax.axis_index("ctx")
        self.outer = lax.axis_size("ctx") // 2
        self.owners = owner_count(rows, width, by_rows, self.outer)
        self.stride = self.outer // self.owners
        self.inner = lax.rem(self.ctx, 2)
        self.line = self.ctx // 2
        self.mine = self.line // self.stride
        self.half = rows // 2

    def cols(self, k):
        return pl.ds(pl.multiple_of(k * self.width, self.width), self.width)

    def member(self, chip, core):
        return pl.ds(pl.multiple_of((chip * 2 + core) * self.rows, 64), self.rows)

    def half_rows(self, inner):
        return pl.ds(pl.multiple_of(inner * self.half, 16), self.half)

    def piece(self, j, base):
        if self.by_rows:
            n = self.half // self.owners
            return pl.ds(pl.multiple_of(base + j * n, 16), n), pl.ds(0, self.width)
        n = self.width // self.owners
        return pl.ds(pl.multiple_of(base, 16), self.half), pl.ds(pl.multiple_of(j * n, 128), n)

    def m_copy(self, k, chip):
        return remote(
            self.part.at[self.member(chip, 1 - self.core), self.cols(k)], self.m_buf.at[k, chip],
            self.sems.at[0, k, chip], self.sems.at[1, k, chip], group=self.group + 1 - 2 * self.core,
        )

    def x_copy(self, k, chip, sender):
        return remote(
            self.x_src.at[k, chip], self.x_buf.at[k, sender], self.sems.at[2, k, chip], self.sems.at[3, k, sender],
            group=chip * 2 + self.core,
        )

    def y_copy(self, k):
        return remote(
            self.y_src.at[k, self.half_rows(1 - self.inner)], self.y_buf.at[k], self.sems.at[4, k, 0], self.sems.at[5, k, 0],
            ctx=self.ctx + 1 - 2 * self.inner,
        )

    def z_copy(self, k, j, sender):
        rows, cols = self.piece(j, 0)
        return remote(
            self.z_src.at[k, rows, cols], self.z_buf.at[k, sender], self.sems.at[6, k, j], self.sems.at[7, k, sender],
            ctx=j * self.stride * 2 + self.inner,
        )

    def b_copy(self, k, line, j):
        rows, cols = self.piece(j, self.inner * self.half)
        return remote(
            self.full.at[k, rows, cols], self.full.at[k, rows, cols], self.sems.at[8, k, line], self.sems.at[9, k, j],
            ctx=line * 2 + self.inner,
        )

    def f_copy(self, k, inner):
        rows = self.half_rows(inner)
        return remote(
            self.full.at[k, rows], self.full.at[k, rows], self.sems.at[10, k, 0], self.sems.at[11, k, 0],
            ctx=self.ctx + 1 - 2 * self.inner,
        )

    def other_chips(self, body):
        for d in range(1, self.chips):
            body(lax.rem(self.chip + d, self.chips))

    def other_owners(self, body):
        if self.stride == 1:
            for d in range(1, self.owners):
                body(lax.rem(self.mine + d, self.owners))
        else:
            for j in range(self.owners):
                pl.when(j * self.stride != self.line)(lambda j=j: body(j))

    def other_lines(self, body):
        loop(1, self.outer, lambda d: body(lax.rem(self.line + d, self.outer)))

    def if_owner(self, body):
        if self.stride == 1:
            body()
        else:
            pl.when(self.mine * self.stride == self.line)(body)

    def m_start(self, k):
        for chip in range(self.chips):
            self.m_copy(k, chip).start()

    def m_done(self, k):
        for chip in range(self.chips):
            self.m_copy(k, chip).wait_recv()
            own = self.part[self.member(chip, self.core), self.cols(k)].astype(f32)
            self.x_src[k, chip] = (own + self.m_buf[k, chip].astype(f32)).astype(bf16)
        self.other_chips(lambda chip: self.x_copy(k, chip, self.chip).start())

    def x_done(self, k):
        total = self.x_src[k, self.chip].astype(f32)
        for d in range(1, self.chips):
            chip = lax.rem(self.chip + d, self.chips)
            self.x_copy(k, chip, chip).wait_recv()
            total = total + self.x_buf[k, chip].astype(f32)
        self.y_src[k] = total.astype(bf16)
        self.y_copy(k).start()

    def y_done(self, k):
        self.y_copy(k).wait_recv()
        own = self.y_src[k, self.half_rows(self.inner), :].astype(f32)
        self.z_src[k] = (own + self.y_buf[k].astype(f32)).astype(bf16)
        self.other_owners(lambda j: self.z_copy(k, j, self.line).start())

    def z_done(self, k):
        def run():
            rows, cols = self.piece(self.mine, 0)
            self.other_lines(lambda line: self.z_copy(k, self.mine, line).wait_recv())
            self.z_buf[k, self.line] = self.z_src[k, rows, cols]
            total = self.z_buf[k, 0].astype(f32)
            for line in range(1, self.outer):
                total = total + self.z_buf[k, line].astype(f32)
            rows, cols = self.piece(self.mine, self.inner * self.half)
            self.full[k, rows, cols] = total.astype(bf16)
            self.other_lines(lambda line: self.b_copy(k, line, self.mine).start())

        self.if_owner(run)

    def b_done(self, k):
        self.other_owners(lambda j: self.b_copy(k, self.line, j).wait_recv())
        self.f_copy(k, self.inner).start()

    def f_done(self, k):
        self.f_copy(k, 1 - self.inner).wait_recv()
        self.out[:, self.cols(k)] = self.full[k]

    def drain(self, k):
        for chip in range(self.chips):
            self.m_copy(k, chip).wait_send()
        self.other_chips(lambda chip: self.x_copy(k, chip, self.chip).wait_send())
        self.y_copy(k).wait_send()
        self.other_owners(lambda j: self.z_copy(k, j, self.line).wait_send())
        self.if_owner(lambda: self.other_lines(lambda line: self.b_copy(k, line, self.mine).wait_send()))
        self.f_copy(k, self.inner).wait_send()

    def wave(self, t):
        for lag, act in ((4, self.f_done), (3, self.b_done), (2, self.z_done), (1, self.y_done), (0, self.x_done)):
            k = t - lag
            pl.when(jnp.logical_and(k >= 0, k < self.chunks))(lambda k=k, act=act: act(k))

    @staticmethod
    def scratch(chunks, rows, width, by_rows, group, count):
        chips, outer = group // 2, count // 2
        owners = owner_count(rows, width, by_rows, outer)
        half = rows // 2
        piece = (half // owners, width) if by_rows else (half, width // owners)
        bufs = [(chunks, chips, rows, width), (chunks, chips, rows, width), (chunks, rows, width),
                (chunks, half, width), (chunks, half, width), (chunks, outer) + piece, (chunks, rows, width)]
        return [(b, bf16) for b in bufs] + [pltpu.SemaphoreType.DMA((12, chunks, max(chips, outer, 2)))]


class Small:
    def __init__(self, held, got, sends, recvs):
        self.held, self.got, self.sends, self.recvs = held, got, sends, recvs

    def copy(self, h, j, sender):
        return remote(
            self.held.at[h], self.got.at[h, sender], self.sends.at[h, j], self.recvs.at[h, sender], **{HOPS[h]: j}
        )

    def others(self, h, body):
        size, mine = lax.axis_size(HOPS[h]), lax.axis_index(HOPS[h])
        loop(1, size, lambda d: body(lax.rem(mine + d, size)))

    def start(self, h):
        mine = lax.axis_index(HOPS[h])
        self.others(h, lambda j: self.copy(h, j, mine).start())

    def done(self, h):
        self.others(h, lambda j: self.copy(h, j, j).wait_recv())
        self.got[h, lax.axis_index(HOPS[h])] = self.held[h]
        total = self.got[h, 0]
        for j in range(1, lax.axis_size(HOPS[h])):
            total = total + self.got[h, j]
        self.held[h + 1] = total

    def drain(self):
        for h in range(2):
            mine = lax.axis_index(HOPS[h])
            self.others(h, lambda j: self.copy(h, j, mine).wait_send())

    @staticmethod
    def scratch(height, group, count):
        widest = max(group, count)
        dma = pltpu.SemaphoreType.DMA
        return [((3, height, HALF), f32), ((2, widest, height, HALF), f32), dma((2, widest)), dma((2, widest))]


def masks():
    rows = lax.broadcasted_iota(jnp.int32, (HALF, HALF), 0)
    cols = lax.broadcasted_iota(jnp.int32, (HALF, HALF), 1)
    return rows >= cols, cols < HEADDIM


def both(q):
    return slice(q * HALF, (q + 1) * HALF)


def pair_decays(cum, cum_t, p, causal):
    rolled = pltpu.roll(cum, lax.rem(HALF - 2 * p, HALF), 1)
    out = []
    for q in range(2):
        for a in range(2):
            gaps = rolled[both(q), a : a + 1] - cum_t[q, pl.ds(2 * p + a, 1), :]
            out.append(jnp.exp(jnp.where(causal, gaps, -jnp.inf)))
    return out


TILES = DIN // TILE
PIECES = 2 * TILES + 1
DT0 = DIN + CONVW - 2 * NSTATE


def front_kernel(
    tok, tok_any, wcat, wout, gain, cw, cb, db, dl,
    nt, nth, rhalo, cin, xb, spb, vout, cumout, st0, loc, ylocal, gate, decs_out, wfull, wofull, sin,
    sel, halo, nh_s, ext, w, cin_s, xs_s, bt, scores, out_cat, dt_cat, cum_t, tot1x, decs,
    halo_sem, x_send, x_recv, m_send, m_recv, w_own, w_store, dec_send, dec_recv, *exchange,
):
    i = pl.program_id(0)
    seqs = tok.shape[0]
    count = lax.axis_size("ctx")
    me = lax.axis_index("ctx")
    sems = (x_send, x_recv, m_send, m_recv, w_own)
    zx, wo = Spread(wcat, w, sems), Spread(wout, wofull, sems)
    last = PIECES

    def unit_cols(u):
        return pl.ds(pl.multiple_of(u * TILE, TILE), TILE)

    def piece(p):
        at = jnp.where(p <= TILES, DIN + (p - 1) * TILE, (p - 1 - TILES) * TILE)
        return pl.ds(pl.multiple_of(at, TILE), TILE)

    first_piece = pl.ds(DT0, 2 * NSTATE + HALF)
    ex = Exchange(False, lambda u, rows: sin.at[:, rows, unit_cols(u)], exchange[:9], exchange[9])
    halo_copy = remote(
        tok_any.at[:, pl.ds(SPAN - RIM, RIM), :], halo, halo_sem.at[0], halo_sem.at[1], ctx=lax.rem(me + 1, count)
    )
    keep_w = pltpu.make_async_copy(w, wfull, w_store.at[0])

    def dec_copy(block, sender):
        rows = pl.ds(pl.multiple_of(sender * 8, 8), 8)
        return remote(decs.at[:, rows, :], decs.at[:, rows, :], dec_send.at[block], dec_recv.at[sender], ctx=block)

    def other_blocks(body):
        loop(1, count, lambda d: body(lax.rem(me + d, count)))

    def conv_tile(s, cols_w, cols_c):
        cin_s[s] = mm(ext[s], w[:, cols_w])
        cin[s] = cin_s[s].astype(bf16)
        o = cb[:, cols_c]
        for k in range(KCONV):
            o = o + cw[k : k + 1, cols_c] * cin_s[s, RIM - KCONV + 1 + k : RIM - KCONV + 1 + k + SPAN, :]
        sg = gate_of(o)
        a = o * sg
        xb[s] = a.astype(bf16)
        spb[s] = (sg + a * (1.0 - sg)).astype(bf16)
        return a

    def unit_decays(u):
        for s in range(seqs):
            ex.decx[s] = spread(decs[s], sel.at[:, unit_cols(u)])

    @pl.when(i == 0)
    def _():
        meet(("ctx", "group"))
        pl.when(me < count - 1)(lambda: halo_copy.start())
        zx.start(0, first_piece)
        zx.start_chip(0)
        zx.start(1, piece(1))
        zx.start(2, piece(2))
        wo.start_chip(1)
        sel[...] = head_map()

        @pl.when(me == 0)
        def _():
            halo[...] = jnp.zeros_like(halo)

        def norm_main(s):
            nm = normalized(tok[s], gain[...])[2]
            ext[s, RIM:] = nm
            nt[:, pl.ds(pl.multiple_of(s * SPAN, SPAN), SPAN)] = jnp.transpose(nm.astype(f32)).astype(bf16)

        loop(0, seqs, norm_main)

        @pl.when(me > 0)
        def _():
            halo_copy.wait_recv()

        def norm_halo(s):
            nh = normalized(halo[s], gain[...])[2]
            ext[s, 0:RIM] = nh
            nh_s[pl.ds(pl.multiple_of(s * RIM, RIM), RIM), :] = nh.astype(f32)
            rhalo[s] = halo[s]

        loop(0, seqs, norm_halo)
        nth[...] = jnp.transpose(nh_s[...]).astype(bf16)
        zx.forward(0, first_piece)
        zx.finish_chip(0)

    @pl.when(i + 1 < PIECES)
    def _():
        zx.forward(i + 1, piece(i + 1))

    @pl.when(i + 3 < PIECES)
    def _():
        zx.start(i + 3, piece(i + 3))

    @pl.when(i + 3 == PIECES)
    def _():
        wo.start(last, slice(None))

    @pl.when(i == 0)
    def _():
        zx.finish(0, first_piece)

        def delta(s):
            a = conv_tile(s, slice(DT0, DT0 + TILE), slice(DIN, DIN + TILE))
            bb, cc = a[:, :NSTATE].astype(bf16), a[:, NSTATE:].astype(bf16)
            bt[s] = jnp.transpose(a[:, :NSTATE]).astype(bf16)
            for q in range(2):
                scores[s, q] = mm_nt(cc[both(q)], bb[both(q)])
            v = mm(ext[s, RIM:], w[:, DT0 + TILE :]) + db[...]
            vout[s] = v
            dt = softplus(v)
            cum = exact_mm(triangle(SPAN, True), -jnp.exp(dl[...]) * dt)
            cumout[s] = cum
            for q in range(2):
                cum_t[s, q] = jnp.transpose(cum[both(q)])
            e_in, e_out, tot0, tot1, total = local_decays(cum)
            decs[s, pl.ds(pl.multiple_of(me * 8, 8), 8), :] = rows_of(total)
            out_cat[s] = jnp.concatenate(halves(dt * e_out), axis=1)
            dt_cat[s] = jnp.concatenate(halves(dt), axis=1)
            tot1x[s] = spread(rows_of(tot1), sel)

        loop(0, seqs, delta)
        other_blocks(lambda b: dec_copy(b, me).start())

    @pl.when(jnp.logical_and(i >= 1, i < PIECES))
    def _():
        zx.finish(i, piece(i))

    def act_at(lag, act):
        u = i - 1 - lag
        pl.when(jnp.logical_and(u >= 0, u < TILES))(lambda: act(u))

    def close(u):
        unit_decays(u)
        ex.close(u)

    def scan(u):
        unit_decays(u)
        ex.scan(u)

    def middle(u):
        unit_decays(u)
        ex.middle(u)

    @pl.when(i == 3)
    def _():
        other_blocks(lambda b: dec_copy(b, b).wait_recv())

    act_at(CLOSE_LAG, close)
    act_at(SCAN_LAG, scan)
    act_at(MIDDLE_LAG, middle)

    @pl.when(jnp.logical_and(i >= 1, i <= TILES))
    def _():
        u = i - 1
        cols = unit_cols(u)

        def x_tile(s):
            a = conv_tile(s, piece(i), cols)
            xs_s[s, :, cols] = a.astype(bf16)
            xw = (a * mm(out_cat[s], sel[:, cols])).astype(bf16)
            s0 = mm(bt[s, :, :HALF], xw[:HALF])
            s1 = mm(bt[s, :, HALF:], xw[HALF:])
            st0[s] = s0.astype(bf16)
            low = (tot1x[s, :, cols][0:1] * s0 + s1).astype(bf16)
            loc[s] = low
            ex.buf[u, s] = low

        loop(0, seqs, x_tile)
        ex.start(u)

    @pl.when(i > TILES)
    def _():
        u = i - 1 - TILES
        causal, low_lanes = masks()

        def intra(s):
            cum = cumout[s]
            dtx = mm(dt_cat[s], sel[:, unit_cols(u)])
            for h in range(2):
                p = 2 * u + h
                lanes = slice(h * HALF, (h + 1) * HALF)
                decays = pair_decays(cum, cum_t.at[s], p, causal)
                for q in range(2):
                    rows = both(q)
                    m = jnp.concatenate([(decays[2 * q + a] * scores[s, q]).astype(bf16) for a in range(2)], axis=1)
                    x = xs_s[s, rows, pl.ds(pl.multiple_of(p * HALF, HALF), HALF)].astype(f32) * dtx[rows, lanes]
                    x = jnp.concatenate([jnp.where(low_lanes, x, 0.0), jnp.where(low_lanes, 0.0, x)], axis=0)
                    ylocal[s, rows, lanes] = mm(m, x.astype(bf16)).astype(bf16)
            gate[s] = mm(ext[s, RIM:], w[:, piece(i)]).astype(bf16)

        loop(0, seqs, intra)

    @pl.when(i == PIECES - 1)
    def _():
        keep_w.start()
        decs_out[...] = decs[...]
        wo.forward(last, slice(None))
        loop(TILES + TILES - CLOSE_LAG, TILES, close)
        loop(0, TILES, ex.finish)
        wo.finish(last, slice(None))
        wo.finish_chip(1)
        zx.drain_chip(0)
        wo.drain_chip(1)
        zx.drain(0, first_piece)
        loop(1, PIECES, lambda p: zx.drain(p, piece(p)))
        wo.drain(last, slice(None))
        other_blocks(lambda b: dec_copy(b, me).wait_send())
        pl.when(me < count - 1)(lambda: halo_copy.wait_send())
        keep_w.wait()


def middle_kernel(
    rel, tok, cot, ylocal, gate, xb, vin, cumin, st0, sin, decs, wout, skip, ggain,
    mixed, mlow, dyout, ggate, wred, dir1, gskip, gggain, dxs, dbc, later,
    sel, cum_t, einx, ys, gs, ss, s_in, dcs, dy_s, ml_s, g_s, dg_s, *exchange,
):
    i = pl.program_id(0)
    seqs = dy_s.shape[0]
    ex = Exchange(True, lambda u, rows: later.at[pl.ds(u, 1), rows, :], exchange[:9], exchange[9])

    def wave(t):
        def act_at(lag, act):
            u = lax.div(t - lag, 2)

            def run():
                ex.decx[0] = spread(decs[u], sel)
                act(u)

            pl.when(jnp.logical_and(t >= lag, jnp.logical_and(2 * u + lag == t, u < seqs)))(run)

        act_at(6, ex.close)
        act_at(5, ex.scan)
        act_at(4, ex.middle)

    @pl.when(i == 0)
    def _():
        meet(("ctx",))
        sel[...] = head_map()
        gskip[...] = jnp.zeros_like(gskip)
        gggain[...] = jnp.zeros_like(gggain)

    wave(2 * i)

    @pl.when(i < seqs)
    def _():
        s = i
        cum = cumin[0]
        e_in, e_out, tot0, tot1, total = local_decays(cum)
        einx[...] = spread(e_in, sel)
        tot0x = spread(rows_of(tot0), sel)[0:1]
        s_in[0] = sin[0]
        s_in[1] = (tot0x * sin[0].astype(f32) + st0[0].astype(f32)).astype(bf16)
        cc = xb[0, :, DIN + NSTATE :]

        def gate_step(j, total_sq):
            cols = pl.ds(pl.multiple_of(j * TILE, TILE), TILE)
            for q in range(2):
                rows = both(q)
                ys[rows, cols] = ylocal[0, rows, cols].astype(f32) + einx[rows, cols] * mm(cc[rows], s_in[q, :, cols])
            y = ys[:, cols] + skip[:, cols] * xb[0, :, cols].astype(f32)
            g = gate[0, :, cols].astype(f32)
            gated = y * (g * gate_of(g))
            gs[:, cols] = gated
            sq = gated * gated
            return total_sq + sq[:, :HALF] + sq[:, HALF:]

        wave(2 * i + 1)
        sq = lax.fori_loop(0, DIN // TILE, gate_step, jnp.zeros((SPAN, HALF), f32))
        inv = lax.rsqrt(jnp.sum(sq, axis=1, keepdims=True) * (1.0 / DIN) + EPS)
        live = (lax.broadcasted_iota(jnp.int32, (SPAN, 1), 0) < rel[s]).astype(f32)
        drive = (live * cot[0].astype(f32)).astype(bf16)

        def back_step(j, acc):
            cols = pl.ds(pl.multiple_of(j * TILE, TILE), TILE)
            gm = mm_nt(drive, wout[cols, :])
            gated = gs[:, cols]
            unit = gated * inv
            low = (unit * ggain[:, cols]).astype(bf16)
            mlow[0, :, cols] = low
            ml_s[s, :, cols] = low
            gggain[:, cols] += jnp.sum(gm * unit, axis=0, keepdims=True)
            scaled = gm * ggain[:, cols]
            ss[:, cols] = scaled
            prod = scaled * gated
            return acc + prod[:, :HALF] + prod[:, HALF:]

        dots = lax.fori_loop(0, DIN // TILE, back_step, jnp.zeros((SPAN, HALF), f32))
        dots = jnp.sum(dots, axis=1, keepdims=True) * (1.0 / DIN)
        corr = inv * inv * inv * dots
        cct = jnp.transpose(cc.astype(f32)).astype(bf16)
        acc = jnp.zeros((SPAN, HALF), f32)
        dc = [jnp.zeros((HALF, HALF), f32) for _ in range(2)]
        for j in range(DIN // TILE):
            cols = slice(j * TILE, (j + 1) * TILE)
            g = gate[0, :, cols].astype(f32)
            sg = gate_of(g)
            sl = g * sg
            grad_gated = inv * ss[:, cols] - gs[:, cols] * corr
            dy = grad_gated * sl
            yn = ys[:, cols]
            x = xb[0, :, cols].astype(f32)
            y = yn + skip[:, cols] * x
            ggate[0, :, cols] = (grad_gated * y * (sg + sl * (1.0 - sg))).astype(bf16)
            dyb = dy.astype(bf16)
            dyout[0, :, cols] = dyb
            dy_s[s, :, cols] = dyb
            gskip[:, cols] += jnp.sum(dy * x, axis=0, keepdims=True)
            acc = acc + gather_heads(dy * yn, sel[:HALF, cols])
            dye = (dy * einx[:, cols]).astype(bf16)
            d0 = mm(cct[:, :HALF], dye[:HALF])
            d1 = mm(cct[:, HALF:], dye[HALF:])
            dir1[0, :, cols] = d1.astype(bf16)
            ex.buf[s, 0, :, cols] = (d0 + tot0x[:, cols] * d1).astype(bf16)
            for q in range(2):
                dc[q] = dc[q] + mm_nt(dye[both(q)], s_in[q, :, cols])
        wred[0] = acc
        for q in range(2):
            dcs[s, both(q)] = dc[q]
        ex.start(s)

    @pl.when(i >= seqs)
    def _():
        s = i - seqs
        causal, low_lanes = masks()
        cum = cumin[0]
        for q in range(2):
            cum_t[q] = jnp.transpose(cum[both(q)])
        einx[...] = spread(softplus(vin[0]), sel)
        bb = xb[0, :, DIN : DIN + NSTATE]
        cc = xb[0, :, DIN + NSTATE :]
        for q in range(2):
            g_s[q] = mm_nt(cc[both(q)], bb[both(q)])
        dg_s[...] = jnp.zeros_like(dg_s)

        def pair_step(p):
            cols = pl.ds(pl.multiple_of(p * HALF, HALF), HALF)
            decays = pair_decays(cum, cum_t, p, causal)
            for q in range(2):
                rows = both(q)
                xsb = (xb[0, rows, cols].astype(f32) * einx[rows, cols]).astype(bf16)
                dyb = dy_s[s, rows, cols]
                dyf = dyb.astype(f32)
                grads = []
                for a in range(2):
                    m = (decays[2 * q + a] * g_s[q]).astype(bf16)
                    grads.append(mm_tn(m, dyb))
                    mine = low_lanes if a == 0 else jnp.logical_not(low_lanes)
                    dm = mm_nt(jnp.where(mine, dyf, 0.0).astype(bf16), xsb)
                    dg_s[q] += dm * decays[2 * q + a]
                dxs[0, rows, cols] = jnp.where(low_lanes, grads[0], grads[1]).astype(bf16)

        loop(0, PAIRS // 2, pair_step)
        wave(2 * i + 1)
        loop(PAIRS // 2, PAIRS, pair_step)
        for q in range(2):
            rows = both(q)
            dg = dg_s[q].astype(bf16)
            dbc[0, rows, :NSTATE] = mm_tn(dg, cc[rows])
            dbc[0, rows, NSTATE:] = mm(dg, bb[rows]) + dcs[s, rows]
        live = (lax.broadcasted_iota(jnp.int32, (SPAN, 1), 0) < rel[s]).astype(f32)
        for j in range(D // TILE):
            cols = slice(j * TILE, (j + 1) * TILE)
            mixed[0, :, cols] = (live * (tok[0, :, cols].astype(f32) + mm(ml_s[s], wout[:, cols]))).astype(bf16)

    @pl.when(i == 2 * seqs - 1)
    def _():
        loop(4 * seqs, 2 * seqs + 5, wave)
        loop(0, seqs, ex.finish)


def back_kernel(
    rel, tok, cot, rhalo, gain, ggate, wfull, cin, xb, spb, bc, dy, dxs, dir1, later, sin, loc,
    vin, cumin, wred, dbc, cw, dl, skip, nt, nth, pgate, pout, gskip, gggain,
    gtok, rgate, rout, rconv, small_out, ggain_out,
    sel, dt_cat, eo_cat, tots, db_s, qacc, ends, gp, gz_s, gzh_s, pconv, gcw, gcb, gdb, gdl, ggain,
    rim_out, rim_in, rim_send, rim_recv, *comm,
):
    i = pl.program_id(0)
    seqs = rhalo.shape[0]
    count = lax.axis_size("ctx")
    me = lax.axis_index("ctx")
    members = lax.axis_size("group")
    gates = Reducer(pgate, rgate, D // members, GATE_CHUNK, False, comm[0:7], comm[7])
    outs = Reducer(pout, rout, DIN // members, OUT_CHUNK, True, comm[8:15], comm[15])
    convs = Reducer(pconv, rconv, D // members, CONV_CHUNK, False, comm[16:23], comm[23])
    little, least = Small(*comm[24:28]), Small(*comm[28:32])
    last_x = TILES - 1
    bc_step = TILES

    def wave(t):
        gates.wave(t - 4)
        outs.wave(t - 4 - gates.chunks)
        convs.wave(t - 2 * bc_step - 1)

    def rim_copy(q):
        return remote(rim_out.at[q], rim_in.at[q], rim_send.at[q], rim_recv.at[q], ctx=lax.rem(me + count - 1, count))

    def span(s):
        return pl.ds(pl.multiple_of(s * SPAN, SPAN), SPAN)

    def edge(s):
        return pl.ds(pl.multiple_of(s * RIM, RIM), RIM)

    def back(rows, grad):
        rows, inv, _ = normalized(rows, gain[...])
        ggain[...] += jnp.sum(grad * rows * inv, axis=0, keepdims=True)
        gained = gain[...] * grad
        mean = jnp.mean(gained * rows, axis=-1, keepdims=True)
        return inv * gained - rows * (inv * inv * inv * mean)

    @pl.when(i == 0)
    def _():
        meet(("ctx", "group"))
        for r in (gates, outs):
            loop(0, r.chunks, r.m_start)
        sel[...] = head_map()
        for acc in (db_s, qacc, ends, gcw, gcb, gdb, gdl, ggain):
            acc[...] = jnp.zeros_like(acc)
        gp[0:RIM] = jnp.zeros((RIM, TILE), f32)
        gp[RIM + SPAN :] = jnp.zeros((8, TILE), f32)
        pconv[:, CONVW + HALF :] = jnp.zeros((D, GZW - CONVW - HALF), bf16)

        def setup(s):
            dt = softplus(vin[s])
            _, e_out, _, tot1, total = local_decays(cumin[s])
            dt_cat[s] = jnp.concatenate(halves(dt), axis=1)
            eo_cat[s] = jnp.concatenate(halves(e_out), axis=1)
            both_rows = jnp.concatenate([rows_of(tot1), rows_of(total)], axis=0)
            tots[s] = spread(both_rows, sel)

        loop(0, seqs, setup)

    def conv_back(s, dact, cols):
        gco = dact * spb[s].astype(f32)
        gp[RIM : RIM + SPAN] = gco
        gcb[:, cols] += jnp.sum(gco, axis=0, keepdims=True)
        own = cin[s, RIM:].astype(f32)
        before = cin[s, :RIM].astype(f32)
        main = jnp.zeros((SPAN, TILE), f32)
        rim = jnp.zeros((RIM, TILE), f32)
        for k in range(KCONV):
            ahead = KCONV - 1 - k
            moved = gco if ahead == 0 else gp[RIM + ahead : RIM + ahead + SPAN]
            early = gp[ahead : ahead + RIM]
            main = main + cw[k : k + 1, cols] * moved
            rim = rim + cw[k : k + 1, cols] * early
            gcw[k : k + 1, cols] += jnp.sum(own * moved, axis=0, keepdims=True) + jnp.sum(
                before * early, axis=0, keepdims=True
            )
        gz_s[span(s), cols] = main.astype(bf16)
        gzh_s[edge(s), cols] = rim.astype(bf16)

    def partial(cols):
        pconv[:, cols] = (mm(nt[...], gz_s[:, cols]) + mm(nth[...], gzh_s[:, cols])).astype(bf16)

    wave(2 * i)

    @pl.when(jnp.logical_and(lax.rem(i, 2) == 0, jnp.logical_and(i >= 2, i <= bc_step)))
    def _():
        convs.m_done(lax.div(i, 2) - 1)

    @pl.when(i == bc_step + 1)
    def _():
        convs.m_done(convs.chunks - 1)

    @pl.when(i < bc_step)
    def _():
        cols = pl.ds(pl.multiple_of(i * TILE, TILE), TILE)

        def x_tile(s):
            dte = mm(dt_cat[s], sel[:, cols])
            eo = mm(eo_cat[s], sel[:, cols])
            near = later[s]
            near32 = near.astype(f32)
            tot = tots[s, :, cols]
            reach = [(dir1[s].astype(f32) + tot[0:1] * near32).astype(bf16), near]
            fed = jnp.concatenate(
                [mm(bc[s, both(q), :NSTATE], reach[q]) for q in range(2)], axis=0
            )
            x = xb[s].astype(f32)
            dx_s = dxs[s].astype(f32) + eo * fed
            qacc[s] += gather_heads(x * dx_s, sel[:HALF, cols])
            xw = (x * dte * eo).astype(bf16)
            for q in range(2):
                db_s[s, both(q)] += mm_nt(xw[both(q)], reach[q])
            held = near32 * (tot[8:9] * sin[s].astype(f32) + loc[s].astype(f32))
            ends[s] += gather_heads(rows_of(jnp.sum(held, axis=0, keepdims=True)), sel[:HALF, cols])
            conv_back(s, dte * dx_s + skip[:, cols] * dy[s].astype(f32), cols)

        loop(0, seqs // 2, x_tile)

        @pl.when(i == 0)
        def _():
            for r in (gates, outs):
                loop(0, r.chunks, r.m_done)

        wave(2 * i + 1)
        loop(seqs // 2, seqs, x_tile)
        partial(cols)

        @pl.when(lax.rem(i, 2) == 1)
        def _():
            convs.m_start(lax.div(i, 2))

    @pl.when(i == bc_step)
    def _():
        cols = slice(DIN, CONVW)

        def bc_tile(s):
            conv_back(s, jnp.concatenate([dbc[s, :, :NSTATE] + db_s[s], dbc[s, :, NSTATE:]], axis=1), cols)
            v = vin[s]
            dt = softplus(v)
            q = qacc[s]
            at_end = lax.broadcasted_iota(jnp.int32, (SPAN, 1), 0) == SPAN - 1
            dcum = wred[s] - dt * q + jnp.where(at_end, ends[s][0:1], 0.0)
            glog = exact_mm(triangle(SPAN, False), dcum)
            rate = jnp.exp(dl[...])
            gpd = (q - rate * glog) * sigmoid(v)
            lanes = lax.broadcasted_iota(jnp.int32, (SPAN, HALF), 1) < HEADS
            gpd = jnp.where(lanes, gpd, 0.0)
            gz_s[span(s), CONVW : CONVW + HALF] = gpd.astype(bf16)
            gdb[...] += jnp.sum(gpd, axis=0, keepdims=True)
            gdl[...] += -rate * jnp.sum(dt * glog, axis=0, keepdims=True)

        loop(0, seqs, bc_tile)
        wave(2 * i + 1)
        partial(cols)
        pconv[:, CONVW : CONVW + HALF] = mm(nt[...], gz_s[:, CONVW : CONVW + HALF]).astype(bf16)
        convs.m_start(convs.chunks - 1)
        rows = [gcw[k : k + 1, j * HALF : (j + 1) * HALF] for k in range(KCONV) for j in range(CONVW // HALF)]
        rows += [gcb[:, j * HALF : (j + 1) * HALF] for j in range(CONVW // HALF)]
        rows += [gdb[...], gdl[...]]
        rows += [gskip[:, j * HALF : (j + 1) * HALF] for j in range(PAIRS)]
        rows += [gggain[:, j * HALF : (j + 1) * HALF] for j in range(PAIRS)]
        for r, row in enumerate(rows):
            little.held[0, r : r + 1, :] = row
        little.start(0)
        edges = mm_nt(gzh_s[...], wfull[:, DIN:ZXW])
        for q in range(seqs):
            rim_out[q] = back(rhalo[q], edges[q * RIM : (q + 1) * RIM]).astype(bf16)
            pl.when(me > 0)(lambda q=q: rim_copy(q).start())

        @pl.when(me == count - 1)
        def _():
            rim_in[...] = jnp.zeros_like(rim_in)

    @pl.when(i == bc_step + 2)
    def _():
        little.done(0)
        little.start(1)

    @pl.when(i > bc_step)
    def _():
        s = i - bc_step - 1
        grad = mm_nt(gz_s[span(s), :], wfull[:, DIN:]) + mm_nt(ggate[0], wfull[:, :DIN])
        wave(2 * i + 1)
        live = (lax.broadcasted_iota(jnp.int32, (SPAN, 1), 0) < rel[s]).astype(f32)
        out = live * cot[0].astype(f32) + back(tok[0], grad)
        gtok[0, : SPAN - RIM] = out[: SPAN - RIM].astype(bf16)
        pl.when(me < count - 1)(lambda: rim_copy(s).wait_recv())
        gtok[0, SPAN - RIM :] = (out[SPAN - RIM :] + rim_in[s].astype(f32)).astype(bf16)

    @pl.when(i == bc_step + seqs)
    def _():
        least.held[0] = jnp.zeros_like(least.held[0])
        for j in range(D // HALF):
            least.held[0, j : j + 1, :] = ggain[:, j * HALF : (j + 1) * HALF]
        least.start(0)
        little.done(1)
        small_out[...] = little.held[2]
        least.done(0)
        least.start(1)
        loop(2 * (bc_step + seqs) + 2, 2 * bc_step + 1 + convs.chunks + 4, wave)
        for r in (gates, outs, convs):
            loop(0, r.chunks, r.drain)
        little.drain()
        for q in range(seqs):
            pl.when(me > 0)(lambda q=q: rim_copy(q).wait_send())
        least.done(1)
        ggain_out[...] = least.held[2]
        least.drain()


def whole(shape):
    zeros = (0,) * len(shape)
    return pl.BlockSpec(shape, lambda s: zeros, pipeline_mode=pl.Buffered(1))


def summed(shape):
    zeros = (0,) * len(shape)
    return pl.BlockSpec(shape, lambda s: zeros)


def per_seq(*shape):
    zeros = (0,) * len(shape)
    return pl.BlockSpec((1,) + shape, lambda s: (s,) + zeros)


SMEM = pl.BlockSpec(memory_space=pltpu.SMEM)
ANY = pl.BlockSpec(memory_space=pl.ANY)


def staged(seqs, phase, *shape):
    zeros = (0,) * len(shape)
    if phase == 0:
        return pl.BlockSpec((1,) + shape, lambda i: (jnp.minimum(i, seqs - 1),) + zeros)
    if phase == 1:
        return pl.BlockSpec((1,) + shape, lambda i: (jnp.maximum(i - seqs, 0),) + zeros)
    return pl.BlockSpec((1,) + shape, lambda i: (lax.rem(i, seqs),) + zeros)


def call(kernel, steps, in_specs, outs, scratch, name, collective=None):
    params = dict(vmem_limit_bytes=VMEM_LIMIT)
    if collective is not None:
        params.update(collective_id=collective, has_side_effects=True)
    return pl.pallas_call(
        kernel,
        grid=(steps,),
        in_specs=in_specs,
        out_specs=[o[0] for o in outs],
        out_shape=[jax.ShapeDtypeStruct(o[1], o[2]) for o in outs],
        scratch_shapes=[pltpu.VMEM(*sc) if isinstance(sc, tuple) else sc for sc in scratch],
        compiler_params=pltpu.CompilerParams(**params),
        name=name,
    )


def lanes_of(v):
    return jnp.pad(v[None, :], ((0, 0), (0, HALF - v.shape[0])))


def local(
    tokens_in, seq_lengths, norm_gain, w_zx, w_delta, w_out, conv_weight, conv_bias,
    delta_bias, decay_log, skip_gain, gated_gain, cotangent,
):
    seqs = tokens_in.shape[0]
    count = lax.axis_size("ctx")
    group = lax.axis_size("group")
    chips = max(group // 2, 1)
    rel = seq_lengths - lax.axis_index("ctx") * SPAN
    gain = norm_gain[None, :]
    cb = conv_bias[None, :]
    db = lanes_of(delta_bias)
    dl = lanes_of(decay_log)
    skip = jnp.repeat(skip_gain, HEADDIM)[None, :]
    ggain = gated_gain[None, :]
    wcat = jnp.concatenate([w_zx, jnp.pad(w_delta, ((0, 0), (0, HALF - HEADS)))], axis=1)
    dma = pltpu.SemaphoreType.DMA
    at0 = lambda *shape: staged(seqs, 0, *shape)
    at1 = lambda *shape: staged(seqs, 1, *shape)
    at01 = lambda *shape: staged(seqs, 2, *shape)

    def tiled(rows, first, lead=None):
        def index(i):
            u = jnp.clip(i - first, 0, TILES - 1)
            return (0, 0, u if lead is None else jnp.where(i == 0, lead, u))

        return pl.BlockSpec((seqs, rows, TILE), index)

    state = (seqs, NSTATE, DIN)
    nt, nth, rhalo, cin, xb, spb, vraw, cum, st0, loc, ylocal, gate, decs, wfull, wofull, state_in = call(
        front_kernel,
        PIECES,
        [whole((seqs, SPAN, D)), ANY, ANY, ANY, whole((1, D)), whole((KCONV, CONVW)), whole((1, CONVW)), whole((1, HALF)),
         whole((1, HALF))],
        [
            (summed((D, seqs * SPAN)), (D, seqs * SPAN), bf16),
            (summed((D, seqs * RIM)), (D, seqs * RIM), bf16),
            (summed((seqs, RIM, D)), (seqs, RIM, D), bf16),
            (tiled(RIM + SPAN, 1, TILES), (seqs, RIM + SPAN, CONVW), bf16),
            (tiled(SPAN, 1, TILES), (seqs, SPAN, CONVW), bf16),
            (tiled(SPAN, 1, TILES), (seqs, SPAN, CONVW), bf16),
            (summed((seqs, SPAN, HALF)), (seqs, SPAN, HALF), f32),
            (summed((seqs, SPAN, HALF)), (seqs, SPAN, HALF), f32),
            (tiled(NSTATE, 1), state, bf16),
            (tiled(NSTATE, 1), state, bf16),
            (tiled(SPAN, TILES + 1), (seqs, SPAN, DIN), bf16),
            (tiled(SPAN, TILES + 1), (seqs, SPAN, DIN), bf16),
            (summed((seqs, count * 8, HALF)), (seqs, count * 8, HALF), f32),
            (ANY, (D, ZXW + HALF), bf16),
            (ANY, (DIN, D), bf16),
            (ANY, state, bf16),
        ],
        [((2 * HALF, DIN), bf16), ((seqs, RIM, D), bf16), ((seqs * RIM, D), f32), ((seqs, RIM + SPAN, D), bf16), ((D, ZXW + HALF), bf16),
         ((seqs, RIM + SPAN, TILE), f32), ((seqs, SPAN, DIN), bf16), ((seqs, NSTATE, SPAN), bf16),
         ((seqs, 2, HALF, HALF), f32), ((seqs, SPAN, 2 * HALF), bf16), ((seqs, SPAN, 2 * HALF), bf16),
         ((seqs, 2, HALF, HALF), f32), ((seqs, 8, DIN), f32), ((seqs, count * 8, HALF), f32)]
        + [dma((2,))] + [dma((PIECES + 1, chips))] * 4 + [dma((2,)), dma((1,)), dma((count,)), dma((count,))]
        + Exchange.scratch(TILES, seqs, TILE, count),
        "front",
        0,
    )(tokens_in, tokens_in, wcat, w_out, gain, conv_weight, cb, db, dl)

    mixed_out, mlow, dy, ggate, wred, dir1, gskip, gggain, dxs, dbc, later = call(
        middle_kernel,
        2 * seqs,
        [SMEM, at1(SPAN, D), at0(SPAN, D), at0(SPAN, DIN), at0(SPAN, DIN), at01(SPAN, CONVW), at01(SPAN, HALF),
         at01(SPAN, HALF), at0(NSTATE, DIN), at0(NSTATE, DIN), whole((seqs, count * 8, HALF)), whole((DIN, D)),
         whole((1, DIN)), whole((1, DIN))],
        [
            (at1(SPAN, D), (seqs, SPAN, D), bf16),
            (at0(SPAN, DIN), (seqs, SPAN, DIN), bf16),
            (at0(SPAN, DIN), (seqs, SPAN, DIN), bf16),
            (at0(SPAN, DIN), (seqs, SPAN, DIN), bf16),
            (at0(SPAN, HALF), (seqs, SPAN, HALF), f32),
            (at0(NSTATE, DIN), (seqs, NSTATE, DIN), bf16),
            (summed((1, DIN)), (1, DIN), f32),
            (summed((1, DIN)), (1, DIN), f32),
            (at1(SPAN, DIN), (seqs, SPAN, DIN), bf16),
            (at1(SPAN, 2 * NSTATE), (seqs, SPAN, 2 * NSTATE), f32),
            (ANY, (seqs, NSTATE, DIN), bf16),
        ],
        [((2 * HALF, DIN), bf16), ((2, HALF, HALF), f32), ((SPAN, DIN), f32), ((SPAN, DIN), f32), ((SPAN, DIN), f32),
         ((SPAN, DIN), f32), ((2, NSTATE, DIN), bf16), ((seqs, SPAN, HALF), f32), ((seqs, SPAN, DIN), bf16),
         ((seqs, SPAN, DIN), bf16), ((2, HALF, HALF), f32), ((2, HALF, HALF), f32)]
        + Exchange.scratch(seqs, 1, DIN, count),
        "middle",
        1,
    )(rel, tokens_in, cotangent, ylocal, gate, xb, vraw, cum, st0, state_in, decs, wofull, skip, ggain)

    live = (jnp.arange(SPAN, dtype=jnp.int32)[None, :] < rel[:, None]).astype(f32)[:, :, None]
    drive = (live * cotangent.astype(f32)).astype(bf16)
    flat = lambda v: v.reshape(-1, v.shape[-1])
    p_out = mm_tn(flat(mlow), flat(drive)).astype(bf16)
    p_gate = mm(nt, flat(ggate)).astype(bf16)

    def tile_in(rows, tiles):
        return pl.BlockSpec((seqs, rows, TILE), lambda i: (0, 0, jnp.minimum(i, tiles - 1)))

    def late(*shape):
        zeros = (0,) * len(shape)
        return pl.BlockSpec((1,) + shape, lambda i: (jnp.clip(i - TILES - 1, 0, seqs - 1),) + zeros)

    bc_spec = pl.BlockSpec((seqs, SPAN, TILE), lambda i: (0, 0, TILES), pipeline_mode=pl.Buffered(1))
    sizes = (KCONV * CONVW, CONVW, HALF, HALF, DIN, DIN)
    height = sum(sizes) // HALF
    gtok, r_gate, r_out, r_conv, small, g_gain = call(
        back_kernel,
        TILES + 1 + seqs,
        [SMEM, late(SPAN, D), late(SPAN, D), whole((seqs, RIM, D)), whole((1, D)), late(SPAN, DIN), whole((D, ZXW + HALF)),
         tile_in(RIM + SPAN, TILES + 1), tile_in(SPAN, TILES + 1), tile_in(SPAN, TILES + 1), bc_spec, tile_in(SPAN, TILES),
         tile_in(SPAN, TILES), tile_in(NSTATE, TILES), tile_in(NSTATE, TILES), tile_in(NSTATE, TILES), tile_in(NSTATE, TILES),
         whole((seqs, SPAN, HALF)), whole((seqs, SPAN, HALF)), whole((seqs, SPAN, HALF)), whole((seqs, SPAN, 2 * NSTATE)),
         whole((KCONV, CONVW)), whole((1, HALF)), whole((1, DIN)), whole((D, seqs * SPAN)), whole((D, seqs * RIM)),
         whole((D, DIN)), whole((DIN, D)), whole((1, DIN)), whole((1, DIN))],
        [
            (late(SPAN, D), (seqs, SPAN, D), bf16),
            (summed((D // group, DIN)), (D // group, DIN), bf16),
            (summed((DIN // group, D)), (DIN // group, D), bf16),
            (summed((D // group, GZW)), (D // group, GZW), bf16),
            (summed((height, HALF)), (height, HALF), f32),
            (summed((8, HALF)), (8, HALF), f32),
        ],
        [((2 * HALF, DIN), bf16), ((seqs, SPAN, 2 * HALF), bf16), ((seqs, SPAN, 2 * HALF), bf16), ((seqs, 16, DIN), f32),
         ((seqs, SPAN, NSTATE), f32), ((seqs, SPAN, HALF), f32), ((seqs, 8, HALF), f32), ((RIM + SPAN + 8, TILE), f32),
         ((seqs * SPAN, CONVW + HALF), bf16), ((seqs * RIM, CONVW), bf16), ((D, GZW), bf16), ((KCONV, CONVW), f32),
         ((1, CONVW), f32), ((1, HALF), f32), ((1, HALF), f32), ((1, D), f32), ((seqs, RIM, D), bf16), ((seqs, RIM, D), bf16),
         dma((seqs,)), dma((seqs,))]
        + Reducer.scratch(DIN // GATE_CHUNK, D // group, GATE_CHUNK, False, group, count)
        + Reducer.scratch(D // OUT_CHUNK, DIN // group, OUT_CHUNK, True, group, count)
        + Reducer.scratch(GZW // CONV_CHUNK, D // group, CONV_CHUNK, False, group, count)
        + Small.scratch(height, group, count)
        + Small.scratch(8, group, count),
        "back",
        2,
    )(rel, tokens_in, cotangent, rhalo, gain, ggate, wfull, cin, xb, spb, xb, dy, dxs, dir1, later, state_in, loc,
      vraw, cum, wred, dbc, conv_weight, dl, skip, nt, nth, p_gate, p_out, gskip, gggain)

    g_zx = jnp.concatenate([r_gate, r_conv[:, :CONVW]], axis=1).astype(f32)
    g_delta = r_conv[:, CONVW : CONVW + HEADS].astype(f32)
    small = small.reshape(-1)
    at = 0
    pieces = []
    for size in sizes:
        pieces.append(small[at : at + size])
        at += size
    return (
        mixed_out, gtok, g_gain.reshape(-1)[:D], g_zx, g_delta, r_out.astype(f32), pieces[0].reshape(KCONV, CONVW), pieces[1],
        pieces[2][:HEADS], pieces[3][:HEADS], pieces[4].reshape(HEADS, HEADDIM).sum(1), pieces[5],
    )


def solution(mesh):
    rows = P("group", "ctx", None)
    own = P("group", None)
    in_specs = (rows, P("group"), P(), own, own, own, P(), P(), P(), P(), P(), P(), rows)
    out_specs = (rows, rows, P(), own, own, own, P(), P(), P(), P(), P(), P())
    return jax.shard_map(local, mesh=mesh, in_specs=in_specs, out_specs=out_specs, check_vma=False)
```

```python
import jax
import jax.numpy as jnp
from jax import lax
from jax.experimental import pallas as pl
from jax.experimental.pallas import tpu as pltpu
from jax.sharding import PartitionSpec as P

D = 768
HEADS = 24
HEADDIM = 64
NSTATE = 128
KCONV = 4
SPAN = 256
DIN = 1536
CONVW = 1792
ZXW = 3328
RIM = 16
HALF = 128
TILE = 256
PAIRS = 12
EPS = 1e-05

f32 = jnp.float32
bf16 = jnp.bfloat16
NT = (((1,), (1,)), ((), ()))
TN = (((0,), (0,)), ((), ()))
VMEM_LIMIT = 62 * 1024 * 1024
GATE_CHUNK = 512
OUT_CHUNK = 256
CONV_CHUNK = 512
BACK_LAGS = (5, 7, 9)
STAGE_LAG = 2
MIDDLE_LAG = 2
SCAN_LAG = 4
HOPS = ("group", "ctx")
CLOSE_LAG = 6
GZW = 2048


def mm(a, b):
    return jnp.dot(a, b, preferred_element_type=f32)


def mm_nt(a, b):
    return lax.dot_general(a, b, NT, preferred_element_type=f32)


def mm_tn(a, b):
    return lax.dot_general(a, b, TN, preferred_element_type=f32)


def halves(v):
    high = v.astype(bf16)
    return high, (v - high.astype(f32)).astype(bf16)


def head_map():
    rows = lax.broadcasted_iota(jnp.int32, (2 * HALF, DIN), 0) % HALF
    cols = lax.broadcasted_iota(jnp.int32, (2 * HALF, DIN), 1) // HEADDIM
    return jnp.where(rows == cols, 1.0, 0.0).astype(bf16)


def spread(v, sel):
    return mm(jnp.concatenate(halves(v), axis=1), sel[...])


def gather_heads(v, sel_part):
    high, low = halves(v)
    return mm_nt(high, sel_part) + mm_nt(low, sel_part)


def triangle(size, lower):
    rows = lax.broadcasted_iota(jnp.int32, (size, size), 0)
    cols = lax.broadcasted_iota(jnp.int32, (size, size), 1)
    keep = rows >= cols if lower else rows <= cols
    return jnp.where(keep, 1.0, 0.0).astype(f32)


def exact_mm(a, b):
    return jnp.dot(a, b, precision=lax.Precision.HIGHEST, preferred_element_type=f32)


def softplus(v):
    return jnp.maximum(v, 0.0) + jnp.log1p(jnp.exp(-jnp.abs(v)))


def sigmoid(v):
    return 1.0 / (1.0 + jnp.exp(-v))


def gate_of(v):
    return 0.5 * jnp.tanh(0.5 * v) + 0.5


def local_decays(cum):
    mid, end = cum[HALF - 1 : HALF], cum[SPAN - 1 : SPAN]
    rows = lax.broadcasted_iota(jnp.int32, (SPAN, 1), 0)
    first = rows < HALF
    start = jnp.where(first, 0.0, mid)
    stop = jnp.where(first, mid, end)
    return jnp.exp(cum - start), jnp.exp(stop - cum), jnp.exp(mid), jnp.exp(end - mid), jnp.exp(end)


def rows_of(v):
    return jnp.broadcast_to(v, (8, v.shape[1]))


def normalized(rows, gain):
    rows = rows.astype(f32)
    inv = lax.rsqrt(jnp.mean(rows * rows, axis=-1, keepdims=True) + EPS)
    return rows, inv, (rows * inv * gain).astype(bf16)


def remote(src, dst, send_sem, recv_sem, **where):
    return pltpu.make_async_remote_copy(
        src_ref=src, dst_ref=dst, send_sem=send_sem, recv_sem=recv_sem,
        device_id=where, device_id_type=pl.DeviceIdType.MESH,
    )


def loop(start, stop, body):
    def step(i, c):
        body(i)
        return c

    lax.fori_loop(start, stop, step, 0)


def meet(axes):
    barrier = pltpu.get_barrier_semaphore()
    total = 0
    for axis in axes:
        size = lax.axis_size(axis)
        me = lax.axis_index(axis)

        def greet(d):
            pl.semaphore_signal(
                barrier, inc=1, device_id={axis: lax.rem(me + d, size)}, device_id_type=pl.DeviceIdType.MESH
            )

        loop(1, size, greet)
        total += size - 1
    pl.semaphore_wait(barrier, total)


class Exchange:
    def __init__(self, reverse, out_at, bufs, sems):
        self.reverse, self.out_at, self.sems = reverse, out_at, sems
        self.buf, self.y_buf, self.z_src, self.z_buf, self.z_back, self.p_buf, self.mine_buf, self.their_buf, self.decx = bufs
        self.depth = self.buf.shape[1]
        ctx = lax.axis_index("ctx")
        self.ctx = ctx
        self.outer = lax.axis_size("ctx") // 2
        self.owners = min(self.outer, 4)
        self.stride = self.outer // self.owners
        self.inner = lax.rem(ctx, 2)
        self.line = ctx // 2
        self.mine = self.line // self.stride
        self.half = NSTATE // 2
        self.rows = self.half // self.owners

    def half_rows(self, inner):
        return pl.ds(pl.multiple_of(inner * self.half, self.half), self.half)

    def part(self, j):
        return pl.ds(pl.multiple_of(j * self.rows, self.rows), self.rows)

    def other_owners(self, body):
        if self.stride == 1:
            loop(1, self.owners, lambda d: body(lax.rem(self.mine + d, self.owners)))
        else:
            loop(0, self.owners, lambda j: pl.when(j * self.stride != self.line)(lambda: body(j)))

    def other_lines(self, body):
        loop(1, self.outer, lambda d: body(lax.rem(self.line + d, self.outer)))

    def if_owner(self, body):
        if self.stride == 1:
            body()
        else:
            pl.when(self.mine * self.stride == self.line)(body)

    def y_copy(self, u):
        return remote(
            self.buf.at[u, :, self.half_rows(1 - self.inner)], self.y_buf.at[u], self.sems.at[0, u, 0], self.sems.at[1, u, 0],
            ctx=self.ctx + 1 - 2 * self.inner,
        )

    def z_copy(self, u, j, sender):
        return remote(
            self.z_src.at[u, :, self.part(j)], self.z_buf.at[u, sender], self.sems.at[2, u, j], self.sems.at[3, u, sender],
            ctx=j * self.stride * 2 + self.inner,
        )

    def b_copy(self, u, line, j):
        return remote(
            self.z_back.at[u, line], self.p_buf.at[u, :, self.part(j)], self.sems.at[4, u, line], self.sems.at[5, u, j],
            ctx=line * 2 + self.inner,
        )

    def f_copy(self, u, inner):
        return remote(
            self.their_buf.at[u], self.out_at(u, self.half_rows(inner)), self.sems.at[6, u, 0], self.sems.at[7, u, 0],
            ctx=self.ctx + 1 - 2 * self.inner,
        )

    def keep(self, u):
        return pltpu.make_async_copy(self.mine_buf.at[u], self.out_at(u, self.half_rows(self.inner)), self.sems.at[8, u, 0])

    def decay(self, a, block):
        return self.decx[a, pl.ds(pl.multiple_of(block * 8, 8), 8), :][0:1]

    def pair(self, u, a):
        own = self.buf[u, a, self.half_rows(self.inner), :].astype(f32)
        other = self.y_buf[u, a].astype(f32)
        first = self.inner == 0
        return jnp.where(first, own, other), jnp.where(first, other, own)

    def start(self, u):
        self.y_copy(u).start()

    def middle(self, u):
        self.y_copy(u).wait_recv()
        for a in range(self.depth):
            s0, s1 = self.pair(u, a)
            if self.reverse:
                total = s0 + self.decay(a, 2 * self.line) * s1
            else:
                total = self.decay(a, 2 * self.line + 1) * s0 + s1
            self.z_src[u, a] = total.astype(bf16)
        self.other_owners(lambda j: self.z_copy(u, j, self.line).start())

    def scan(self, u):
        def run():
            self.other_lines(lambda line: self.z_copy(u, self.mine, line).wait_recv())
            self.z_buf[u, self.line] = self.z_src[u, :, self.part(self.mine), :]
            for a in range(self.depth):

                def step(k, carry):
                    line = self.outer - 1 - k if self.reverse else k
                    self.z_back[u, line, a] = carry.astype(bf16)
                    both_decays = self.decay(a, 2 * line) * self.decay(a, 2 * line + 1)
                    return both_decays * carry + self.z_buf[u, line, a].astype(f32)

                lax.fori_loop(0, self.outer, step, jnp.zeros(self.z_buf.shape[3:], f32))
            self.other_lines(lambda line: self.b_copy(u, line, self.mine).start())
            self.p_buf[u, :, self.part(self.mine), :] = self.z_back[u, self.line]

        self.if_owner(run)

    def close(self, u):
        self.other_owners(lambda j: self.b_copy(u, self.line, j).wait_recv())
        for a in range(self.depth):
            s0, s1 = self.pair(u, a)
            near = self.p_buf[u, a].astype(f32)
            if self.reverse:
                far = s1 + self.decay(a, 2 * self.line + 1) * near
            else:
                far = s0 + self.decay(a, 2 * self.line) * near
            keeps_near = self.inner == (1 if self.reverse else 0)
            self.mine_buf[u, a] = jnp.where(keeps_near, near, far).astype(bf16)
            self.their_buf[u, a] = jnp.where(keeps_near, far, near).astype(bf16)
        self.f_copy(u, self.inner).start()
        self.keep(u).start()

    def finish(self, u):
        self.f_copy(u, 1 - self.inner).wait_recv()
        self.keep(u).wait()
        self.y_copy(u).wait_send()
        self.other_owners(lambda j: self.z_copy(u, j, self.line).wait_send())
        self.if_owner(lambda: self.other_lines(lambda line: self.b_copy(u, line, self.mine).wait_send()))
        self.f_copy(u, self.inner).wait_send()

    @staticmethod
    def scratch(units, depth, lanes, count):
        outer = count // 2
        half = NSTATE // 2
        rows = half // min(outer, 4)
        bufs = [(units, depth, NSTATE, lanes), (units, depth, half, lanes), (units, depth, half, lanes),
                (units, outer, depth, rows, lanes), (units, outer, depth, rows, lanes), (units, depth, half, lanes),
                (units, depth, half, lanes), (units, depth, half, lanes)]
        return (
            [(b, bf16) for b in bufs]
            + [((depth, count * 8, lanes), f32)]
            + [pltpu.SemaphoreType.DMA((9, units, max(outer, 4)))]
        )


class Spread:
    def __init__(self, shard, full, sems):
        self.shard, self.full = shard, full
        self.x_send, self.x_recv, self.m_send, self.m_recv, self.own = sems
        size = lax.axis_size("group")
        self.cores = 2 if size % 2 == 0 else 1
        self.chips = size // self.cores
        self.me = lax.axis_index("group")
        self.core = lax.rem(self.me, self.cores)
        self.chip = self.me // self.cores
        self.rows = shard.shape[0]

    def place(self, member, cols):
        return self.full.at[pl.ds(pl.multiple_of(member * self.rows, 32), self.rows), cols]

    def across(self, p, cols, d):
        peer = lax.rem(self.chip + d, self.chips) * self.cores + self.core
        return remote(
            self.shard.at[:, cols], self.place(self.me, cols), self.x_send.at[p, d], self.x_recv.at[p, d], group=peer
        )

    def mate(self, p, cols, d):
        member = lax.rem(self.chip + self.chips - d, self.chips) * self.cores + self.core
        src = self.shard.at[:, cols] if d == 0 else self.place(member, cols)
        return remote(
            src, self.place(member, cols), self.m_send.at[p, d], self.m_recv.at[p, d],
            group=self.me + 1 - 2 * self.core,
        )

    def keep(self, p):
        return pltpu.make_async_copy(self.shard, self.place(self.me, slice(None)), self.own.at[p])

    def start_chip(self, p):
        if self.cores == 2:
            self.mate(p, slice(None), 0).start()
        self.keep(p).start()

    def finish_chip(self, p):
        if self.cores == 2:
            self.mate(p, slice(None), 0).wait_recv()
        self.keep(p).wait()

    def start(self, p, cols):
        for d in range(1, self.chips):
            self.across(p, cols, d).start()

    def forward(self, p, cols):
        for d in range(1, self.chips):
            self.across(p, cols, d).wait_recv()
            if self.cores == 2:
                self.mate(p, cols, d).start()

    def finish(self, p, cols):
        if self.cores == 2:
            for d in range(1, self.chips):
                self.mate(p, cols, d).wait_recv()

    def drain(self, p, cols):
        for d in range(1, self.chips):
            self.across(p, cols, d).wait_send()
            if self.cores == 2:
                self.mate(p, cols, d).wait_send()

    def drain_chip(self, p):
        if self.cores == 2:
            self.mate(p, slice(None), 0).wait_send()


def owner_count(rows, width, by_rows, outer):
    fits = lambda n: (rows // 2) % (16 * n) == 0 if by_rows else width % (128 * n) == 0
    return max(n for n in (1, 2, 4) if outer % n == 0 and fits(n))


class Reducer:
    def __init__(self, part, out, rows, width, by_rows, bufs, sems):
        self.part, self.out, self.rows, self.width, self.by_rows = part, out, rows, width, by_rows
        self.m_buf, self.x_buf, self.y_src, self.y_buf, self.z_src, self.z_buf, self.full = bufs
        self.x_src = self.m_buf
        self.sems = sems
        self.chunks = part.shape[1] // width
        self.group = lax.axis_index("group")
        self.cores = 2
        self.chips = lax.axis_size("group") // 2
        self.core = lax.rem(self.group, 2)
        self.chip = self.group // 2
        self.ctx = lax.axis_index("ctx")
        self.outer = lax.axis_size("ctx") // 2
        self.owners = owner_count(rows, width, by_rows, self.outer)
        self.stride = self.outer // self.owners
        self.inner = lax.rem(self.ctx, 2)
        self.line = self.ctx // 2
        self.mine = self.line // self.stride
        self.half = rows // 2

    def cols(self, k):
        return pl.ds(pl.multiple_of(k * self.width, self.width), self.width)

    def member(self, chip, core):
        return pl.ds(pl.multiple_of((chip * 2 + core) * self.rows, 64), self.rows)

    def half_rows(self, inner):
        return pl.ds(pl.multiple_of(inner * self.half, 16), self.half)

    def piece(self, j, base):
        if self.by_rows:
            n = self.half // self.owners
            return pl.ds(pl.multiple_of(base + j * n, 16), n), pl.ds(0, self.width)
        n = self.width // self.owners
        return pl.ds(pl.multiple_of(base, 16), self.half), pl.ds(pl.multiple_of(j * n, 128), n)

    def m_copy(self, k, chip):
        return remote(
            self.part.at[self.member(chip, 1 - self.core), self.cols(k)], self.m_buf.at[k, chip],
            self.sems.at[0, k, chip], self.sems.at[1, k, chip], group=self.group + 1 - 2 * self.core,
        )

    def x_copy(self, k, chip, sender):
        return remote(
            self.x_src.at[k, chip], self.x_buf.at[k, sender], self.sems.at[2, k, chip], self.sems.at[3, k, sender],
            group=chip * 2 + self.core,
        )

    def y_copy(self, k):
        return remote(
            self.y_src.at[k, self.half_rows(1 - self.inner)], self.y_buf.at[k], self.sems.at[4, k, 0], self.sems.at[5, k, 0],
            ctx=self.ctx + 1 - 2 * self.inner,
        )

    def z_copy(self, k, j, sender):
        rows, cols = self.piece(j, 0)
        return remote(
            self.z_src.at[k, rows, cols], self.z_buf.at[k, sender], self.sems.at[6, k, j], self.sems.at[7, k, sender],
            ctx=j * self.stride * 2 + self.inner,
        )

    def b_copy(self, k, line, j):
        rows, cols = self.piece(j, self.inner * self.half)
        return remote(
            self.full.at[k, rows, cols], self.full.at[k, rows, cols], self.sems.at[8, k, line], self.sems.at[9, k, j],
            ctx=line * 2 + self.inner,
        )

    def f_copy(self, k, inner):
        rows = self.half_rows(inner)
        return remote(
            self.full.at[k, rows], self.full.at[k, rows], self.sems.at[10, k, 0], self.sems.at[11, k, 0],
            ctx=self.ctx + 1 - 2 * self.inner,
        )

    def other_chips(self, body):
        for d in range(1, self.chips):
            body(lax.rem(self.chip + d, self.chips))

    def other_owners(self, body):
        if self.stride == 1:
            for d in range(1, self.owners):
                body(lax.rem(self.mine + d, self.owners))
        else:
            for j in range(self.owners):
                pl.when(j * self.stride != self.line)(lambda j=j: body(j))

    def other_lines(self, body):
        loop(1, self.outer, lambda d: body(lax.rem(self.line + d, self.outer)))

    def if_owner(self, body):
        if self.stride == 1:
            body()
        else:
            pl.when(self.mine * self.stride == self.line)(body)

    def m_start(self, k):
        for chip in range(self.chips):
            self.m_copy(k, chip).start()

    def m_done(self, k):
        for chip in range(self.chips):
            self.m_copy(k, chip).wait_recv()
            own = self.part[self.member(chip, self.core), self.cols(k)].astype(f32)
            self.x_src[k, chip] = (own + self.m_buf[k, chip].astype(f32)).astype(bf16)
        self.other_chips(lambda chip: self.x_copy(k, chip, self.chip).start())

    def x_done(self, k):
        total = self.x_src[k, self.chip].astype(f32)
        for d in range(1, self.chips):
            chip = lax.rem(self.chip + d, self.chips)
            self.x_copy(k, chip, chip).wait_recv()
            total = total + self.x_buf[k, chip].astype(f32)
        self.y_src[k] = total.astype(bf16)
        self.y_copy(k).start()

    def y_done(self, k):
        self.y_copy(k).wait_recv()
        own = self.y_src[k, self.half_rows(self.inner), :].astype(f32)
        self.z_src[k] = (own + self.y_buf[k].astype(f32)).astype(bf16)
        self.other_owners(lambda j: self.z_copy(k, j, self.line).start())

    def z_done(self, k):
        def run():
            rows, cols = self.piece(self.mine, 0)
            self.other_lines(lambda line: self.z_copy(k, self.mine, line).wait_recv())
            self.z_buf[k, self.line] = self.z_src[k, rows, cols]
            total = self.z_buf[k, 0].astype(f32)
            for line in range(1, self.outer):
                total = total + self.z_buf[k, line].astype(f32)
            rows, cols = self.piece(self.mine, self.inner * self.half)
            self.full[k, rows, cols] = total.astype(bf16)
            self.other_lines(lambda line: self.b_copy(k, line, self.mine).start())

        self.if_owner(run)

    def b_done(self, k):
        self.other_owners(lambda j: self.b_copy(k, self.line, j).wait_recv())
        self.f_copy(k, self.inner).start()

    def f_done(self, k):
        self.f_copy(k, 1 - self.inner).wait_recv()
        self.out[:, self.cols(k)] = self.full[k]

    def drain(self, k):
        for chip in range(self.chips):
            self.m_copy(k, chip).wait_send()
        self.other_chips(lambda chip: self.x_copy(k, chip, self.chip).wait_send())
        self.y_copy(k).wait_send()
        self.other_owners(lambda j: self.z_copy(k, j, self.line).wait_send())
        self.if_owner(lambda: self.other_lines(lambda line: self.b_copy(k, line, self.mine).wait_send()))
        self.f_copy(k, self.inner).wait_send()

    def wave(self, t):
        for lag, act in ((4, self.f_done), (3, self.b_done), (2, self.z_done), (1, self.y_done), (0, self.x_done)):
            k = t - lag * STAGE_LAG
            pl.when(jnp.logical_and(k >= 0, k < self.chunks))(lambda k=k, act=act: act(k))

    @staticmethod
    def scratch(chunks, rows, width, by_rows, group, count):
        chips, outer = group // 2, count // 2
        owners = owner_count(rows, width, by_rows, outer)
        half = rows // 2
        piece = (half // owners, width) if by_rows else (half, width // owners)
        bufs = [(chunks, chips, rows, width), (chunks, chips, rows, width), (chunks, rows, width),
                (chunks, half, width), (chunks, half, width), (chunks, outer) + piece, (chunks, rows, width)]
        return [(b, bf16) for b in bufs] + [pltpu.SemaphoreType.DMA((12, chunks, max(chips, outer, 2)))]


class Small:
    def __init__(self, held, got, sends, recvs):
        self.held, self.got, self.sends, self.recvs = held, got, sends, recvs

    def copy(self, h, j, sender):
        return remote(
            self.held.at[h], self.got.at[h, sender], self.sends.at[h, j], self.recvs.at[h, sender], **{HOPS[h]: j}
        )

    def others(self, h, body):
        size, mine = lax.axis_size(HOPS[h]), lax.axis_index(HOPS[h])
        loop(1, size, lambda d: body(lax.rem(mine + d, size)))

    def start(self, h):
        mine = lax.axis_index(HOPS[h])
        self.others(h, lambda j: self.copy(h, j, mine).start())

    def done(self, h):
        self.others(h, lambda j: self.copy(h, j, j).wait_recv())
        self.got[h, lax.axis_index(HOPS[h])] = self.held[h]
        total = self.got[h, 0]
        for j in range(1, lax.axis_size(HOPS[h])):
            total = total + self.got[h, j]
        self.held[h + 1] = total

    def drain(self):
        for h in range(2):
            mine = lax.axis_index(HOPS[h])
            self.others(h, lambda j: self.copy(h, j, mine).wait_send())

    @staticmethod
    def scratch(height, group, count):
        widest = max(group, count)
        dma = pltpu.SemaphoreType.DMA
        return [((3, height, HALF), f32), ((2, widest, height, HALF), f32), dma((2, widest)), dma((2, widest))]


def masks():
    rows = lax.broadcasted_iota(jnp.int32, (HALF, HALF), 0)
    cols = lax.broadcasted_iota(jnp.int32, (HALF, HALF), 1)
    return rows >= cols, cols < HEADDIM


def both(q):
    return slice(q * HALF, (q + 1) * HALF)


def pair_decays(cum, cum_t, p, causal):
    rolled = pltpu.roll(cum, lax.rem(HALF - 2 * p, HALF), 1)
    out = []
    for q in range(2):
        for a in range(2):
            gaps = rolled[both(q), a : a + 1] - cum_t[q, pl.ds(2 * p + a, 1), :]
            out.append(jnp.exp(jnp.where(causal, gaps, -jnp.inf)))
    return out


TILES = DIN // TILE
PIECES = 2 * TILES + 1
DT0 = DIN + CONVW - 2 * NSTATE


def front_kernel(
    tok, tok_any, wcat, wout, gain, cw, cb, db, dl,
    nt, nth, rhalo, cin, xb, spb, vout, cumout, st0, loc, ylocal, gate, decs_out, wfull, wofull, sin,
    sel, halo, nh_s, ext, w, cin_s, xs_s, bt, scores, out_cat, dt_cat, cum_t, tot1x, decs,
    halo_sem, x_send, x_recv, m_send, m_recv, w_own, w_store, dec_send, dec_recv, *exchange,
):
    i = pl.program_id(0)
    seqs = tok.shape[0]
    count = lax.axis_size("ctx")
    me = lax.axis_index("ctx")
    sems = (x_send, x_recv, m_send, m_recv, w_own)
    zx, wo = Spread(wcat, w, sems), Spread(wout, wofull, sems)
    last = PIECES

    def unit_cols(u):
        return pl.ds(pl.multiple_of(u * TILE, TILE), TILE)

    def piece(p):
        at = jnp.where(p <= TILES, DIN + (p - 1) * TILE, (p - 1 - TILES) * TILE)
        return pl.ds(pl.multiple_of(at, TILE), TILE)

    first_piece = pl.ds(DT0, 2 * NSTATE + HALF)
    ex = Exchange(False, lambda u, rows: sin.at[:, rows, unit_cols(u)], exchange[:9], exchange[9])
    halo_copy = remote(
        tok_any.at[:, pl.ds(SPAN - RIM, RIM), :], halo, halo_sem.at[0], halo_sem.at[1], ctx=lax.rem(me + 1, count)
    )
    keep_w = pltpu.make_async_copy(w, wfull, w_store.at[0])

    def dec_copy(block, sender):
        rows = pl.ds(pl.multiple_of(sender * 8, 8), 8)
        return remote(decs.at[:, rows, :], decs.at[:, rows, :], dec_send.at[block], dec_recv.at[sender], ctx=block)

    def other_blocks(body):
        loop(1, count, lambda d: body(lax.rem(me + d, count)))

    def conv_tile(s, cols_w, cols_c):
        cin_s[s] = mm(ext[s], w[:, cols_w])
        cin[s] = cin_s[s].astype(bf16)
        o = cb[:, cols_c]
        for k in range(KCONV):
            o = o + cw[k : k + 1, cols_c] * cin_s[s, RIM - KCONV + 1 + k : RIM - KCONV + 1 + k + SPAN, :]
        sg = gate_of(o)
        a = o * sg
        xb[s] = a.astype(bf16)
        spb[s] = (sg + a * (1.0 - sg)).astype(bf16)
        return a

    def unit_decays(u):
        for s in range(seqs):
            ex.decx[s] = spread(decs[s], sel.at[:, unit_cols(u)])

    @pl.when(i == 0)
    def _():
        meet(("ctx", "group"))
        pl.when(me < count - 1)(lambda: halo_copy.start())
        zx.start(0, first_piece)
        zx.start_chip(0)
        zx.start(1, piece(1))
        zx.start(2, piece(2))
        wo.start_chip(1)
        sel[...] = head_map()

        @pl.when(me == 0)
        def _():
            halo[...] = jnp.zeros_like(halo)

        def norm_main(s):
            nm = normalized(tok[s], gain[...])[2]
            ext[s, RIM:] = nm
            nt[:, pl.ds(pl.multiple_of(s * SPAN, SPAN), SPAN)] = jnp.transpose(nm.astype(f32)).astype(bf16)

        loop(0, seqs, norm_main)

        @pl.when(me > 0)
        def _():
            halo_copy.wait_recv()

        def norm_halo(s):
            nh = normalized(halo[s], gain[...])[2]
            ext[s, 0:RIM] = nh
            nh_s[pl.ds(pl.multiple_of(s * RIM, RIM), RIM), :] = nh.astype(f32)
            rhalo[s] = halo[s]

        loop(0, seqs, norm_halo)
        nth[...] = jnp.transpose(nh_s[...]).astype(bf16)
        zx.forward(0, first_piece)
        zx.finish_chip(0)

    @pl.when(i + 1 < PIECES)
    def _():
        zx.forward(i + 1, piece(i + 1))

    @pl.when(i + 3 < PIECES)
    def _():
        zx.start(i + 3, piece(i + 3))

    @pl.when(i + 3 == PIECES)
    def _():
        wo.start(last, slice(None))

    @pl.when(i == 0)
    def _():
        zx.finish(0, first_piece)

        def delta(s):
            a = conv_tile(s, slice(DT0, DT0 + TILE), slice(DIN, DIN + TILE))
            bb, cc = a[:, :NSTATE].astype(bf16), a[:, NSTATE:].astype(bf16)
            bt[s] = jnp.transpose(a[:, :NSTATE]).astype(bf16)
            for q in range(2):
                scores[s, q] = mm_nt(cc[both(q)], bb[both(q)])
            v = mm(ext[s, RIM:], w[:, DT0 + TILE :]) + db[...]
            vout[s] = v
            dt = softplus(v)
            cum = exact_mm(triangle(SPAN, True), -jnp.exp(dl[...]) * dt)
            cumout[s] = cum
            for q in range(2):
                cum_t[s, q] = jnp.transpose(cum[both(q)])
            e_in, e_out, tot0, tot1, total = local_decays(cum)
            decs[s, pl.ds(pl.multiple_of(me * 8, 8), 8), :] = rows_of(total)
            out_cat[s] = jnp.concatenate(halves(dt * e_out), axis=1)
            dt_cat[s] = jnp.concatenate(halves(dt), axis=1)
            tot1x[s] = spread(rows_of(tot1), sel)

        loop(0, seqs, delta)
        other_blocks(lambda b: dec_copy(b, me).start())

    @pl.when(jnp.logical_and(i >= 1, i < PIECES))
    def _():
        zx.finish(i, piece(i))

    def act_at(t, lag, act):
        u = t - 1 - lag
        pl.when(jnp.logical_and(u >= 0, u < TILES))(lambda: act(u))

    def close(u):
        unit_decays(u)
        ex.close(u)

    def scan(u):
        unit_decays(u)
        ex.scan(u)

    def middle(u):
        unit_decays(u)
        ex.middle(u)

    @pl.when(i == 3)
    def _():
        other_blocks(lambda b: dec_copy(b, b).wait_recv())

    def wave(t):
        act_at(t, CLOSE_LAG, close)
        act_at(t, SCAN_LAG, scan)
        act_at(t, MIDDLE_LAG, middle)

    wave(i)

    @pl.when(jnp.logical_and(i >= 1, i <= TILES))
    def _():
        u = i - 1
        cols = unit_cols(u)

        def x_tile(s):
            a = conv_tile(s, piece(i), cols)
            xs_s[s, :, cols] = a.astype(bf16)
            xw = (a * mm(out_cat[s], sel[:, cols])).astype(bf16)
            s0 = mm(bt[s, :, :HALF], xw[:HALF])
            s1 = mm(bt[s, :, HALF:], xw[HALF:])
            st0[s] = s0.astype(bf16)
            low = (tot1x[s, :, cols][0:1] * s0 + s1).astype(bf16)
            loc[s] = low
            ex.buf[u, s] = low

        loop(0, seqs, x_tile)
        ex.start(u)

    @pl.when(i > TILES)
    def _():
        u = i - 1 - TILES
        causal, low_lanes = masks()

        def intra(s):
            cum = cumout[s]
            dtx = mm(dt_cat[s], sel[:, unit_cols(u)])
            for h in range(2):
                p = 2 * u + h
                lanes = slice(h * HALF, (h + 1) * HALF)
                decays = pair_decays(cum, cum_t.at[s], p, causal)
                for q in range(2):
                    rows = both(q)
                    m = jnp.concatenate([(decays[2 * q + a] * scores[s, q]).astype(bf16) for a in range(2)], axis=1)
                    x = xs_s[s, rows, pl.ds(pl.multiple_of(p * HALF, HALF), HALF)].astype(f32) * dtx[rows, lanes]
                    x = jnp.concatenate([jnp.where(low_lanes, x, 0.0), jnp.where(low_lanes, 0.0, x)], axis=0)
                    ylocal[s, rows, lanes] = mm(m, x.astype(bf16)).astype(bf16)
            gate[s] = mm(ext[s, RIM:], w[:, piece(i)]).astype(bf16)

        loop(0, seqs, intra)

    @pl.when(i == PIECES - 1)
    def _():
        keep_w.start()
        decs_out[...] = decs[...]
        wo.forward(last, slice(None))
        loop(PIECES, TILES + CLOSE_LAG + 1, wave)
        loop(0, TILES, ex.finish)
        wo.finish(last, slice(None))
        wo.finish_chip(1)
        zx.drain_chip(0)
        wo.drain_chip(1)
        zx.drain(0, first_piece)
        loop(1, PIECES, lambda p: zx.drain(p, piece(p)))
        wo.drain(last, slice(None))
        other_blocks(lambda b: dec_copy(b, me).wait_send())
        pl.when(me < count - 1)(lambda: halo_copy.wait_send())
        keep_w.wait()


def middle_kernel(
    rel, tok, cot, ylocal, gate, xb, vin, cumin, st0, sin, decs, wout, skip, ggain,
    mixed, mlow, dyout, ggate, wred, dir1, gskip, gggain, dxs, dbc, later,
    sel, cum_t, einx, ys, gs, ss, s_in, dcs, dy_s, ml_s, g_s, dg_s, *exchange,
):
    i = pl.program_id(0)
    seqs = dy_s.shape[0]
    ex = Exchange(True, lambda u, rows: later.at[pl.ds(u, 1), rows, :], exchange[:9], exchange[9])

    def wave(t):
        def act_at(lag, act):
            u = lax.div(t - lag, 2)

            def run():
                ex.decx[0] = spread(decs[u], sel)
                act(u)

            pl.when(jnp.logical_and(t >= lag, jnp.logical_and(2 * u + lag == t, u < seqs)))(run)

        act_at(BACK_LAGS[2], ex.close)
        act_at(BACK_LAGS[1], ex.scan)
        act_at(BACK_LAGS[0], ex.middle)

    @pl.when(i == 0)
    def _():
        meet(("ctx",))
        sel[...] = head_map()
        gskip[...] = jnp.zeros_like(gskip)
        gggain[...] = jnp.zeros_like(gggain)

    wave(2 * i)

    @pl.when(i < seqs)
    def _():
        s = i
        cum = cumin[0]
        e_in, e_out, tot0, tot1, total = local_decays(cum)
        einx[...] = spread(e_in, sel)
        tot0x = spread(rows_of(tot0), sel)[0:1]
        s_in[0] = sin[0]
        s_in[1] = (tot0x * sin[0].astype(f32) + st0[0].astype(f32)).astype(bf16)
        cc = xb[0, :, DIN + NSTATE :]

        def gate_step(j, total_sq):
            cols = pl.ds(pl.multiple_of(j * TILE, TILE), TILE)
            for q in range(2):
                rows = both(q)
                ys[rows, cols] = ylocal[0, rows, cols].astype(f32) + einx[rows, cols] * mm(cc[rows], s_in[q, :, cols])
            y = ys[:, cols] + skip[:, cols] * xb[0, :, cols].astype(f32)
            g = gate[0, :, cols].astype(f32)
            gated = y * (g * gate_of(g))
            gs[:, cols] = gated
            sq = gated * gated
            return total_sq + sq[:, :HALF] + sq[:, HALF:]

        wave(2 * i + 1)
        sq = lax.fori_loop(0, DIN // TILE, gate_step, jnp.zeros((SPAN, HALF), f32))
        inv = lax.rsqrt(jnp.sum(sq, axis=1, keepdims=True) * (1.0 / DIN) + EPS)
        live = (lax.broadcasted_iota(jnp.int32, (SPAN, 1), 0) < rel[s]).astype(f32)
        drive = (live * cot[0].astype(f32)).astype(bf16)

        def back_step(j, acc):
            cols = pl.ds(pl.multiple_of(j * TILE, TILE), TILE)
            gm = mm_nt(drive, wout[cols, :])
            gated = gs[:, cols]
            unit = gated * inv
            low = (unit * ggain[:, cols]).astype(bf16)
            mlow[0, :, cols] = low
            ml_s[s, :, cols] = low
            gggain[:, cols] += jnp.sum(gm * unit, axis=0, keepdims=True)
            scaled = gm * ggain[:, cols]
            ss[:, cols] = scaled
            prod = scaled * gated
            return acc + prod[:, :HALF] + prod[:, HALF:]

        dots = lax.fori_loop(0, DIN // TILE, back_step, jnp.zeros((SPAN, HALF), f32))
        dots = jnp.sum(dots, axis=1, keepdims=True) * (1.0 / DIN)
        corr = inv * inv * inv * dots
        cct = jnp.transpose(cc.astype(f32)).astype(bf16)
        acc = jnp.zeros((SPAN, HALF), f32)
        dc = [jnp.zeros((HALF, HALF), f32) for _ in range(2)]
        for j in range(DIN // TILE):
            cols = slice(j * TILE, (j + 1) * TILE)
            g = gate[0, :, cols].astype(f32)
            sg = gate_of(g)
            sl = g * sg
            grad_gated = inv * ss[:, cols] - gs[:, cols] * corr
            dy = grad_gated * sl
            yn = ys[:, cols]
            x = xb[0, :, cols].astype(f32)
            y = yn + skip[:, cols] * x
            ggate[0, :, cols] = (grad_gated * y * (sg + sl * (1.0 - sg))).astype(bf16)
            dyb = dy.astype(bf16)
            dyout[0, :, cols] = dyb
            dy_s[s, :, cols] = dyb
            gskip[:, cols] += jnp.sum(dy * x, axis=0, keepdims=True)
            acc = acc + gather_heads(dy * yn, sel[:HALF, cols])
            dye = (dy * einx[:, cols]).astype(bf16)
            d0 = mm(cct[:, :HALF], dye[:HALF])
            d1 = mm(cct[:, HALF:], dye[HALF:])
            dir1[0, :, cols] = d1.astype(bf16)
            ex.buf[s, 0, :, cols] = (d0 + tot0x[:, cols] * d1).astype(bf16)
            for q in range(2):
                dc[q] = dc[q] + mm_nt(dye[both(q)], s_in[q, :, cols])
        wred[0] = acc
        for q in range(2):
            dcs[s, both(q)] = dc[q]
        ex.start(s)

    @pl.when(i >= seqs)
    def _():
        s = i - seqs
        causal, low_lanes = masks()
        cum = cumin[0]
        for q in range(2):
            cum_t[q] = jnp.transpose(cum[both(q)])
        einx[...] = spread(softplus(vin[0]), sel)
        bb = xb[0, :, DIN : DIN + NSTATE]
        cc = xb[0, :, DIN + NSTATE :]
        for q in range(2):
            g_s[q] = mm_nt(cc[both(q)], bb[both(q)])
        dg_s[...] = jnp.zeros_like(dg_s)

        def pair_step(p):
            cols = pl.ds(pl.multiple_of(p * HALF, HALF), HALF)
            decays = pair_decays(cum, cum_t, p, causal)
            for q in range(2):
                rows = both(q)
                xsb = (xb[0, rows, cols].astype(f32) * einx[rows, cols]).astype(bf16)
                dyb = dy_s[s, rows, cols]
                dyf = dyb.astype(f32)
                grads = []
                for a in range(2):
                    m = (decays[2 * q + a] * g_s[q]).astype(bf16)
                    grads.append(mm_tn(m, dyb))
                    mine = low_lanes if a == 0 else jnp.logical_not(low_lanes)
                    dm = mm_nt(jnp.where(mine, dyf, 0.0).astype(bf16), xsb)
                    dg_s[q] += dm * decays[2 * q + a]
                dxs[0, rows, cols] = jnp.where(low_lanes, grads[0], grads[1]).astype(bf16)

        loop(0, PAIRS // 2, pair_step)
        wave(2 * i + 1)
        loop(PAIRS // 2, PAIRS, pair_step)
        for q in range(2):
            rows = both(q)
            dg = dg_s[q].astype(bf16)
            dbc[0, rows, :NSTATE] = mm_tn(dg, cc[rows])
            dbc[0, rows, NSTATE:] = mm(dg, bb[rows]) + dcs[s, rows]
        live = (lax.broadcasted_iota(jnp.int32, (SPAN, 1), 0) < rel[s]).astype(f32)
        for j in range(D // TILE):
            cols = slice(j * TILE, (j + 1) * TILE)
            mixed[0, :, cols] = (live * (tok[0, :, cols].astype(f32) + mm(ml_s[s], wout[:, cols]))).astype(bf16)

    @pl.when(i == 2 * seqs - 1)
    def _():
        loop(4 * seqs, 2 * seqs + BACK_LAGS[2] - 1, wave)
        loop(0, seqs, ex.finish)


def back_kernel(
    rel, tok, cot, rhalo, gain, ggate, wfull, cin, xb, spb, bc, dy, dxs, dir1, later, sin, loc,
    vin, cumin, wred, dbc, cw, dl, skip, nt, nth, pgate, pout, gskip, gggain,
    gtok, rgate, rout, rconv, small_out, ggain_out,
    sel, dt_cat, eo_cat, tots, db_s, qacc, ends, gp, gz_s, gzh_s, pconv, gcw, gcb, gdb, gdl, ggain,
    rim_out, rim_in, rim_send, rim_recv, *comm,
):
    i = pl.program_id(0)
    seqs = rhalo.shape[0]
    count = lax.axis_size("ctx")
    me = lax.axis_index("ctx")
    members = lax.axis_size("group")
    gates = Reducer(pgate, rgate, D // members, GATE_CHUNK, False, comm[0:7], comm[7])
    outs = Reducer(pout, rout, DIN // members, OUT_CHUNK, True, comm[8:15], comm[15])
    convs = Reducer(pconv, rconv, D // members, CONV_CHUNK, False, comm[16:23], comm[23])
    little, least = Small(*comm[24:28]), Small(*comm[28:32])
    last_x = TILES - 1
    bc_step = TILES

    def wave(t):
        gates.wave(t - 4)
        outs.wave(t - 4 - gates.chunks)
        convs.wave(t - 2 * bc_step - 1)

    def rim_copy(q):
        return remote(rim_out.at[q], rim_in.at[q], rim_send.at[q], rim_recv.at[q], ctx=lax.rem(me + count - 1, count))

    def span(s):
        return pl.ds(pl.multiple_of(s * SPAN, SPAN), SPAN)

    def edge(s):
        return pl.ds(pl.multiple_of(s * RIM, RIM), RIM)

    def back(rows, grad):
        rows, inv, _ = normalized(rows, gain[...])
        ggain[...] += jnp.sum(grad * rows * inv, axis=0, keepdims=True)
        gained = gain[...] * grad
        mean = jnp.mean(gained * rows, axis=-1, keepdims=True)
        return inv * gained - rows * (inv * inv * inv * mean)

    @pl.when(i == 0)
    def _():
        meet(("ctx", "group"))
        for r in (gates, outs):
            loop(0, r.chunks, r.m_start)
        sel[...] = head_map()
        for acc in (db_s, qacc, ends, gcw, gcb, gdb, gdl, ggain):
            acc[...] = jnp.zeros_like(acc)
        gp[0:RIM] = jnp.zeros((RIM, TILE), f32)
        gp[RIM + SPAN :] = jnp.zeros((8, TILE), f32)
        pconv[:, CONVW + HALF :] = jnp.zeros((D, GZW - CONVW - HALF), bf16)

        def setup(s):
            dt = softplus(vin[s])
            _, e_out, _, tot1, total = local_decays(cumin[s])
            dt_cat[s] = jnp.concatenate(halves(dt), axis=1)
            eo_cat[s] = jnp.concatenate(halves(e_out), axis=1)
            both_rows = jnp.concatenate([rows_of(tot1), rows_of(total)], axis=0)
            tots[s] = spread(both_rows, sel)

        loop(0, seqs, setup)

    def conv_back(s, dact, cols):
        gco = dact * spb[s].astype(f32)
        gp[RIM : RIM + SPAN] = gco
        gcb[:, cols] += jnp.sum(gco, axis=0, keepdims=True)
        own = cin[s, RIM:].astype(f32)
        before = cin[s, :RIM].astype(f32)
        main = jnp.zeros((SPAN, TILE), f32)
        rim = jnp.zeros((RIM, TILE), f32)
        for k in range(KCONV):
            ahead = KCONV - 1 - k
            moved = gco if ahead == 0 else gp[RIM + ahead : RIM + ahead + SPAN]
            early = gp[ahead : ahead + RIM]
            main = main + cw[k : k + 1, cols] * moved
            rim = rim + cw[k : k + 1, cols] * early
            gcw[k : k + 1, cols] += jnp.sum(own * moved, axis=0, keepdims=True) + jnp.sum(
                before * early, axis=0, keepdims=True
            )
        gz_s[span(s), cols] = main.astype(bf16)
        gzh_s[edge(s), cols] = rim.astype(bf16)

    def partial(cols):
        pconv[:, cols] = (mm(nt[...], gz_s[:, cols]) + mm(nth[...], gzh_s[:, cols])).astype(bf16)

    wave(2 * i)

    @pl.when(jnp.logical_and(lax.rem(i, 2) == 0, jnp.logical_and(i >= 2, i <= bc_step)))
    def _():
        convs.m_done(lax.div(i, 2) - 1)

    @pl.when(i == bc_step + 1)
    def _():
        convs.m_done(convs.chunks - 1)

    @pl.when(i < bc_step)
    def _():
        cols = pl.ds(pl.multiple_of(i * TILE, TILE), TILE)

        def x_tile(s):
            dte = mm(dt_cat[s], sel[:, cols])
            eo = mm(eo_cat[s], sel[:, cols])
            near = later[s]
            near32 = near.astype(f32)
            tot = tots[s, :, cols]
            reach = [(dir1[s].astype(f32) + tot[0:1] * near32).astype(bf16), near]
            fed = jnp.concatenate(
                [mm(bc[s, both(q), :NSTATE], reach[q]) for q in range(2)], axis=0
            )
            x = xb[s].astype(f32)
            dx_s = dxs[s].astype(f32) + eo * fed
            qacc[s] += gather_heads(x * dx_s, sel[:HALF, cols])
            xw = (x * dte * eo).astype(bf16)
            for q in range(2):
                db_s[s, both(q)] += mm_nt(xw[both(q)], reach[q])
            held = near32 * (tot[8:9] * sin[s].astype(f32) + loc[s].astype(f32))
            ends[s] += gather_heads(rows_of(jnp.sum(held, axis=0, keepdims=True)), sel[:HALF, cols])
            conv_back(s, dte * dx_s + skip[:, cols] * dy[s].astype(f32), cols)

        loop(0, seqs // 2, x_tile)

        @pl.when(i == 0)
        def _():
            for r in (gates, outs):
                loop(0, r.chunks, r.m_done)

        wave(2 * i + 1)
        loop(seqs // 2, seqs, x_tile)
        partial(cols)

        @pl.when(lax.rem(i, 2) == 1)
        def _():
            convs.m_start(lax.div(i, 2))

    @pl.when(i == bc_step)
    def _():
        cols = slice(DIN, CONVW)

        def bc_tile(s):
            conv_back(s, jnp.concatenate([dbc[s, :, :NSTATE] + db_s[s], dbc[s, :, NSTATE:]], axis=1), cols)
            v = vin[s]
            dt = softplus(v)
            q = qacc[s]
            at_end = lax.broadcasted_iota(jnp.int32, (SPAN, 1), 0) == SPAN - 1
            dcum = wred[s] - dt * q + jnp.where(at_end, ends[s][0:1], 0.0)
            glog = exact_mm(triangle(SPAN, False), dcum)
            rate = jnp.exp(dl[...])
            gpd = (q - rate * glog) * sigmoid(v)
            lanes = lax.broadcasted_iota(jnp.int32, (SPAN, HALF), 1) < HEADS
            gpd = jnp.where(lanes, gpd, 0.0)
            gz_s[span(s), CONVW : CONVW + HALF] = gpd.astype(bf16)
            gdb[...] += jnp.sum(gpd, axis=0, keepdims=True)
            gdl[...] += -rate * jnp.sum(dt * glog, axis=0, keepdims=True)

        loop(0, seqs, bc_tile)
        wave(2 * i + 1)
        partial(cols)
        pconv[:, CONVW : CONVW + HALF] = mm(nt[...], gz_s[:, CONVW : CONVW + HALF]).astype(bf16)
        convs.m_start(convs.chunks - 1)
        rows = [gcw[k : k + 1, j * HALF : (j + 1) * HALF] for k in range(KCONV) for j in range(CONVW // HALF)]
        rows += [gcb[:, j * HALF : (j + 1) * HALF] for j in range(CONVW // HALF)]
        rows += [gdb[...], gdl[...]]
        rows += [gskip[:, j * HALF : (j + 1) * HALF] for j in range(PAIRS)]
        rows += [gggain[:, j * HALF : (j + 1) * HALF] for j in range(PAIRS)]
        for r, row in enumerate(rows):
            little.held[0, r : r + 1, :] = row
        little.start(0)
        edges = mm_nt(gzh_s[...], wfull[:, DIN:ZXW])
        for q in range(seqs):
            rim_out[q] = back(rhalo[q], edges[q * RIM : (q + 1) * RIM]).astype(bf16)
            pl.when(me > 0)(lambda q=q: rim_copy(q).start())

        @pl.when(me == count - 1)
        def _():
            rim_in[...] = jnp.zeros_like(rim_in)

    @pl.when(i == bc_step + 2)
    def _():
        little.done(0)
        little.start(1)

    @pl.when(i > bc_step)
    def _():
        s = i - bc_step - 1
        grad = mm_nt(gz_s[span(s), :], wfull[:, DIN:]) + mm_nt(ggate[0], wfull[:, :DIN])
        wave(2 * i + 1)
        live = (lax.broadcasted_iota(jnp.int32, (SPAN, 1), 0) < rel[s]).astype(f32)
        out = live * cot[0].astype(f32) + back(tok[0], grad)
        gtok[0, : SPAN - RIM] = out[: SPAN - RIM].astype(bf16)
        pl.when(me < count - 1)(lambda: rim_copy(s).wait_recv())
        gtok[0, SPAN - RIM :] = (out[SPAN - RIM :] + rim_in[s].astype(f32)).astype(bf16)

    @pl.when(i == bc_step + seqs)
    def _():
        least.held[0] = jnp.zeros_like(least.held[0])
        for j in range(D // HALF):
            least.held[0, j : j + 1, :] = ggain[:, j * HALF : (j + 1) * HALF]
        least.start(0)
        little.done(1)
        small_out[...] = little.held[2]
        least.done(0)
        least.start(1)
        loop(2 * (bc_step + seqs) + 2, 2 * bc_step + 1 + convs.chunks + 4 * STAGE_LAG, wave)
        for r in (gates, outs, convs):
            loop(0, r.chunks, r.drain)
        little.drain()
        for q in range(seqs):
            pl.when(me > 0)(lambda q=q: rim_copy(q).wait_send())
        least.done(1)
        ggain_out[...] = least.held[2]
        least.drain()


def whole(shape):
    zeros = (0,) * len(shape)
    return pl.BlockSpec(shape, lambda s: zeros, pipeline_mode=pl.Buffered(1))


def summed(shape):
    zeros = (0,) * len(shape)
    return pl.BlockSpec(shape, lambda s: zeros)


def per_seq(*shape):
    zeros = (0,) * len(shape)
    return pl.BlockSpec((1,) + shape, lambda s: (s,) + zeros)


SMEM = pl.BlockSpec(memory_space=pltpu.SMEM)
ANY = pl.BlockSpec(memory_space=pl.ANY)


def staged(seqs, phase, *shape):
    zeros = (0,) * len(shape)
    if phase == 0:
        return pl.BlockSpec((1,) + shape, lambda i: (jnp.minimum(i, seqs - 1),) + zeros)
    if phase == 1:
        return pl.BlockSpec((1,) + shape, lambda i: (jnp.maximum(i - seqs, 0),) + zeros)
    return pl.BlockSpec((1,) + shape, lambda i: (lax.rem(i, seqs),) + zeros)


def call(kernel, steps, in_specs, outs, scratch, name, collective=None):
    params = dict(vmem_limit_bytes=VMEM_LIMIT)
    if collective is not None:
        params.update(collective_id=collective, has_side_effects=True)
    return pl.pallas_call(
        kernel,
        grid=(steps,),
        in_specs=in_specs,
        out_specs=[o[0] for o in outs],
        out_shape=[jax.ShapeDtypeStruct(o[1], o[2]) for o in outs],
        scratch_shapes=[pltpu.VMEM(*sc) if isinstance(sc, tuple) else sc for sc in scratch],
        compiler_params=pltpu.CompilerParams(**params),
        name=name,
    )


def lanes_of(v):
    return jnp.pad(v[None, :], ((0, 0), (0, HALF - v.shape[0])))


def local(
    tokens_in, seq_lengths, norm_gain, w_zx, w_delta, w_out, conv_weight, conv_bias,
    delta_bias, decay_log, skip_gain, gated_gain, cotangent,
):
    seqs = tokens_in.shape[0]
    count = lax.axis_size("ctx")
    group = lax.axis_size("group")
    chips = max(group // 2, 1)
    rel = seq_lengths - lax.axis_index("ctx") * SPAN
    gain = norm_gain[None, :]
    cb = conv_bias[None, :]
    db = lanes_of(delta_bias)
    dl = lanes_of(decay_log)
    skip = jnp.repeat(skip_gain, HEADDIM)[None, :]
    ggain = gated_gain[None, :]
    wcat = jnp.concatenate([w_zx, jnp.pad(w_delta, ((0, 0), (0, HALF - HEADS)))], axis=1)
    dma = pltpu.SemaphoreType.DMA
    at0 = lambda *shape: staged(seqs, 0, *shape)
    at1 = lambda *shape: staged(seqs, 1, *shape)
    at01 = lambda *shape: staged(seqs, 2, *shape)

    def tiled(rows, first, lead=None):
        def index(i):
            u = jnp.clip(i - first, 0, TILES - 1)
            return (0, 0, u if lead is None else jnp.where(i == 0, lead, u))

        return pl.BlockSpec((seqs, rows, TILE), index)

    state = (seqs, NSTATE, DIN)
    nt, nth, rhalo, cin, xb, spb, vraw, cum, st0, loc, ylocal, gate, decs, wfull, wofull, state_in = call(
        front_kernel,
        PIECES,
        [whole((seqs, SPAN, D)), ANY, ANY, ANY, whole((1, D)), whole((KCONV, CONVW)), whole((1, CONVW)), whole((1, HALF)),
         whole((1, HALF))],
        [
            (summed((D, seqs * SPAN)), (D, seqs * SPAN), bf16),
            (summed((D, seqs * RIM)), (D, seqs * RIM), bf16),
            (summed((seqs, RIM, D)), (seqs, RIM, D), bf16),
            (tiled(RIM + SPAN, 1, TILES), (seqs, RIM + SPAN, CONVW), bf16),
            (tiled(SPAN, 1, TILES), (seqs, SPAN, CONVW), bf16),
            (tiled(SPAN, 1, TILES), (seqs, SPAN, CONVW), bf16),
            (summed((seqs, SPAN, HALF)), (seqs, SPAN, HALF), f32),
            (summed((seqs, SPAN, HALF)), (seqs, SPAN, HALF), f32),
            (tiled(NSTATE, 1), state, bf16),
            (tiled(NSTATE, 1), state, bf16),
            (tiled(SPAN, TILES + 1), (seqs, SPAN, DIN), bf16),
            (tiled(SPAN, TILES + 1), (seqs, SPAN, DIN), bf16),
            (summed((seqs, count * 8, HALF)), (seqs, count * 8, HALF), f32),
            (ANY, (D, ZXW + HALF), bf16),
            (ANY, (DIN, D), bf16),
            (ANY, state, bf16),
        ],
        [((2 * HALF, DIN), bf16), ((seqs, RIM, D), bf16), ((seqs * RIM, D), f32), ((seqs, RIM + SPAN, D), bf16), ((D, ZXW + HALF), bf16),
         ((seqs, RIM + SPAN, TILE), f32), ((seqs, SPAN, DIN), bf16), ((seqs, NSTATE, SPAN), bf16),
         ((seqs, 2, HALF, HALF), f32), ((seqs, SPAN, 2 * HALF), bf16), ((seqs, SPAN, 2 * HALF), bf16),
         ((seqs, 2, HALF, HALF), f32), ((seqs, 8, DIN), f32), ((seqs, count * 8, HALF), f32)]
        + [dma((2,))] + [dma((PIECES + 1, chips))] * 4 + [dma((2,)), dma((1,)), dma((count,)), dma((count,))]
        + Exchange.scratch(TILES, seqs, TILE, count),
        "front",
        0,
    )(tokens_in, tokens_in, wcat, w_out, gain, conv_weight, cb, db, dl)

    mixed_out, mlow, dy, ggate, wred, dir1, gskip, gggain, dxs, dbc, later = call(
        middle_kernel,
        2 * seqs,
        [SMEM, at1(SPAN, D), at0(SPAN, D), at0(SPAN, DIN), at0(SPAN, DIN), at01(SPAN, CONVW), at01(SPAN, HALF),
         at01(SPAN, HALF), at0(NSTATE, DIN), at0(NSTATE, DIN), whole((seqs, count * 8, HALF)), whole((DIN, D)),
         whole((1, DIN)), whole((1, DIN))],
        [
            (at1(SPAN, D), (seqs, SPAN, D), bf16),
            (at0(SPAN, DIN), (seqs, SPAN, DIN), bf16),
            (at0(SPAN, DIN), (seqs, SPAN, DIN), bf16),
            (at0(SPAN, DIN), (seqs, SPAN, DIN), bf16),
            (at0(SPAN, HALF), (seqs, SPAN, HALF), f32),
            (at0(NSTATE, DIN), (seqs, NSTATE, DIN), bf16),
            (summed((1, DIN)), (1, DIN), f32),
            (summed((1, DIN)), (1, DIN), f32),
            (at1(SPAN, DIN), (seqs, SPAN, DIN), bf16),
            (at1(SPAN, 2 * NSTATE), (seqs, SPAN, 2 * NSTATE), f32),
            (ANY, (seqs, NSTATE, DIN), bf16),
        ],
        [((2 * HALF, DIN), bf16), ((2, HALF, HALF), f32), ((SPAN, DIN), f32), ((SPAN, DIN), f32), ((SPAN, DIN), f32),
         ((SPAN, DIN), f32), ((2, NSTATE, DIN), bf16), ((seqs, SPAN, HALF), f32), ((seqs, SPAN, DIN), bf16),
         ((seqs, SPAN, DIN), bf16), ((2, HALF, HALF), f32), ((2, HALF, HALF), f32)]
        + Exchange.scratch(seqs, 1, DIN, count),
        "middle",
        1,
    )(rel, tokens_in, cotangent, ylocal, gate, xb, vraw, cum, st0, state_in, decs, wofull, skip, ggain)

    live = (jnp.arange(SPAN, dtype=jnp.int32)[None, :] < rel[:, None]).astype(f32)[:, :, None]
    drive = (live * cotangent.astype(f32)).astype(bf16)
    flat = lambda v: v.reshape(-1, v.shape[-1])
    p_out = mm_tn(flat(mlow), flat(drive)).astype(bf16)
    p_gate = mm(nt, flat(ggate)).astype(bf16)

    def tile_in(rows, tiles):
        return pl.BlockSpec((seqs, rows, TILE), lambda i: (0, 0, jnp.minimum(i, tiles - 1)))

    def late(*shape):
        zeros = (0,) * len(shape)
        return pl.BlockSpec((1,) + shape, lambda i: (jnp.clip(i - TILES - 1, 0, seqs - 1),) + zeros)

    bc_spec = pl.BlockSpec((seqs, SPAN, TILE), lambda i: (0, 0, TILES), pipeline_mode=pl.Buffered(1))
    sizes = (KCONV * CONVW, CONVW, HALF, HALF, DIN, DIN)
    height = sum(sizes) // HALF
    gtok, r_gate, r_out, r_conv, small, g_gain = call(
        back_kernel,
        TILES + 1 + seqs,
        [SMEM, late(SPAN, D), late(SPAN, D), whole((seqs, RIM, D)), whole((1, D)), late(SPAN, DIN), whole((D, ZXW + HALF)),
         tile_in(RIM + SPAN, TILES + 1), tile_in(SPAN, TILES + 1), tile_in(SPAN, TILES + 1), bc_spec, tile_in(SPAN, TILES),
         tile_in(SPAN, TILES), tile_in(NSTATE, TILES), tile_in(NSTATE, TILES), tile_in(NSTATE, TILES), tile_in(NSTATE, TILES),
         whole((seqs, SPAN, HALF)), whole((seqs, SPAN, HALF)), whole((seqs, SPAN, HALF)), whole((seqs, SPAN, 2 * NSTATE)),
         whole((KCONV, CONVW)), whole((1, HALF)), whole((1, DIN)), whole((D, seqs * SPAN)), whole((D, seqs * RIM)),
         whole((D, DIN)), whole((DIN, D)), whole((1, DIN)), whole((1, DIN))],
        [
            (late(SPAN, D), (seqs, SPAN, D), bf16),
            (summed((D // group, DIN)), (D // group, DIN), bf16),
            (summed((DIN // group, D)), (DIN // group, D), bf16),
            (summed((D // group, GZW)), (D // group, GZW), bf16),
            (summed((height, HALF)), (height, HALF), f32),
            (summed((8, HALF)), (8, HALF), f32),
        ],
        [((2 * HALF, DIN), bf16), ((seqs, SPAN, 2 * HALF), bf16), ((seqs, SPAN, 2 * HALF), bf16), ((seqs, 16, DIN), f32),
         ((seqs, SPAN, NSTATE), f32), ((seqs, SPAN, HALF), f32), ((seqs, 8, HALF), f32), ((RIM + SPAN + 8, TILE), f32),
         ((seqs * SPAN, CONVW + HALF), bf16), ((seqs * RIM, CONVW), bf16), ((D, GZW), bf16), ((KCONV, CONVW), f32),
         ((1, CONVW), f32), ((1, HALF), f32), ((1, HALF), f32), ((1, D), f32), ((seqs, RIM, D), bf16), ((seqs, RIM, D), bf16),
         dma((seqs,)), dma((seqs,))]
        + Reducer.scratch(DIN // GATE_CHUNK, D // group, GATE_CHUNK, False, group, count)
        + Reducer.scratch(D // OUT_CHUNK, DIN // group, OUT_CHUNK, True, group, count)
        + Reducer.scratch(GZW // CONV_CHUNK, D // group, CONV_CHUNK, False, group, count)
        + Small.scratch(height, group, count)
        + Small.scratch(8, group, count),
        "back",
        2,
    )(rel, tokens_in, cotangent, rhalo, gain, ggate, wfull, cin, xb, spb, xb, dy, dxs, dir1, later, state_in, loc,
      vraw, cum, wred, dbc, conv_weight, dl, skip, nt, nth, p_gate, p_out, gskip, gggain)

    g_zx = jnp.concatenate([r_gate, r_conv[:, :CONVW]], axis=1).astype(f32)
    g_delta = r_conv[:, CONVW : CONVW + HEADS].astype(f32)
    small = small.reshape(-1)
    at = 0
    pieces = []
    for size in sizes:
        pieces.append(small[at : at + size])
        at += size
    return (
        mixed_out, gtok, g_gain.reshape(-1)[:D], g_zx, g_delta, r_out.astype(f32), pieces[0].reshape(KCONV, CONVW), pieces[1],
        pieces[2][:HEADS], pieces[3][:HEADS], pieces[4].reshape(HEADS, HEADDIM).sum(1), pieces[5],
    )


def solution(mesh):
    rows = P("group", "ctx", None)
    own = P("group", None)
    in_specs = (rows, P("group"), P(), own, own, own, P(), P(), P(), P(), P(), P(), rows)
    out_specs = (rows, rows, P(), own, own, own, P(), P(), P(), P(), P(), P())
    return jax.shard_map(local, mesh=mesh, in_specs=in_specs, out_specs=out_specs, check_vma=False)
```

```python
import jax
import jax.numpy as jnp
from jax import lax
from jax.experimental import pallas as pl
from jax.experimental.pallas import tpu as pltpu
from jax.sharding import PartitionSpec as P

D = 768
HEADS = 24
HEADDIM = 64
NSTATE = 128
KCONV = 4
SPAN = 256
DIN = 1536
CONVW = 1792
ZXW = 3328
RIM = 16
HALF = 128
TILE = 256
PAIRS = 12
EPS = 1e-05

f32 = jnp.float32
bf16 = jnp.bfloat16
NT = (((1,), (1,)), ((), ()))
TN = (((0,), (0,)), ((), ()))
VMEM_LIMIT = 63 * 1024 * 1024
GATE_CHUNK = 512
OUT_CHUNK = 256
CONV_CHUNK = 512
BACK_LAGS = (5, 7, 9)
STAGE_LAG = 4
MIDDLE_LAG = 2
SCAN_LAG = 4
HOPS = ("group", "ctx")
SMALL_ROWS = 88
CLOSE_LAG = 6
GZW = 2048


def mm(a, b):
    return jnp.dot(a, b, preferred_element_type=f32)


def mm_nt(a, b):
    return lax.dot_general(a, b, NT, preferred_element_type=f32)


def mm_tn(a, b):
    return lax.dot_general(a, b, TN, preferred_element_type=f32)


def halves(v):
    high = v.astype(bf16)
    return high, (v - high.astype(f32)).astype(bf16)


def head_map():
    rows = lax.broadcasted_iota(jnp.int32, (2 * HALF, DIN), 0) % HALF
    cols = lax.broadcasted_iota(jnp.int32, (2 * HALF, DIN), 1) // HEADDIM
    return jnp.where(rows == cols, 1.0, 0.0).astype(bf16)


def spread(v, sel):
    return mm(jnp.concatenate(halves(v), axis=1), sel[...])


def gather_heads(v, sel_part):
    high, low = halves(v)
    return mm_nt(high, sel_part) + mm_nt(low, sel_part)


def triangle(size, lower):
    rows = lax.broadcasted_iota(jnp.int32, (size, size), 0)
    cols = lax.broadcasted_iota(jnp.int32, (size, size), 1)
    keep = rows >= cols if lower else rows <= cols
    return jnp.where(keep, 1.0, 0.0).astype(f32)


def exact_mm(a, b):
    return jnp.dot(a, b, precision=lax.Precision.HIGHEST, preferred_element_type=f32)


def softplus(v):
    return jnp.maximum(v, 0.0) + jnp.log1p(jnp.exp(-jnp.abs(v)))


def sigmoid(v):
    return 1.0 / (1.0 + jnp.exp(-v))


def gate_of(v):
    return 0.5 * jnp.tanh(0.5 * v) + 0.5


def local_decays(cum):
    mid, end = cum[HALF - 1 : HALF], cum[SPAN - 1 : SPAN]
    rows = lax.broadcasted_iota(jnp.int32, (SPAN, 1), 0)
    first = rows < HALF
    start = jnp.where(first, 0.0, mid)
    stop = jnp.where(first, mid, end)
    return jnp.exp(cum - start), jnp.exp(stop - cum), jnp.exp(mid), jnp.exp(end - mid), jnp.exp(end)


def rows_of(v):
    return jnp.broadcast_to(v, (8, v.shape[1]))


def lane_row(ref):
    lanes = lax.broadcasted_iota(jnp.int32, (1, HALF), 1)
    row = jnp.zeros((1, HALF), f32)
    for h in range(HEADS):
        row = jnp.where(lanes == h, ref[h], row)
    return row


def row_of(ref):
    return ref[...].reshape(1, ref.shape[0])


def live_rows(lengths, s):
    start = lax.axis_index("ctx") * SPAN
    return (lax.broadcasted_iota(jnp.int32, (SPAN, 1), 0) + start < lengths[s]).astype(f32)


def normalized(rows, gain):
    rows = rows.astype(f32)
    inv = lax.rsqrt(jnp.mean(rows * rows, axis=-1, keepdims=True) + EPS)
    return rows, inv, (rows * inv * gain).astype(bf16)


def remote(src, dst, send_sem, recv_sem, **where):
    return pltpu.make_async_remote_copy(
        src_ref=src, dst_ref=dst, send_sem=send_sem, recv_sem=recv_sem,
        device_id=where, device_id_type=pl.DeviceIdType.MESH,
    )


def loop(start, stop, body):
    def step(i, c):
        body(i)
        return c

    lax.fori_loop(start, stop, step, 0)


def meet(axes):
    barrier = pltpu.get_barrier_semaphore()
    total = 0
    for axis in axes:
        size = lax.axis_size(axis)
        me = lax.axis_index(axis)

        def greet(d):
            pl.semaphore_signal(
                barrier, inc=1, device_id={axis: lax.rem(me + d, size)}, device_id_type=pl.DeviceIdType.MESH
            )

        loop(1, size, greet)
        total += size - 1
    pl.semaphore_wait(barrier, total)


class Exchange:
    def __init__(self, reverse, out_at, bufs, sems):
        self.reverse, self.out_at, self.sems = reverse, out_at, sems
        self.buf, self.y_buf, self.z_src, self.z_buf, self.z_back, self.p_buf, self.mine_buf, self.their_buf, self.decx = bufs
        self.depth = self.buf.shape[1]
        ctx = lax.axis_index("ctx")
        self.ctx = ctx
        self.outer = lax.axis_size("ctx") // 2
        self.owners = min(self.outer, 4)
        self.stride = self.outer // self.owners
        self.inner = lax.rem(ctx, 2)
        self.line = ctx // 2
        self.mine = self.line // self.stride
        self.half = NSTATE // 2
        self.rows = self.half // self.owners

    def half_rows(self, inner):
        return pl.ds(pl.multiple_of(inner * self.half, self.half), self.half)

    def part(self, j):
        return pl.ds(pl.multiple_of(j * self.rows, self.rows), self.rows)

    def other_owners(self, body):
        if self.stride == 1:
            loop(1, self.owners, lambda d: body(lax.rem(self.mine + d, self.owners)))
        else:
            loop(0, self.owners, lambda j: pl.when(j * self.stride != self.line)(lambda: body(j)))

    def other_lines(self, body):
        loop(1, self.outer, lambda d: body(lax.rem(self.line + d, self.outer)))

    def if_owner(self, body):
        if self.stride == 1:
            body()
        else:
            pl.when(self.mine * self.stride == self.line)(body)

    def y_copy(self, u):
        return remote(
            self.buf.at[u, :, self.half_rows(1 - self.inner)], self.y_buf.at[u], self.sems.at[0, u, 0], self.sems.at[1, u, 0],
            ctx=self.ctx + 1 - 2 * self.inner,
        )

    def z_copy(self, u, j, sender):
        return remote(
            self.z_src.at[u, :, self.part(j)], self.z_buf.at[u, sender], self.sems.at[2, u, j], self.sems.at[3, u, sender],
            ctx=j * self.stride * 2 + self.inner,
        )

    def b_copy(self, u, line, j):
        return remote(
            self.z_back.at[u, line], self.p_buf.at[u, :, self.part(j)], self.sems.at[4, u, line], self.sems.at[5, u, j],
            ctx=line * 2 + self.inner,
        )

    def f_copy(self, u, inner):
        return remote(
            self.their_buf.at[u], self.out_at(u, self.half_rows(inner)), self.sems.at[6, u, 0], self.sems.at[7, u, 0],
            ctx=self.ctx + 1 - 2 * self.inner,
        )

    def keep(self, u):
        return pltpu.make_async_copy(self.mine_buf.at[u], self.out_at(u, self.half_rows(self.inner)), self.sems.at[8, u, 0])

    def decay(self, a, block):
        return self.decx[a, pl.ds(pl.multiple_of(block * 8, 8), 8), :][0:1]

    def pair(self, u, a):
        own = self.buf[u, a, self.half_rows(self.inner), :].astype(f32)
        other = self.y_buf[u, a].astype(f32)
        first = self.inner == 0
        return jnp.where(first, own, other), jnp.where(first, other, own)

    def start(self, u):
        self.y_copy(u).start()

    def middle(self, u):
        self.y_copy(u).wait_recv()
        for a in range(self.depth):
            s0, s1 = self.pair(u, a)
            if self.reverse:
                total = s0 + self.decay(a, 2 * self.line) * s1
            else:
                total = self.decay(a, 2 * self.line + 1) * s0 + s1
            self.z_src[u, a] = total.astype(bf16)
        self.other_owners(lambda j: self.z_copy(u, j, self.line).start())

    def scan(self, u):
        def run():
            self.other_lines(lambda line: self.z_copy(u, self.mine, line).wait_recv())
            self.z_buf[u, self.line] = self.z_src[u, :, self.part(self.mine), :]
            for a in range(self.depth):

                def step(k, carry):
                    line = self.outer - 1 - k if self.reverse else k
                    self.z_back[u, line, a] = carry.astype(bf16)
                    both_decays = self.decay(a, 2 * line) * self.decay(a, 2 * line + 1)
                    return both_decays * carry + self.z_buf[u, line, a].astype(f32)

                lax.fori_loop(0, self.outer, step, jnp.zeros(self.z_buf.shape[3:], f32))
            self.other_lines(lambda line: self.b_copy(u, line, self.mine).start())
            self.p_buf[u, :, self.part(self.mine), :] = self.z_back[u, self.line]

        self.if_owner(run)

    def close(self, u):
        self.other_owners(lambda j: self.b_copy(u, self.line, j).wait_recv())
        for a in range(self.depth):
            s0, s1 = self.pair(u, a)
            near = self.p_buf[u, a].astype(f32)
            if self.reverse:
                far = s1 + self.decay(a, 2 * self.line + 1) * near
            else:
                far = s0 + self.decay(a, 2 * self.line) * near
            keeps_near = self.inner == (1 if self.reverse else 0)
            self.mine_buf[u, a] = jnp.where(keeps_near, near, far).astype(bf16)
            self.their_buf[u, a] = jnp.where(keeps_near, far, near).astype(bf16)
        self.f_copy(u, self.inner).start()
        self.keep(u).start()

    def finish(self, u):
        self.f_copy(u, 1 - self.inner).wait_recv()
        self.keep(u).wait()
        self.y_copy(u).wait_send()
        self.other_owners(lambda j: self.z_copy(u, j, self.line).wait_send())
        self.if_owner(lambda: self.other_lines(lambda line: self.b_copy(u, line, self.mine).wait_send()))
        self.f_copy(u, self.inner).wait_send()

    @staticmethod
    def scratch(units, depth, lanes, count):
        outer = count // 2
        half = NSTATE // 2
        rows = half // min(outer, 4)
        bufs = [(units, depth, NSTATE, lanes), (units, depth, half, lanes), (units, depth, half, lanes),
                (units, outer, depth, rows, lanes), (units, outer, depth, rows, lanes), (units, depth, half, lanes),
                (units, depth, half, lanes), (units, depth, half, lanes)]
        return (
            [(b, bf16) for b in bufs]
            + [((depth, count * 8, lanes), f32)]
            + [pltpu.SemaphoreType.DMA((9, units, max(outer, 4)))]
        )


class Spread:
    def __init__(self, shard, full, sems):
        self.shard, self.full = shard, full
        self.x_send, self.x_recv, self.m_send, self.m_recv, self.own = sems
        size = lax.axis_size("group")
        self.cores = 2 if size % 2 == 0 else 1
        self.chips = size // self.cores
        self.me = lax.axis_index("group")
        self.core = lax.rem(self.me, self.cores)
        self.chip = self.me // self.cores
        self.rows = shard.shape[0]

    def place(self, member, cols):
        return self.full.at[pl.ds(pl.multiple_of(member * self.rows, 32), self.rows), cols]

    def across(self, p, cols, d):
        peer = lax.rem(self.chip + d, self.chips) * self.cores + self.core
        return remote(
            self.shard.at[:, cols], self.place(self.me, cols), self.x_send.at[p, d], self.x_recv.at[p, d], group=peer
        )

    def mate(self, p, cols, d):
        member = lax.rem(self.chip + self.chips - d, self.chips) * self.cores + self.core
        src = self.shard.at[:, cols] if d == 0 else self.place(member, cols)
        return remote(
            src, self.place(member, cols), self.m_send.at[p, d], self.m_recv.at[p, d],
            group=self.me + 1 - 2 * self.core,
        )

    def keep(self, p):
        return pltpu.make_async_copy(self.shard, self.place(self.me, slice(None)), self.own.at[p])

    def start_chip(self, p):
        if self.cores == 2:
            self.mate(p, slice(None), 0).start()
        self.keep(p).start()

    def finish_chip(self, p):
        if self.cores == 2:
            self.mate(p, slice(None), 0).wait_recv()
        self.keep(p).wait()

    def start(self, p, cols):
        for d in range(1, self.chips):
            self.across(p, cols, d).start()

    def forward(self, p, cols):
        for d in range(1, self.chips):
            self.across(p, cols, d).wait_recv()
            if self.cores == 2:
                self.mate(p, cols, d).start()

    def finish(self, p, cols):
        if self.cores == 2:
            for d in range(1, self.chips):
                self.mate(p, cols, d).wait_recv()

    def drain(self, p, cols):
        for d in range(1, self.chips):
            self.across(p, cols, d).wait_send()
            if self.cores == 2:
                self.mate(p, cols, d).wait_send()

    def drain_chip(self, p):
        if self.cores == 2:
            self.mate(p, slice(None), 0).wait_send()


def owner_count(rows, width, by_rows, outer):
    fits = lambda n: (rows // 2) % (16 * n) == 0 if by_rows else width % (128 * n) == 0
    return max(n for n in (1, 2, 4) if outer % n == 0 and fits(n))


class Reducer:
    def __init__(self, part, out, rows, width, by_rows, group_bufs, ctx_bufs):
        self.part, self.out, self.rows, self.width, self.by_rows = part, out, rows, width, by_rows
        if group_bufs is not None:
            self.m_buf, self.x_buf, self.g_sems = group_bufs
        self.ships = ctx_bufs is not None
        if self.ships:
            self.y_src, self.y_buf, self.z_src, self.z_buf, self.full, self.c_sems = ctx_bufs
        else:
            self.y_src = out
        self.chunks = self.y_src.shape[0]
        self.base = 0
        self.group = lax.axis_index("group")
        self.cores = 2
        self.chips = lax.axis_size("group") // 2
        self.core = lax.rem(self.group, 2)
        self.chip = self.group // 2
        self.ctx = lax.axis_index("ctx")
        self.outer = lax.axis_size("ctx") // 2
        self.owners = owner_count(rows, width, by_rows, self.outer)
        self.stride = self.outer // self.owners
        self.inner = lax.rem(self.ctx, 2)
        self.line = self.ctx // 2
        self.mine = self.line // self.stride
        self.half = rows // 2

    def cols(self, k):
        return pl.ds(pl.multiple_of(k * self.width, self.width), self.width)

    def member(self, chip, core):
        return pl.ds(pl.multiple_of((chip * 2 + core) * self.rows, 64), self.rows)

    def half_rows(self, inner):
        return pl.ds(pl.multiple_of(inner * self.half, 16), self.half)

    def piece(self, j, base):
        if self.by_rows:
            n = self.half // self.owners
            return pl.ds(pl.multiple_of(base + j * n, 16), n), pl.ds(0, self.width)
        n = self.width // self.owners
        return pl.ds(pl.multiple_of(base, 16), self.half), pl.ds(pl.multiple_of(j * n, 128), n)

    def m_copy(self, k, chip):
        return remote(
            self.part.at[self.member(chip, 1 - self.core), self.cols(k)], self.m_buf.at[k, chip],
            self.g_sems.at[0, k, chip], self.g_sems.at[1, k, chip], group=self.group + 1 - 2 * self.core,
        )

    def x_copy(self, k, chip, sender):
        return remote(
            self.m_buf.at[k, chip], self.x_buf.at[k, sender], self.g_sems.at[2, k, chip], self.g_sems.at[3, k, sender],
            group=chip * 2 + self.core,
        )

    def y_copy(self, k):
        return remote(
            self.y_src.at[k, self.half_rows(1 - self.inner)], self.y_buf.at[k], self.c_sems.at[0, k, 0], self.c_sems.at[1, k, 0],
            ctx=self.ctx + 1 - 2 * self.inner,
        )

    def z_copy(self, k, j, sender):
        rows, cols = self.piece(j, 0)
        return remote(
            self.z_src.at[k, rows, cols], self.z_buf.at[k, sender], self.c_sems.at[2, k, j], self.c_sems.at[3, k, sender],
            ctx=j * self.stride * 2 + self.inner,
        )

    def b_copy(self, k, line, j):
        rows, cols = self.piece(j, self.inner * self.half)
        return remote(
            self.full.at[k, rows, cols], self.full.at[k, rows, cols], self.c_sems.at[4, k, line], self.c_sems.at[5, k, j],
            ctx=line * 2 + self.inner,
        )

    def f_copy(self, k, inner):
        rows = self.half_rows(inner)
        return remote(
            self.full.at[k, rows], self.full.at[k, rows], self.c_sems.at[6, k, 0], self.c_sems.at[7, k, 0],
            ctx=self.ctx + 1 - 2 * self.inner,
        )

    def other_chips(self, body):
        for d in range(1, self.chips):
            body(lax.rem(self.chip + d, self.chips))

    def other_owners(self, body):
        if self.stride == 1:
            for d in range(1, self.owners):
                body(lax.rem(self.mine + d, self.owners))
        else:
            for j in range(self.owners):
                pl.when(j * self.stride != self.line)(lambda j=j: body(j))

    def other_lines(self, body):
        loop(1, self.outer, lambda d: body(lax.rem(self.line + d, self.outer)))

    def if_owner(self, body):
        if self.stride == 1:
            body()
        else:
            pl.when(self.mine * self.stride == self.line)(body)

    def m_start(self, k):
        for chip in range(self.chips):
            self.m_copy(k, chip).start()

    def m_done(self, k):
        for chip in range(self.chips):
            self.m_copy(k, chip).wait_recv()
            own = self.part[self.member(chip, self.core), self.cols(k)].astype(f32)
            self.m_buf[k, chip] = (own + self.m_buf[k, chip].astype(f32)).astype(bf16)
        self.other_chips(lambda chip: self.x_copy(k, chip, self.chip).start())

    def x_done(self, k):
        total = self.m_buf[k, self.chip].astype(f32)
        for d in range(1, self.chips):
            chip = lax.rem(self.chip + d, self.chips)
            self.x_copy(k, chip, chip).wait_recv()
            total = total + self.x_buf[k, chip].astype(f32)
        self.y_src[k] = total.astype(bf16)
        if self.ships:
            self.y_start(k)

    def y_start(self, k):
        self.y_copy(k).start()

    def y_done(self, k):
        self.y_copy(k).wait_recv()
        own = self.y_src[k, self.half_rows(self.inner), :].astype(f32)
        self.z_src[k] = (own + self.y_buf[k].astype(f32)).astype(bf16)
        self.other_owners(lambda j: self.z_copy(k, j, self.line).start())

    def z_done(self, k):
        def run():
            rows, cols = self.piece(self.mine, 0)
            self.other_lines(lambda line: self.z_copy(k, self.mine, line).wait_recv())
            self.z_buf[k, self.line] = self.z_src[k, rows, cols]
            total = self.z_buf[k, 0].astype(f32)
            for line in range(1, self.outer):
                total = total + self.z_buf[k, line].astype(f32)
            rows, cols = self.piece(self.mine, self.inner * self.half)
            self.full[k, rows, cols] = total.astype(bf16)
            self.other_lines(lambda line: self.b_copy(k, line, self.mine).start())

        self.if_owner(run)

    def b_done(self, k):
        self.other_owners(lambda j: self.b_copy(k, self.line, j).wait_recv())
        self.f_copy(k, self.inner).start()

    def f_done(self, k):
        self.f_copy(k, 1 - self.inner).wait_recv()
        self.out[:, pl.ds(pl.multiple_of(self.base + k * self.width, 128), self.width)] = self.full[k]

    def drain_group(self, k):
        for chip in range(self.chips):
            self.m_copy(k, chip).wait_send()
        self.other_chips(lambda chip: self.x_copy(k, chip, self.chip).wait_send())

    def drain_ctx(self, k):
        self.y_copy(k).wait_send()
        self.other_owners(lambda j: self.z_copy(k, j, self.line).wait_send())
        self.if_owner(lambda: self.other_lines(lambda line: self.b_copy(k, line, self.mine).wait_send()))
        self.f_copy(k, self.inner).wait_send()

    def wave(self, t, acts, chunk_at):
        for order, act in reversed(list(enumerate(acts))):
            k, is_due = chunk_at(t - order * STAGE_LAG)
            pl.when(is_due)(lambda k=k, act=act: act(k))

    def each(self, t):
        return t, jnp.logical_and(t >= 0, t < self.chunks)

    @staticmethod
    def group_scratch(chunks, rows, width, group):
        chips = group // 2
        buf = ((chunks, chips, rows, width), bf16)
        return [buf, buf, pltpu.SemaphoreType.DMA((4, chunks, max(chips, 2)))]

    @staticmethod
    def ctx_scratch(chunks, rows, width, by_rows, count):
        outer = count // 2
        owners = owner_count(rows, width, by_rows, outer)
        half = rows // 2
        piece = (half // owners, width) if by_rows else (half, width // owners)
        bufs = [(chunks, half, width), (chunks, half, width), (chunks, outer) + piece, (chunks, rows, width)]
        return [(b, bf16) for b in bufs] + [pltpu.SemaphoreType.DMA((8, chunks, max(outer, 2)))]


class Small:
    def __init__(self, held, got, sends, recvs):
        self.held, self.got, self.sends, self.recvs = held, got, sends, recvs

    def copy(self, h, j, sender):
        return remote(
            self.held.at[h], self.got.at[h, sender], self.sends.at[h, j], self.recvs.at[h, sender], **{HOPS[h]: j}
        )

    def others(self, h, body):
        size, mine = lax.axis_size(HOPS[h]), lax.axis_index(HOPS[h])
        loop(1, size, lambda d: body(lax.rem(mine + d, size)))

    def start(self, h):
        mine = lax.axis_index(HOPS[h])
        self.others(h, lambda j: self.copy(h, j, mine).start())

    def done(self, h):
        self.others(h, lambda j: self.copy(h, j, j).wait_recv())
        self.got[h, lax.axis_index(HOPS[h])] = self.held[h]
        total = self.got[h, 0]
        for j in range(1, lax.axis_size(HOPS[h])):
            total = total + self.got[h, j]
        self.held[h + 1] = total

    def drain(self):
        for h in range(2):
            mine = lax.axis_index(HOPS[h])
            self.others(h, lambda j: self.copy(h, j, mine).wait_send())

    @staticmethod
    def scratch(height, group, count):
        widest = max(group, count)
        dma = pltpu.SemaphoreType.DMA
        return [((3, height, HALF), f32), ((2, widest, height, HALF), f32), dma((2, widest)), dma((2, widest))]


def masks():
    rows = lax.broadcasted_iota(jnp.int32, (HALF, HALF), 0)
    cols = lax.broadcasted_iota(jnp.int32, (HALF, HALF), 1)
    return rows >= cols, cols < HEADDIM


def both(q):
    return slice(q * HALF, (q + 1) * HALF)


def pair_decays(cum, cum_t, p, causal):
    rolled = pltpu.roll(cum, lax.rem(HALF - 2 * p, HALF), 1)
    out = []
    for q in range(2):
        for a in range(2):
            gaps = rolled[both(q), a : a + 1] - cum_t[q, pl.ds(2 * p + a, 1), :]
            out.append(jnp.exp(jnp.where(causal, gaps, -jnp.inf)))
    return out


TILES = DIN // TILE
PIECES = 2 * TILES + 1
DT0 = DIN + CONVW - 2 * NSTATE


def front_kernel(
    tok, tok_any, wzx, wdl, wout, gain, cw, cb_in, db, dl,
    nt, nth, rhalo, cin, xb, spb, vout, cumout, st0, loc, ylocal, gate, decs_out, wfull, wdfull, wofull, sin,
    sel, halo, nh_s, ext, w, wd, cb, cin_s, xs_s, bt, scores, out_cat, dt_cat, cum_t, tot1x, decs,
    halo_sem, x_send, x_recv, m_send, m_recv, w_own, w_store, dec_send, dec_recv, *exchange,
):
    i = pl.program_id(0)
    seqs = tok.shape[0]
    count = lax.axis_size("ctx")
    me = lax.axis_index("ctx")
    sems = (x_send, x_recv, m_send, m_recv, w_own)
    zx, wo, de = Spread(wzx, w, sems), Spread(wout, wofull, sems), Spread(wdl, wd, sems)
    last, small_piece = PIECES, PIECES + 1

    def unit_cols(u):
        return pl.ds(pl.multiple_of(u * TILE, TILE), TILE)

    def piece(p):
        at = jnp.where(p <= TILES, DIN + (p - 1) * TILE, (p - 1 - TILES) * TILE)
        return pl.ds(pl.multiple_of(at, TILE), TILE)

    first_piece = pl.ds(DT0, 2 * NSTATE)
    ex = Exchange(False, lambda u, rows: sin.at[:, rows, unit_cols(u)], exchange[:9], exchange[9])
    halo_copy = remote(
        tok_any.at[:, pl.ds(SPAN - RIM, RIM), :], halo, halo_sem.at[0], halo_sem.at[1], ctx=lax.rem(me + 1, count)
    )
    keep_w = pltpu.make_async_copy(w, wfull, w_store.at[0])
    keep_d = pltpu.make_async_copy(wd, wdfull, w_store.at[1])

    def dec_copy(block, sender):
        rows = pl.ds(pl.multiple_of(sender * 8, 8), 8)
        return remote(decs.at[:, rows, :], decs.at[:, rows, :], dec_send.at[block], dec_recv.at[sender], ctx=block)

    def other_blocks(body):
        loop(1, count, lambda d: body(lax.rem(me + d, count)))

    def conv_tile(s, cols_w, cols_c):
        cin_s[s] = mm(ext[s], w[:, cols_w])
        cin[s] = cin_s[s].astype(bf16)
        o = cb[:, cols_c]
        for k in range(KCONV):
            o = o + cw[k : k + 1, cols_c] * cin_s[s, RIM - KCONV + 1 + k : RIM - KCONV + 1 + k + SPAN, :]
        sg = gate_of(o)
        a = o * sg
        xb[s] = a.astype(bf16)
        spb[s] = (sg + a * (1.0 - sg)).astype(bf16)
        return a

    def unit_decays(u):
        for s in range(seqs):
            ex.decx[s] = spread(decs[s], sel.at[:, unit_cols(u)])

    @pl.when(i == 0)
    def _():
        meet(("ctx", "group"))
        pl.when(me < count - 1)(lambda: halo_copy.start())
        de.start(small_piece, slice(None))
        zx.start(0, first_piece)
        de.start_chip(2)
        zx.start_chip(0)
        cb[...] = row_of(cb_in)
        zx.start(1, piece(1))
        zx.start(2, piece(2))
        wo.start_chip(1)
        sel[...] = head_map()

        @pl.when(me == 0)
        def _():
            halo[...] = jnp.zeros_like(halo)

        def norm_main(s):
            nm = normalized(tok[s], row_of(gain))[2]
            ext[s, RIM:] = nm
            nt[:, pl.ds(pl.multiple_of(s * SPAN, SPAN), SPAN)] = jnp.transpose(nm.astype(f32)).astype(bf16)

        loop(0, seqs, norm_main)

        @pl.when(me > 0)
        def _():
            halo_copy.wait_recv()

        def norm_halo(s):
            nh = normalized(halo[s], row_of(gain))[2]
            ext[s, 0:RIM] = nh
            nh_s[pl.ds(pl.multiple_of(s * RIM, RIM), RIM), :] = nh.astype(f32)
            rhalo[s] = halo[s]

        loop(0, seqs, norm_halo)
        nth[...] = jnp.transpose(nh_s[...]).astype(bf16)
        de.forward(small_piece, slice(None))
        zx.forward(0, first_piece)
        zx.finish_chip(0)
        de.finish_chip(2)

    @pl.when(i + 1 < PIECES)
    def _():
        zx.forward(i + 1, piece(i + 1))

    @pl.when(i + 3 < PIECES)
    def _():
        zx.start(i + 3, piece(i + 3))

    @pl.when(i + 3 == PIECES)
    def _():
        wo.start(last, slice(None))

    @pl.when(i == 0)
    def _():
        zx.finish(0, first_piece)
        de.finish(small_piece, slice(None))
        shift, rate = lane_row(db), jnp.exp(lane_row(dl))

        def delta(s):
            a = conv_tile(s, slice(DT0, DT0 + TILE), slice(DIN, DIN + TILE))
            bb, cc = a[:, :NSTATE].astype(bf16), a[:, NSTATE:].astype(bf16)
            bt[s] = jnp.transpose(a[:, :NSTATE]).astype(bf16)
            for q in range(2):
                scores[s, q] = mm_nt(cc[both(q)], bb[both(q)])
            v = mm(ext[s, RIM:], wd[...]) + shift
            vout[s] = v
            dt = softplus(v)
            cum = exact_mm(triangle(SPAN, True), -rate * dt)
            cumout[s] = cum
            for q in range(2):
                cum_t[s, q] = jnp.transpose(cum[both(q)])
            e_in, e_out, tot0, tot1, total = local_decays(cum)
            decs[s, pl.ds(pl.multiple_of(me * 8, 8), 8), :] = rows_of(total)
            out_cat[s] = jnp.concatenate(halves(dt * e_out), axis=1)
            dt_cat[s] = jnp.concatenate(halves(dt), axis=1)
            tot1x[s] = spread(rows_of(tot1), sel)

        loop(0, seqs, delta)
        other_blocks(lambda b: dec_copy(b, me).start())

    @pl.when(jnp.logical_and(i >= 1, i < PIECES))
    def _():
        zx.finish(i, piece(i))

    def act_at(t, lag, act):
        u = t - 1 - lag
        pl.when(jnp.logical_and(u >= 0, u < TILES))(lambda: act(u))

    def close(u):
        unit_decays(u)
        ex.close(u)

    def scan(u):
        unit_decays(u)
        ex.scan(u)

    def middle(u):
        unit_decays(u)
        ex.middle(u)

    @pl.when(i == 3)
    def _():
        other_blocks(lambda b: dec_copy(b, b).wait_recv())

    def wave(t):
        act_at(t, CLOSE_LAG, close)
        act_at(t, SCAN_LAG, scan)
        act_at(t, MIDDLE_LAG, middle)

    wave(i)

    @pl.when(jnp.logical_and(i >= 1, i <= TILES))
    def _():
        u = i - 1
        cols = unit_cols(u)

        def x_tile(s):
            a = conv_tile(s, piece(i), cols)
            xs_s[s, :, cols] = a.astype(bf16)
            xw = (a * mm(out_cat[s], sel[:, cols])).astype(bf16)
            s0 = mm(bt[s, :, :HALF], xw[:HALF])
            s1 = mm(bt[s, :, HALF:], xw[HALF:])
            st0[s] = s0.astype(bf16)
            low = (tot1x[s, :, cols][0:1] * s0 + s1).astype(bf16)
            loc[s] = low
            ex.buf[u, s] = low

        loop(0, seqs, x_tile)
        ex.start(u)

    @pl.when(i > TILES)
    def _():
        u = i - 1 - TILES
        causal, low_lanes = masks()

        def intra(s):
            cum = cumout[s]
            dtx = mm(dt_cat[s], sel[:, unit_cols(u)])
            for h in range(2):
                p = 2 * u + h
                lanes = slice(h * HALF, (h + 1) * HALF)
                decays = pair_decays(cum, cum_t.at[s], p, causal)
                for q in range(2):
                    rows = both(q)
                    m = jnp.concatenate([(decays[2 * q + a] * scores[s, q]).astype(bf16) for a in range(2)], axis=1)
                    x = xs_s[s, rows, pl.ds(pl.multiple_of(p * HALF, HALF), HALF)].astype(f32) * dtx[rows, lanes]
                    x = jnp.concatenate([jnp.where(low_lanes, x, 0.0), jnp.where(low_lanes, 0.0, x)], axis=0)
                    ylocal[s, rows, lanes] = mm(m, x.astype(bf16)).astype(bf16)
            gate[s] = mm(ext[s, RIM:], w[:, piece(i)]).astype(bf16)

        loop(0, seqs, intra)

    @pl.when(i == PIECES - 1)
    def _():
        keep_w.start()
        keep_d.start()
        decs_out[...] = decs[...]
        wo.forward(last, slice(None))
        loop(PIECES, TILES + CLOSE_LAG + 1, wave)
        loop(0, TILES, ex.finish)
        wo.finish(last, slice(None))
        wo.finish_chip(1)
        zx.drain_chip(0)
        wo.drain_chip(1)
        de.drain_chip(2)
        de.drain(small_piece, slice(None))
        zx.drain(0, first_piece)
        loop(1, PIECES, lambda p: zx.drain(p, piece(p)))
        wo.drain(last, slice(None))
        other_blocks(lambda b: dec_copy(b, me).wait_send())
        pl.when(me < count - 1)(lambda: halo_copy.wait_send())
        keep_w.wait()
        keep_d.wait()


def middle_kernel(
    lengths, skip_in, tok, cot, ylocal, gate, xb, vin, cumin, st0, sin, decs, wout, ggain_in, nt,
    mixed, dyout, ggate, wred, dir1, gskip, gggain, dxs, dbc, xgate, xout, later,
    sel, skip, ggain, cum_t, einx, ys, gs, ss, s_in, dcs, dy_s, ml_s, gg_s, dr_s, pgate, pout, g_s, dg_s, *exchange,
):
    i = pl.program_id(0)
    seqs = dy_s.shape[0]
    ex = Exchange(True, lambda u, rows: later.at[pl.ds(u, 1), rows, :], exchange[:9], exchange[9])
    members = lax.axis_size("group")
    gates = Reducer(pgate, xgate, D // members, GATE_CHUNK, False, exchange[10:13], None)
    outs = Reducer(pout, xout, DIN // members, OUT_CHUNK, True, exchange[13:16], None)

    def span(s):
        return pl.ds(pl.multiple_of(s * SPAN, SPAN), SPAN)

    def group_wave(t):
        gates.wave(t - 2 * seqs - 3, [gates.x_done], gates.each)
        outs.wave(t - 2 * seqs - 3 - gates.chunks, [outs.x_done], outs.each)

    def wave(t):
        group_wave(t)

        def act_at(lag, act):
            u = lax.div(t - lag, 2)

            def run():
                ex.decx[0] = spread(decs[u], sel)
                act(u)

            pl.when(jnp.logical_and(t >= lag, jnp.logical_and(2 * u + lag == t, u < seqs)))(run)

        act_at(BACK_LAGS[2], ex.close)
        act_at(BACK_LAGS[1], ex.scan)
        act_at(BACK_LAGS[0], ex.middle)

    @pl.when(i == 0)
    def _():
        meet(("ctx", "group"))
        sel[...] = head_map()
        skip[...] = spread(rows_of(lane_row(skip_in)), sel)[0:1]
        ggain[...] = row_of(ggain_in)
        gskip[...] = jnp.zeros_like(gskip)
        gggain[...] = jnp.zeros_like(gggain)

    wave(2 * i)

    @pl.when(i < seqs)
    def _():
        s = i
        cum = cumin[0]
        e_in, e_out, tot0, tot1, total = local_decays(cum)
        einx[...] = spread(e_in, sel)
        tot0x = spread(rows_of(tot0), sel)[0:1]
        s_in[0] = sin[0]
        s_in[1] = (tot0x * sin[0].astype(f32) + st0[0].astype(f32)).astype(bf16)
        cc = xb[0, :, DIN + NSTATE :]

        def gate_step(j, total_sq):
            cols = pl.ds(pl.multiple_of(j * TILE, TILE), TILE)
            for q in range(2):
                rows = both(q)
                ys[rows, cols] = ylocal[0, rows, cols].astype(f32) + einx[rows, cols] * mm(cc[rows], s_in[q, :, cols])
            y = ys[:, cols] + skip[:, cols] * xb[0, :, cols].astype(f32)
            g = gate[0, :, cols].astype(f32)
            gated = y * (g * gate_of(g))
            gs[:, cols] = gated
            sq = gated * gated
            return total_sq + sq[:, :HALF] + sq[:, HALF:]

        wave(2 * i + 1)
        sq = lax.fori_loop(0, DIN // TILE, gate_step, jnp.zeros((SPAN, HALF), f32))
        inv = lax.rsqrt(jnp.sum(sq, axis=1, keepdims=True) * (1.0 / DIN) + EPS)
        live = live_rows(lengths, s)
        drive = (live * cot[0].astype(f32)).astype(bf16)
        dr_s[span(s), :] = drive

        def back_step(j, acc):
            cols = pl.ds(pl.multiple_of(j * TILE, TILE), TILE)
            gm = mm_nt(drive, wout[cols, :])
            gated = gs[:, cols]
            unit = gated * inv
            ml_s[span(s), cols] = (unit * ggain[:, cols]).astype(bf16)
            gggain[:, cols] += jnp.sum(gm * unit, axis=0, keepdims=True)
            scaled = gm * ggain[:, cols]
            ss[:, cols] = scaled
            prod = scaled * gated
            return acc + prod[:, :HALF] + prod[:, HALF:]

        dots = lax.fori_loop(0, DIN // TILE, back_step, jnp.zeros((SPAN, HALF), f32))
        dots = jnp.sum(dots, axis=1, keepdims=True) * (1.0 / DIN)
        corr = inv * inv * inv * dots
        cct = jnp.transpose(cc.astype(f32)).astype(bf16)
        acc = jnp.zeros((SPAN, HALF), f32)
        dc = [jnp.zeros((HALF, HALF), f32) for _ in range(2)]
        for j in range(DIN // TILE):
            cols = slice(j * TILE, (j + 1) * TILE)
            g = gate[0, :, cols].astype(f32)
            sg = gate_of(g)
            sl = g * sg
            grad_gated = inv * ss[:, cols] - gs[:, cols] * corr
            dy = grad_gated * sl
            yn = ys[:, cols]
            x = xb[0, :, cols].astype(f32)
            y = yn + skip[:, cols] * x
            low = (grad_gated * y * (sg + sl * (1.0 - sg))).astype(bf16)
            ggate[0, :, cols] = low
            gg_s[span(s), cols] = low
            dyb = dy.astype(bf16)
            dyout[0, :, cols] = dyb
            dy_s[s, :, cols] = dyb
            gskip[:, cols] += jnp.sum(dy * x, axis=0, keepdims=True)
            acc = acc + gather_heads(dy * yn, sel[:HALF, cols])
            dye = (dy * einx[:, cols]).astype(bf16)
            d0 = mm(cct[:, :HALF], dye[:HALF])
            d1 = mm(cct[:, HALF:], dye[HALF:])
            dir1[0, :, cols] = d1.astype(bf16)
            ex.buf[s, 0, :, cols] = (d0 + tot0x[:, cols] * d1).astype(bf16)
            for q in range(2):
                dc[q] = dc[q] + mm_nt(dye[both(q)], s_in[q, :, cols])
        wred[0] = acc
        for q in range(2):
            dcs[s, both(q)] = dc[q]
        ex.start(s)

    @pl.when(i >= seqs)
    def _():
        s = i - seqs
        causal, low_lanes = masks()
        cum = cumin[0]
        for q in range(2):
            cum_t[q] = jnp.transpose(cum[both(q)])
        einx[...] = spread(softplus(vin[0]), sel)
        bb = xb[0, :, DIN : DIN + NSTATE]
        cc = xb[0, :, DIN + NSTATE :]
        for q in range(2):
            g_s[q] = mm_nt(cc[both(q)], bb[both(q)])
        dg_s[...] = jnp.zeros_like(dg_s)

        def pair_step(p):
            cols = pl.ds(pl.multiple_of(p * HALF, HALF), HALF)
            decays = pair_decays(cum, cum_t, p, causal)
            for q in range(2):
                rows = both(q)
                xsb = (xb[0, rows, cols].astype(f32) * einx[rows, cols]).astype(bf16)
                dyb = dy_s[s, rows, cols]
                dyf = dyb.astype(f32)
                grads = []
                for a in range(2):
                    m = (decays[2 * q + a] * g_s[q]).astype(bf16)
                    grads.append(mm_tn(m, dyb))
                    mine = low_lanes if a == 0 else jnp.logical_not(low_lanes)
                    dm = mm_nt(jnp.where(mine, dyf, 0.0).astype(bf16), xsb)
                    dg_s[q] += dm * decays[2 * q + a]
                dxs[0, rows, cols] = jnp.where(low_lanes, grads[0], grads[1]).astype(bf16)

        @pl.when(s == 0)
        def _():
            for k in range(gates.chunks):
                cols = slice(k * GATE_CHUNK, (k + 1) * GATE_CHUNK)
                pgate[:, cols] = mm(nt[...], gg_s[:, cols]).astype(bf16)
                gates.m_start(k)

        @pl.when(s == 1)
        def _():
            loop(0, outs.chunks, outs.m_done)

        loop(0, PAIRS // 2, pair_step)
        wave(2 * i + 1)

        @pl.when(s == 0)
        def _():
            loop(0, gates.chunks, gates.m_done)

            def out_rows(r):
                rows = pl.ds(pl.multiple_of(r * TILE, TILE), TILE)
                pout[rows, :] = mm_tn(ml_s[:, rows], dr_s[...]).astype(bf16)

            loop(0, DIN // TILE, out_rows)
            loop(0, outs.chunks, outs.m_start)

        loop(PAIRS // 2, PAIRS, pair_step)
        for q in range(2):
            rows = both(q)
            dg = dg_s[q].astype(bf16)
            dbc[0, rows, :NSTATE] = mm_tn(dg, cc[rows])
            dbc[0, rows, NSTATE:] = mm(dg, bb[rows]) + dcs[s, rows]
        live = live_rows(lengths, s)
        for j in range(D // TILE):
            cols = slice(j * TILE, (j + 1) * TILE)
            mixed[0, :, cols] = (live * (tok[0, :, cols].astype(f32) + mm(ml_s[span(s), :], wout[:, cols]))).astype(bf16)

    @pl.when(i == 2 * seqs - 1)
    def _():
        loop(4 * seqs, max(2 * seqs + BACK_LAGS[2] - 1, 2 * seqs + 3 + gates.chunks + outs.chunks), wave)
        loop(0, seqs, ex.finish)
        for r in (gates, outs):
            loop(0, r.chunks, r.drain_group)


def back_kernel(
    lengths, dl, skip_in, tok, cot, rhalo, gain, ggate, w_any, wd, cin, xb, spb, bc, dy, dxs, dir1, later, sin, loc,
    vin, cumin, wred, dbc, cw, nt, nth, xgate, xout, gskip, gggain,
    gtok, rzx, rout, small_out, ggain_out,
    sel, skip, wfull, w_sem, dt_cat, eo_cat, tots, db_s, qacc, ends, gp, gz_s, gzh_s, pconv, gcw, gcb, gdb, gdl, ggain,
    rim_out, rim_in, rim_send, rim_recv, *comm,
):
    i = pl.program_id(0)
    seqs = rhalo.shape[0]
    count = lax.axis_size("ctx")
    me = lax.axis_index("ctx")
    members = lax.axis_size("group")
    gates = Reducer(None, rzx, D // members, GATE_CHUNK, False, None, (xgate,) + comm[0:5])
    outs = Reducer(None, rout, DIN // members, OUT_CHUNK, True, None, (xout,) + comm[5:10])
    convs = Reducer(pconv, rzx, D // members, CONV_CHUNK, False, comm[10:13], comm[13:19])
    convs.base = DIN
    load_w = pltpu.make_async_copy(w_any, wfull, w_sem.at[0])
    little, least = Small(*comm[19:23]), Small(*comm[23:27])
    bc_step = TILES

    last_conv = 2 * bc_step + 5

    def conv_at(t):
        k = lax.div(t - 7, 4)
        even = jnp.logical_and(t >= 7, jnp.logical_and(lax.rem(t - 7, 4) == 0, k < convs.chunks - 1))
        last = t == last_conv
        return jnp.where(last, convs.chunks - 1, k), jnp.logical_or(even, last)

    def wave(t):
        for r, at in ((gates, 2), (outs, 2 + gates.chunks)):
            r.wave(t - at, [r.y_done, r.z_done, r.b_done, r.f_done], r.each)
        convs.wave(t, [convs.x_done, convs.y_done, convs.z_done, convs.b_done, convs.f_done], conv_at)

    def rim_copy(q):
        return remote(rim_out.at[q], rim_in.at[q], rim_send.at[q], rim_recv.at[q], ctx=lax.rem(me + count - 1, count))

    def span(s):
        return pl.ds(pl.multiple_of(s * SPAN, SPAN), SPAN)

    def edge(s):
        return pl.ds(pl.multiple_of(s * RIM, RIM), RIM)

    def back(rows, grad):
        rows, inv, _ = normalized(rows, row_of(gain))
        ggain[...] += jnp.sum(grad * rows * inv, axis=0, keepdims=True)
        gained = row_of(gain) * grad
        mean = jnp.mean(gained * rows, axis=-1, keepdims=True)
        return inv * gained - rows * (inv * inv * inv * mean)

    @pl.when(i == 0)
    def _():
        meet(("ctx", "group"))
        for r in (gates, outs):
            loop(0, r.chunks, r.y_start)
        load_w.start()
        sel[...] = head_map()
        skip[...] = spread(rows_of(lane_row(skip_in)), sel)[0:1]
        for acc in (db_s, qacc, ends, gcw, gcb, gdb, gdl, ggain):
            acc[...] = jnp.zeros_like(acc)
        gp[0:RIM] = jnp.zeros((RIM, TILE), f32)
        gp[RIM + SPAN :] = jnp.zeros((8, TILE), f32)
        pconv[:, CONVW + HALF :] = jnp.zeros((D, GZW - CONVW - HALF), bf16)

        def setup(s):
            dt = softplus(vin[s])
            _, e_out, _, tot1, total = local_decays(cumin[s])
            dt_cat[s] = jnp.concatenate(halves(dt), axis=1)
            eo_cat[s] = jnp.concatenate(halves(e_out), axis=1)
            both_rows = jnp.concatenate([rows_of(tot1), rows_of(total)], axis=0)
            tots[s] = spread(both_rows, sel)

        loop(0, seqs, setup)

    def conv_back(s, dact, cols):
        gco = dact * spb[s].astype(f32)
        gp[RIM : RIM + SPAN] = gco
        gcb[:, cols] += jnp.sum(gco, axis=0, keepdims=True)
        own = cin[s, RIM:].astype(f32)
        before = cin[s, :RIM].astype(f32)
        main = jnp.zeros((SPAN, TILE), f32)
        rim = jnp.zeros((RIM, TILE), f32)
        for k in range(KCONV):
            ahead = KCONV - 1 - k
            moved = gco if ahead == 0 else gp[RIM + ahead : RIM + ahead + SPAN]
            early = gp[ahead : ahead + RIM]
            main = main + cw[k : k + 1, cols] * moved
            rim = rim + cw[k : k + 1, cols] * early
            gcw[k : k + 1, cols] += jnp.sum(own * moved, axis=0, keepdims=True) + jnp.sum(
                before * early, axis=0, keepdims=True
            )
        gz_s[span(s), cols] = main.astype(bf16)
        gzh_s[edge(s), cols] = rim.astype(bf16)

    def partial(cols):
        pconv[:, cols] = (mm(nt[...], gz_s[:, cols]) + mm(nth[...], gzh_s[:, cols])).astype(bf16)

    wave(2 * i)

    @pl.when(i < bc_step)
    def _():
        cols = pl.ds(pl.multiple_of(i * TILE, TILE), TILE)

        def x_tile(s):
            dte = mm(dt_cat[s], sel[:, cols])
            eo = mm(eo_cat[s], sel[:, cols])
            near = later[s]
            near32 = near.astype(f32)
            tot = tots[s, :, cols]
            reach = [(dir1[s].astype(f32) + tot[0:1] * near32).astype(bf16), near]
            fed = jnp.concatenate(
                [mm(bc[s, both(q), :NSTATE], reach[q]) for q in range(2)], axis=0
            )
            x = xb[s].astype(f32)
            dx_s = dxs[s].astype(f32) + eo * fed
            qacc[s] += gather_heads(x * dx_s, sel[:HALF, cols])
            xw = (x * dte * eo).astype(bf16)
            for q in range(2):
                db_s[s, both(q)] += mm_nt(xw[both(q)], reach[q])
            held = near32 * (tot[8:9] * sin[s].astype(f32) + loc[s].astype(f32))
            ends[s] += gather_heads(rows_of(jnp.sum(held, axis=0, keepdims=True)), sel[:HALF, cols])
            conv_back(s, dte * dx_s + skip[:, cols] * dy[s].astype(f32), cols)

        loop(0, seqs // 2, x_tile)

        @pl.when(jnp.logical_and(lax.rem(i, 2) == 0, i >= 2))
        def _():
            convs.m_done(lax.div(i, 2) - 1)

        wave(2 * i + 1)
        loop(seqs // 2, seqs, x_tile)
        partial(cols)

        @pl.when(lax.rem(i, 2) == 1)
        def _():
            convs.m_start(lax.div(i, 2))

    @pl.when(i == bc_step)
    def _():
        cols = slice(DIN, CONVW)
        rate = jnp.exp(lane_row(dl))

        def bc_tile(s):
            conv_back(s, jnp.concatenate([dbc[s, :, :NSTATE] + db_s[s], dbc[s, :, NSTATE:]], axis=1), cols)
            v = vin[s]
            dt = softplus(v)
            q = qacc[s]
            at_end = lax.broadcasted_iota(jnp.int32, (SPAN, 1), 0) == SPAN - 1
            dcum = wred[s] - dt * q + jnp.where(at_end, ends[s][0:1], 0.0)
            glog = exact_mm(triangle(SPAN, False), dcum)
            gpd = (q - rate * glog) * sigmoid(v)
            lanes = lax.broadcasted_iota(jnp.int32, (SPAN, HALF), 1) < HEADS
            gpd = jnp.where(lanes, gpd, 0.0)
            gz_s[span(s), CONVW : CONVW + HALF] = gpd.astype(bf16)
            gdb[...] += jnp.sum(gpd, axis=0, keepdims=True)
            gdl[...] += -rate * jnp.sum(dt * glog, axis=0, keepdims=True)

        loop(0, seqs, bc_tile)
        convs.m_done(convs.chunks - 2)
        wave(2 * i + 1)
        partial(cols)
        pconv[:, CONVW : CONVW + HALF] = mm(nt[...], gz_s[:, CONVW : CONVW + HALF]).astype(bf16)
        convs.m_start(convs.chunks - 1)
        rows = [gcw[k : k + 1, j * HALF : (j + 1) * HALF] for k in range(KCONV) for j in range(CONVW // HALF)]
        rows += [gcb[:, j * HALF : (j + 1) * HALF] for j in range(CONVW // HALF)]
        rows += [gdb[...], gdl[...]]
        rows += [gather_heads(rows_of(gskip[...]), sel[:HALF])[0:1]]
        rows += [gggain[:, j * HALF : (j + 1) * HALF] for j in range(PAIRS)]
        little.held[0, SMALL_ROWS - 8 :] = jnp.zeros((8, HALF), f32)
        for r, row in enumerate(rows):
            little.held[0, r : r + 1, :] = row
        little.start(0)
        load_w.wait()
        edges = mm_nt(gzh_s[...], wfull[:, DIN:ZXW])
        for q in range(seqs):
            rim_out[q] = back(rhalo[q], edges[q * RIM : (q + 1) * RIM]).astype(bf16)
            pl.when(me > 0)(lambda q=q: rim_copy(q).start())

        @pl.when(me == count - 1)
        def _():
            rim_in[...] = jnp.zeros_like(rim_in)

    @pl.when(i == bc_step + 2)
    def _():
        little.done(0)
        little.start(1)

    @pl.when(i > bc_step)
    def _():
        s = i - bc_step - 1
        grad = mm_nt(gz_s[span(s), :CONVW], wfull[:, DIN:]) + mm_nt(ggate[0], wfull[:, :DIN])
        grad = grad + mm_nt(gz_s[span(s), CONVW:], wd[...])

        @pl.when(s == 0)
        def _():
            convs.m_done(convs.chunks - 1)

        wave(2 * i + 1)
        live = live_rows(lengths, s)
        out = live * cot[0].astype(f32) + back(tok[0], grad)
        gtok[0, : SPAN - RIM] = out[: SPAN - RIM].astype(bf16)
        pl.when(me < count - 1)(lambda: rim_copy(s).wait_recv())
        gtok[0, SPAN - RIM :] = (out[SPAN - RIM :] + rim_in[s].astype(f32)).astype(bf16)

    @pl.when(i == bc_step + seqs)
    def _():
        least.held[0] = jnp.zeros_like(least.held[0])
        for j in range(D // HALF):
            least.held[0, j : j + 1, :] = ggain[:, j * HALF : (j + 1) * HALF]
        least.start(0)
        little.done(1)
        small_out[...] = little.held[2]
        least.done(0)
        least.start(1)
        loop(2 * (bc_step + seqs) + 2, last_conv + 4 * STAGE_LAG + 1, wave)
        for r in (gates, outs, convs):
            loop(0, r.chunks, r.drain_ctx)
        loop(0, convs.chunks, convs.drain_group)
        little.drain()
        for q in range(seqs):
            pl.when(me > 0)(lambda q=q: rim_copy(q).wait_send())
        least.done(1)
        ggain_out[...] = least.held[2]
        least.drain()


def done_kernel(rzx, rout, small, gain_sum, g_gain, g_zx, g_delta, g_out, g_cw, g_cb, g_db, g_dl, g_skip, g_gated):
    g_zx[...] = rzx[:, :ZXW].astype(f32)
    g_delta[...] = rzx[:, ZXW : ZXW + HEADS].astype(f32)
    g_out[...] = rout[...].astype(f32)
    tiles = CONVW // HALF
    for k in range(KCONV):
        for j in range(tiles):
            g_cw[k : k + 1, j * HALF : (j + 1) * HALF] = small[k * tiles + j : k * tiles + j + 1, :]
    at = KCONV * tiles
    for j in range(tiles):
        g_cb[j * HALF : (j + 1) * HALF] = small[at + j, :]
    at += tiles
    for ref in (g_db, g_dl, g_skip):
        ref[...] = small[at, :][:HEADS]
        at += 1
    for j in range(PAIRS):
        g_gated[j * HALF : (j + 1) * HALF] = small[at + j, :]
    for j in range(D // HALF):
        g_gain[j * HALF : (j + 1) * HALF] = gain_sum[j, :]


def whole(shape):
    zeros = (0,) * len(shape)
    return pl.BlockSpec(shape, lambda s: zeros, pipeline_mode=pl.Buffered(1))


def summed(shape):
    zeros = (0,) * len(shape)
    return pl.BlockSpec(shape, lambda s: zeros)


def per_seq(*shape):
    zeros = (0,) * len(shape)
    return pl.BlockSpec((1,) + shape, lambda s: (s,) + zeros)


SMEM = pl.BlockSpec(memory_space=pltpu.SMEM)
ANY = pl.BlockSpec(memory_space=pl.ANY)


def staged(seqs, phase, *shape):
    zeros = (0,) * len(shape)
    if phase == 0:
        return pl.BlockSpec((1,) + shape, lambda i: (jnp.minimum(i, seqs - 1),) + zeros)
    if phase == 1:
        return pl.BlockSpec((1,) + shape, lambda i: (jnp.maximum(i - seqs, 0),) + zeros)
    return pl.BlockSpec((1,) + shape, lambda i: (lax.rem(i, seqs),) + zeros)


def call(kernel, steps, in_specs, outs, scratch, name, collective=None):
    params = dict(vmem_limit_bytes=VMEM_LIMIT)
    if collective is not None:
        params.update(collective_id=collective, has_side_effects=True)
    return pl.pallas_call(
        kernel,
        grid=(steps,),
        in_specs=in_specs,
        out_specs=[o[0] for o in outs],
        out_shape=[jax.ShapeDtypeStruct(o[1], o[2]) for o in outs],
        scratch_shapes=[pltpu.VMEM(*sc) if isinstance(sc, tuple) else sc for sc in scratch],
        compiler_params=pltpu.CompilerParams(**params),
        name=name,
    )


def local(
    tokens_in, seq_lengths, norm_gain, w_zx, w_delta, w_out, conv_weight, conv_bias,
    delta_bias, decay_log, skip_gain, gated_gain, cotangent,
):
    seqs = tokens_in.shape[0]
    count = lax.axis_size("ctx")
    group = lax.axis_size("group")
    chips = max(group // 2, 1)
    w_delta = jnp.pad(w_delta, ((0, 0), (0, HALF - HEADS)))
    dma = pltpu.SemaphoreType.DMA
    at0 = lambda *shape: staged(seqs, 0, *shape)
    at1 = lambda *shape: staged(seqs, 1, *shape)
    at01 = lambda *shape: staged(seqs, 2, *shape)

    def tiled(rows, first, lead=None):
        def index(i):
            u = jnp.clip(i - first, 0, TILES - 1)
            return (0, 0, u if lead is None else jnp.where(i == 0, lead, u))

        return pl.BlockSpec((seqs, rows, TILE), index)

    state = (seqs, NSTATE, DIN)
    nt, nth, rhalo, cin, xb, spb, vraw, cum, st0, loc, ylocal, gate, decs, wfull, wdfull, wofull, state_in = call(
        front_kernel,
        PIECES,
        [whole((seqs, SPAN, D)), ANY, ANY, ANY, ANY, whole((D,)), whole((KCONV, CONVW)), whole((CONVW,)), SMEM, SMEM],
        [
            (summed((D, seqs * SPAN)), (D, seqs * SPAN), bf16),
            (summed((D, seqs * RIM)), (D, seqs * RIM), bf16),
            (summed((seqs, RIM, D)), (seqs, RIM, D), bf16),
            (tiled(RIM + SPAN, 1, TILES), (seqs, RIM + SPAN, CONVW), bf16),
            (tiled(SPAN, 1, TILES), (seqs, SPAN, CONVW), bf16),
            (tiled(SPAN, 1, TILES), (seqs, SPAN, CONVW), bf16),
            (summed((seqs, SPAN, HALF)), (seqs, SPAN, HALF), f32),
            (summed((seqs, SPAN, HALF)), (seqs, SPAN, HALF), f32),
            (tiled(NSTATE, 1), state, bf16),
            (tiled(NSTATE, 1), state, bf16),
            (tiled(SPAN, TILES + 1), (seqs, SPAN, DIN), bf16),
            (tiled(SPAN, TILES + 1), (seqs, SPAN, DIN), bf16),
            (summed((seqs, count * 8, HALF)), (seqs, count * 8, HALF), f32),
            (ANY, (D, ZXW), bf16),
            (ANY, (D, HALF), bf16),
            (ANY, (DIN, D), bf16),
            (ANY, state, bf16),
        ],
        [((2 * HALF, DIN), bf16), ((seqs, RIM, D), bf16), ((seqs * RIM, D), f32), ((seqs, RIM + SPAN, D), bf16), ((D, ZXW), bf16),
         ((D, HALF), bf16), ((1, CONVW), f32),
         ((seqs, RIM + SPAN, TILE), f32), ((seqs, SPAN, DIN), bf16), ((seqs, NSTATE, SPAN), bf16),
         ((seqs, 2, HALF, HALF), f32), ((seqs, SPAN, 2 * HALF), bf16), ((seqs, SPAN, 2 * HALF), bf16),
         ((seqs, 2, HALF, HALF), f32), ((seqs, 8, DIN), f32), ((seqs, count * 8, HALF), f32)]
        + [dma((2,))] + [dma((PIECES + 2, chips))] * 4 + [dma((3,)), dma((2,)), dma((count,)), dma((count,))]
        + Exchange.scratch(TILES, seqs, TILE, count),
        "front",
        0,
    )(tokens_in, tokens_in, w_zx, w_delta, w_out, norm_gain, conv_weight, conv_bias, delta_bias, decay_log)

    x_gate_shape = (DIN // GATE_CHUNK, D // group, GATE_CHUNK)
    x_out_shape = (D // OUT_CHUNK, DIN // group, OUT_CHUNK)
    mixed_out, dy, ggate, wred, dir1, gskip, gggain, dxs, dbc, x_gate, x_out, later = call(
        middle_kernel,
        2 * seqs,
        [SMEM, SMEM, at1(SPAN, D), at0(SPAN, D), at0(SPAN, DIN), at0(SPAN, DIN), at01(SPAN, CONVW), at01(SPAN, HALF),
         at01(SPAN, HALF), at0(NSTATE, DIN), at0(NSTATE, DIN), whole((seqs, count * 8, HALF)), whole((DIN, D)),
         whole((DIN,)), whole((D, seqs * SPAN))],
        [
            (at1(SPAN, D), (seqs, SPAN, D), bf16),
            (at0(SPAN, DIN), (seqs, SPAN, DIN), bf16),
            (at0(SPAN, DIN), (seqs, SPAN, DIN), bf16),
            (at0(SPAN, HALF), (seqs, SPAN, HALF), f32),
            (at0(NSTATE, DIN), (seqs, NSTATE, DIN), bf16),
            (summed((1, DIN)), (1, DIN), f32),
            (summed((1, DIN)), (1, DIN), f32),
            (at1(SPAN, DIN), (seqs, SPAN, DIN), bf16),
            (at1(SPAN, 2 * NSTATE), (seqs, SPAN, 2 * NSTATE), f32),
            (summed(x_gate_shape), x_gate_shape, bf16),
            (summed(x_out_shape), x_out_shape, bf16),
            (ANY, (seqs, NSTATE, DIN), bf16),
        ],
        [((2 * HALF, DIN), bf16), ((1, DIN), f32), ((1, DIN), f32), ((2, HALF, HALF), f32), ((SPAN, DIN), f32), ((SPAN, DIN), f32), ((SPAN, DIN), f32),
         ((SPAN, DIN), f32), ((2, NSTATE, DIN), bf16), ((seqs, SPAN, HALF), f32), ((seqs, SPAN, DIN), bf16),
         ((seqs * SPAN, DIN), bf16), ((seqs * SPAN, DIN), bf16), ((seqs * SPAN, D), bf16), ((D, DIN), bf16), ((DIN, D), bf16),
         ((2, HALF, HALF), f32), ((2, HALF, HALF), f32)]
        + Exchange.scratch(seqs, 1, DIN, count)
        + Reducer.group_scratch(*x_gate_shape, group)
        + Reducer.group_scratch(*x_out_shape, group),
        "middle",
        1,
    )(seq_lengths, skip_gain, tokens_in, cotangent, ylocal, gate, xb, vraw, cum, st0, state_in, decs, wofull, gated_gain, nt)

    def tile_in(rows, tiles):
        return pl.BlockSpec((seqs, rows, TILE), lambda i: (0, 0, jnp.minimum(i, tiles - 1)))

    def late(*shape):
        zeros = (0,) * len(shape)
        return pl.BlockSpec((1,) + shape, lambda i: (jnp.clip(i - TILES - 1, 0, seqs - 1),) + zeros)

    bc_spec = pl.BlockSpec((seqs, SPAN, TILE), lambda i: (0, 0, TILES), pipeline_mode=pl.Buffered(1))
    height = SMALL_ROWS
    x_conv_shape = (GZW // CONV_CHUNK, D // group, CONV_CHUNK)
    gtok, r_zx, r_out, small, gain_sum = call(
        back_kernel,
        TILES + 1 + seqs,
        [SMEM, SMEM, SMEM, late(SPAN, D), late(SPAN, D), whole((seqs, RIM, D)), whole((D,)), late(SPAN, DIN), ANY, whole((D, HALF)),
         tile_in(RIM + SPAN, TILES + 1), tile_in(SPAN, TILES + 1), tile_in(SPAN, TILES + 1), bc_spec, tile_in(SPAN, TILES),
         tile_in(SPAN, TILES), tile_in(NSTATE, TILES), tile_in(NSTATE, TILES), tile_in(NSTATE, TILES), tile_in(NSTATE, TILES),
         whole((seqs, SPAN, HALF)), whole((seqs, SPAN, HALF)), whole((seqs, SPAN, HALF)), whole((seqs, SPAN, 2 * NSTATE)),
         whole((KCONV, CONVW)), whole((D, seqs * SPAN)), whole((D, seqs * RIM)),
         whole(x_gate_shape), whole(x_out_shape), whole((1, DIN)), whole((1, DIN))],
        [
            (late(SPAN, D), (seqs, SPAN, D), bf16),
            (summed((D // group, DIN + GZW)), (D // group, DIN + GZW), bf16),
            (summed((DIN // group, D)), (DIN // group, D), bf16),
            (summed((height, HALF)), (height, HALF), f32),
            (summed((8, HALF)), (8, HALF), f32),
        ],
        [((2 * HALF, DIN), bf16), ((1, DIN), f32), ((D, ZXW), bf16), dma((1,)), ((seqs, SPAN, 2 * HALF), bf16),
         ((seqs, SPAN, 2 * HALF), bf16), ((seqs, 16, DIN), f32),
         ((seqs, SPAN, NSTATE), f32), ((seqs, SPAN, HALF), f32), ((seqs, 8, HALF), f32), ((RIM + SPAN + 8, TILE), f32),
         ((seqs * SPAN, CONVW + HALF), bf16), ((seqs * RIM, CONVW), bf16), ((D, GZW), bf16), ((KCONV, CONVW), f32),
         ((1, CONVW), f32), ((1, HALF), f32), ((1, HALF), f32), ((1, D), f32), ((seqs, RIM, D), bf16), ((seqs, RIM, D), bf16),
         dma((seqs,)), dma((seqs,))]
        + Reducer.ctx_scratch(*x_gate_shape, False, count)
        + Reducer.ctx_scratch(*x_out_shape, True, count)
        + Reducer.group_scratch(*x_conv_shape, group)
        + [(x_conv_shape, bf16)]
        + Reducer.ctx_scratch(*x_conv_shape, False, count)
        + Small.scratch(height, group, count)
        + Small.scratch(8, group, count),
        "back",
        2,
    )(seq_lengths, decay_log, skip_gain, tokens_in, cotangent, rhalo, norm_gain, ggate, wfull, wdfull, cin, xb, spb, xb, dy, dxs, dir1, later, state_in, loc,
      vraw, cum, wred, dbc, conv_weight, nt, nth, x_gate, x_out, gskip, gggain)

    shapes = [(D,), (D // group, ZXW), (D // group, HEADS), (DIN // group, D), (KCONV, CONVW), (CONVW,), (HEADS,), (HEADS,),
              (HEADS,), (DIN,)]
    grads = pl.pallas_call(
        done_kernel,
        out_shape=[jax.ShapeDtypeStruct(shape, f32) for shape in shapes],
        name="done",
    )(r_zx, r_out, small, gain_sum)
    return (mixed_out, gtok, *grads)


def solution(mesh):
    rows = P("group", "ctx", None)
    own = P("group", None)
    in_specs = (rows, P("group"), P(), own, own, own, P(), P(), P(), P(), P(), P(), rows)
    out_specs = (rows, rows, P(), own, own, own, P(), P(), P(), P(), P(), P())
    return jax.shard_map(local, mesh=mesh, in_specs=in_specs, out_specs=out_specs, check_vma=False)
```

```python
import jax
import jax.numpy as jnp
from jax import lax
from jax.experimental import pallas as pl
from jax.experimental.pallas import tpu as pltpu
from jax.sharding import PartitionSpec as P

D = 768
HEADS = 24
HEADDIM = 64
NSTATE = 128
KCONV = 4
SPAN = 256
DIN = 1536
CONVW = 1792
ZXW = 3328
RIM = 16
HALF = 128
TILE = 256
PAIRS = 12
EPS = 1e-05

f32 = jnp.float32
bf16 = jnp.bfloat16
NT = (((1,), (1,)), ((), ()))
TN = (((0,), (0,)), ((), ()))
VMEM_LIMIT = 63 * 1024 * 1024
GATE_CHUNK = 512
OUT_CHUNK = 256
CONV_CHUNK = 512
BACK_LAGS = (4, 7, 9)
STAGE_LAG = 4
CONV_LAG = 3
MIDDLE_LAG = 2
SCAN_LAG = 4
HOPS = ("group", "ctx")
SMALL_ROWS = 88
CLOSE_LAG = 6
GZW = 2048


def mm(a, b):
    return jnp.dot(a, b, preferred_element_type=f32)


def mm_nt(a, b):
    return lax.dot_general(a, b, NT, preferred_element_type=f32)


def mm_tn(a, b):
    return lax.dot_general(a, b, TN, preferred_element_type=f32)


def halves(v):
    high = v.astype(bf16)
    return high, (v - high.astype(f32)).astype(bf16)


def head_map():
    rows = lax.broadcasted_iota(jnp.int32, (2 * HALF, DIN), 0) % HALF
    cols = lax.broadcasted_iota(jnp.int32, (2 * HALF, DIN), 1) // HEADDIM
    return jnp.where(rows == cols, 1.0, 0.0).astype(bf16)


def spread(v, sel):
    return mm(jnp.concatenate(halves(v), axis=1), sel[...])


def gather_heads(v, sel_part):
    high, low = halves(v)
    return mm_nt(high, sel_part) + mm_nt(low, sel_part)


def triangle(size, lower):
    rows = lax.broadcasted_iota(jnp.int32, (size, size), 0)
    cols = lax.broadcasted_iota(jnp.int32, (size, size), 1)
    keep = rows >= cols if lower else rows <= cols
    return jnp.where(keep, 1.0, 0.0).astype(f32)


def running_sum(v, lower):
    rest, terms = v, []
    for _ in range(3):
        high = rest.astype(bf16)
        rest = rest - high.astype(f32)
        terms.append(high)
    tri = triangle(v.shape[0], lower).astype(bf16)
    return mm(tri, terms[0]) + (mm(tri, terms[1]) + mm(tri, terms[2]))


def softplus(v):
    return jnp.maximum(v, 0.0) + jnp.log1p(jnp.exp(-jnp.abs(v)))


def sigmoid(v):
    return 1.0 / (1.0 + jnp.exp(-v))


def gate_of(v):
    return 0.5 * jnp.tanh(0.5 * v) + 0.5


def local_decays(cum):
    mid, end = cum[HALF - 1 : HALF], cum[SPAN - 1 : SPAN]
    rows = lax.broadcasted_iota(jnp.int32, (SPAN, 1), 0)
    first = rows < HALF
    start = jnp.where(first, 0.0, mid)
    stop = jnp.where(first, mid, end)
    return jnp.exp(cum - start), jnp.exp(stop - cum), jnp.exp(mid), jnp.exp(end - mid), jnp.exp(end)


def rows_of(v):
    return jnp.broadcast_to(v, (8, v.shape[1]))


def lane_row(ref):
    lanes = lax.broadcasted_iota(jnp.int32, (1, HALF), 1)
    row = jnp.zeros((1, HALF), f32)
    for h in range(HEADS):
        row = jnp.where(lanes == h, ref[h], row)
    return row


def row_of(ref):
    return ref[...].reshape(1, ref.shape[0])


def live_rows(lengths, s):
    start = lax.axis_index("ctx") * SPAN
    return (lax.broadcasted_iota(jnp.int32, (SPAN, 1), 0) + start < lengths[s]).astype(f32)


def normalized(rows, gain):
    rows = rows.astype(f32)
    inv = lax.rsqrt(jnp.mean(rows * rows, axis=-1, keepdims=True) + EPS)
    return rows, inv, (rows * inv * gain).astype(bf16)


def remote(src, dst, send_sem, recv_sem, **where):
    return pltpu.make_async_remote_copy(
        src_ref=src, dst_ref=dst, send_sem=send_sem, recv_sem=recv_sem,
        device_id=where, device_id_type=pl.DeviceIdType.MESH,
    )


def loop(start, stop, body):
    def step(i, c):
        body(i)
        return c

    lax.fori_loop(start, stop, step, 0)


def greet(axes):
    barrier = pltpu.get_barrier_semaphore()
    for axis in axes:
        size = lax.axis_size(axis)
        me = lax.axis_index(axis)

        def signal(d, axis=axis, size=size, me=me):
            pl.semaphore_signal(
                barrier, inc=1, device_id={axis: lax.rem(me + d, size)}, device_id_type=pl.DeviceIdType.MESH
            )

        loop(1, size, signal)


def settle(axes):
    pl.semaphore_wait(pltpu.get_barrier_semaphore(), sum(lax.axis_size(axis) - 1 for axis in axes))


def meet(axes):
    greet(axes)
    settle(axes)


class Exchange:
    def __init__(self, reverse, out_at, bufs, sems):
        self.reverse, self.out_at, self.sems = reverse, out_at, sems
        self.buf, self.y_buf, self.z_src, self.z_buf, self.z_back, self.p_buf, self.mine_buf, self.their_buf, self.decx = bufs
        self.depth = self.buf.shape[1]
        ctx = lax.axis_index("ctx")
        self.ctx = ctx
        self.outer = lax.axis_size("ctx") // 2
        self.owners = min(self.outer, 4)
        self.stride = self.outer // self.owners
        self.inner = lax.rem(ctx, 2)
        self.line = ctx // 2
        self.mine = self.line // self.stride
        self.half = NSTATE // 2
        self.rows = self.half // self.owners

    def half_rows(self, inner):
        return pl.ds(pl.multiple_of(inner * self.half, self.half), self.half)

    def part(self, j):
        return pl.ds(pl.multiple_of(j * self.rows, self.rows), self.rows)

    def other_owners(self, body):
        if self.stride == 1:
            loop(1, self.owners, lambda d: body(lax.rem(self.mine + d, self.owners)))
        else:
            loop(0, self.owners, lambda j: pl.when(j * self.stride != self.line)(lambda: body(j)))

    def other_lines(self, body):
        loop(1, self.outer, lambda d: body(lax.rem(self.line + d, self.outer)))

    def if_owner(self, body):
        if self.stride == 1:
            body()
        else:
            pl.when(self.mine * self.stride == self.line)(body)

    def y_copy(self, u):
        return remote(
            self.buf.at[u, :, self.half_rows(1 - self.inner)], self.y_buf.at[u], self.sems.at[0, u, 0], self.sems.at[1, u, 0],
            ctx=self.ctx + 1 - 2 * self.inner,
        )

    def z_copy(self, u, j, sender):
        return remote(
            self.z_src.at[u, :, self.part(j)], self.z_buf.at[u, sender], self.sems.at[2, u, j], self.sems.at[3, u, sender],
            ctx=j * self.stride * 2 + self.inner,
        )

    def b_copy(self, u, line, j):
        return remote(
            self.z_back.at[u, line], self.p_buf.at[u, :, self.part(j)], self.sems.at[4, u, line], self.sems.at[5, u, j],
            ctx=line * 2 + self.inner,
        )

    def f_copy(self, u, inner):
        return remote(
            self.their_buf.at[u], self.out_at(u, self.half_rows(inner)), self.sems.at[6, u, 0], self.sems.at[7, u, 0],
            ctx=self.ctx + 1 - 2 * self.inner,
        )

    def keep(self, u):
        return pltpu.make_async_copy(self.mine_buf.at[u], self.out_at(u, self.half_rows(self.inner)), self.sems.at[8, u, 0])

    def decay(self, a, block):
        return self.decx[a, pl.ds(pl.multiple_of(block * 8, 8), 8), :][0:1]

    def pair(self, u, a):
        own = self.buf[u, a, self.half_rows(self.inner), :].astype(f32)
        other = self.y_buf[u, a].astype(f32)
        first = self.inner == 0
        return jnp.where(first, own, other), jnp.where(first, other, own)

    def start(self, u):
        self.y_copy(u).start()

    def middle(self, u):
        self.y_copy(u).wait_recv()
        for a in range(self.depth):
            s0, s1 = self.pair(u, a)
            if self.reverse:
                total = s0 + self.decay(a, 2 * self.line) * s1
            else:
                total = self.decay(a, 2 * self.line + 1) * s0 + s1
            self.z_src[u, a] = total.astype(bf16)
        self.other_owners(lambda j: self.z_copy(u, j, self.line).start())

    def scan(self, u):
        def run():
            self.other_lines(lambda line: self.z_copy(u, self.mine, line).wait_recv())
            self.z_buf[u, self.line] = self.z_src[u, :, self.part(self.mine), :]
            for a in range(self.depth):

                def step(k, carry):
                    line = self.outer - 1 - k if self.reverse else k
                    self.z_back[u, line, a] = carry.astype(bf16)
                    both_decays = self.decay(a, 2 * line) * self.decay(a, 2 * line + 1)
                    return both_decays * carry + self.z_buf[u, line, a].astype(f32)

                lax.fori_loop(0, self.outer, step, jnp.zeros(self.z_buf.shape[3:], f32))
            self.other_lines(lambda line: self.b_copy(u, line, self.mine).start())
            self.p_buf[u, :, self.part(self.mine), :] = self.z_back[u, self.line]

        self.if_owner(run)

    def close(self, u):
        self.other_owners(lambda j: self.b_copy(u, self.line, j).wait_recv())
        for a in range(self.depth):
            s0, s1 = self.pair(u, a)
            near = self.p_buf[u, a].astype(f32)
            if self.reverse:
                far = s1 + self.decay(a, 2 * self.line + 1) * near
            else:
                far = s0 + self.decay(a, 2 * self.line) * near
            keeps_near = self.inner == (1 if self.reverse else 0)
            self.mine_buf[u, a] = jnp.where(keeps_near, near, far).astype(bf16)
            self.their_buf[u, a] = jnp.where(keeps_near, far, near).astype(bf16)
        self.f_copy(u, self.inner).start()
        self.keep(u).start()

    def finish(self, u):
        self.f_copy(u, 1 - self.inner).wait_recv()
        self.keep(u).wait()
        self.y_copy(u).wait_send()
        self.other_owners(lambda j: self.z_copy(u, j, self.line).wait_send())
        self.if_owner(lambda: self.other_lines(lambda line: self.b_copy(u, line, self.mine).wait_send()))
        self.f_copy(u, self.inner).wait_send()

    @staticmethod
    def scratch(units, depth, lanes, count):
        outer = count // 2
        half = NSTATE // 2
        rows = half // min(outer, 4)
        bufs = [(units, depth, NSTATE, lanes), (units, depth, half, lanes), (units, depth, half, lanes),
                (units, outer, depth, rows, lanes), (units, outer, depth, rows, lanes), (units, depth, half, lanes),
                (units, depth, half, lanes), (units, depth, half, lanes)]
        return (
            [(b, bf16) for b in bufs]
            + [((depth, count * 8, lanes), f32)]
            + [pltpu.SemaphoreType.DMA((9, units, max(outer, 4)))]
        )


class Spread:
    def __init__(self, shard, full, sems):
        self.shard, self.full = shard, full
        self.x_send, self.x_recv, self.m_send, self.m_recv, self.own = sems
        size = lax.axis_size("group")
        self.cores = 2 if size % 2 == 0 else 1
        self.chips = size // self.cores
        self.me = lax.axis_index("group")
        self.core = lax.rem(self.me, self.cores)
        self.chip = self.me // self.cores
        self.rows = shard.shape[0]

    def place(self, member, cols):
        return self.full.at[pl.ds(pl.multiple_of(member * self.rows, 32), self.rows), cols]

    def across(self, p, cols, d):
        peer = lax.rem(self.chip + d, self.chips) * self.cores + self.core
        return remote(
            self.shard.at[:, cols], self.place(self.me, cols), self.x_send.at[p, d], self.x_recv.at[p, d], group=peer
        )

    def mate(self, p, cols, d):
        member = lax.rem(self.chip + self.chips - d, self.chips) * self.cores + self.core
        src = self.shard.at[:, cols] if d == 0 else self.place(member, cols)
        return remote(
            src, self.place(member, cols), self.m_send.at[p, d], self.m_recv.at[p, d],
            group=self.me + 1 - 2 * self.core,
        )

    def keep(self, p):
        return pltpu.make_async_copy(self.shard, self.place(self.me, slice(None)), self.own.at[p])

    def start_chip(self, p):
        if self.cores == 2:
            self.mate(p, slice(None), 0).start()
        self.keep(p).start()

    def finish_chip(self, p):
        if self.cores == 2:
            self.mate(p, slice(None), 0).wait_recv()
        self.keep(p).wait()

    def start(self, p, cols):
        for d in range(1, self.chips):
            self.across(p, cols, d).start()

    def forward(self, p, cols):
        for d in range(1, self.chips):
            self.across(p, cols, d).wait_recv()
            if self.cores == 2:
                self.mate(p, cols, d).start()

    def finish(self, p, cols):
        if self.cores == 2:
            for d in range(1, self.chips):
                self.mate(p, cols, d).wait_recv()

    def drain(self, p, cols):
        for d in range(1, self.chips):
            self.across(p, cols, d).wait_send()
            if self.cores == 2:
                self.mate(p, cols, d).wait_send()

    def drain_chip(self, p):
        if self.cores == 2:
            self.mate(p, slice(None), 0).wait_send()


def owner_count(rows, width, by_rows, outer):
    fits = lambda n: (rows // 2) % (16 * n) == 0 if by_rows else width % (128 * n) == 0
    return max(n for n in (1, 2, 4) if outer % n == 0 and fits(n))


class Reducer:
    def __init__(self, part, out, rows, width, by_rows, group_bufs, ctx_bufs):
        self.part, self.out, self.rows, self.width, self.by_rows = part, out, rows, width, by_rows
        if group_bufs is not None:
            self.m_buf, self.x_buf, self.g_sems = group_bufs
        self.ships = ctx_bufs is not None
        if self.ships:
            self.y_src, self.y_buf, self.z_src, self.z_buf, self.full, self.c_sems = ctx_bufs
        else:
            self.y_src = out
        self.chunks = self.y_src.shape[0]
        self.base = 0
        self.group = lax.axis_index("group")
        self.cores = 2
        self.chips = lax.axis_size("group") // 2
        self.core = lax.rem(self.group, 2)
        self.chip = self.group // 2
        self.ctx = lax.axis_index("ctx")
        self.outer = lax.axis_size("ctx") // 2
        self.owners = owner_count(rows, width, by_rows, self.outer)
        self.stride = self.outer // self.owners
        self.inner = lax.rem(self.ctx, 2)
        self.line = self.ctx // 2
        self.mine = self.line // self.stride
        self.half = rows // 2

    def cols(self, k):
        return pl.ds(pl.multiple_of(k * self.width, self.width), self.width)

    def member(self, chip, core):
        return pl.ds(pl.multiple_of((chip * 2 + core) * self.rows, 64), self.rows)

    def half_rows(self, inner):
        return pl.ds(pl.multiple_of(inner * self.half, 16), self.half)

    def piece(self, j, base):
        if self.by_rows:
            n = self.half // self.owners
            return pl.ds(pl.multiple_of(base + j * n, 16), n), pl.ds(0, self.width)
        n = self.width // self.owners
        return pl.ds(pl.multiple_of(base, 16), self.half), pl.ds(pl.multiple_of(j * n, 128), n)

    def m_copy(self, k, chip):
        return remote(
            self.part.at[self.member(chip, 1 - self.core), self.cols(k)], self.m_buf.at[k, chip],
            self.g_sems.at[0, k, chip], self.g_sems.at[1, k, chip], group=self.group + 1 - 2 * self.core,
        )

    def x_copy(self, k, chip, sender):
        return remote(
            self.m_buf.at[k, chip], self.x_buf.at[k, sender], self.g_sems.at[2, k, chip], self.g_sems.at[3, k, sender],
            group=chip * 2 + self.core,
        )

    def y_copy(self, k):
        return remote(
            self.y_src.at[k, self.half_rows(1 - self.inner)], self.y_buf.at[k], self.c_sems.at[0, k, 0], self.c_sems.at[1, k, 0],
            ctx=self.ctx + 1 - 2 * self.inner,
        )

    def z_copy(self, k, j, sender):
        rows, cols = self.piece(j, 0)
        return remote(
            self.z_src.at[k, rows, cols], self.z_buf.at[k, sender], self.c_sems.at[2, k, j], self.c_sems.at[3, k, sender],
            ctx=j * self.stride * 2 + self.inner,
        )

    def b_copy(self, k, line, j):
        rows, cols = self.piece(j, self.inner * self.half)
        return remote(
            self.full.at[k, rows, cols], self.full.at[k, rows, cols], self.c_sems.at[4, k, line], self.c_sems.at[5, k, j],
            ctx=line * 2 + self.inner,
        )

    def f_copy(self, k, inner):
        rows = self.half_rows(inner)
        return remote(
            self.full.at[k, rows], self.full.at[k, rows], self.c_sems.at[6, k, 0], self.c_sems.at[7, k, 0],
            ctx=self.ctx + 1 - 2 * self.inner,
        )

    def other_chips(self, body):
        for d in range(1, self.chips):
            body(lax.rem(self.chip + d, self.chips))

    def other_owners(self, body):
        if self.stride == 1:
            for d in range(1, self.owners):
                body(lax.rem(self.mine + d, self.owners))
        else:
            for j in range(self.owners):
                pl.when(j * self.stride != self.line)(lambda j=j: body(j))

    def other_lines(self, body):
        loop(1, self.outer, lambda d: body(lax.rem(self.line + d, self.outer)))

    def if_owner(self, body):
        if self.stride == 1:
            body()
        else:
            pl.when(self.mine * self.stride == self.line)(body)

    def m_start(self, k):
        for chip in range(self.chips):
            self.m_copy(k, chip).start()

    def m_done(self, k):
        for chip in range(self.chips):
            self.m_copy(k, chip).wait_recv()
            own = self.part[self.member(chip, self.core), self.cols(k)].astype(f32)
            self.m_buf[k, chip] = (own + self.m_buf[k, chip].astype(f32)).astype(bf16)
        self.other_chips(lambda chip: self.x_copy(k, chip, self.chip).start())

    def x_done(self, k):
        total = self.m_buf[k, self.chip].astype(f32)
        for d in range(1, self.chips):
            chip = lax.rem(self.chip + d, self.chips)
            self.x_copy(k, chip, chip).wait_recv()
            total = total + self.x_buf[k, chip].astype(f32)
        self.y_src[k] = total.astype(bf16)
        if self.ships:
            self.y_start(k)

    def y_start(self, k):
        self.y_copy(k).start()

    def y_done(self, k):
        self.y_copy(k).wait_recv()
        own = self.y_src[k, self.half_rows(self.inner), :].astype(f32)
        self.z_src[k] = (own + self.y_buf[k].astype(f32)).astype(bf16)
        self.other_owners(lambda j: self.z_copy(k, j, self.line).start())

    def z_done(self, k):
        def run():
            rows, cols = self.piece(self.mine, 0)
            self.other_lines(lambda line: self.z_copy(k, self.mine, line).wait_recv())
            self.z_buf[k, self.line] = self.z_src[k, rows, cols]
            total = self.z_buf[k, 0].astype(f32)
            for line in range(1, self.outer):
                total = total + self.z_buf[k, line].astype(f32)
            rows, cols = self.piece(self.mine, self.inner * self.half)
            self.full[k, rows, cols] = total.astype(bf16)
            self.other_lines(lambda line: self.b_copy(k, line, self.mine).start())

        self.if_owner(run)

    def b_done(self, k):
        self.other_owners(lambda j: self.b_copy(k, self.line, j).wait_recv())
        self.f_copy(k, self.inner).start()

    def f_done(self, k):
        self.f_copy(k, 1 - self.inner).wait_recv()
        self.out[:, pl.ds(pl.multiple_of(self.base + k * self.width, 128), self.width)] = self.full[k]

    def drain_group(self, k):
        for chip in range(self.chips):
            self.m_copy(k, chip).wait_send()
        self.other_chips(lambda chip: self.x_copy(k, chip, self.chip).wait_send())

    def drain_ctx(self, k):
        self.y_copy(k).wait_send()
        self.other_owners(lambda j: self.z_copy(k, j, self.line).wait_send())
        self.if_owner(lambda: self.other_lines(lambda line: self.b_copy(k, line, self.mine).wait_send()))
        self.f_copy(k, self.inner).wait_send()

    def wave(self, t, acts, chunk_at, lag=STAGE_LAG):
        for order, act in reversed(list(enumerate(acts))):
            k, is_due = chunk_at(t - order * lag)
            pl.when(is_due)(lambda k=k, act=act: act(k))

    def each(self, t):
        return t, jnp.logical_and(t >= 0, t < self.chunks)

    @staticmethod
    def group_scratch(chunks, rows, width, group):
        chips = group // 2
        buf = ((chunks, chips, rows, width), bf16)
        return [buf, buf, pltpu.SemaphoreType.DMA((4, chunks, max(chips, 2)))]

    @staticmethod
    def ctx_scratch(chunks, rows, width, by_rows, count):
        outer = count // 2
        owners = owner_count(rows, width, by_rows, outer)
        half = rows // 2
        piece = (half // owners, width) if by_rows else (half, width // owners)
        bufs = [(chunks, half, width), (chunks, half, width), (chunks, outer) + piece, (chunks, rows, width)]
        return [(b, bf16) for b in bufs] + [pltpu.SemaphoreType.DMA((8, chunks, max(outer, 2)))]


class Small:
    def __init__(self, held, got, sends, recvs):
        self.held, self.got, self.sends, self.recvs = held, got, sends, recvs

    def copy(self, h, j, sender):
        return remote(
            self.held.at[h], self.got.at[h, sender], self.sends.at[h, j], self.recvs.at[h, sender], **{HOPS[h]: j}
        )

    def others(self, h, body):
        size, mine = lax.axis_size(HOPS[h]), lax.axis_index(HOPS[h])
        loop(1, size, lambda d: body(lax.rem(mine + d, size)))

    def start(self, h):
        mine = lax.axis_index(HOPS[h])
        self.others(h, lambda j: self.copy(h, j, mine).start())

    def done(self, h):
        self.others(h, lambda j: self.copy(h, j, j).wait_recv())
        self.got[h, lax.axis_index(HOPS[h])] = self.held[h]
        total = self.got[h, 0]
        for j in range(1, lax.axis_size(HOPS[h])):
            total = total + self.got[h, j]
        self.held[h + 1] = total

    def drain(self):
        for h in range(2):
            mine = lax.axis_index(HOPS[h])
            self.others(h, lambda j: self.copy(h, j, mine).wait_send())

    @staticmethod
    def scratch(height, group, count):
        widest = max(group, count)
        dma = pltpu.SemaphoreType.DMA
        return [((3, height, HALF), f32), ((2, widest, height, HALF), f32), dma((2, widest)), dma((2, widest))]


def masks():
    rows = lax.broadcasted_iota(jnp.int32, (HALF, HALF), 0)
    cols = lax.broadcasted_iota(jnp.int32, (HALF, HALF), 1)
    return rows >= cols, cols < HEADDIM


def both(q):
    return slice(q * HALF, (q + 1) * HALF)


def pair_decays(cum, cum_t, p, causal):
    rolled = pltpu.roll(cum, lax.rem(HALF - 2 * p, HALF), 1)
    out = []
    for q in range(2):
        for a in range(2):
            gaps = rolled[both(q), a : a + 1] - cum_t[q, pl.ds(2 * p + a, 1), :]
            out.append(jnp.exp(jnp.where(causal, gaps, -jnp.inf)))
    return out


TILES = DIN // TILE
PIECES = 2 * TILES + 1
DT0 = DIN + CONVW - 2 * NSTATE
AHEAD = 5


def front_kernel(
    tok, tok_any, wzx, wdl, wout, gain, cw, cb_in, db, dl,
    nt, nth, rhalo, cin, xb, spb, vout, cumout, st0, loc, ylocal, gate, decs_out, wfull, wdfull, wofull, sin,
    sel, halo, nh_s, ext, w, wd, cb, cin_s, xs_s, bt, scores, out_cat, dt_cat, cum_t, tot1x, decs,
    halo_sem, x_send, x_recv, m_send, m_recv, w_own, w_store, dec_send, dec_recv, *exchange,
):
    i = pl.program_id(0)
    seqs = tok.shape[0]
    count = lax.axis_size("ctx")
    me = lax.axis_index("ctx")
    sems = (x_send, x_recv, m_send, m_recv, w_own)
    zx, wo, de = Spread(wzx, w, sems), Spread(wout, wofull, sems), Spread(wdl, wd, sems)
    last, small_piece = PIECES, PIECES + 1

    def unit_cols(u):
        return pl.ds(pl.multiple_of(u * TILE, TILE), TILE)

    def piece(p):
        at = jnp.where(p <= TILES, DIN + (p - 1) * TILE, (p - 1 - TILES) * TILE)
        return pl.ds(pl.multiple_of(at, TILE), TILE)

    first_piece = pl.ds(DT0, 2 * NSTATE)
    ex = Exchange(False, lambda u, rows: sin.at[:, rows, unit_cols(u)], exchange[:9], exchange[9])
    halo_copy = remote(
        tok_any.at[:, pl.ds(SPAN - RIM, RIM), :], halo, halo_sem.at[0], halo_sem.at[1], ctx=lax.rem(me + 1, count)
    )
    keep_w = pltpu.make_async_copy(w, wfull, w_store.at[0])
    keep_d = pltpu.make_async_copy(wd, wdfull, w_store.at[1])

    def dec_copy(block, sender):
        rows = pl.ds(pl.multiple_of(sender * 8, 8), 8)
        return remote(decs.at[:, rows, :], decs.at[:, rows, :], dec_send.at[block], dec_recv.at[sender], ctx=block)

    def other_blocks(body):
        loop(1, count, lambda d: body(lax.rem(me + d, count)))

    def conv_tile(s, cols_w, cols_c):
        cin_s[s] = mm(ext[s], w[:, cols_w])
        cin[s] = cin_s[s].astype(bf16)
        o = cb[:, cols_c]
        for k in range(KCONV):
            o = o + cw[k : k + 1, cols_c] * cin_s[s, RIM - KCONV + 1 + k : RIM - KCONV + 1 + k + SPAN, :]
        sg = gate_of(o)
        a = o * sg
        xb[s] = a.astype(bf16)
        spb[s] = (sg + a * (1.0 - sg)).astype(bf16)
        return a

    def unit_decays(u):
        for s in range(seqs):
            ex.decx[s] = spread(decs[s], sel.at[:, unit_cols(u)])

    @pl.when(i == 0)
    def _():
        meet(("ctx", "group"))
        pl.when(me < count - 1)(lambda: halo_copy.start())
        de.start(small_piece, slice(None))
        zx.start(0, first_piece)
        de.start_chip(2)
        zx.start_chip(0)
        cb[...] = row_of(cb_in)
        for p in range(1, AHEAD):
            zx.start(p, piece(p))
        wo.start_chip(1)
        sel[...] = head_map()

        @pl.when(me == 0)
        def _():
            halo[...] = jnp.zeros_like(halo)

        def norm_main(s):
            nm = normalized(tok[s], row_of(gain))[2]
            ext[s, RIM:] = nm
            nt[:, pl.ds(pl.multiple_of(s * SPAN, SPAN), SPAN)] = jnp.transpose(nm.astype(f32)).astype(bf16)

        loop(0, seqs, norm_main)

        @pl.when(me > 0)
        def _():
            halo_copy.wait_recv()

        def norm_halo(s):
            nh = normalized(halo[s], row_of(gain))[2]
            ext[s, 0:RIM] = nh
            nh_s[pl.ds(pl.multiple_of(s * RIM, RIM), RIM), :] = nh.astype(f32)
            rhalo[s] = halo[s]

        loop(0, seqs, norm_halo)
        nth[...] = jnp.transpose(nh_s[...]).astype(bf16)
        de.forward(small_piece, slice(None))
        zx.forward(0, first_piece)
        zx.finish_chip(0)
        de.finish_chip(2)

    @pl.when(i + 1 < PIECES)
    def _():
        zx.forward(i + 1, piece(i + 1))

    @pl.when(i + AHEAD < PIECES)
    def _():
        zx.start(i + AHEAD, piece(i + AHEAD))

    @pl.when(i + AHEAD == PIECES)
    def _():
        wo.start(last, slice(None))

    @pl.when(i == 0)
    def _():
        zx.finish(0, first_piece)
        de.finish(small_piece, slice(None))
        shift, rate = lane_row(db), jnp.exp(lane_row(dl))

        def delta(s):
            a = conv_tile(s, slice(DT0, DT0 + TILE), slice(DIN, DIN + TILE))
            bb, cc = a[:, :NSTATE].astype(bf16), a[:, NSTATE:].astype(bf16)
            bt[s] = jnp.transpose(a[:, :NSTATE]).astype(bf16)
            for q in range(2):
                scores[s, q] = mm_nt(cc[both(q)], bb[both(q)])
            v = mm(ext[s, RIM:], wd[...]) + shift
            vout[s] = v
            dt = softplus(v)
            cum = running_sum(-rate * dt, True)
            cumout[s] = cum
            for q in range(2):
                cum_t[s, q] = jnp.transpose(cum[both(q)])
            e_in, e_out, tot0, tot1, total = local_decays(cum)
            decs[s, pl.ds(pl.multiple_of(me * 8, 8), 8), :] = rows_of(total)
            out_cat[s] = jnp.concatenate(halves(dt * e_out), axis=1)
            dt_cat[s] = jnp.concatenate(halves(dt), axis=1)
            tot1x[s] = spread(rows_of(tot1), sel)

        loop(0, seqs, delta)
        other_blocks(lambda b: dec_copy(b, me).start())

    @pl.when(jnp.logical_and(i >= 1, i < PIECES))
    def _():
        zx.finish(i, piece(i))

    def act_at(t, lag, act):
        u = t - 1 - lag
        pl.when(jnp.logical_and(u >= 0, u < TILES))(lambda: act(u))

    def close(u):
        unit_decays(u)
        ex.close(u)

    def scan(u):
        unit_decays(u)
        ex.scan(u)

    def middle(u):
        unit_decays(u)
        ex.middle(u)

    @pl.when(i == 3)
    def _():
        other_blocks(lambda b: dec_copy(b, b).wait_recv())

    def wave(t):
        act_at(t, CLOSE_LAG, close)
        act_at(t, SCAN_LAG, scan)
        act_at(t, MIDDLE_LAG, middle)

    wave(i)

    @pl.when(jnp.logical_and(i >= 1, i <= TILES))
    def _():
        u = i - 1
        cols = unit_cols(u)

        def x_tile(s):
            a = conv_tile(s, piece(i), cols)
            xs_s[s, :, cols] = a.astype(bf16)
            xw = (a * mm(out_cat[s], sel[:, cols])).astype(bf16)
            s0 = mm(bt[s, :, :HALF], xw[:HALF])
            s1 = mm(bt[s, :, HALF:], xw[HALF:])
            st0[s] = s0.astype(bf16)
            low = (tot1x[s, :, cols][0:1] * s0 + s1).astype(bf16)
            loc[s] = low
            ex.buf[u, s] = low

        loop(0, seqs, x_tile)
        ex.start(u)

    @pl.when(i > TILES)
    def _():
        u = i - 1 - TILES
        causal, low_lanes = masks()

        def intra(s):
            cum = cumout[s]
            dtx = mm(dt_cat[s], sel[:, unit_cols(u)])
            for h in range(2):
                p = 2 * u + h
                lanes = slice(h * HALF, (h + 1) * HALF)
                decays = pair_decays(cum, cum_t.at[s], p, causal)
                for q in range(2):
                    rows = both(q)
                    m = jnp.concatenate([(decays[2 * q + a] * scores[s, q]).astype(bf16) for a in range(2)], axis=1)
                    x = xs_s[s, rows, pl.ds(pl.multiple_of(p * HALF, HALF), HALF)].astype(f32) * dtx[rows, lanes]
                    x = jnp.concatenate([jnp.where(low_lanes, x, 0.0), jnp.where(low_lanes, 0.0, x)], axis=0)
                    ylocal[s, rows, lanes] = mm(m, x.astype(bf16)).astype(bf16)
            gate[s] = mm(ext[s, RIM:], w[:, piece(i)]).astype(bf16)

        loop(0, seqs, intra)

    @pl.when(i == PIECES - 1)
    def _():
        keep_w.start()
        keep_d.start()
        decs_out[...] = decs[...]
        wo.forward(last, slice(None))
        loop(PIECES, TILES + CLOSE_LAG + 1, wave)
        loop(0, TILES, ex.finish)
        wo.finish(last, slice(None))
        wo.finish_chip(1)
        zx.drain_chip(0)
        wo.drain_chip(1)
        de.drain_chip(2)
        de.drain(small_piece, slice(None))
        zx.drain(0, first_piece)
        loop(1, PIECES, lambda p: zx.drain(p, piece(p)))
        wo.drain(last, slice(None))
        other_blocks(lambda b: dec_copy(b, me).wait_send())
        pl.when(me < count - 1)(lambda: halo_copy.wait_send())
        keep_w.wait()
        keep_d.wait()


def middle_kernel(
    lengths, skip_in, tok, cot, ylocal, gate, xb, vin, cumin, st0, sin, decs, wout, ggain_in, nt,
    mixed, dyout, ggate, wred, dir1, gskip, gggain, dxs, dbc, xgate, xout, later,
    sel, skip, ggain, cum_t, einx, ys, gs, ss, s_in, dcs, dy_s, ml_s, gg_s, dr_s, pgate, pout, g_s, dg_s, *exchange,
):
    i = pl.program_id(0)
    seqs = dy_s.shape[0]
    ex = Exchange(True, lambda u, rows: later.at[pl.ds(u, 1), rows, :], exchange[:9], exchange[9])
    members = lax.axis_size("group")
    gates = Reducer(pgate, xgate, D // members, GATE_CHUNK, False, exchange[10:13], None)
    outs = Reducer(pout, xout, DIN // members, OUT_CHUNK, True, exchange[13:16], None)

    def span(s):
        return pl.ds(pl.multiple_of(s * SPAN, SPAN), SPAN)

    def group_wave(t):
        gates.wave(t - 2 * seqs - 3, [gates.x_done], gates.each)
        outs.wave(t - 2 * seqs - 3 - gates.chunks, [outs.x_done], outs.each)

    def wave(t):
        group_wave(t)

        def act_at(lag, act):
            u = lax.div(t - lag, 2)

            def run():
                ex.decx[0] = spread(decs[u], sel)
                act(u)

            pl.when(jnp.logical_and(t >= lag, jnp.logical_and(2 * u + lag == t, u < seqs)))(run)

        act_at(BACK_LAGS[2], ex.close)
        act_at(BACK_LAGS[1], ex.scan)
        act_at(BACK_LAGS[0], ex.middle)

    @pl.when(i == 0)
    def _():
        greet(("ctx", "group"))
        sel[...] = head_map()
        skip[...] = spread(rows_of(lane_row(skip_in)), sel)[0:1]
        ggain[...] = row_of(ggain_in)
        gskip[...] = jnp.zeros_like(gskip)
        gggain[...] = jnp.zeros_like(gggain)

    @pl.when(i == 1)
    def _():
        settle(("ctx", "group"))

    @pl.when(jnp.logical_and(i >= 1, i <= seqs))
    def _():
        ex.start(i - 1)

    wave(2 * i)

    @pl.when(i < seqs)
    def _():
        s = i
        cum = cumin[0]
        e_in, e_out, tot0, tot1, total = local_decays(cum)
        einx[...] = spread(e_in, sel)
        tot0x = spread(rows_of(tot0), sel)[0:1]
        s_in[0] = sin[0]
        s_in[1] = (tot0x * sin[0].astype(f32) + st0[0].astype(f32)).astype(bf16)
        cc = xb[0, :, DIN + NSTATE :]

        def gate_step(j, total_sq):
            cols = pl.ds(pl.multiple_of(j * TILE, TILE), TILE)
            for q in range(2):
                rows = both(q)
                ys[rows, cols] = ylocal[0, rows, cols].astype(f32) + einx[rows, cols] * mm(cc[rows], s_in[q, :, cols])
            y = ys[:, cols] + skip[:, cols] * xb[0, :, cols].astype(f32)
            g = gate[0, :, cols].astype(f32)
            gated = y * (g * gate_of(g))
            gs[:, cols] = gated
            sq = gated * gated
            return total_sq + sq[:, :HALF] + sq[:, HALF:]

        wave(2 * i + 1)
        sq = lax.fori_loop(0, DIN // TILE, gate_step, jnp.zeros((SPAN, HALF), f32))
        inv = lax.rsqrt(jnp.sum(sq, axis=1, keepdims=True) * (1.0 / DIN) + EPS)
        live = live_rows(lengths, s)
        drive = (live * cot[0].astype(f32)).astype(bf16)
        dr_s[span(s), :] = drive

        def back_step(j, acc):
            cols = pl.ds(pl.multiple_of(j * TILE, TILE), TILE)
            gm = mm_nt(drive, wout[cols, :])
            gated = gs[:, cols]
            unit = gated * inv
            ml_s[span(s), cols] = (unit * ggain[:, cols]).astype(bf16)
            gggain[:, cols] += jnp.sum(gm * unit, axis=0, keepdims=True)
            scaled = gm * ggain[:, cols]
            ss[:, cols] = scaled
            prod = scaled * gated
            return acc + prod[:, :HALF] + prod[:, HALF:]

        dots = lax.fori_loop(0, DIN // TILE, back_step, jnp.zeros((SPAN, HALF), f32))
        dots = jnp.sum(dots, axis=1, keepdims=True) * (1.0 / DIN)
        corr = inv * inv * inv * dots
        cct = jnp.transpose(cc.astype(f32)).astype(bf16)
        acc = jnp.zeros((SPAN, HALF), f32)
        dc = [jnp.zeros((HALF, HALF), f32) for _ in range(2)]
        for j in range(DIN // TILE):
            cols = slice(j * TILE, (j + 1) * TILE)
            g = gate[0, :, cols].astype(f32)
            sg = gate_of(g)
            sl = g * sg
            grad_gated = inv * ss[:, cols] - gs[:, cols] * corr
            dy = grad_gated * sl
            yn = ys[:, cols]
            x = xb[0, :, cols].astype(f32)
            y = yn + skip[:, cols] * x
            low = (grad_gated * y * (sg + sl * (1.0 - sg))).astype(bf16)
            ggate[0, :, cols] = low
            gg_s[span(s), cols] = low
            dyb = dy.astype(bf16)
            dyout[0, :, cols] = dyb
            dy_s[s, :, cols] = dyb
            gskip[:, cols] += jnp.sum(dy * x, axis=0, keepdims=True)
            acc = acc + gather_heads(dy * yn, sel[:HALF, cols])
            dye = (dy * einx[:, cols]).astype(bf16)
            d0 = mm(cct[:, :HALF], dye[:HALF])
            d1 = mm(cct[:, HALF:], dye[HALF:])
            dir1[0, :, cols] = d1.astype(bf16)
            ex.buf[s, 0, :, cols] = (d0 + tot0x[:, cols] * d1).astype(bf16)
            for q in range(2):
                dc[q] = dc[q] + mm_nt(dye[both(q)], s_in[q, :, cols])
        wred[0] = acc
        for q in range(2):
            dcs[s, both(q)] = dc[q]

    @pl.when(i >= seqs)
    def _():
        s = i - seqs
        causal, low_lanes = masks()
        cum = cumin[0]
        for q in range(2):
            cum_t[q] = jnp.transpose(cum[both(q)])
        einx[...] = spread(softplus(vin[0]), sel)
        bb = xb[0, :, DIN : DIN + NSTATE]
        cc = xb[0, :, DIN + NSTATE :]
        for q in range(2):
            g_s[q] = mm_nt(cc[both(q)], bb[both(q)])
        dg_s[...] = jnp.zeros_like(dg_s)

        def pair_step(p):
            cols = pl.ds(pl.multiple_of(p * HALF, HALF), HALF)
            decays = pair_decays(cum, cum_t, p, causal)
            for q in range(2):
                rows = both(q)
                xsb = (xb[0, rows, cols].astype(f32) * einx[rows, cols]).astype(bf16)
                dyb = dy_s[s, rows, cols]
                dyf = dyb.astype(f32)
                grads = []
                for a in range(2):
                    m = (decays[2 * q + a] * g_s[q]).astype(bf16)
                    grads.append(mm_tn(m, dyb))
                    mine = low_lanes if a == 0 else jnp.logical_not(low_lanes)
                    dm = mm_nt(jnp.where(mine, dyf, 0.0).astype(bf16), xsb)
                    dg_s[q] += dm * decays[2 * q + a]
                dxs[0, rows, cols] = jnp.where(low_lanes, grads[0], grads[1]).astype(bf16)

        @pl.when(s == 0)
        def _():
            for k in range(gates.chunks):
                cols = slice(k * GATE_CHUNK, (k + 1) * GATE_CHUNK)
                pgate[:, cols] = mm(nt[...], gg_s[:, cols]).astype(bf16)
                gates.m_start(k)

        @pl.when(s == 1)
        def _():
            loop(0, outs.chunks, outs.m_done)

        def two_pairs(pp):
            for h in range(2):
                pair_step(2 * pp + h)

        loop(0, PAIRS // 4, two_pairs)
        wave(2 * i + 1)

        @pl.when(s == 0)
        def _():
            loop(0, gates.chunks, gates.m_done)

            def out_rows(r):
                rows = pl.ds(pl.multiple_of(r * TILE, TILE), TILE)
                pout[rows, :] = mm_tn(ml_s[:, rows], dr_s[...]).astype(bf16)

            loop(0, DIN // TILE, out_rows)
            loop(0, outs.chunks, outs.m_start)

        loop(PAIRS // 4, PAIRS // 2, two_pairs)
        for q in range(2):
            rows = both(q)
            dg = dg_s[q].astype(bf16)
            dbc[0, rows, :NSTATE] = mm_tn(dg, cc[rows])
            dbc[0, rows, NSTATE:] = mm(dg, bb[rows]) + dcs[s, rows]
        live = live_rows(lengths, s)
        for j in range(D // TILE):
            cols = slice(j * TILE, (j + 1) * TILE)
            mixed[0, :, cols] = (live * (tok[0, :, cols].astype(f32) + mm(ml_s[span(s), :], wout[:, cols]))).astype(bf16)

    @pl.when(i == 2 * seqs - 1)
    def _():
        loop(4 * seqs, max(2 * seqs + BACK_LAGS[2] - 1, 2 * seqs + 3 + gates.chunks + outs.chunks), wave)
        loop(0, seqs, ex.finish)
        for r in (gates, outs):
            loop(0, r.chunks, r.drain_group)


def back_kernel(
    lengths, dl, skip_in, tok, cot, rhalo, gain, ggate, w_any, wd, cin, xb, spb, bc, dy, dxs, dir1, later, sin, loc,
    vin, cumin, wred, dbc, cw, nt, nth, xgate, xout, gskip, gggain,
    gtok, rzx, rout, small_out, ggain_out,
    sel, skip, wfull, w_sem, dt_cat, eo_cat, tots, db_s, qacc, ends, gp, gz_s, gzh_s, pconv, gcw, gcb, gdb, gdl, ggain,
    rim_out, rim_in, rim_send, rim_recv, *comm,
):
    i = pl.program_id(0)
    seqs = rhalo.shape[0]
    count = lax.axis_size("ctx")
    me = lax.axis_index("ctx")
    members = lax.axis_size("group")
    gates = Reducer(None, rzx, D // members, GATE_CHUNK, False, None, (xgate,) + comm[0:5])
    outs = Reducer(None, rout, DIN // members, OUT_CHUNK, True, None, (xout,) + comm[5:10])
    convs = Reducer(pconv, rzx, D // members, CONV_CHUNK, False, comm[10:13], comm[13:19])
    convs.base = DIN
    load_w = pltpu.make_async_copy(w_any, wfull, w_sem.at[0])
    little, least = Small(*comm[19:23]), Small(*comm[23:27])
    bc_step = TILES

    last_conv = 2 * bc_step + 5

    def conv_at(t):
        k = lax.div(t - 7, 4)
        even = jnp.logical_and(t >= 7, jnp.logical_and(lax.rem(t - 7, 4) == 0, k < convs.chunks - 1))
        last = t == last_conv
        return jnp.where(last, convs.chunks - 1, k), jnp.logical_or(even, last)

    def wave(t):
        for r, at in ((gates, 2), (outs, 2 + gates.chunks)):
            r.wave(t - at, [r.y_done, r.z_done, r.b_done, r.f_done], r.each)
        convs.wave(t, [convs.x_done, convs.y_done, convs.z_done, convs.b_done, convs.f_done], conv_at, CONV_LAG)

    def rim_copy(q):
        return remote(rim_out.at[q], rim_in.at[q], rim_send.at[q], rim_recv.at[q], ctx=lax.rem(me + count - 1, count))

    def span(s):
        return pl.ds(pl.multiple_of(s * SPAN, SPAN), SPAN)

    def edge(s):
        return pl.ds(pl.multiple_of(s * RIM, RIM), RIM)

    def back(rows, grad):
        rows, inv, _ = normalized(rows, row_of(gain))
        ggain[...] += jnp.sum(grad * rows * inv, axis=0, keepdims=True)
        gained = row_of(gain) * grad
        mean = jnp.mean(gained * rows, axis=-1, keepdims=True)
        return inv * gained - rows * (inv * inv * inv * mean)

    @pl.when(i == 0)
    def _():
        meet(("ctx", "group"))
        for r in (gates, outs):
            loop(0, r.chunks, r.y_start)
        load_w.start()
        sel[...] = head_map()
        skip[...] = spread(rows_of(lane_row(skip_in)), sel)[0:1]
        for acc in (db_s, qacc, ends, gcw, gcb, gdb, gdl, ggain):
            acc[...] = jnp.zeros_like(acc)
        gp[0:RIM] = jnp.zeros((RIM, TILE), f32)
        gp[RIM + SPAN :] = jnp.zeros((8, TILE), f32)
        pconv[:, CONVW + HALF :] = jnp.zeros((D, GZW - CONVW - HALF), bf16)

        def setup(s):
            dt = softplus(vin[s])
            _, e_out, _, tot1, total = local_decays(cumin[s])
            dt_cat[s] = jnp.concatenate(halves(dt), axis=1)
            eo_cat[s] = jnp.concatenate(halves(e_out), axis=1)
            both_rows = jnp.concatenate([rows_of(tot1), rows_of(total)], axis=0)
            tots[s] = spread(both_rows, sel)

        loop(0, seqs, setup)

    def conv_back(s, dact, cols):
        gco = dact * spb[s].astype(f32)
        gp[RIM : RIM + SPAN] = gco
        gcb[:, cols] += jnp.sum(gco, axis=0, keepdims=True)
        own = cin[s, RIM:].astype(f32)
        before = cin[s, :RIM].astype(f32)
        main = jnp.zeros((SPAN, TILE), f32)
        rim = jnp.zeros((RIM, TILE), f32)
        for k in range(KCONV):
            ahead = KCONV - 1 - k
            moved = gco if ahead == 0 else gp[RIM + ahead : RIM + ahead + SPAN]
            early = gp[ahead : ahead + RIM]
            main = main + cw[k : k + 1, cols] * moved
            rim = rim + cw[k : k + 1, cols] * early
            gcw[k : k + 1, cols] += jnp.sum(own * moved, axis=0, keepdims=True) + jnp.sum(
                before * early, axis=0, keepdims=True
            )
        gz_s[span(s), cols] = main.astype(bf16)
        gzh_s[edge(s), cols] = rim.astype(bf16)

    def partial(cols):
        pconv[:, cols] = (mm(nt[...], gz_s[:, cols]) + mm(nth[...], gzh_s[:, cols])).astype(bf16)

    wave(2 * i)

    @pl.when(i < bc_step)
    def _():
        cols = pl.ds(pl.multiple_of(i * TILE, TILE), TILE)

        def x_tile(s):
            dte = mm(dt_cat[s], sel[:, cols])
            eo = mm(eo_cat[s], sel[:, cols])
            near = later[s]
            near32 = near.astype(f32)
            tot = tots[s, :, cols]
            reach = [(dir1[s].astype(f32) + tot[0:1] * near32).astype(bf16), near]
            fed = jnp.concatenate(
                [mm(bc[s, both(q), :NSTATE], reach[q]) for q in range(2)], axis=0
            )
            x = xb[s].astype(f32)
            dx_s = dxs[s].astype(f32) + eo * fed
            qacc[s] += gather_heads(x * dx_s, sel[:HALF, cols])
            xw = (x * dte * eo).astype(bf16)
            for q in range(2):
                db_s[s, both(q)] += mm_nt(xw[both(q)], reach[q])
            held = near32 * (tot[8:9] * sin[s].astype(f32) + loc[s].astype(f32))
            ends[s] += gather_heads(rows_of(jnp.sum(held, axis=0, keepdims=True)), sel[:HALF, cols])
            conv_back(s, dte * dx_s + skip[:, cols] * dy[s].astype(f32), cols)

        loop(0, seqs // 2, x_tile)

        @pl.when(jnp.logical_and(lax.rem(i, 2) == 0, i >= 2))
        def _():
            convs.m_done(lax.div(i, 2) - 1)

        wave(2 * i + 1)
        loop(seqs // 2, seqs, x_tile)
        partial(cols)

        @pl.when(lax.rem(i, 2) == 1)
        def _():
            convs.m_start(lax.div(i, 2))

    @pl.when(i == bc_step)
    def _():
        cols = slice(DIN, CONVW)
        rate = jnp.exp(lane_row(dl))

        def bc_tile(s):
            conv_back(s, jnp.concatenate([dbc[s, :, :NSTATE] + db_s[s], dbc[s, :, NSTATE:]], axis=1), cols)
            v = vin[s]
            dt = softplus(v)
            q = qacc[s]
            at_end = lax.broadcasted_iota(jnp.int32, (SPAN, 1), 0) == SPAN - 1
            dcum = wred[s] - dt * q + jnp.where(at_end, ends[s][0:1], 0.0)
            glog = running_sum(dcum, False)
            gpd = (q - rate * glog) * sigmoid(v)
            lanes = lax.broadcasted_iota(jnp.int32, (SPAN, HALF), 1) < HEADS
            gpd = jnp.where(lanes, gpd, 0.0)
            gz_s[span(s), CONVW : CONVW + HALF] = gpd.astype(bf16)
            gdb[...] += jnp.sum(gpd, axis=0, keepdims=True)
            gdl[...] += -rate * jnp.sum(dt * glog, axis=0, keepdims=True)

        loop(0, seqs, bc_tile)
        convs.m_done(convs.chunks - 2)
        wave(2 * i + 1)
        partial(cols)
        pconv[:, CONVW : CONVW + HALF] = mm(nt[...], gz_s[:, CONVW : CONVW + HALF]).astype(bf16)
        convs.m_start(convs.chunks - 1)
        rows = [gcw[k : k + 1, j * HALF : (j + 1) * HALF] for k in range(KCONV) for j in range(CONVW // HALF)]
        rows += [gcb[:, j * HALF : (j + 1) * HALF] for j in range(CONVW // HALF)]
        rows += [gdb[...], gdl[...]]
        rows += [gather_heads(rows_of(gskip[...]), sel[:HALF])[0:1]]
        rows += [gggain[:, j * HALF : (j + 1) * HALF] for j in range(PAIRS)]
        little.held[0, SMALL_ROWS - 8 :] = jnp.zeros((8, HALF), f32)
        for r, row in enumerate(rows):
            little.held[0, r : r + 1, :] = row
        little.start(0)
        load_w.wait()
        edges = mm_nt(gzh_s[...], wfull[:, DIN:ZXW])
        for q in range(seqs):
            rim_out[q] = back(rhalo[q], edges[q * RIM : (q + 1) * RIM]).astype(bf16)
            pl.when(me > 0)(lambda q=q: rim_copy(q).start())

        @pl.when(me == count - 1)
        def _():
            rim_in[...] = jnp.zeros_like(rim_in)

    @pl.when(i == bc_step + 2)
    def _():
        little.done(0)
        little.start(1)

    @pl.when(i > bc_step)
    def _():
        s = i - bc_step - 1
        grad = mm_nt(gz_s[span(s), :CONVW], wfull[:, DIN:]) + mm_nt(ggate[0], wfull[:, :DIN])
        grad = grad + mm_nt(gz_s[span(s), CONVW:], wd[...])

        @pl.when(s == 0)
        def _():
            convs.m_done(convs.chunks - 1)

        wave(2 * i + 1)
        live = live_rows(lengths, s)
        out = live * cot[0].astype(f32) + back(tok[0], grad)
        gtok[0, : SPAN - RIM] = out[: SPAN - RIM].astype(bf16)
        pl.when(me < count - 1)(lambda: rim_copy(s).wait_recv())
        gtok[0, SPAN - RIM :] = (out[SPAN - RIM :] + rim_in[s].astype(f32)).astype(bf16)

    @pl.when(i == bc_step + seqs)
    def _():
        least.held[0] = jnp.zeros_like(least.held[0])
        for j in range(D // HALF):
            least.held[0, j : j + 1, :] = ggain[:, j * HALF : (j + 1) * HALF]
        least.start(0)
        little.done(1)
        small_out[...] = little.held[2]
        ends_at = max(last_conv + 4 * CONV_LAG, 1 + gates.chunks + outs.chunks + 3 * STAGE_LAG) + 1
        here = 2 * (bc_step + seqs) + 2
        loop(here, min(here + 2, ends_at), wave)
        least.done(0)
        least.start(1)
        loop(here + 2, ends_at, wave)
        for r in (gates, outs, convs):
            loop(0, r.chunks, r.drain_ctx)
        loop(0, convs.chunks, convs.drain_group)
        little.drain()
        for q in range(seqs):
            pl.when(me > 0)(lambda q=q: rim_copy(q).wait_send())
        least.done(1)
        ggain_out[...] = least.held[2]
        least.drain()


def done_kernel(rzx, rout, small, gain_sum, g_gain, g_zx, g_delta, g_out, g_cw, g_cb, g_db, g_dl, g_skip, g_gated):
    g_zx[...] = rzx[:, :ZXW].astype(f32)
    g_delta[...] = rzx[:, ZXW : ZXW + HEADS].astype(f32)
    g_out[...] = rout[...].astype(f32)
    tiles = CONVW // HALF
    for k in range(KCONV):
        for j in range(tiles):
            g_cw[k : k + 1, j * HALF : (j + 1) * HALF] = small[k * tiles + j : k * tiles + j + 1, :]
    at = KCONV * tiles
    for j in range(tiles):
        g_cb[j * HALF : (j + 1) * HALF] = small[at + j, :]
    at += tiles
    for ref in (g_db, g_dl, g_skip):
        ref[...] = small[at, :][:HEADS]
        at += 1
    for j in range(PAIRS):
        g_gated[j * HALF : (j + 1) * HALF] = small[at + j, :]
    for j in range(D // HALF):
        g_gain[j * HALF : (j + 1) * HALF] = gain_sum[j, :]


def whole(shape):
    zeros = (0,) * len(shape)
    return pl.BlockSpec(shape, lambda s: zeros, pipeline_mode=pl.Buffered(1))


def summed(shape):
    zeros = (0,) * len(shape)
    return pl.BlockSpec(shape, lambda s: zeros)


def per_seq(*shape):
    zeros = (0,) * len(shape)
    return pl.BlockSpec((1,) + shape, lambda s: (s,) + zeros)


SMEM = pl.BlockSpec(memory_space=pltpu.SMEM)
ANY = pl.BlockSpec(memory_space=pl.ANY)


def staged(seqs, phase, *shape):
    zeros = (0,) * len(shape)
    if phase == 0:
        return pl.BlockSpec((1,) + shape, lambda i: (jnp.minimum(i, seqs - 1),) + zeros)
    if phase == 1:
        return pl.BlockSpec((1,) + shape, lambda i: (jnp.maximum(i - seqs, 0),) + zeros)
    return pl.BlockSpec((1,) + shape, lambda i: (lax.rem(i, seqs),) + zeros)


def call(kernel, steps, in_specs, outs, scratch, name, collective=None):
    params = dict(vmem_limit_bytes=VMEM_LIMIT)
    if collective is not None:
        params.update(collective_id=collective, has_side_effects=True)
    return pl.pallas_call(
        kernel,
        grid=(steps,),
        in_specs=in_specs,
        out_specs=[o[0] for o in outs],
        out_shape=[jax.ShapeDtypeStruct(o[1], o[2]) for o in outs],
        scratch_shapes=[pltpu.VMEM(*sc) if isinstance(sc, tuple) else sc for sc in scratch],
        compiler_params=pltpu.CompilerParams(**params),
        name=name,
    )


def local(
    tokens_in, seq_lengths, norm_gain, w_zx, w_delta, w_out, conv_weight, conv_bias,
    delta_bias, decay_log, skip_gain, gated_gain, cotangent,
):
    seqs = tokens_in.shape[0]
    count = lax.axis_size("ctx")
    group = lax.axis_size("group")
    chips = max(group // 2, 1)
    w_delta = jnp.pad(w_delta, ((0, 0), (0, HALF - HEADS)))
    dma = pltpu.SemaphoreType.DMA
    at0 = lambda *shape: staged(seqs, 0, *shape)
    at1 = lambda *shape: staged(seqs, 1, *shape)
    at01 = lambda *shape: staged(seqs, 2, *shape)

    def tiled(rows, first, lead=None):
        def index(i):
            u = jnp.clip(i - first, 0, TILES - 1)
            return (0, 0, u if lead is None else jnp.where(i == 0, lead, u))

        return pl.BlockSpec((seqs, rows, TILE), index)

    state = (seqs, NSTATE, DIN)
    nt, nth, rhalo, cin, xb, spb, vraw, cum, st0, loc, ylocal, gate, decs, wfull, wdfull, wofull, state_in = call(
        front_kernel,
        PIECES,
        [whole((seqs, SPAN, D)), ANY, ANY, ANY, ANY, whole((D,)), whole((KCONV, CONVW)), whole((CONVW,)), SMEM, SMEM],
        [
            (summed((D, seqs * SPAN)), (D, seqs * SPAN), bf16),
            (summed((D, seqs * RIM)), (D, seqs * RIM), bf16),
            (summed((seqs, RIM, D)), (seqs, RIM, D), bf16),
            (tiled(RIM + SPAN, 1, TILES), (seqs, RIM + SPAN, CONVW), bf16),
            (tiled(SPAN, 1, TILES), (seqs, SPAN, CONVW), bf16),
            (tiled(SPAN, 1, TILES), (seqs, SPAN, CONVW), bf16),
            (summed((seqs, SPAN, HALF)), (seqs, SPAN, HALF), f32),
            (summed((seqs, SPAN, HALF)), (seqs, SPAN, HALF), f32),
            (tiled(NSTATE, 1), state, bf16),
            (tiled(NSTATE, 1), state, bf16),
            (tiled(SPAN, TILES + 1), (seqs, SPAN, DIN), bf16),
            (tiled(SPAN, TILES + 1), (seqs, SPAN, DIN), bf16),
            (summed((seqs, count * 8, HALF)), (seqs, count * 8, HALF), f32),
            (ANY, (D, ZXW), bf16),
            (ANY, (D, HALF), bf16),
            (ANY, (DIN, D), bf16),
            (ANY, state, bf16),
        ],
        [((2 * HALF, DIN), bf16), ((seqs, RIM, D), bf16), ((seqs * RIM, D), f32), ((seqs, RIM + SPAN, D), bf16), ((D, ZXW), bf16),
         ((D, HALF), bf16), ((1, CONVW), f32),
         ((seqs, RIM + SPAN, TILE), f32), ((seqs, SPAN, DIN), bf16), ((seqs, NSTATE, SPAN), bf16),
         ((seqs, 2, HALF, HALF), f32), ((seqs, SPAN, 2 * HALF), bf16), ((seqs, SPAN, 2 * HALF), bf16),
         ((seqs, 2, HALF, HALF), f32), ((seqs, 8, DIN), f32), ((seqs, count * 8, HALF), f32)]
        + [dma((2,))] + [dma((PIECES + 2, chips))] * 4 + [dma((3,)), dma((2,)), dma((count,)), dma((count,))]
        + Exchange.scratch(TILES, seqs, TILE, count),
        "front",
        0,
    )(tokens_in, tokens_in, w_zx, w_delta, w_out, norm_gain, conv_weight, conv_bias, delta_bias, decay_log)

    x_gate_shape = (DIN // GATE_CHUNK, D // group, GATE_CHUNK)
    x_out_shape = (D // OUT_CHUNK, DIN // group, OUT_CHUNK)
    mixed_out, dy, ggate, wred, dir1, gskip, gggain, dxs, dbc, x_gate, x_out, later = call(
        middle_kernel,
        2 * seqs,
        [SMEM, SMEM, at1(SPAN, D), at0(SPAN, D), at0(SPAN, DIN), at0(SPAN, DIN), at01(SPAN, CONVW), at01(SPAN, HALF),
         at01(SPAN, HALF), at0(NSTATE, DIN), at0(NSTATE, DIN), whole((seqs, count * 8, HALF)), whole((DIN, D)),
         whole((DIN,)), whole((D, seqs * SPAN))],
        [
            (at1(SPAN, D), (seqs, SPAN, D), bf16),
            (at0(SPAN, DIN), (seqs, SPAN, DIN), bf16),
            (at0(SPAN, DIN), (seqs, SPAN, DIN), bf16),
            (at0(SPAN, HALF), (seqs, SPAN, HALF), f32),
            (at0(NSTATE, DIN), (seqs, NSTATE, DIN), bf16),
            (summed((1, DIN)), (1, DIN), f32),
            (summed((1, DIN)), (1, DIN), f32),
            (at1(SPAN, DIN), (seqs, SPAN, DIN), bf16),
            (at1(SPAN, 2 * NSTATE), (seqs, SPAN, 2 * NSTATE), f32),
            (summed(x_gate_shape), x_gate_shape, bf16),
            (summed(x_out_shape), x_out_shape, bf16),
            (ANY, (seqs, NSTATE, DIN), bf16),
        ],
        [((2 * HALF, DIN), bf16), ((1, DIN), f32), ((1, DIN), f32), ((2, HALF, HALF), f32), ((SPAN, DIN), f32), ((SPAN, DIN), f32), ((SPAN, DIN), f32),
         ((SPAN, DIN), f32), ((2, NSTATE, DIN), bf16), ((seqs, SPAN, HALF), f32), ((seqs, SPAN, DIN), bf16),
         ((seqs * SPAN, DIN), bf16), ((seqs * SPAN, DIN), bf16), ((seqs * SPAN, D), bf16), ((D, DIN), bf16), ((DIN, D), bf16),
         ((2, HALF, HALF), f32), ((2, HALF, HALF), f32)]
        + Exchange.scratch(seqs, 1, DIN, count)
        + Reducer.group_scratch(*x_gate_shape, group)
        + Reducer.group_scratch(*x_out_shape, group),
        "middle",
        1,
    )(seq_lengths, skip_gain, tokens_in, cotangent, ylocal, gate, xb, vraw, cum, st0, state_in, decs, wofull, gated_gain, nt)

    def tile_in(rows, tiles):
        return pl.BlockSpec((seqs, rows, TILE), lambda i: (0, 0, jnp.minimum(i, tiles - 1)))

    def late(*shape):
        zeros = (0,) * len(shape)
        return pl.BlockSpec((1,) + shape, lambda i: (jnp.clip(i - TILES - 1, 0, seqs - 1),) + zeros)

    bc_spec = pl.BlockSpec((seqs, SPAN, TILE), lambda i: (0, 0, TILES), pipeline_mode=pl.Buffered(1))
    height = SMALL_ROWS
    x_conv_shape = (GZW // CONV_CHUNK, D // group, CONV_CHUNK)
    gtok, r_zx, r_out, small, gain_sum = call(
        back_kernel,
        TILES + 1 + seqs,
        [SMEM, SMEM, SMEM, late(SPAN, D), late(SPAN, D), whole((seqs, RIM, D)), whole((D,)), late(SPAN, DIN), ANY, whole((D, HALF)),
         tile_in(RIM + SPAN, TILES + 1), tile_in(SPAN, TILES + 1), tile_in(SPAN, TILES + 1), bc_spec, tile_in(SPAN, TILES),
         tile_in(SPAN, TILES), tile_in(NSTATE, TILES), tile_in(NSTATE, TILES), tile_in(NSTATE, TILES), tile_in(NSTATE, TILES),
         whole((seqs, SPAN, HALF)), whole((seqs, SPAN, HALF)), whole((seqs, SPAN, HALF)), whole((seqs, SPAN, 2 * NSTATE)),
         whole((KCONV, CONVW)), whole((D, seqs * SPAN)), whole((D, seqs * RIM)),
         whole(x_gate_shape), whole(x_out_shape), whole((1, DIN)), whole((1, DIN))],
        [
            (late(SPAN, D), (seqs, SPAN, D), bf16),
            (summed((D // group, DIN + GZW)), (D // group, DIN + GZW), bf16),
            (summed((DIN // group, D)), (DIN // group, D), bf16),
            (summed((height, HALF)), (height, HALF), f32),
            (summed((8, HALF)), (8, HALF), f32),
        ],
        [((2 * HALF, DIN), bf16), ((1, DIN), f32), ((D, ZXW), bf16), dma((1,)), ((seqs, SPAN, 2 * HALF), bf16),
         ((seqs, SPAN, 2 * HALF), bf16), ((seqs, 16, DIN), f32),
         ((seqs, SPAN, NSTATE), f32), ((seqs, SPAN, HALF), f32), ((seqs, 8, HALF), f32), ((RIM + SPAN + 8, TILE), f32),
         ((seqs * SPAN, CONVW + HALF), bf16), ((seqs * RIM, CONVW), bf16), ((D, GZW), bf16), ((KCONV, CONVW), f32),
         ((1, CONVW), f32), ((1, HALF), f32), ((1, HALF), f32), ((1, D), f32), ((seqs, RIM, D), bf16), ((seqs, RIM, D), bf16),
         dma((seqs,)), dma((seqs,))]
        + Reducer.ctx_scratch(*x_gate_shape, False, count)
        + Reducer.ctx_scratch(*x_out_shape, True, count)
        + Reducer.group_scratch(*x_conv_shape, group)
        + [(x_conv_shape, bf16)]
        + Reducer.ctx_scratch(*x_conv_shape, False, count)
        + Small.scratch(height, group, count)
        + Small.scratch(8, group, count),
        "back",
        2,
    )(seq_lengths, decay_log, skip_gain, tokens_in, cotangent, rhalo, norm_gain, ggate, wfull, wdfull, cin, xb, spb, xb, dy, dxs, dir1, later, state_in, loc,
      vraw, cum, wred, dbc, conv_weight, nt, nth, x_gate, x_out, gskip, gggain)

    shapes = [(D,), (D // group, ZXW), (D // group, HEADS), (DIN // group, D), (KCONV, CONVW), (CONVW,), (HEADS,), (HEADS,),
              (HEADS,), (DIN,)]
    grads = pl.pallas_call(
        done_kernel,
        out_shape=[jax.ShapeDtypeStruct(shape, f32) for shape in shapes],
        name="done",
    )(r_zx, r_out, small, gain_sum)
    return (mixed_out, gtok, *grads)


def solution(mesh):
    rows = P("group", "ctx", None)
    own = P("group", None)
    in_specs = (rows, P("group"), P(), own, own, own, P(), P(), P(), P(), P(), P(), rows)
    out_specs = (rows, rows, P(), own, own, own, P(), P(), P(), P(), P(), P())
    return jax.shard_map(local, mesh=mesh, in_specs=in_specs, out_specs=out_specs, check_vma=False)
```

```python
import jax
import jax.numpy as jnp
from jax import lax
from jax.experimental import pallas as pl
from jax.experimental.pallas import tpu as pltpu
from jax.sharding import PartitionSpec as P

D = 768
HEADS = 24
HEADDIM = 64
NSTATE = 128
KCONV = 4
SPAN = 256
DIN = 1536
CONVW = 1792
ZXW = 3328
RIM = 16
HALF = 128
TILE = 256
PAIRS = 12
EPS = 1e-05

f32 = jnp.float32
bf16 = jnp.bfloat16
NT = (((1,), (1,)), ((), ()))
TN = (((0,), (0,)), ((), ()))
VMEM_LIMIT = 63 * 1024 * 1024
GATE_CHUNK = 512
OUT_CHUNK = 256
CONV_CHUNK = 512
BACK_LAGS = (4, 7, 9)
STAGE_LAG = 4
CONV_LAG = 3
MIDDLE_LAG = 2
SCAN_LAG = 4
HOPS = ("group", "ctx")
SMALL_ROWS = 88
CLOSE_LAG = 6
GZW = 2048


def mm(a, b):
    return jnp.dot(a, b, preferred_element_type=f32)


def mm_nt(a, b):
    return lax.dot_general(a, b, NT, preferred_element_type=f32)


def mm_tn(a, b):
    return lax.dot_general(a, b, TN, preferred_element_type=f32)


def halves(v):
    high = v.astype(bf16)
    return high, (v - high.astype(f32)).astype(bf16)


def head_map():
    rows = lax.broadcasted_iota(jnp.int32, (2 * HALF, DIN), 0) % HALF
    cols = lax.broadcasted_iota(jnp.int32, (2 * HALF, DIN), 1) // HEADDIM
    return jnp.where(rows == cols, 1.0, 0.0).astype(bf16)


def spread(v, sel):
    return mm(jnp.concatenate(halves(v), axis=1), sel[...])


def gather_heads(v, sel_part):
    high, low = halves(v)
    return mm_nt(high, sel_part) + mm_nt(low, sel_part)


def triangle(size, lower):
    rows = lax.broadcasted_iota(jnp.int32, (size, size), 0)
    cols = lax.broadcasted_iota(jnp.int32, (size, size), 1)
    keep = rows >= cols if lower else rows <= cols
    return jnp.where(keep, 1.0, 0.0).astype(f32)


def running_sum(v, lower):
    rest, terms = v, []
    for _ in range(3):
        high = rest.astype(bf16)
        rest = rest - high.astype(f32)
        terms.append(high)
    tri = triangle(v.shape[0], lower).astype(bf16)
    return mm(tri, terms[0]) + (mm(tri, terms[1]) + mm(tri, terms[2]))


def softplus(v):
    return jnp.maximum(v, 0.0) + jnp.log1p(jnp.exp(-jnp.abs(v)))


def sigmoid(v):
    return 1.0 / (1.0 + jnp.exp(-v))


def gate_of(v):
    return 0.5 * jnp.tanh(0.5 * v) + 0.5


def local_decays(cum):
    mid, end = cum[HALF - 1 : HALF], cum[SPAN - 1 : SPAN]
    rows = lax.broadcasted_iota(jnp.int32, (SPAN, 1), 0)
    first = rows < HALF
    start = jnp.where(first, 0.0, mid)
    stop = jnp.where(first, mid, end)
    return jnp.exp(cum - start), jnp.exp(stop - cum), jnp.exp(mid), jnp.exp(end - mid), jnp.exp(end)


def rows_of(v):
    return jnp.broadcast_to(v, (8, v.shape[1]))


def lane_row(ref):
    lanes = lax.broadcasted_iota(jnp.int32, (1, HALF), 1)
    row = jnp.zeros((1, HALF), f32)
    for h in range(HEADS):
        row = jnp.where(lanes == h, ref[h], row)
    return row


def row_of(ref):
    return ref[...].reshape(1, ref.shape[0])


def live_rows(lengths, s):
    start = lax.axis_index("ctx") * SPAN
    return (lax.broadcasted_iota(jnp.int32, (SPAN, 1), 0) + start < lengths[s]).astype(f32)


def normalized(rows, gain):
    rows = rows.astype(f32)
    inv = lax.rsqrt(jnp.mean(rows * rows, axis=-1, keepdims=True) + EPS)
    return rows, inv, (rows * inv * gain).astype(bf16)


def remote(src, dst, send_sem, recv_sem, **where):
    return pltpu.make_async_remote_copy(
        src_ref=src, dst_ref=dst, send_sem=send_sem, recv_sem=recv_sem,
        device_id=where, device_id_type=pl.DeviceIdType.MESH,
    )


def loop(start, stop, body):
    def step(i, c):
        body(i)
        return c

    lax.fori_loop(start, stop, step, 0)


def greet(axes):
    barrier = pltpu.get_barrier_semaphore()
    for axis in axes:
        size = lax.axis_size(axis)
        me = lax.axis_index(axis)

        def signal(d, axis=axis, size=size, me=me):
            pl.semaphore_signal(
                barrier, inc=1, device_id={axis: lax.rem(me + d, size)}, device_id_type=pl.DeviceIdType.MESH
            )

        loop(1, size, signal)


def settle(axes):
    pl.semaphore_wait(pltpu.get_barrier_semaphore(), sum(lax.axis_size(axis) - 1 for axis in axes))


def meet(axes):
    greet(axes)
    settle(axes)


class Exchange:
    def __init__(self, reverse, out_at, bufs, sems):
        self.reverse, self.out_at, self.sems = reverse, out_at, sems
        self.buf, self.y_buf, self.z_src, self.z_buf, self.z_back, self.p_buf, self.mine_buf, self.their_buf, self.decx = bufs
        self.depth = self.buf.shape[1]
        ctx = lax.axis_index("ctx")
        self.ctx = ctx
        self.outer = lax.axis_size("ctx") // 2
        self.owners = min(self.outer, 4)
        self.stride = self.outer // self.owners
        self.inner = lax.rem(ctx, 2)
        self.line = ctx // 2
        self.mine = self.line // self.stride
        self.half = NSTATE // 2
        self.rows = self.half // self.owners

    def half_rows(self, inner):
        return pl.ds(pl.multiple_of(inner * self.half, self.half), self.half)

    def part(self, j):
        return pl.ds(pl.multiple_of(j * self.rows, self.rows), self.rows)

    def other_owners(self, body):
        if self.stride == 1:
            loop(1, self.owners, lambda d: body(lax.rem(self.mine + d, self.owners)))
        else:
            loop(0, self.owners, lambda j: pl.when(j * self.stride != self.line)(lambda: body(j)))

    def other_lines(self, body):
        loop(1, self.outer, lambda d: body(lax.rem(self.line + d, self.outer)))

    def if_owner(self, body):
        if self.stride == 1:
            body()
        else:
            pl.when(self.mine * self.stride == self.line)(body)

    def y_copy(self, u):
        return remote(
            self.buf.at[u, :, self.half_rows(1 - self.inner)], self.y_buf.at[u], self.sems.at[0, u, 0], self.sems.at[1, u, 0],
            ctx=self.ctx + 1 - 2 * self.inner,
        )

    def z_copy(self, u, j, sender):
        return remote(
            self.z_src.at[u, :, self.part(j)], self.z_buf.at[u, sender], self.sems.at[2, u, j], self.sems.at[3, u, sender],
            ctx=j * self.stride * 2 + self.inner,
        )

    def b_copy(self, u, line, j):
        return remote(
            self.z_back.at[u, line], self.p_buf.at[u, :, self.part(j)], self.sems.at[4, u, line], self.sems.at[5, u, j],
            ctx=line * 2 + self.inner,
        )

    def f_copy(self, u, inner):
        return remote(
            self.their_buf.at[u], self.out_at(u, self.half_rows(inner)), self.sems.at[6, u, 0], self.sems.at[7, u, 0],
            ctx=self.ctx + 1 - 2 * self.inner,
        )

    def keep(self, u):
        return pltpu.make_async_copy(self.mine_buf.at[u], self.out_at(u, self.half_rows(self.inner)), self.sems.at[8, u, 0])

    def decay(self, a, block):
        return self.decx[a, pl.ds(pl.multiple_of(block * 8, 8), 8), :][0:1]

    def pair(self, u, a):
        own = self.buf[u, a, self.half_rows(self.inner), :].astype(f32)
        other = self.y_buf[u, a].astype(f32)
        first = self.inner == 0
        return jnp.where(first, own, other), jnp.where(first, other, own)

    def start(self, u):
        self.y_copy(u).start()

    def middle(self, u):
        self.y_copy(u).wait_recv()
        for a in range(self.depth):
            s0, s1 = self.pair(u, a)
            if self.reverse:
                total = s0 + self.decay(a, 2 * self.line) * s1
            else:
                total = self.decay(a, 2 * self.line + 1) * s0 + s1
            self.z_src[u, a] = total.astype(bf16)
        self.other_owners(lambda j: self.z_copy(u, j, self.line).start())

    def scan(self, u):
        def run():
            self.other_lines(lambda line: self.z_copy(u, self.mine, line).wait_recv())
            self.z_buf[u, self.line] = self.z_src[u, :, self.part(self.mine), :]
            for a in range(self.depth):

                def step(k, carry):
                    line = self.outer - 1 - k if self.reverse else k
                    self.z_back[u, line, a] = carry.astype(bf16)
                    both_decays = self.decay(a, 2 * line) * self.decay(a, 2 * line + 1)
                    return both_decays * carry + self.z_buf[u, line, a].astype(f32)

                lax.fori_loop(0, self.outer, step, jnp.zeros(self.z_buf.shape[3:], f32))
            self.other_lines(lambda line: self.b_copy(u, line, self.mine).start())
            self.p_buf[u, :, self.part(self.mine), :] = self.z_back[u, self.line]

        self.if_owner(run)

    def close(self, u):
        self.other_owners(lambda j: self.b_copy(u, self.line, j).wait_recv())
        for a in range(self.depth):
            s0, s1 = self.pair(u, a)
            near = self.p_buf[u, a].astype(f32)
            if self.reverse:
                far = s1 + self.decay(a, 2 * self.line + 1) * near
            else:
                far = s0 + self.decay(a, 2 * self.line) * near
            keeps_near = self.inner == (1 if self.reverse else 0)
            self.mine_buf[u, a] = jnp.where(keeps_near, near, far).astype(bf16)
            self.their_buf[u, a] = jnp.where(keeps_near, far, near).astype(bf16)
        self.f_copy(u, self.inner).start()
        self.keep(u).start()

    def finish(self, u):
        self.f_copy(u, 1 - self.inner).wait_recv()
        self.keep(u).wait()
        self.y_copy(u).wait_send()
        self.other_owners(lambda j: self.z_copy(u, j, self.line).wait_send())
        self.if_owner(lambda: self.other_lines(lambda line: self.b_copy(u, line, self.mine).wait_send()))
        self.f_copy(u, self.inner).wait_send()

    @staticmethod
    def scratch(units, depth, lanes, count):
        outer = count // 2
        half = NSTATE // 2
        rows = half // min(outer, 4)
        bufs = [(units, depth, NSTATE, lanes), (units, depth, half, lanes), (units, depth, half, lanes),
                (units, outer, depth, rows, lanes), (units, outer, depth, rows, lanes), (units, depth, half, lanes),
                (units, depth, half, lanes), (units, depth, half, lanes)]
        return (
            [(b, bf16) for b in bufs]
            + [((depth, count * 8, lanes), f32)]
            + [pltpu.SemaphoreType.DMA((9, units, max(outer, 4)))]
        )


class Spread:
    def __init__(self, shard, full, sems):
        self.shard, self.full = shard, full
        self.x_send, self.x_recv, self.m_send, self.m_recv, self.own = sems
        size = lax.axis_size("group")
        self.cores = 2 if size % 2 == 0 else 1
        self.chips = size // self.cores
        self.me = lax.axis_index("group")
        self.core = lax.rem(self.me, self.cores)
        self.chip = self.me // self.cores
        self.rows = shard.shape[0]

    def place(self, member, cols):
        return self.full.at[pl.ds(pl.multiple_of(member * self.rows, 32), self.rows), cols]

    def across(self, p, cols, d):
        peer = lax.rem(self.chip + d, self.chips) * self.cores + self.core
        return remote(
            self.shard.at[:, cols], self.place(self.me, cols), self.x_send.at[p, d], self.x_recv.at[p, d], group=peer
        )

    def mate(self, p, cols, d):
        member = lax.rem(self.chip + self.chips - d, self.chips) * self.cores + self.core
        src = self.shard.at[:, cols] if d == 0 else self.place(member, cols)
        return remote(
            src, self.place(member, cols), self.m_send.at[p, d], self.m_recv.at[p, d],
            group=self.me + 1 - 2 * self.core,
        )

    def keep(self, p):
        return pltpu.make_async_copy(self.shard, self.place(self.me, slice(None)), self.own.at[p])

    def start_chip(self, p):
        if self.cores == 2:
            self.mate(p, slice(None), 0).start()
        self.keep(p).start()

    def finish_chip(self, p):
        if self.cores == 2:
            self.mate(p, slice(None), 0).wait_recv()
        self.keep(p).wait()

    def start(self, p, cols):
        for d in range(1, self.chips):
            self.across(p, cols, d).start()

    def forward(self, p, cols):
        for d in range(1, self.chips):
            self.across(p, cols, d).wait_recv()
            if self.cores == 2:
                self.mate(p, cols, d).start()

    def finish(self, p, cols):
        if self.cores == 2:
            for d in range(1, self.chips):
                self.mate(p, cols, d).wait_recv()

    def drain(self, p, cols):
        for d in range(1, self.chips):
            self.across(p, cols, d).wait_send()
            if self.cores == 2:
                self.mate(p, cols, d).wait_send()

    def drain_chip(self, p):
        if self.cores == 2:
            self.mate(p, slice(None), 0).wait_send()


def owner_count(rows, width, by_rows, outer):
    fits = lambda n: (rows // 2) % (16 * n) == 0 if by_rows else width % (128 * n) == 0
    return max(n for n in (1, 2, 4) if outer % n == 0 and fits(n))


class Reducer:
    def __init__(self, part, out, rows, width, by_rows, group_bufs, ctx_bufs):
        self.part, self.out, self.rows, self.width, self.by_rows = part, out, rows, width, by_rows
        if group_bufs is not None:
            self.m_buf, self.x_buf, self.g_sems = group_bufs
        self.ships = ctx_bufs is not None
        if self.ships:
            self.y_src, self.y_buf, self.z_src, self.z_buf, self.full, self.c_sems = ctx_bufs
        else:
            self.y_src = out
        self.chunks = self.y_src.shape[0]
        self.base = 0
        self.group = lax.axis_index("group")
        self.cores = 2
        self.chips = lax.axis_size("group") // 2
        self.core = lax.rem(self.group, 2)
        self.chip = self.group // 2
        self.ctx = lax.axis_index("ctx")
        self.outer = lax.axis_size("ctx") // 2
        self.owners = owner_count(rows, width, by_rows, self.outer)
        self.stride = self.outer // self.owners
        self.inner = lax.rem(self.ctx, 2)
        self.line = self.ctx // 2
        self.mine = self.line // self.stride
        self.half = rows // 2

    def cols(self, k):
        return pl.ds(pl.multiple_of(k * self.width, self.width), self.width)

    def member(self, chip, core):
        return pl.ds(pl.multiple_of((chip * 2 + core) * self.rows, 64), self.rows)

    def half_rows(self, inner):
        return pl.ds(pl.multiple_of(inner * self.half, 16), self.half)

    def piece(self, j, base):
        if self.by_rows:
            n = self.half // self.owners
            return pl.ds(pl.multiple_of(base + j * n, 16), n), pl.ds(0, self.width)
        n = self.width // self.owners
        return pl.ds(pl.multiple_of(base, 16), self.half), pl.ds(pl.multiple_of(j * n, 128), n)

    def m_copy(self, k, chip):
        return remote(
            self.part.at[self.member(chip, 1 - self.core), self.cols(k)], self.m_buf.at[k, chip],
            self.g_sems.at[0, k, chip], self.g_sems.at[1, k, chip], group=self.group + 1 - 2 * self.core,
        )

    def x_copy(self, k, chip, sender):
        return remote(
            self.m_buf.at[k, chip], self.x_buf.at[k, sender], self.g_sems.at[2, k, chip], self.g_sems.at[3, k, sender],
            group=chip * 2 + self.core,
        )

    def y_copy(self, k):
        return remote(
            self.y_src.at[k, self.half_rows(1 - self.inner)], self.y_buf.at[k], self.c_sems.at[0, k, 0], self.c_sems.at[1, k, 0],
            ctx=self.ctx + 1 - 2 * self.inner,
        )

    def z_copy(self, k, j, sender):
        rows, cols = self.piece(j, 0)
        return remote(
            self.z_src.at[k, rows, cols], self.z_buf.at[k, sender], self.c_sems.at[2, k, j], self.c_sems.at[3, k, sender],
            ctx=j * self.stride * 2 + self.inner,
        )

    def b_copy(self, k, line, j):
        rows, cols = self.piece(j, self.inner * self.half)
        return remote(
            self.full.at[k, rows, cols], self.full.at[k, rows, cols], self.c_sems.at[4, k, line], self.c_sems.at[5, k, j],
            ctx=line * 2 + self.inner,
        )

    def f_copy(self, k, inner):
        rows = self.half_rows(inner)
        return remote(
            self.full.at[k, rows], self.full.at[k, rows], self.c_sems.at[6, k, 0], self.c_sems.at[7, k, 0],
            ctx=self.ctx + 1 - 2 * self.inner,
        )

    def other_chips(self, body):
        for d in range(1, self.chips):
            body(lax.rem(self.chip + d, self.chips))

    def other_owners(self, body):
        if self.stride == 1:
            for d in range(1, self.owners):
                body(lax.rem(self.mine + d, self.owners))
        else:
            for j in range(self.owners):
                pl.when(j * self.stride != self.line)(lambda j=j: body(j))

    def other_lines(self, body):
        loop(1, self.outer, lambda d: body(lax.rem(self.line + d, self.outer)))

    def if_owner(self, body):
        if self.stride == 1:
            body()
        else:
            pl.when(self.mine * self.stride == self.line)(body)

    def m_start(self, k):
        for chip in range(self.chips):
            self.m_copy(k, chip).start()

    def m_done(self, k):
        for chip in range(self.chips):
            self.m_copy(k, chip).wait_recv()
            own = self.part[self.member(chip, self.core), self.cols(k)].astype(f32)
            self.m_buf[k, chip] = (own + self.m_buf[k, chip].astype(f32)).astype(bf16)
        self.other_chips(lambda chip: self.x_copy(k, chip, self.chip).start())

    def x_done(self, k):
        total = self.m_buf[k, self.chip].astype(f32)
        for d in range(1, self.chips):
            chip = lax.rem(self.chip + d, self.chips)
            self.x_copy(k, chip, chip).wait_recv()
            total = total + self.x_buf[k, chip].astype(f32)
        self.y_src[k] = total.astype(bf16)
        if self.ships:
            self.y_start(k)

    def y_start(self, k):
        self.y_copy(k).start()

    def y_done(self, k):
        self.y_copy(k).wait_recv()
        own = self.y_src[k, self.half_rows(self.inner), :].astype(f32)
        self.z_src[k] = (own + self.y_buf[k].astype(f32)).astype(bf16)
        self.other_owners(lambda j: self.z_copy(k, j, self.line).start())

    def z_done(self, k):
        def run():
            rows, cols = self.piece(self.mine, 0)
            self.other_lines(lambda line: self.z_copy(k, self.mine, line).wait_recv())
            self.z_buf[k, self.line] = self.z_src[k, rows, cols]
            total = self.z_buf[k, 0].astype(f32)
            for line in range(1, self.outer):
                total = total + self.z_buf[k, line].astype(f32)
            rows, cols = self.piece(self.mine, self.inner * self.half)
            self.full[k, rows, cols] = total.astype(bf16)
            self.other_lines(lambda line: self.b_copy(k, line, self.mine).start())

        self.if_owner(run)

    def b_done(self, k):
        self.other_owners(lambda j: self.b_copy(k, self.line, j).wait_recv())
        self.f_copy(k, self.inner).start()

    def f_done(self, k):
        self.f_copy(k, 1 - self.inner).wait_recv()
        self.out[:, pl.ds(pl.multiple_of(self.base + k * self.width, 128), self.width)] = self.full[k]

    def drain_group(self, k):
        for chip in range(self.chips):
            self.m_copy(k, chip).wait_send()
        self.other_chips(lambda chip: self.x_copy(k, chip, self.chip).wait_send())

    def drain_ctx(self, k):
        self.y_copy(k).wait_send()
        self.other_owners(lambda j: self.z_copy(k, j, self.line).wait_send())
        self.if_owner(lambda: self.other_lines(lambda line: self.b_copy(k, line, self.mine).wait_send()))
        self.f_copy(k, self.inner).wait_send()

    def wave(self, t, acts, chunk_at, lag=STAGE_LAG):
        for order, act in reversed(list(enumerate(acts))):
            k, is_due = chunk_at(t - order * lag)
            pl.when(is_due)(lambda k=k, act=act: act(k))

    def each(self, t):
        return t, jnp.logical_and(t >= 0, t < self.chunks)

    @staticmethod
    def group_scratch(chunks, rows, width, group):
        chips = group // 2
        buf = ((chunks, chips, rows, width), bf16)
        return [buf, buf, pltpu.SemaphoreType.DMA((4, chunks, max(chips, 2)))]

    @staticmethod
    def ctx_scratch(chunks, rows, width, by_rows, count):
        outer = count // 2
        owners = owner_count(rows, width, by_rows, outer)
        half = rows // 2
        piece = (half // owners, width) if by_rows else (half, width // owners)
        bufs = [(chunks, half, width), (chunks, half, width), (chunks, outer) + piece, (chunks, rows, width)]
        return [(b, bf16) for b in bufs] + [pltpu.SemaphoreType.DMA((8, chunks, max(outer, 2)))]


class Small:
    def __init__(self, held, got, sends, recvs):
        self.held, self.got, self.sends, self.recvs = held, got, sends, recvs

    def copy(self, h, j, sender):
        return remote(
            self.held.at[h], self.got.at[h, sender], self.sends.at[h, j], self.recvs.at[h, sender], **{HOPS[h]: j}
        )

    def others(self, h, body):
        size, mine = lax.axis_size(HOPS[h]), lax.axis_index(HOPS[h])
        loop(1, size, lambda d: body(lax.rem(mine + d, size)))

    def start(self, h):
        mine = lax.axis_index(HOPS[h])
        self.others(h, lambda j: self.copy(h, j, mine).start())

    def done(self, h):
        self.others(h, lambda j: self.copy(h, j, j).wait_recv())
        self.got[h, lax.axis_index(HOPS[h])] = self.held[h]
        total = self.got[h, 0]
        for j in range(1, lax.axis_size(HOPS[h])):
            total = total + self.got[h, j]
        self.held[h + 1] = total

    def drain(self):
        for h in range(2):
            mine = lax.axis_index(HOPS[h])
            self.others(h, lambda j: self.copy(h, j, mine).wait_send())

    @staticmethod
    def scratch(height, group, count):
        widest = max(group, count)
        dma = pltpu.SemaphoreType.DMA
        return [((3, height, HALF), f32), ((2, widest, height, HALF), f32), dma((2, widest)), dma((2, widest))]


def masks():
    rows = lax.broadcasted_iota(jnp.int32, (HALF, HALF), 0)
    cols = lax.broadcasted_iota(jnp.int32, (HALF, HALF), 1)
    return rows >= cols, cols < HEADDIM


def both(q):
    return slice(q * HALF, (q + 1) * HALF)


def pair_decays(cum, cum_t, p, causal):
    rolled = pltpu.roll(cum, lax.rem(HALF - 2 * p, HALF), 1)
    out = []
    for q in range(2):
        for a in range(2):
            gaps = rolled[both(q), a : a + 1] - cum_t[q, pl.ds(2 * p + a, 1), :]
            out.append(jnp.exp(jnp.where(causal, gaps, -jnp.inf)))
    return out


TILES = DIN // TILE
PIECES = 2 * TILES + 1
DT0 = DIN + CONVW - 2 * NSTATE
AHEAD = 5


def front_kernel(
    tok, tok_any, wzx, wdl, wout, gain, cw, cb_in, db, dl,
    nt, nth, rhalo, cin, xb, spb, vout, cumout, st0, loc, ylocal, gate, decs_out, wfull, wdfull, wofull, sin,
    sel, halo, nh_s, ext, w, wd, cb, cin_s, xs_s, bt, scores, out_cat, dt_cat, cum_t, tot1x, decs,
    halo_sem, x_send, x_recv, m_send, m_recv, w_own, w_store, dec_send, dec_recv, *exchange,
):
    i = pl.program_id(0)
    seqs = tok.shape[0]
    count = lax.axis_size("ctx")
    me = lax.axis_index("ctx")
    sems = (x_send, x_recv, m_send, m_recv, w_own)
    zx, wo, de = Spread(wzx, w, sems), Spread(wout, wofull, sems), Spread(wdl, wd, sems)
    last, small_piece = PIECES, PIECES + 1

    def unit_cols(u):
        return pl.ds(pl.multiple_of(u * TILE, TILE), TILE)

    def piece(p):
        at = jnp.where(p <= TILES, DIN + (p - 1) * TILE, (p - 1 - TILES) * TILE)
        return pl.ds(pl.multiple_of(at, TILE), TILE)

    first_piece = pl.ds(DT0, 2 * NSTATE)
    ex = Exchange(False, lambda u, rows: sin.at[:, rows, unit_cols(u)], exchange[:9], exchange[9])
    halo_copy = remote(
        tok_any.at[:, pl.ds(SPAN - RIM, RIM), :], halo, halo_sem.at[0], halo_sem.at[1], ctx=lax.rem(me + 1, count)
    )
    keep_w = pltpu.make_async_copy(w, wfull, w_store.at[0])
    keep_d = pltpu.make_async_copy(wd, wdfull, w_store.at[1])

    def dec_copy(block, sender):
        rows = pl.ds(pl.multiple_of(sender * 8, 8), 8)
        return remote(decs.at[:, rows, :], decs.at[:, rows, :], dec_send.at[block], dec_recv.at[sender], ctx=block)

    def other_blocks(body):
        loop(1, count, lambda d: body(lax.rem(me + d, count)))

    def conv_tile(s, cols_w, cols_c):
        cin_s[s] = mm(ext[s], w[:, cols_w])
        cin[s] = cin_s[s].astype(bf16)
        o = cb[:, cols_c]
        for k in range(KCONV):
            o = o + cw[k : k + 1, cols_c] * cin_s[s, RIM - KCONV + 1 + k : RIM - KCONV + 1 + k + SPAN, :]
        sg = gate_of(o)
        a = o * sg
        xb[s] = a.astype(bf16)
        spb[s] = (sg + a * (1.0 - sg)).astype(bf16)
        return a

    def unit_decays(u):
        for s in range(seqs):
            ex.decx[s] = spread(decs[s], sel.at[:, unit_cols(u)])

    @pl.when(i == 0)
    def _():
        meet(("ctx", "group"))
        pl.when(me < count - 1)(lambda: halo_copy.start())
        de.start(small_piece, slice(None))
        zx.start(0, first_piece)
        de.start_chip(2)
        zx.start_chip(0)
        cb[...] = row_of(cb_in)
        for p in range(1, AHEAD):
            zx.start(p, piece(p))
        wo.start_chip(1)
        sel[...] = head_map()

        @pl.when(me == 0)
        def _():
            halo[...] = jnp.zeros_like(halo)

        def norm_main(s):
            nm = normalized(tok[s], row_of(gain))[2]
            ext[s, RIM:] = nm
            nt[:, pl.ds(pl.multiple_of(s * SPAN, SPAN), SPAN)] = jnp.transpose(nm.astype(f32)).astype(bf16)

        loop(0, seqs, norm_main)

        @pl.when(me > 0)
        def _():
            halo_copy.wait_recv()

        def norm_halo(s):
            nh = normalized(halo[s], row_of(gain))[2]
            ext[s, 0:RIM] = nh
            nh_s[pl.ds(pl.multiple_of(s * RIM, RIM), RIM), :] = nh.astype(f32)
            rhalo[s] = halo[s]

        loop(0, seqs, norm_halo)
        nth[...] = jnp.transpose(nh_s[...]).astype(bf16)
        de.forward(small_piece, slice(None))
        zx.forward(0, first_piece)
        zx.finish_chip(0)
        de.finish_chip(2)

    @pl.when(i + 1 < PIECES)
    def _():
        zx.forward(i + 1, piece(i + 1))

    @pl.when(i + AHEAD < PIECES)
    def _():
        zx.start(i + AHEAD, piece(i + AHEAD))

    @pl.when(i + AHEAD == PIECES)
    def _():
        wo.start(last, slice(None))

    @pl.when(i == 0)
    def _():
        zx.finish(0, first_piece)
        de.finish(small_piece, slice(None))
        shift, rate = lane_row(db), jnp.exp(lane_row(dl))

        def delta(s):
            a = conv_tile(s, slice(DT0, DT0 + TILE), slice(DIN, DIN + TILE))
            bb, cc = a[:, :NSTATE].astype(bf16), a[:, NSTATE:].astype(bf16)
            bt[s] = jnp.transpose(a[:, :NSTATE]).astype(bf16)
            for q in range(2):
                scores[s, q] = mm_nt(cc[both(q)], bb[both(q)])
            v = mm(ext[s, RIM:], wd[...]) + shift
            vout[s] = v
            dt = softplus(v)
            cum = running_sum(-rate * dt, True)
            cumout[s] = cum
            for q in range(2):
                cum_t[s, q] = jnp.transpose(cum[both(q)])
            e_in, e_out, tot0, tot1, total = local_decays(cum)
            decs[s, pl.ds(pl.multiple_of(me * 8, 8), 8), :] = rows_of(total)
            out_cat[s] = jnp.concatenate(halves(dt * e_out), axis=1)
            dt_cat[s] = jnp.concatenate(halves(dt), axis=1)
            tot1x[s] = spread(rows_of(tot1), sel)

        loop(0, seqs, delta)
        other_blocks(lambda b: dec_copy(b, me).start())

    @pl.when(jnp.logical_and(i >= 1, i < PIECES))
    def _():
        zx.finish(i, piece(i))

    def act_at(t, lag, act):
        u = t - 1 - lag
        pl.when(jnp.logical_and(u >= 0, u < TILES))(lambda: act(u))

    def close(u):
        unit_decays(u)
        ex.close(u)

    def scan(u):
        unit_decays(u)
        ex.scan(u)

    def middle(u):
        unit_decays(u)
        ex.middle(u)

    @pl.when(i == 3)
    def _():
        other_blocks(lambda b: dec_copy(b, b).wait_recv())

    def wave(t):
        act_at(t, CLOSE_LAG, close)
        act_at(t, SCAN_LAG, scan)
        act_at(t, MIDDLE_LAG, middle)

    wave(i)

    @pl.when(jnp.logical_and(i >= 1, i <= TILES))
    def _():
        u = i - 1
        cols = unit_cols(u)

        def x_tile(s):
            a = conv_tile(s, piece(i), cols)
            xs_s[s, :, cols] = a.astype(bf16)
            xw = (a * mm(out_cat[s], sel[:, cols])).astype(bf16)
            s0 = mm(bt[s, :, :HALF], xw[:HALF])
            s1 = mm(bt[s, :, HALF:], xw[HALF:])
            st0[s] = s0.astype(bf16)
            low = (tot1x[s, :, cols][0:1] * s0 + s1).astype(bf16)
            loc[s] = low
            ex.buf[u, s] = low

        loop(0, seqs, x_tile)
        ex.start(u)

    @pl.when(i > TILES)
    def _():
        u = i - 1 - TILES
        causal, low_lanes = masks()

        def intra(s):
            cum = cumout[s]
            dtx = mm(dt_cat[s], sel[:, unit_cols(u)])
            for h in range(2):
                p = 2 * u + h
                lanes = slice(h * HALF, (h + 1) * HALF)
                decays = pair_decays(cum, cum_t.at[s], p, causal)
                for q in range(2):
                    rows = both(q)
                    m = jnp.concatenate([(decays[2 * q + a] * scores[s, q]).astype(bf16) for a in range(2)], axis=1)
                    x = xs_s[s, rows, pl.ds(pl.multiple_of(p * HALF, HALF), HALF)].astype(f32) * dtx[rows, lanes]
                    x = jnp.concatenate([jnp.where(low_lanes, x, 0.0), jnp.where(low_lanes, 0.0, x)], axis=0)
                    ylocal[s, rows, lanes] = mm(m, x.astype(bf16)).astype(bf16)
            gate[s] = mm(ext[s, RIM:], w[:, piece(i)]).astype(bf16)

        loop(0, seqs, intra)

    @pl.when(i == PIECES - 1)
    def _():
        keep_w.start()
        keep_d.start()
        decs_out[...] = decs[...]
        wo.forward(last, slice(None))
        loop(PIECES, TILES + CLOSE_LAG + 1, wave)
        loop(0, TILES, ex.finish)
        wo.finish(last, slice(None))
        wo.finish_chip(1)
        zx.drain_chip(0)
        wo.drain_chip(1)
        de.drain_chip(2)
        de.drain(small_piece, slice(None))
        zx.drain(0, first_piece)
        loop(1, PIECES, lambda p: zx.drain(p, piece(p)))
        wo.drain(last, slice(None))
        other_blocks(lambda b: dec_copy(b, me).wait_send())
        pl.when(me < count - 1)(lambda: halo_copy.wait_send())
        keep_w.wait()
        keep_d.wait()


def middle_kernel(
    lengths, skip_in, tok, cot, ylocal, gate, xb, vin, cumin, st0, sin, decs, wout, ggain_in, nt,
    mixed, dyout, ggate, wred, dir1, gskip, gggain, dxs, dbc, xgate, xout, later,
    sel, skip, ggain, cum_t, einx, ys, gs, ss, s_in, dcs, dy_s, ml_s, gg_s, dr_s, pgate, pout, g_s, dg_s, *exchange,
):
    i = pl.program_id(0)
    seqs = dy_s.shape[0]
    ex = Exchange(True, lambda u, rows: later.at[pl.ds(u, 1), rows, :], exchange[:9], exchange[9])
    members = lax.axis_size("group")
    gates = Reducer(pgate, xgate, D // members, GATE_CHUNK, False, exchange[10:13], None)
    outs = Reducer(pout, xout, DIN // members, OUT_CHUNK, True, exchange[13:16], None)

    def span(s):
        return pl.ds(pl.multiple_of(s * SPAN, SPAN), SPAN)

    def group_wave(t):
        gates.wave(t - 2 * seqs - 3, [gates.x_done], gates.each)
        outs.wave(t - 2 * seqs - 3 - gates.chunks, [outs.x_done], outs.each)

    def wave(t):
        group_wave(t)

        def act_at(lag, act):
            u = lax.div(t - lag, 2)

            def run():
                ex.decx[0] = spread(decs[u], sel)
                act(u)

            pl.when(jnp.logical_and(t >= lag, jnp.logical_and(2 * u + lag == t, u < seqs)))(run)

        act_at(BACK_LAGS[2], ex.close)
        act_at(BACK_LAGS[1], ex.scan)
        act_at(BACK_LAGS[0], ex.middle)

    @pl.when(i == 0)
    def _():
        greet(("ctx", "group"))
        sel[...] = head_map()
        skip[...] = spread(rows_of(lane_row(skip_in)), sel)[0:1]
        ggain[...] = row_of(ggain_in)
        gskip[...] = jnp.zeros_like(gskip)
        gggain[...] = jnp.zeros_like(gggain)

    @pl.when(i == 1)
    def _():
        settle(("ctx", "group"))

    @pl.when(jnp.logical_and(i >= 1, i <= seqs))
    def _():
        ex.start(i - 1)

    wave(2 * i)

    @pl.when(i < seqs)
    def _():
        s = i
        cum = cumin[0]
        e_in, e_out, tot0, tot1, total = local_decays(cum)
        einx[...] = spread(e_in, sel)
        tot0x = spread(rows_of(tot0), sel)[0:1]
        s_in[0] = sin[0]
        s_in[1] = (tot0x * sin[0].astype(f32) + st0[0].astype(f32)).astype(bf16)
        cc = xb[0, :, DIN + NSTATE :]

        def gate_step(j, total_sq):
            cols = pl.ds(pl.multiple_of(j * TILE, TILE), TILE)
            for q in range(2):
                rows = both(q)
                ys[rows, cols] = ylocal[0, rows, cols].astype(f32) + einx[rows, cols] * mm(cc[rows], s_in[q, :, cols])
            y = ys[:, cols] + skip[:, cols] * xb[0, :, cols].astype(f32)
            g = gate[0, :, cols].astype(f32)
            gated = y * (g * gate_of(g))
            gs[:, cols] = gated
            sq = gated * gated
            return total_sq + sq[:, :HALF] + sq[:, HALF:]

        wave(2 * i + 1)
        sq = lax.fori_loop(0, DIN // TILE, gate_step, jnp.zeros((SPAN, HALF), f32))
        inv = lax.rsqrt(jnp.sum(sq, axis=1, keepdims=True) * (1.0 / DIN) + EPS)
        live = live_rows(lengths, s)
        drive = (live * cot[0].astype(f32)).astype(bf16)
        dr_s[span(s), :] = drive

        def back_step(j, acc):
            cols = pl.ds(pl.multiple_of(j * TILE, TILE), TILE)
            gm = mm_nt(drive, wout[cols, :])
            gated = gs[:, cols]
            unit = gated * inv
            ml_s[span(s), cols] = (unit * ggain[:, cols]).astype(bf16)
            gggain[:, cols] += jnp.sum(gm * unit, axis=0, keepdims=True)
            scaled = gm * ggain[:, cols]
            ss[:, cols] = scaled
            prod = scaled * gated
            return acc + prod[:, :HALF] + prod[:, HALF:]

        dots = lax.fori_loop(0, DIN // TILE, back_step, jnp.zeros((SPAN, HALF), f32))
        dots = jnp.sum(dots, axis=1, keepdims=True) * (1.0 / DIN)
        corr = inv * inv * inv * dots
        cct = jnp.transpose(cc.astype(f32)).astype(bf16)
        acc = jnp.zeros((SPAN, HALF), f32)
        dc = [jnp.zeros((HALF, HALF), f32) for _ in range(2)]
        for j in range(DIN // TILE):
            cols = slice(j * TILE, (j + 1) * TILE)
            g = gate[0, :, cols].astype(f32)
            sg = gate_of(g)
            sl = g * sg
            grad_gated = inv * ss[:, cols] - gs[:, cols] * corr
            dy = grad_gated * sl
            yn = ys[:, cols]
            x = xb[0, :, cols].astype(f32)
            y = yn + skip[:, cols] * x
            low = (grad_gated * y * (sg + sl * (1.0 - sg))).astype(bf16)
            ggate[0, :, cols] = low
            gg_s[span(s), cols] = low
            dyb = dy.astype(bf16)
            dyout[0, :, cols] = dyb
            dy_s[s, :, cols] = dyb
            gskip[:, cols] += jnp.sum(dy * x, axis=0, keepdims=True)
            acc = acc + gather_heads(dy * yn, sel[:HALF, cols])
            dye = (dy * einx[:, cols]).astype(bf16)
            d0 = mm(cct[:, :HALF], dye[:HALF])
            d1 = mm(cct[:, HALF:], dye[HALF:])
            dir1[0, :, cols] = d1.astype(bf16)
            ex.buf[s, 0, :, cols] = (d0 + tot0x[:, cols] * d1).astype(bf16)
            for q in range(2):
                dc[q] = dc[q] + mm_nt(dye[both(q)], s_in[q, :, cols])
        wred[0] = acc
        for q in range(2):
            dcs[s, both(q)] = dc[q]

    @pl.when(i >= seqs)
    def _():
        s = i - seqs
        causal, low_lanes = masks()
        cum = cumin[0]
        for q in range(2):
            cum_t[q] = jnp.transpose(cum[both(q)])
        einx[...] = spread(softplus(vin[0]), sel)
        bb = xb[0, :, DIN : DIN + NSTATE]
        cc = xb[0, :, DIN + NSTATE :]
        for q in range(2):
            g_s[q] = mm_nt(cc[both(q)], bb[both(q)])
        dg_s[...] = jnp.zeros_like(dg_s)

        def pair_step(p):
            cols = pl.ds(pl.multiple_of(p * HALF, HALF), HALF)
            decays = pair_decays(cum, cum_t, p, causal)
            for q in range(2):
                rows = both(q)
                xsb = (xb[0, rows, cols].astype(f32) * einx[rows, cols]).astype(bf16)
                dyb = dy_s[s, rows, cols]
                dyf = dyb.astype(f32)
                grads = []
                for a in range(2):
                    m = (decays[2 * q + a] * g_s[q]).astype(bf16)
                    grads.append(mm_tn(m, dyb))
                    mine = low_lanes if a == 0 else jnp.logical_not(low_lanes)
                    dm = mm_nt(jnp.where(mine, dyf, 0.0).astype(bf16), xsb)
                    dg_s[q] += dm * decays[2 * q + a]
                dxs[0, rows, cols] = jnp.where(low_lanes, grads[0], grads[1]).astype(bf16)

        @pl.when(s == 0)
        def _():
            for k in range(gates.chunks):
                cols = slice(k * GATE_CHUNK, (k + 1) * GATE_CHUNK)
                pgate[:, cols] = mm(nt[...], gg_s[:, cols]).astype(bf16)
                gates.m_start(k)

        @pl.when(s == 1)
        def _():
            loop(0, outs.chunks, outs.m_done)

        def two_pairs(pp):
            for h in range(2):
                pair_step(2 * pp + h)

        loop(0, PAIRS // 4, two_pairs)
        wave(2 * i + 1)

        @pl.when(s == 0)
        def _():
            loop(0, gates.chunks, gates.m_done)

            def out_rows(r):
                rows = pl.ds(pl.multiple_of(r * TILE, TILE), TILE)
                pout[rows, :] = mm_tn(ml_s[:, rows], dr_s[...]).astype(bf16)

            loop(0, DIN // TILE, out_rows)
            loop(0, outs.chunks, outs.m_start)

        loop(PAIRS // 4, PAIRS // 2, two_pairs)
        for q in range(2):
            rows = both(q)
            dg = dg_s[q].astype(bf16)
            dbc[0, rows, :NSTATE] = mm_tn(dg, cc[rows])
            dbc[0, rows, NSTATE:] = mm(dg, bb[rows]) + dcs[s, rows]
        live = live_rows(lengths, s)
        for j in range(D // TILE):
            cols = slice(j * TILE, (j + 1) * TILE)
            mixed[0, :, cols] = (live * (tok[0, :, cols].astype(f32) + mm(ml_s[span(s), :], wout[:, cols]))).astype(bf16)

    @pl.when(i == 2 * seqs - 1)
    def _():
        loop(4 * seqs, max(2 * seqs + BACK_LAGS[2] - 1, 2 * seqs + 3 + gates.chunks + outs.chunks), wave)
        loop(0, seqs, ex.finish)
        for r in (gates, outs):
            loop(0, r.chunks, r.drain_group)


def back_kernel(
    lengths, dl, skip_in, tok, cot, rhalo, gain, ggate, w_any, wd, cin, xb, spb, bc, dy, dxs, dir1, later, sin, loc,
    vin, cumin, wred, dbc, cw, nt, nth, xgate, xout, gskip, gggain,
    gtok, rzx, rout, small_out, ggain_out,
    sel, skip, wfull, w_sem, dt_cat, eo_cat, tots, db_s, qacc, ends, gp, gz_s, gzh_s, pconv, gcw, gcb, gdb, gdl, ggain,
    rim_out, rim_in, rim_send, rim_recv, *comm,
):
    i = pl.program_id(0)
    seqs = rhalo.shape[0]
    count = lax.axis_size("ctx")
    me = lax.axis_index("ctx")
    members = lax.axis_size("group")
    gates = Reducer(None, rzx, D // members, GATE_CHUNK, False, None, (xgate,) + comm[0:5])
    outs = Reducer(None, rout, DIN // members, OUT_CHUNK, True, None, (xout,) + comm[5:10])
    convs = Reducer(pconv, rzx, D // members, CONV_CHUNK, False, comm[10:13], comm[13:19])
    convs.base = DIN
    load_w = pltpu.make_async_copy(w_any, wfull, w_sem.at[0])
    little, least = Small(*comm[19:23]), Small(*comm[23:27])
    bc_step = TILES

    last_conv = 2 * bc_step + 5

    def conv_at(t):
        k = lax.div(t - 7, 4)
        even = jnp.logical_and(t >= 7, jnp.logical_and(lax.rem(t - 7, 4) == 0, k < convs.chunks - 1))
        last = t == last_conv
        return jnp.where(last, convs.chunks - 1, k), jnp.logical_or(even, last)

    def wave(t):
        for r, at in ((gates, 2), (outs, 2 + gates.chunks)):
            r.wave(t - at, [r.y_done, r.z_done, r.b_done, r.f_done], r.each)
        convs.wave(t, [convs.x_done, convs.y_done, convs.z_done, convs.b_done, convs.f_done], conv_at, CONV_LAG)

    def rim_copy(q):
        return remote(rim_out.at[q], rim_in.at[q], rim_send.at[q], rim_recv.at[q], ctx=lax.rem(me + count - 1, count))

    def span(s):
        return pl.ds(pl.multiple_of(s * SPAN, SPAN), SPAN)

    def edge(s):
        return pl.ds(pl.multiple_of(s * RIM, RIM), RIM)

    def back(rows, grad):
        rows, inv, _ = normalized(rows, row_of(gain))
        ggain[...] += jnp.sum(grad * rows * inv, axis=0, keepdims=True)
        gained = row_of(gain) * grad
        mean = jnp.mean(gained * rows, axis=-1, keepdims=True)
        return inv * gained - rows * (inv * inv * inv * mean)

    @pl.when(i == 0)
    def _():
        meet(("ctx", "group"))
        for r in (gates, outs):
            loop(0, r.chunks, r.y_start)
        load_w.start()
        sel[...] = head_map()
        skip[...] = spread(rows_of(lane_row(skip_in)), sel)[0:1]
        for acc in (db_s, qacc, ends, gcw, gcb, gdb, gdl, ggain):
            acc[...] = jnp.zeros_like(acc)
        for slot in range(2):
            gp[slot, 0:RIM] = jnp.zeros((RIM, TILE), f32)
            gp[slot, RIM + SPAN :] = jnp.zeros((8, TILE), f32)
        pconv[:, CONVW + HALF :] = jnp.zeros((D, GZW - CONVW - HALF), bf16)

        def setup(s):
            dt = softplus(vin[s])
            _, e_out, _, tot1, total = local_decays(cumin[s])
            dt_cat[s] = jnp.concatenate(halves(dt), axis=1)
            eo_cat[s] = jnp.concatenate(halves(e_out), axis=1)
            both_rows = jnp.concatenate([rows_of(tot1), rows_of(total)], axis=0)
            tots[s] = spread(both_rows, sel)

        loop(0, seqs, setup)

    def conv_back(s, dact, cols, slot=0):
        gco = dact * spb[s].astype(f32)
        gp[slot, RIM : RIM + SPAN] = gco
        gcb[:, cols] += jnp.sum(gco, axis=0, keepdims=True)
        own = cin[s, RIM:].astype(f32)
        before = cin[s, :RIM].astype(f32)
        main = jnp.zeros((SPAN, TILE), f32)
        rim = jnp.zeros((RIM, TILE), f32)
        for k in range(KCONV):
            ahead = KCONV - 1 - k
            moved = gco if ahead == 0 else gp[slot, RIM + ahead : RIM + ahead + SPAN]
            early = gp[slot, ahead : ahead + RIM]
            main = main + cw[k : k + 1, cols] * moved
            rim = rim + cw[k : k + 1, cols] * early
            gcw[k : k + 1, cols] += jnp.sum(own * moved, axis=0, keepdims=True) + jnp.sum(
                before * early, axis=0, keepdims=True
            )
        gz_s[span(s), cols] = main.astype(bf16)
        gzh_s[edge(s), cols] = rim.astype(bf16)

    def partial(cols):
        pconv[:, cols] = (mm(nt[...], gz_s[:, cols]) + mm(nth[...], gzh_s[:, cols])).astype(bf16)

    wave(2 * i)

    @pl.when(i < bc_step)
    def _():
        cols = pl.ds(pl.multiple_of(i * TILE, TILE), TILE)

        def x_tile(s, slot):
            dte = mm(dt_cat[s], sel[:, cols])
            eo = mm(eo_cat[s], sel[:, cols])
            near = later[s]
            near32 = near.astype(f32)
            tot = tots[s, :, cols]
            reach = [(dir1[s].astype(f32) + tot[0:1] * near32).astype(bf16), near]
            fed = jnp.concatenate(
                [mm(bc[s, both(q), :NSTATE], reach[q]) for q in range(2)], axis=0
            )
            x = xb[s].astype(f32)
            dx_s = dxs[s].astype(f32) + eo * fed
            qacc[s] += gather_heads(x * dx_s, sel[:HALF, cols])
            xw = (x * dte * eo).astype(bf16)
            for q in range(2):
                db_s[s, both(q)] += mm_nt(xw[both(q)], reach[q])
            held = near32 * (tot[8:9] * sin[s].astype(f32) + loc[s].astype(f32))
            ends[s] += gather_heads(rows_of(jnp.sum(held, axis=0, keepdims=True)), sel[:HALF, cols])
            conv_back(s, dte * dx_s + skip[:, cols] * dy[s].astype(f32), cols, slot)

        def two_seqs(h):
            for slot in range(2):
                x_tile(2 * h + slot, slot)

        loop(0, seqs // 4, two_seqs)

        @pl.when(jnp.logical_and(lax.rem(i, 2) == 0, i >= 2))
        def _():
            convs.m_done(lax.div(i, 2) - 1)

        wave(2 * i + 1)
        loop(seqs // 4, seqs // 2, two_seqs)
        partial(cols)

        @pl.when(lax.rem(i, 2) == 1)
        def _():
            convs.m_start(lax.div(i, 2))

    @pl.when(i == bc_step)
    def _():
        cols = slice(DIN, CONVW)
        rate = jnp.exp(lane_row(dl))

        def bc_tile(s):
            conv_back(s, jnp.concatenate([dbc[s, :, :NSTATE] + db_s[s], dbc[s, :, NSTATE:]], axis=1), cols)
            v = vin[s]
            dt = softplus(v)
            q = qacc[s]
            at_end = lax.broadcasted_iota(jnp.int32, (SPAN, 1), 0) == SPAN - 1
            dcum = wred[s] - dt * q + jnp.where(at_end, ends[s][0:1], 0.0)
            glog = running_sum(dcum, False)
            gpd = (q - rate * glog) * sigmoid(v)
            lanes = lax.broadcasted_iota(jnp.int32, (SPAN, HALF), 1) < HEADS
            gpd = jnp.where(lanes, gpd, 0.0)
            gz_s[span(s), CONVW : CONVW + HALF] = gpd.astype(bf16)
            gdb[...] += jnp.sum(gpd, axis=0, keepdims=True)
            gdl[...] += -rate * jnp.sum(dt * glog, axis=0, keepdims=True)

        loop(0, seqs, bc_tile)
        convs.m_done(convs.chunks - 2)
        wave(2 * i + 1)
        partial(cols)
        pconv[:, CONVW : CONVW + HALF] = mm(nt[...], gz_s[:, CONVW : CONVW + HALF]).astype(bf16)
        convs.m_start(convs.chunks - 1)
        rows = [gcw[k : k + 1, j * HALF : (j + 1) * HALF] for k in range(KCONV) for j in range(CONVW // HALF)]
        rows += [gcb[:, j * HALF : (j + 1) * HALF] for j in range(CONVW // HALF)]
        rows += [gdb[...], gdl[...]]
        rows += [gather_heads(rows_of(gskip[...]), sel[:HALF])[0:1]]
        rows += [gggain[:, j * HALF : (j + 1) * HALF] for j in range(PAIRS)]
        little.held[0, SMALL_ROWS - 8 :] = jnp.zeros((8, HALF), f32)
        for r, row in enumerate(rows):
            little.held[0, r : r + 1, :] = row
        little.start(0)
        load_w.wait()
        edges = mm_nt(gzh_s[...], wfull[:, DIN:ZXW])
        for q in range(seqs):
            rim_out[q] = back(rhalo[q], edges[q * RIM : (q + 1) * RIM]).astype(bf16)
            pl.when(me > 0)(lambda q=q: rim_copy(q).start())

        @pl.when(me == count - 1)
        def _():
            rim_in[...] = jnp.zeros_like(rim_in)

    @pl.when(i == bc_step + 2)
    def _():
        little.done(0)
        little.start(1)

    @pl.when(i > bc_step)
    def _():
        s = i - bc_step - 1
        grad = mm_nt(gz_s[span(s), :CONVW], wfull[:, DIN:]) + mm_nt(ggate[0], wfull[:, :DIN])
        grad = grad + mm_nt(gz_s[span(s), CONVW:], wd[...])

        @pl.when(s == 0)
        def _():
            convs.m_done(convs.chunks - 1)

        wave(2 * i + 1)
        live = live_rows(lengths, s)
        out = live * cot[0].astype(f32) + back(tok[0], grad)
        gtok[0, : SPAN - RIM] = out[: SPAN - RIM].astype(bf16)
        pl.when(me < count - 1)(lambda: rim_copy(s).wait_recv())
        gtok[0, SPAN - RIM :] = (out[SPAN - RIM :] + rim_in[s].astype(f32)).astype(bf16)

    @pl.when(i == bc_step + seqs)
    def _():
        least.held[0] = jnp.zeros_like(least.held[0])
        for j in range(D // HALF):
            least.held[0, j : j + 1, :] = ggain[:, j * HALF : (j + 1) * HALF]
        least.start(0)
        little.done(1)
        small_out[...] = little.held[2]
        ends_at = max(last_conv + 4 * CONV_LAG, 1 + gates.chunks + outs.chunks + 3 * STAGE_LAG) + 1
        here = 2 * (bc_step + seqs) + 2
        loop(here, min(here + 2, ends_at), wave)
        least.done(0)
        least.start(1)
        loop(here + 2, ends_at, wave)
        for r in (gates, outs, convs):
            loop(0, r.chunks, r.drain_ctx)
        loop(0, convs.chunks, convs.drain_group)
        little.drain()
        for q in range(seqs):
            pl.when(me > 0)(lambda q=q: rim_copy(q).wait_send())
        least.done(1)
        ggain_out[...] = least.held[2]
        least.drain()


def done_kernel(
    rzx, rdelta, rout, small, gain_sum,
    g_gain, g_zx, g_delta, g_out, g_cw, g_cb, g_db, g_dl, g_skip, g_gated,
):
    @pl.when(pl.program_id(0) == 0)
    def _():
        tiles = CONVW // HALF
        for k in range(KCONV):
            for j in range(tiles):
                g_cw[k : k + 1, j * HALF : (j + 1) * HALF] = small[k * tiles + j : k * tiles + j + 1, :]
        at = KCONV * tiles
        for j in range(tiles):
            g_cb[j * HALF : (j + 1) * HALF] = small[at + j, :]
        at += tiles
        for ref in (g_db, g_dl, g_skip):
            ref[...] = small[at, :][:HEADS]
            at += 1
        for j in range(PAIRS):
            g_gated[j * HALF : (j + 1) * HALF] = small[at + j, :]
        for j in range(D // HALF):
            g_gain[j * HALF : (j + 1) * HALF] = gain_sum[j, :]
        g_delta[...] = jnp.transpose(rdelta[...].astype(f32))[:HEADS]

    g_zx[...] = rzx[:, :ZXW].astype(f32)
    g_out[...] = rout[...].astype(f32)


def whole(shape):
    zeros = (0,) * len(shape)
    return pl.BlockSpec(shape, lambda s: zeros, pipeline_mode=pl.Buffered(1))


def summed(shape):
    zeros = (0,) * len(shape)
    return pl.BlockSpec(shape, lambda s: zeros)


def per_seq(*shape):
    zeros = (0,) * len(shape)
    return pl.BlockSpec((1,) + shape, lambda s: (s,) + zeros)


SMEM = pl.BlockSpec(memory_space=pltpu.SMEM)
ANY = pl.BlockSpec(memory_space=pl.ANY)


def staged(seqs, phase, *shape):
    zeros = (0,) * len(shape)
    if phase == 0:
        return pl.BlockSpec((1,) + shape, lambda i: (jnp.minimum(i, seqs - 1),) + zeros)
    if phase == 1:
        return pl.BlockSpec((1,) + shape, lambda i: (jnp.maximum(i - seqs, 0),) + zeros)
    return pl.BlockSpec((1,) + shape, lambda i: (lax.rem(i, seqs),) + zeros)


def call(kernel, steps, in_specs, outs, scratch, name, collective=None):
    params = dict(vmem_limit_bytes=VMEM_LIMIT)
    if collective is not None:
        params.update(collective_id=collective, has_side_effects=True)
    return pl.pallas_call(
        kernel,
        grid=(steps,),
        in_specs=in_specs,
        out_specs=[o[0] for o in outs],
        out_shape=[jax.ShapeDtypeStruct(o[1], o[2]) for o in outs],
        scratch_shapes=[pltpu.VMEM(*sc) if isinstance(sc, tuple) else sc for sc in scratch],
        compiler_params=pltpu.CompilerParams(**params),
        name=name,
    )


def local(
    tokens_in, seq_lengths, norm_gain, w_zx, w_delta, w_out, conv_weight, conv_bias,
    delta_bias, decay_log, skip_gain, gated_gain, cotangent,
):
    seqs = tokens_in.shape[0]
    count = lax.axis_size("ctx")
    group = lax.axis_size("group")
    chips = max(group // 2, 1)
    w_delta = jnp.pad(w_delta, ((0, 0), (0, HALF - HEADS)))
    dma = pltpu.SemaphoreType.DMA
    at0 = lambda *shape: staged(seqs, 0, *shape)
    at1 = lambda *shape: staged(seqs, 1, *shape)
    at01 = lambda *shape: staged(seqs, 2, *shape)

    def tiled(rows, first, lead=None):
        def index(i):
            u = jnp.clip(i - first, 0, TILES - 1)
            return (0, 0, u if lead is None else jnp.where(i == 0, lead, u))

        return pl.BlockSpec((seqs, rows, TILE), index)

    state = (seqs, NSTATE, DIN)
    nt, nth, rhalo, cin, xb, spb, vraw, cum, st0, loc, ylocal, gate, decs, wfull, wdfull, wofull, state_in = call(
        front_kernel,
        PIECES,
        [whole((seqs, SPAN, D)), ANY, ANY, ANY, ANY, whole((D,)), whole((KCONV, CONVW)), whole((CONVW,)), SMEM, SMEM],
        [
            (summed((D, seqs * SPAN)), (D, seqs * SPAN), bf16),
            (summed((D, seqs * RIM)), (D, seqs * RIM), bf16),
            (summed((seqs, RIM, D)), (seqs, RIM, D), bf16),
            (tiled(RIM + SPAN, 1, TILES), (seqs, RIM + SPAN, CONVW), bf16),
            (tiled(SPAN, 1, TILES), (seqs, SPAN, CONVW), bf16),
            (tiled(SPAN, 1, TILES), (seqs, SPAN, CONVW), bf16),
            (summed((seqs, SPAN, HALF)), (seqs, SPAN, HALF), f32),
            (summed((seqs, SPAN, HALF)), (seqs, SPAN, HALF), f32),
            (tiled(NSTATE, 1), state, bf16),
            (tiled(NSTATE, 1), state, bf16),
            (tiled(SPAN, TILES + 1), (seqs, SPAN, DIN), bf16),
            (tiled(SPAN, TILES + 1), (seqs, SPAN, DIN), bf16),
            (summed((seqs, count * 8, HALF)), (seqs, count * 8, HALF), f32),
            (ANY, (D, ZXW), bf16),
            (ANY, (D, HALF), bf16),
            (ANY, (DIN, D), bf16),
            (ANY, state, bf16),
        ],
        [((2 * HALF, DIN), bf16), ((seqs, RIM, D), bf16), ((seqs * RIM, D), f32), ((seqs, RIM + SPAN, D), bf16), ((D, ZXW), bf16),
         ((D, HALF), bf16), ((1, CONVW), f32),
         ((seqs, RIM + SPAN, TILE), f32), ((seqs, SPAN, DIN), bf16), ((seqs, NSTATE, SPAN), bf16),
         ((seqs, 2, HALF, HALF), f32), ((seqs, SPAN, 2 * HALF), bf16), ((seqs, SPAN, 2 * HALF), bf16),
         ((seqs, 2, HALF, HALF), f32), ((seqs, 8, DIN), f32), ((seqs, count * 8, HALF), f32)]
        + [dma((2,))] + [dma((PIECES + 2, chips))] * 4 + [dma((3,)), dma((2,)), dma((count,)), dma((count,))]
        + Exchange.scratch(TILES, seqs, TILE, count),
        "front",
        0,
    )(tokens_in, tokens_in, w_zx, w_delta, w_out, norm_gain, conv_weight, conv_bias, delta_bias, decay_log)

    x_gate_shape = (DIN // GATE_CHUNK, D // group, GATE_CHUNK)
    x_out_shape = (D // OUT_CHUNK, DIN // group, OUT_CHUNK)
    mixed_out, dy, ggate, wred, dir1, gskip, gggain, dxs, dbc, x_gate, x_out, later = call(
        middle_kernel,
        2 * seqs,
        [SMEM, SMEM, at1(SPAN, D), at0(SPAN, D), at0(SPAN, DIN), at0(SPAN, DIN), at01(SPAN, CONVW), at01(SPAN, HALF),
         at01(SPAN, HALF), at0(NSTATE, DIN), at0(NSTATE, DIN), whole((seqs, count * 8, HALF)), whole((DIN, D)),
         whole((DIN,)), whole((D, seqs * SPAN))],
        [
            (at1(SPAN, D), (seqs, SPAN, D), bf16),
            (at0(SPAN, DIN), (seqs, SPAN, DIN), bf16),
            (at0(SPAN, DIN), (seqs, SPAN, DIN), bf16),
            (at0(SPAN, HALF), (seqs, SPAN, HALF), f32),
            (at0(NSTATE, DIN), (seqs, NSTATE, DIN), bf16),
            (summed((1, DIN)), (1, DIN), f32),
            (summed((1, DIN)), (1, DIN), f32),
            (at1(SPAN, DIN), (seqs, SPAN, DIN), bf16),
            (at1(SPAN, 2 * NSTATE), (seqs, SPAN, 2 * NSTATE), f32),
            (summed(x_gate_shape), x_gate_shape, bf16),
            (summed(x_out_shape), x_out_shape, bf16),
            (ANY, (seqs, NSTATE, DIN), bf16),
        ],
        [((2 * HALF, DIN), bf16), ((1, DIN), f32), ((1, DIN), f32), ((2, HALF, HALF), f32), ((SPAN, DIN), f32), ((SPAN, DIN), f32), ((SPAN, DIN), f32),
         ((SPAN, DIN), f32), ((2, NSTATE, DIN), bf16), ((seqs, SPAN, HALF), f32), ((seqs, SPAN, DIN), bf16),
         ((seqs * SPAN, DIN), bf16), ((seqs * SPAN, DIN), bf16), ((seqs * SPAN, D), bf16), ((D, DIN), bf16), ((DIN, D), bf16),
         ((2, HALF, HALF), f32), ((2, HALF, HALF), f32)]
        + Exchange.scratch(seqs, 1, DIN, count)
        + Reducer.group_scratch(*x_gate_shape, group)
        + Reducer.group_scratch(*x_out_shape, group),
        "middle",
        1,
    )(seq_lengths, skip_gain, tokens_in, cotangent, ylocal, gate, xb, vraw, cum, st0, state_in, decs, wofull, gated_gain, nt)

    def tile_in(rows, tiles):
        return pl.BlockSpec((seqs, rows, TILE), lambda i: (0, 0, jnp.minimum(i, tiles - 1)))

    def late(*shape):
        zeros = (0,) * len(shape)
        return pl.BlockSpec((1,) + shape, lambda i: (jnp.clip(i - TILES - 1, 0, seqs - 1),) + zeros)

    bc_spec = pl.BlockSpec((seqs, SPAN, TILE), lambda i: (0, 0, TILES), pipeline_mode=pl.Buffered(1))
    height = SMALL_ROWS
    x_conv_shape = (GZW // CONV_CHUNK, D // group, CONV_CHUNK)
    gtok, r_zx, r_out, small, gain_sum = call(
        back_kernel,
        TILES + 1 + seqs,
        [SMEM, SMEM, SMEM, late(SPAN, D), late(SPAN, D), whole((seqs, RIM, D)), whole((D,)), late(SPAN, DIN), ANY, whole((D, HALF)),
         tile_in(RIM + SPAN, TILES + 1), tile_in(SPAN, TILES + 1), tile_in(SPAN, TILES + 1), bc_spec, tile_in(SPAN, TILES),
         tile_in(SPAN, TILES), tile_in(NSTATE, TILES), tile_in(NSTATE, TILES), tile_in(NSTATE, TILES), tile_in(NSTATE, TILES),
         whole((seqs, SPAN, HALF)), whole((seqs, SPAN, HALF)), whole((seqs, SPAN, HALF)), whole((seqs, SPAN, 2 * NSTATE)),
         whole((KCONV, CONVW)), whole((D, seqs * SPAN)), whole((D, seqs * RIM)),
         whole(x_gate_shape), whole(x_out_shape), whole((1, DIN)), whole((1, DIN))],
        [
            (late(SPAN, D), (seqs, SPAN, D), bf16),
            (summed((D // group, DIN + GZW)), (D // group, DIN + GZW), bf16),
            (summed((DIN // group, D)), (DIN // group, D), bf16),
            (summed((height, HALF)), (height, HALF), f32),
            (summed((8, HALF)), (8, HALF), f32),
        ],
        [((2 * HALF, DIN), bf16), ((1, DIN), f32), ((D, ZXW), bf16), dma((1,)), ((seqs, SPAN, 2 * HALF), bf16),
         ((seqs, SPAN, 2 * HALF), bf16), ((seqs, 16, DIN), f32),
         ((seqs, SPAN, NSTATE), f32), ((seqs, SPAN, HALF), f32), ((seqs, 8, HALF), f32), ((2, RIM + SPAN + 8, TILE), f32),
         ((seqs * SPAN, CONVW + HALF), bf16), ((seqs * RIM, CONVW), bf16), ((D, GZW), bf16), ((KCONV, CONVW), f32),
         ((1, CONVW), f32), ((1, HALF), f32), ((1, HALF), f32), ((1, D), f32), ((seqs, RIM, D), bf16), ((seqs, RIM, D), bf16),
         dma((seqs,)), dma((seqs,))]
        + Reducer.ctx_scratch(*x_gate_shape, False, count)
        + Reducer.ctx_scratch(*x_out_shape, True, count)
        + Reducer.group_scratch(*x_conv_shape, group)
        + [(x_conv_shape, bf16)]
        + Reducer.ctx_scratch(*x_conv_shape, False, count)
        + Small.scratch(height, group, count)
        + Small.scratch(8, group, count),
        "back",
        2,
    )(seq_lengths, decay_log, skip_gain, tokens_in, cotangent, rhalo, norm_gain, ggate, wfull, wdfull, cin, xb, spb, xb, dy, dxs, dir1, later, state_in, loc,
      vraw, cum, wred, dbc, conv_weight, nt, nth, x_gate, x_out, gskip, gggain)

    zx_rows, out_rows = D // group, DIN // group
    turns = 2
    halved = lambda rows, cols: pl.BlockSpec((rows // turns, cols), lambda i: (i, 0))
    grad = lambda *shape: (summed(shape), jax.ShapeDtypeStruct(shape, f32))
    specs, shapes = zip(
        grad(D), (halved(zx_rows, ZXW), jax.ShapeDtypeStruct((zx_rows, ZXW), f32)),
        grad(HEADS, zx_rows), (halved(out_rows, D), jax.ShapeDtypeStruct((out_rows, D), f32)), grad(KCONV, CONVW), grad(CONVW),
        grad(HEADS), grad(HEADS), grad(HEADS), grad(DIN),
    )
    results = pl.pallas_call(
        done_kernel,
        grid=(turns,),
        in_specs=[halved(zx_rows, DIN + GZW), pl.BlockSpec((zx_rows, HALF), lambda i: (0, ZXW // HALF)), halved(out_rows, D),
                  whole((SMALL_ROWS, HALF)), whole((8, HALF))],
        out_specs=specs,
        out_shape=shapes,
        name="done",
    )(r_zx, r_zx, r_out, small, gain_sum)
    return (mixed_out, gtok, *results[:2], results[2].T, *results[3:])


def solution(mesh):
    rows = P("group", "ctx", None)
    own = P("group", None)
    in_specs = (rows, P("group"), P(), own, own, own, P(), P(), P(), P(), P(), P(), rows)
    out_specs = (rows, rows, P(), own, own, own, P(), P(), P(), P(), P(), P())
    return jax.shard_map(local, mesh=mesh, in_specs=in_specs, out_specs=out_specs, check_vma=False)
```

```python
import jax
import jax.numpy as jnp
from jax import lax
from jax.experimental import pallas as pl
from jax.experimental.pallas import tpu as pltpu
from jax.sharding import PartitionSpec as P

D = 768
HEADS = 24
HEADDIM = 64
NSTATE = 128
KCONV = 4
SPAN = 256
DIN = 1536
CONVW = 1792
ZXW = 3328
RIM = 16
HALF = 128
TILE = 256
PAIRS = 12
EPS = 1e-05

f32 = jnp.float32
bf16 = jnp.bfloat16
NT = (((1,), (1,)), ((), ()))
TN = (((0,), (0,)), ((), ()))
VMEM_LIMIT = 63 * 1024 * 1024
GATE_CHUNK = 512
OUT_CHUNK = 256
CONV_CHUNK = 512
BACK_LAGS = (4, 7, 9)
STAGE_LAG = 4
CONV_LAG = 3
MIDDLE_LAG = 2
SCAN_LAG = 4
HOPS = ("group", "ctx")
SMALL_ROWS = 88
CLOSE_LAG = 6
GZW = 2048


def mm(a, b):
    return jnp.dot(a, b, preferred_element_type=f32)


def mm_nt(a, b):
    return lax.dot_general(a, b, NT, preferred_element_type=f32)


def mm_tn(a, b):
    return lax.dot_general(a, b, TN, preferred_element_type=f32)


def halves(v):
    high = v.astype(bf16)
    return high, (v - high.astype(f32)).astype(bf16)


def head_map():
    rows = lax.broadcasted_iota(jnp.int32, (2 * HALF, DIN), 0) % HALF
    cols = lax.broadcasted_iota(jnp.int32, (2 * HALF, DIN), 1) // HEADDIM
    return jnp.where(rows == cols, 1.0, 0.0).astype(bf16)


def spread(v, sel):
    return mm(jnp.concatenate(halves(v), axis=1), sel[...])


def gather_heads(v, sel_part):
    high, low = halves(v)
    return mm_nt(high, sel_part) + mm_nt(low, sel_part)


def triangle(size, lower):
    rows = lax.broadcasted_iota(jnp.int32, (size, size), 0)
    cols = lax.broadcasted_iota(jnp.int32, (size, size), 1)
    keep = rows >= cols if lower else rows <= cols
    return jnp.where(keep, 1.0, 0.0).astype(f32)


def running_sum(v, lower):
    rest, terms = v, []
    for _ in range(3):
        high = rest.astype(bf16)
        rest = rest - high.astype(f32)
        terms.append(high)
    tri = triangle(v.shape[0], lower).astype(bf16)
    return mm(tri, terms[0]) + (mm(tri, terms[1]) + mm(tri, terms[2]))


def softplus(v):
    return jnp.maximum(v, 0.0) + jnp.log1p(jnp.exp(-jnp.abs(v)))


def sigmoid(v):
    return 1.0 / (1.0 + jnp.exp(-v))


def gate_of(v):
    return 0.5 * jnp.tanh(0.5 * v) + 0.5


def local_decays(cum):
    mid, end = cum[HALF - 1 : HALF], cum[SPAN - 1 : SPAN]
    rows = lax.broadcasted_iota(jnp.int32, (SPAN, 1), 0)
    first = rows < HALF
    start = jnp.where(first, 0.0, mid)
    stop = jnp.where(first, mid, end)
    return jnp.exp(cum - start), jnp.exp(stop - cum), jnp.exp(mid), jnp.exp(end - mid), jnp.exp(end)


def rows_of(v):
    return jnp.broadcast_to(v, (8, v.shape[1]))


def lane_row(ref):
    lanes = lax.broadcasted_iota(jnp.int32, (1, HALF), 1)
    row = jnp.zeros((1, HALF), f32)
    for h in range(HEADS):
        row = jnp.where(lanes == h, ref[h], row)
    return row


def row_of(ref):
    return ref[...].reshape(1, ref.shape[0])


def live_rows(lengths, s):
    start = lax.axis_index("ctx") * SPAN
    return (lax.broadcasted_iota(jnp.int32, (SPAN, 1), 0) + start < lengths[s]).astype(f32)


def normalized(rows, gain):
    rows = rows.astype(f32)
    inv = lax.rsqrt(jnp.mean(rows * rows, axis=-1, keepdims=True) + EPS)
    return rows, inv, (rows * inv * gain).astype(bf16)


def remote(src, dst, send_sem, recv_sem, **where):
    return pltpu.make_async_remote_copy(
        src_ref=src, dst_ref=dst, send_sem=send_sem, recv_sem=recv_sem,
        device_id=where, device_id_type=pl.DeviceIdType.MESH,
    )


def loop(start, stop, body):
    def step(i, c):
        body(i)
        return c

    lax.fori_loop(start, stop, step, 0)


def greet(axes):
    barrier = pltpu.get_barrier_semaphore()
    for axis in axes:
        size = lax.axis_size(axis)
        me = lax.axis_index(axis)

        def signal(d, axis=axis, size=size, me=me):
            pl.semaphore_signal(
                barrier, inc=1, device_id={axis: lax.rem(me + d, size)}, device_id_type=pl.DeviceIdType.MESH
            )

        loop(1, size, signal)


def settle(axes):
    pl.semaphore_wait(pltpu.get_barrier_semaphore(), sum(lax.axis_size(axis) - 1 for axis in axes))


def meet(axes):
    greet(axes)
    settle(axes)


class Exchange:
    def __init__(self, reverse, out_at, bufs, sems):
        self.reverse, self.out_at, self.sems = reverse, out_at, sems
        self.buf, self.y_buf, self.z_src, self.z_buf, self.z_back, self.p_buf, self.mine_buf, self.their_buf, self.decx = bufs
        self.depth = self.buf.shape[1]
        ctx = lax.axis_index("ctx")
        self.ctx = ctx
        self.outer = lax.axis_size("ctx") // 2
        self.owners = min(self.outer, 4)
        self.stride = self.outer // self.owners
        self.inner = lax.rem(ctx, 2)
        self.line = ctx // 2
        self.mine = self.line // self.stride
        self.half = NSTATE // 2
        self.rows = self.half // self.owners

    def half_rows(self, inner):
        return pl.ds(pl.multiple_of(inner * self.half, self.half), self.half)

    def part(self, j):
        return pl.ds(pl.multiple_of(j * self.rows, self.rows), self.rows)

    def other_owners(self, body):
        if self.stride == 1:
            loop(1, self.owners, lambda d: body(lax.rem(self.mine + d, self.owners)))
        else:
            loop(0, self.owners, lambda j: pl.when(j * self.stride != self.line)(lambda: body(j)))

    def other_lines(self, body):
        loop(1, self.outer, lambda d: body(lax.rem(self.line + d, self.outer)))

    def if_owner(self, body):
        if self.stride == 1:
            body()
        else:
            pl.when(self.mine * self.stride == self.line)(body)

    def y_copy(self, u):
        return remote(
            self.buf.at[u, :, self.half_rows(1 - self.inner)], self.y_buf.at[u], self.sems.at[0, u, 0], self.sems.at[1, u, 0],
            ctx=self.ctx + 1 - 2 * self.inner,
        )

    def z_copy(self, u, j, sender):
        return remote(
            self.z_src.at[u, :, self.part(j)], self.z_buf.at[u, sender], self.sems.at[2, u, j], self.sems.at[3, u, sender],
            ctx=j * self.stride * 2 + self.inner,
        )

    def b_copy(self, u, line, j):
        return remote(
            self.z_back.at[u, line], self.p_buf.at[u, :, self.part(j)], self.sems.at[4, u, line], self.sems.at[5, u, j],
            ctx=line * 2 + self.inner,
        )

    def f_copy(self, u, inner):
        return remote(
            self.their_buf.at[u], self.out_at(u, self.half_rows(inner)), self.sems.at[6, u, 0], self.sems.at[7, u, 0],
            ctx=self.ctx + 1 - 2 * self.inner,
        )

    def keep(self, u):
        return pltpu.make_async_copy(self.mine_buf.at[u], self.out_at(u, self.half_rows(self.inner)), self.sems.at[8, u, 0])

    def decay(self, a, block):
        return self.decx[a, pl.ds(pl.multiple_of(block * 8, 8), 8), :][0:1]

    def pair(self, u, a):
        own = self.buf[u, a, self.half_rows(self.inner), :].astype(f32)
        other = self.y_buf[u, a].astype(f32)
        first = self.inner == 0
        return jnp.where(first, own, other), jnp.where(first, other, own)

    def start(self, u):
        self.y_copy(u).start()

    def middle(self, u):
        self.y_copy(u).wait_recv()
        for a in range(self.depth):
            s0, s1 = self.pair(u, a)
            if self.reverse:
                total = s0 + self.decay(a, 2 * self.line) * s1
            else:
                total = self.decay(a, 2 * self.line + 1) * s0 + s1
            self.z_src[u, a] = total.astype(bf16)
        self.other_owners(lambda j: self.z_copy(u, j, self.line).start())

    def scan(self, u):
        def run():
            self.other_lines(lambda line: self.z_copy(u, self.mine, line).wait_recv())
            self.z_buf[u, self.line] = self.z_src[u, :, self.part(self.mine), :]
            for a in range(self.depth):

                def step(k, carry):
                    line = self.outer - 1 - k if self.reverse else k
                    self.z_back[u, line, a] = carry.astype(bf16)
                    both_decays = self.decay(a, 2 * line) * self.decay(a, 2 * line + 1)
                    return both_decays * carry + self.z_buf[u, line, a].astype(f32)

                lax.fori_loop(0, self.outer, step, jnp.zeros(self.z_buf.shape[3:], f32))
            self.other_lines(lambda line: self.b_copy(u, line, self.mine).start())
            self.p_buf[u, :, self.part(self.mine), :] = self.z_back[u, self.line]

        self.if_owner(run)

    def close(self, u):
        self.other_owners(lambda j: self.b_copy(u, self.line, j).wait_recv())
        for a in range(self.depth):
            s0, s1 = self.pair(u, a)
            near = self.p_buf[u, a].astype(f32)
            if self.reverse:
                far = s1 + self.decay(a, 2 * self.line + 1) * near
            else:
                far = s0 + self.decay(a, 2 * self.line) * near
            keeps_near = self.inner == (1 if self.reverse else 0)
            self.mine_buf[u, a] = jnp.where(keeps_near, near, far).astype(bf16)
            self.their_buf[u, a] = jnp.where(keeps_near, far, near).astype(bf16)
        self.f_copy(u, self.inner).start()
        self.keep(u).start()

    def finish(self, u):
        self.f_copy(u, 1 - self.inner).wait_recv()
        self.keep(u).wait()
        self.y_copy(u).wait_send()
        self.other_owners(lambda j: self.z_copy(u, j, self.line).wait_send())
        self.if_owner(lambda: self.other_lines(lambda line: self.b_copy(u, line, self.mine).wait_send()))
        self.f_copy(u, self.inner).wait_send()

    @staticmethod
    def scratch(units, depth, lanes, count):
        outer = count // 2
        half = NSTATE // 2
        rows = half // min(outer, 4)
        bufs = [(units, depth, NSTATE, lanes), (units, depth, half, lanes), (units, depth, half, lanes),
                (units, outer, depth, rows, lanes), (units, outer, depth, rows, lanes), (units, depth, half, lanes),
                (units, depth, half, lanes), (units, depth, half, lanes)]
        return (
            [(b, bf16) for b in bufs]
            + [((depth, count * 8, lanes), f32)]
            + [pltpu.SemaphoreType.DMA((9, units, max(outer, 4)))]
        )


class Spread:
    def __init__(self, shard, full, sems):
        self.shard, self.full = shard, full
        self.x_send, self.x_recv, self.m_send, self.m_recv, self.own = sems
        size = lax.axis_size("group")
        self.cores = 2 if size % 2 == 0 else 1
        self.chips = size // self.cores
        self.me = lax.axis_index("group")
        self.core = lax.rem(self.me, self.cores)
        self.chip = self.me // self.cores
        self.rows = shard.shape[0]

    def place(self, member, cols):
        return self.full.at[pl.ds(pl.multiple_of(member * self.rows, 32), self.rows), cols]

    def across(self, p, cols, d):
        peer = lax.rem(self.chip + d, self.chips) * self.cores + self.core
        return remote(
            self.shard.at[:, cols], self.place(self.me, cols), self.x_send.at[p, d], self.x_recv.at[p, d], group=peer
        )

    def mate(self, p, cols, d):
        member = lax.rem(self.chip + self.chips - d, self.chips) * self.cores + self.core
        src = self.shard.at[:, cols] if d == 0 else self.place(member, cols)
        return remote(
            src, self.place(member, cols), self.m_send.at[p, d], self.m_recv.at[p, d],
            group=self.me + 1 - 2 * self.core,
        )

    def keep(self, p):
        return pltpu.make_async_copy(self.shard, self.place(self.me, slice(None)), self.own.at[p])

    def start_chip(self, p):
        if self.cores == 2:
            self.mate(p, slice(None), 0).start()
        self.keep(p).start()

    def finish_chip(self, p):
        if self.cores == 2:
            self.mate(p, slice(None), 0).wait_recv()
        self.keep(p).wait()

    def start(self, p, cols):
        for d in range(1, self.chips):
            self.across(p, cols, d).start()

    def forward(self, p, cols):
        for d in range(1, self.chips):
            self.across(p, cols, d).wait_recv()
            if self.cores == 2:
                self.mate(p, cols, d).start()

    def finish(self, p, cols):
        if self.cores == 2:
            for d in range(1, self.chips):
                self.mate(p, cols, d).wait_recv()

    def drain(self, p, cols):
        for d in range(1, self.chips):
            self.across(p, cols, d).wait_send()
            if self.cores == 2:
                self.mate(p, cols, d).wait_send()

    def drain_chip(self, p):
        if self.cores == 2:
            self.mate(p, slice(None), 0).wait_send()


def owner_count(rows, width, by_rows, outer):
    fits = lambda n: (rows // 2) % (16 * n) == 0 if by_rows else width % (128 * n) == 0
    return max(n for n in (1, 2, 4) if outer % n == 0 and fits(n))


class Reducer:
    def __init__(self, part, out, rows, width, by_rows, group_bufs, ctx_bufs):
        self.part, self.out, self.rows, self.width, self.by_rows = part, out, rows, width, by_rows
        if group_bufs is not None:
            self.m_buf, self.x_buf, self.g_sems = group_bufs
        self.ships = ctx_bufs is not None
        if self.ships:
            self.y_src, self.y_buf, self.z_src, self.z_buf, self.full, self.c_sems = ctx_bufs
        else:
            self.y_src = out
        self.chunks = self.y_src.shape[0]
        self.base = 0
        self.group = lax.axis_index("group")
        self.cores = 2
        self.chips = lax.axis_size("group") // 2
        self.core = lax.rem(self.group, 2)
        self.chip = self.group // 2
        self.ctx = lax.axis_index("ctx")
        self.outer = lax.axis_size("ctx") // 2
        self.owners = owner_count(rows, width, by_rows, self.outer)
        self.stride = self.outer // self.owners
        self.inner = lax.rem(self.ctx, 2)
        self.line = self.ctx // 2
        self.mine = self.line // self.stride
        self.half = rows // 2

    def cols(self, k):
        return pl.ds(pl.multiple_of(k * self.width, self.width), self.width)

    def member(self, chip, core):
        return pl.ds(pl.multiple_of((chip * 2 + core) * self.rows, 64), self.rows)

    def half_rows(self, inner):
        return pl.ds(pl.multiple_of(inner * self.half, 16), self.half)

    def piece(self, j, base):
        if self.by_rows:
            n = self.half // self.owners
            return pl.ds(pl.multiple_of(base + j * n, 16), n), pl.ds(0, self.width)
        n = self.width // self.owners
        return pl.ds(pl.multiple_of(base, 16), self.half), pl.ds(pl.multiple_of(j * n, 128), n)

    def m_copy(self, k, chip):
        return remote(
            self.part.at[self.member(chip, 1 - self.core), self.cols(k)], self.m_buf.at[k, chip],
            self.g_sems.at[0, k, chip], self.g_sems.at[1, k, chip], group=self.group + 1 - 2 * self.core,
        )

    def x_copy(self, k, chip, sender):
        return remote(
            self.m_buf.at[k, chip], self.x_buf.at[k, sender], self.g_sems.at[2, k, chip], self.g_sems.at[3, k, sender],
            group=chip * 2 + self.core,
        )

    def y_copy(self, k):
        return remote(
            self.y_src.at[k, self.half_rows(1 - self.inner)], self.y_buf.at[k], self.c_sems.at[0, k, 0], self.c_sems.at[1, k, 0],
            ctx=self.ctx + 1 - 2 * self.inner,
        )

    def z_copy(self, k, j, sender):
        rows, cols = self.piece(j, 0)
        return remote(
            self.z_src.at[k, rows, cols], self.z_buf.at[k, sender], self.c_sems.at[2, k, j], self.c_sems.at[3, k, sender],
            ctx=j * self.stride * 2 + self.inner,
        )

    def b_copy(self, k, line, j):
        rows, cols = self.piece(j, self.inner * self.half)
        return remote(
            self.full.at[k, rows, cols], self.full.at[k, rows, cols], self.c_sems.at[4, k, line], self.c_sems.at[5, k, j],
            ctx=line * 2 + self.inner,
        )

    def f_copy(self, k, inner):
        rows = self.half_rows(inner)
        return remote(
            self.full.at[k, rows], self.full.at[k, rows], self.c_sems.at[6, k, 0], self.c_sems.at[7, k, 0],
            ctx=self.ctx + 1 - 2 * self.inner,
        )

    def other_chips(self, body):
        for d in range(1, self.chips):
            body(lax.rem(self.chip + d, self.chips))

    def other_owners(self, body):
        if self.stride == 1:
            for d in range(1, self.owners):
                body(lax.rem(self.mine + d, self.owners))
        else:
            for j in range(self.owners):
                pl.when(j * self.stride != self.line)(lambda j=j: body(j))

    def other_lines(self, body):
        loop(1, self.outer, lambda d: body(lax.rem(self.line + d, self.outer)))

    def if_owner(self, body):
        if self.stride == 1:
            body()
        else:
            pl.when(self.mine * self.stride == self.line)(body)

    def m_start(self, k):
        for chip in range(self.chips):
            self.m_copy(k, chip).start()

    def m_done(self, k):
        for chip in range(self.chips):
            self.m_copy(k, chip).wait_recv()
            own = self.part[self.member(chip, self.core), self.cols(k)].astype(f32)
            self.m_buf[k, chip] = (own + self.m_buf[k, chip].astype(f32)).astype(bf16)
        self.other_chips(lambda chip: self.x_copy(k, chip, self.chip).start())

    def x_done(self, k):
        total = self.m_buf[k, self.chip].astype(f32)
        for d in range(1, self.chips):
            chip = lax.rem(self.chip + d, self.chips)
            self.x_copy(k, chip, chip).wait_recv()
            total = total + self.x_buf[k, chip].astype(f32)
        self.y_src[k] = total.astype(bf16)
        if self.ships:
            self.y_start(k)

    def y_start(self, k):
        self.y_copy(k).start()

    def y_done(self, k):
        self.y_copy(k).wait_recv()
        own = self.y_src[k, self.half_rows(self.inner), :].astype(f32)
        self.z_src[k] = (own + self.y_buf[k].astype(f32)).astype(bf16)
        self.other_owners(lambda j: self.z_copy(k, j, self.line).start())

    def z_done(self, k):
        def run():
            rows, cols = self.piece(self.mine, 0)
            self.other_lines(lambda line: self.z_copy(k, self.mine, line).wait_recv())
            self.z_buf[k, self.line] = self.z_src[k, rows, cols]
            total = self.z_buf[k, 0].astype(f32)
            for line in range(1, self.outer):
                total = total + self.z_buf[k, line].astype(f32)
            rows, cols = self.piece(self.mine, self.inner * self.half)
            self.full[k, rows, cols] = total.astype(bf16)
            self.other_lines(lambda line: self.b_copy(k, line, self.mine).start())

        self.if_owner(run)

    def b_done(self, k):
        self.other_owners(lambda j: self.b_copy(k, self.line, j).wait_recv())
        self.f_copy(k, self.inner).start()

    def f_done(self, k):
        self.f_copy(k, 1 - self.inner).wait_recv()
        self.out[:, pl.ds(pl.multiple_of(self.base + k * self.width, 128), self.width)] = self.full[k]

    def drain_group(self, k):
        for chip in range(self.chips):
            self.m_copy(k, chip).wait_send()
        self.other_chips(lambda chip: self.x_copy(k, chip, self.chip).wait_send())

    def drain_ctx(self, k):
        self.y_copy(k).wait_send()
        self.other_owners(lambda j: self.z_copy(k, j, self.line).wait_send())
        self.if_owner(lambda: self.other_lines(lambda line: self.b_copy(k, line, self.mine).wait_send()))
        self.f_copy(k, self.inner).wait_send()

    def wave(self, t, acts, chunk_at, lag=STAGE_LAG):
        for order, act in reversed(list(enumerate(acts))):
            k, is_due = chunk_at(t - order * lag)
            pl.when(is_due)(lambda k=k, act=act: act(k))

    def each(self, t):
        return t, jnp.logical_and(t >= 0, t < self.chunks)

    @staticmethod
    def group_scratch(chunks, rows, width, group):
        chips = group // 2
        buf = ((chunks, chips, rows, width), bf16)
        return [buf, buf, pltpu.SemaphoreType.DMA((4, chunks, max(chips, 2)))]

    @staticmethod
    def ctx_scratch(chunks, rows, width, by_rows, count):
        outer = count // 2
        owners = owner_count(rows, width, by_rows, outer)
        half = rows // 2
        piece = (half // owners, width) if by_rows else (half, width // owners)
        bufs = [(chunks, half, width), (chunks, half, width), (chunks, outer) + piece, (chunks, rows, width)]
        return [(b, bf16) for b in bufs] + [pltpu.SemaphoreType.DMA((8, chunks, max(outer, 2)))]


class Small:
    def __init__(self, held, got, sends, recvs):
        self.held, self.got, self.sends, self.recvs = held, got, sends, recvs

    def copy(self, h, j, sender):
        return remote(
            self.held.at[h], self.got.at[h, sender], self.sends.at[h, j], self.recvs.at[h, sender], **{HOPS[h]: j}
        )

    def others(self, h, body):
        size, mine = lax.axis_size(HOPS[h]), lax.axis_index(HOPS[h])
        loop(1, size, lambda d: body(lax.rem(mine + d, size)))

    def start(self, h):
        mine = lax.axis_index(HOPS[h])
        self.others(h, lambda j: self.copy(h, j, mine).start())

    def done(self, h):
        self.others(h, lambda j: self.copy(h, j, j).wait_recv())
        self.got[h, lax.axis_index(HOPS[h])] = self.held[h]
        total = self.got[h, 0]
        for j in range(1, lax.axis_size(HOPS[h])):
            total = total + self.got[h, j]
        self.held[h + 1] = total

    def drain(self):
        for h in range(2):
            mine = lax.axis_index(HOPS[h])
            self.others(h, lambda j: self.copy(h, j, mine).wait_send())

    @staticmethod
    def scratch(height, group, count):
        widest = max(group, count)
        dma = pltpu.SemaphoreType.DMA
        return [((3, height, HALF), f32), ((2, widest, height, HALF), f32), dma((2, widest)), dma((2, widest))]


def masks():
    rows = lax.broadcasted_iota(jnp.int32, (HALF, HALF), 0)
    cols = lax.broadcasted_iota(jnp.int32, (HALF, HALF), 1)
    return rows >= cols, cols < HEADDIM


def both(q):
    return slice(q * HALF, (q + 1) * HALF)


def pair_decays(cum, cum_t, p, causal):
    rolled = pltpu.roll(cum, lax.rem(HALF - 2 * p, HALF), 1)
    out = []
    for q in range(2):
        for a in range(2):
            gaps = rolled[both(q), a : a + 1] - cum_t[q, pl.ds(2 * p + a, 1), :]
            out.append(jnp.exp(jnp.where(causal, gaps, -jnp.inf)))
    return out


TILES = DIN // TILE
PIECES = 2 * TILES + 1
DT0 = DIN + CONVW - 2 * NSTATE
AHEAD = 5


def front_kernel(
    tok, tok_any, wzx, wdl, wout, gain, cw, cb_in, db, dl,
    nt, nth, rhalo, cin, xb, spb, vout, cumout, st0, loc, ylocal, gate, decs_out, wfull, wdfull, wofull, sin,
    sel, halo, nh_s, ext, w, wd, cb, cin_s, xs_s, bt, scores, out_cat, dt_cat, cum_t, tot1x, decs,
    halo_sem, x_send, x_recv, m_send, m_recv, w_own, w_store, dec_send, dec_recv, *exchange,
):
    i = pl.program_id(0)
    seqs = tok.shape[0]
    count = lax.axis_size("ctx")
    me = lax.axis_index("ctx")
    sems = (x_send, x_recv, m_send, m_recv, w_own)
    zx, wo, de = Spread(wzx, w, sems), Spread(wout, wofull, sems), Spread(wdl, wd, sems)
    last, small_piece = PIECES, PIECES + 1

    def unit_cols(u):
        return pl.ds(pl.multiple_of(u * TILE, TILE), TILE)

    def piece(p):
        at = jnp.where(p <= TILES, DIN + (p - 1) * TILE, (p - 1 - TILES) * TILE)
        return pl.ds(pl.multiple_of(at, TILE), TILE)

    first_piece = pl.ds(DT0, 2 * NSTATE)
    ex = Exchange(False, lambda u, rows: sin.at[:, rows, unit_cols(u)], exchange[:9], exchange[9])
    halo_copy = remote(
        tok_any.at[:, pl.ds(SPAN - RIM, RIM), :], halo, halo_sem.at[0], halo_sem.at[1], ctx=lax.rem(me + 1, count)
    )
    keep_w = pltpu.make_async_copy(w, wfull, w_store.at[0])
    keep_d = pltpu.make_async_copy(wd, wdfull, w_store.at[1])

    def dec_copy(block, sender):
        rows = pl.ds(pl.multiple_of(sender * 8, 8), 8)
        return remote(decs.at[:, rows, :], decs.at[:, rows, :], dec_send.at[block], dec_recv.at[sender], ctx=block)

    def other_blocks(body):
        loop(1, count, lambda d: body(lax.rem(me + d, count)))

    def conv_tile(s, cols_w, cols_c):
        cin_s[s] = mm(ext[s], w[:, cols_w])
        cin[s] = cin_s[s].astype(bf16)
        o = cb[:, cols_c]
        for k in range(KCONV):
            o = o + cw[k : k + 1, cols_c] * cin_s[s, RIM - KCONV + 1 + k : RIM - KCONV + 1 + k + SPAN, :]
        sg = gate_of(o)
        a = o * sg
        xb[s] = a.astype(bf16)
        spb[s] = (sg + a * (1.0 - sg)).astype(bf16)
        return a

    def unit_decays(u):
        for s in range(seqs):
            ex.decx[s] = spread(decs[s], sel.at[:, unit_cols(u)])

    @pl.when(i == 0)
    def _():
        meet(("ctx", "group"))
        pl.when(me < count - 1)(lambda: halo_copy.start())
        de.start(small_piece, slice(None))
        zx.start(0, first_piece)
        de.start_chip(2)
        zx.start_chip(0)
        cb[...] = row_of(cb_in)
        for p in range(1, AHEAD):
            zx.start(p, piece(p))
        wo.start_chip(1)
        sel[...] = head_map()

        @pl.when(me == 0)
        def _():
            halo[...] = jnp.zeros_like(halo)

        def norm_main(s):
            nm = normalized(tok[s], row_of(gain))[2]
            ext[s, RIM:] = nm
            nt[:, pl.ds(pl.multiple_of(s * SPAN, SPAN), SPAN)] = jnp.transpose(nm.astype(f32)).astype(bf16)

        loop(0, seqs, norm_main)

        @pl.when(me > 0)
        def _():
            halo_copy.wait_recv()

        def norm_halo(s):
            nh = normalized(halo[s], row_of(gain))[2]
            ext[s, 0:RIM] = nh
            nh_s[pl.ds(pl.multiple_of(s * RIM, RIM), RIM), :] = nh.astype(f32)
            rhalo[s] = halo[s]

        loop(0, seqs, norm_halo)
        nth[...] = jnp.transpose(nh_s[...]).astype(bf16)
        de.forward(small_piece, slice(None))
        zx.forward(0, first_piece)
        zx.finish_chip(0)
        de.finish_chip(2)

    @pl.when(i + 1 < PIECES)
    def _():
        zx.forward(i + 1, piece(i + 1))

    @pl.when(i + AHEAD < PIECES)
    def _():
        zx.start(i + AHEAD, piece(i + AHEAD))

    @pl.when(i + AHEAD == PIECES)
    def _():
        wo.start(last, slice(None))

    @pl.when(i == 0)
    def _():
        zx.finish(0, first_piece)
        de.finish(small_piece, slice(None))
        shift, rate = lane_row(db), jnp.exp(lane_row(dl))

        def delta(s):
            a = conv_tile(s, slice(DT0, DT0 + TILE), slice(DIN, DIN + TILE))
            bb, cc = a[:, :NSTATE].astype(bf16), a[:, NSTATE:].astype(bf16)
            bt[s] = jnp.transpose(a[:, :NSTATE]).astype(bf16)
            for q in range(2):
                scores[s, q] = mm_nt(cc[both(q)], bb[both(q)])
            v = mm(ext[s, RIM:], wd[...]) + shift
            vout[s] = v
            dt = softplus(v)
            cum = running_sum(-rate * dt, True)
            cumout[s] = cum
            for q in range(2):
                cum_t[s, q] = jnp.transpose(cum[both(q)])
            e_in, e_out, tot0, tot1, total = local_decays(cum)
            decs[s, pl.ds(pl.multiple_of(me * 8, 8), 8), :] = rows_of(total)
            out_cat[s] = jnp.concatenate(halves(dt * e_out), axis=1)
            dt_cat[s] = jnp.concatenate(halves(dt), axis=1)
            tot1x[s] = spread(rows_of(tot1), sel)

        loop(0, seqs, delta)
        other_blocks(lambda b: dec_copy(b, me).start())

    @pl.when(jnp.logical_and(i >= 1, i < PIECES))
    def _():
        zx.finish(i, piece(i))

    def act_at(t, lag, act):
        u = t - 1 - lag
        pl.when(jnp.logical_and(u >= 0, u < TILES))(lambda: act(u))

    def close(u):
        unit_decays(u)
        ex.close(u)

    def scan(u):
        unit_decays(u)
        ex.scan(u)

    def middle(u):
        unit_decays(u)
        ex.middle(u)

    @pl.when(i == 3)
    def _():
        other_blocks(lambda b: dec_copy(b, b).wait_recv())

    def wave(t):
        act_at(t, CLOSE_LAG, close)
        act_at(t, SCAN_LAG, scan)
        act_at(t, MIDDLE_LAG, middle)

    wave(i)

    @pl.when(jnp.logical_and(i >= 1, i <= TILES))
    def _():
        u = i - 1
        cols = unit_cols(u)

        def x_tile(s):
            a = conv_tile(s, piece(i), cols)
            xs_s[s, :, cols] = a.astype(bf16)
            xw = (a * mm(out_cat[s], sel[:, cols])).astype(bf16)
            s0 = mm(bt[s, :, :HALF], xw[:HALF])
            s1 = mm(bt[s, :, HALF:], xw[HALF:])
            st0[s] = s0.astype(bf16)
            low = (tot1x[s, :, cols][0:1] * s0 + s1).astype(bf16)
            loc[s] = low
            ex.buf[u, s] = low

        loop(0, seqs, x_tile)
        ex.start(u)

    @pl.when(i > TILES)
    def _():
        u = i - 1 - TILES
        causal, low_lanes = masks()

        def intra(s):
            cum = cumout[s]
            dtx = mm(dt_cat[s], sel[:, unit_cols(u)])
            for h in range(2):
                p = 2 * u + h
                lanes = slice(h * HALF, (h + 1) * HALF)
                decays = pair_decays(cum, cum_t.at[s], p, causal)
                for q in range(2):
                    rows = both(q)
                    m = jnp.concatenate([(decays[2 * q + a] * scores[s, q]).astype(bf16) for a in range(2)], axis=1)
                    x = xs_s[s, rows, pl.ds(pl.multiple_of(p * HALF, HALF), HALF)].astype(f32) * dtx[rows, lanes]
                    x = jnp.concatenate([jnp.where(low_lanes, x, 0.0), jnp.where(low_lanes, 0.0, x)], axis=0)
                    ylocal[s, rows, lanes] = mm(m, x.astype(bf16)).astype(bf16)
            gate[s] = mm(ext[s, RIM:], w[:, piece(i)]).astype(bf16)

        def two_intra(h):
            for b in range(2):
                intra(2 * h + b)

        loop(0, seqs // 2, two_intra)

    @pl.when(i == PIECES - 1)
    def _():
        keep_w.start()
        keep_d.start()
        decs_out[...] = decs[...]
        wo.forward(last, slice(None))
        loop(PIECES, TILES + CLOSE_LAG + 1, wave)
        loop(0, TILES, ex.finish)
        wo.finish(last, slice(None))
        wo.finish_chip(1)
        zx.drain_chip(0)
        wo.drain_chip(1)
        de.drain_chip(2)
        de.drain(small_piece, slice(None))
        zx.drain(0, first_piece)
        loop(1, PIECES, lambda p: zx.drain(p, piece(p)))
        wo.drain(last, slice(None))
        other_blocks(lambda b: dec_copy(b, me).wait_send())
        pl.when(me < count - 1)(lambda: halo_copy.wait_send())
        keep_w.wait()
        keep_d.wait()


def middle_kernel(
    lengths, skip_in, tok, cot, ylocal, gate, xb, vin, cumin, st0, sin, decs, wout, ggain_in, nt,
    mixed, dyout, ggate, wred, dir1, gskip, gggain, dxs, dbc, xgate, xout, later,
    sel, skip, ggain, cum_t, einx, ys, gs, ss, s_in, dcs, dy_s, ml_s, gg_s, dr_s, pgate, pout, g_s, dg_s, *exchange,
):
    i = pl.program_id(0)
    seqs = dy_s.shape[0]
    ex = Exchange(True, lambda u, rows: later.at[pl.ds(u, 1), rows, :], exchange[:9], exchange[9])
    members = lax.axis_size("group")
    gates = Reducer(pgate, xgate, D // members, GATE_CHUNK, False, exchange[10:13], None)
    outs = Reducer(pout, xout, DIN // members, OUT_CHUNK, True, exchange[13:16], None)

    def span(s):
        return pl.ds(pl.multiple_of(s * SPAN, SPAN), SPAN)

    def group_wave(t):
        gates.wave(t - 2 * seqs - 3, [gates.x_done], gates.each)
        outs.wave(t - 2 * seqs - 3 - gates.chunks, [outs.x_done], outs.each)

    def wave(t):
        group_wave(t)

        def act_at(lag, act):
            u = lax.div(t - lag, 2)

            def run():
                ex.decx[0] = spread(decs[u], sel)
                act(u)

            pl.when(jnp.logical_and(t >= lag, jnp.logical_and(2 * u + lag == t, u < seqs)))(run)

        act_at(BACK_LAGS[2], ex.close)
        act_at(BACK_LAGS[1], ex.scan)
        act_at(BACK_LAGS[0], ex.middle)

    @pl.when(i == 0)
    def _():
        greet(("ctx", "group"))
        sel[...] = head_map()
        skip[...] = spread(rows_of(lane_row(skip_in)), sel)[0:1]
        ggain[...] = row_of(ggain_in)
        gskip[...] = jnp.zeros_like(gskip)
        gggain[...] = jnp.zeros_like(gggain)

    @pl.when(i == 1)
    def _():
        settle(("ctx", "group"))

    @pl.when(jnp.logical_and(i >= 1, i <= seqs))
    def _():
        ex.start(i - 1)

    wave(2 * i)

    @pl.when(i < seqs)
    def _():
        s = i
        cum = cumin[0]
        e_in, e_out, tot0, tot1, total = local_decays(cum)
        einx[...] = spread(e_in, sel)
        tot0x = spread(rows_of(tot0), sel)[0:1]
        s_in[0] = sin[0]
        s_in[1] = (tot0x * sin[0].astype(f32) + st0[0].astype(f32)).astype(bf16)
        cc = xb[0, :, DIN + NSTATE :]

        def gate_step(j, total_sq):
            cols = pl.ds(pl.multiple_of(j * TILE, TILE), TILE)
            for q in range(2):
                rows = both(q)
                ys[rows, cols] = ylocal[0, rows, cols].astype(f32) + einx[rows, cols] * mm(cc[rows], s_in[q, :, cols])
            y = ys[:, cols] + skip[:, cols] * xb[0, :, cols].astype(f32)
            g = gate[0, :, cols].astype(f32)
            gated = y * (g * gate_of(g))
            gs[:, cols] = gated
            sq = gated * gated
            return total_sq + sq[:, :HALF] + sq[:, HALF:]

        wave(2 * i + 1)
        sq = lax.fori_loop(0, DIN // TILE, gate_step, jnp.zeros((SPAN, HALF), f32))
        inv = lax.rsqrt(jnp.sum(sq, axis=1, keepdims=True) * (1.0 / DIN) + EPS)
        live = live_rows(lengths, s)
        drive = (live * cot[0].astype(f32)).astype(bf16)
        dr_s[span(s), :] = drive

        def back_step(j, acc):
            cols = pl.ds(pl.multiple_of(j * TILE, TILE), TILE)
            gm = mm_nt(drive, wout[cols, :])
            gated = gs[:, cols]
            unit = gated * inv
            ml_s[span(s), cols] = (unit * ggain[:, cols]).astype(bf16)
            gggain[:, cols] += jnp.sum(gm * unit, axis=0, keepdims=True)
            scaled = gm * ggain[:, cols]
            ss[:, cols] = scaled
            prod = scaled * gated
            return acc + prod[:, :HALF] + prod[:, HALF:]

        dots = lax.fori_loop(0, DIN // TILE, back_step, jnp.zeros((SPAN, HALF), f32))
        dots = jnp.sum(dots, axis=1, keepdims=True) * (1.0 / DIN)
        corr = inv * inv * inv * dots
        cct = jnp.transpose(cc.astype(f32)).astype(bf16)
        acc = jnp.zeros((SPAN, HALF), f32)
        dc = [jnp.zeros((HALF, HALF), f32) for _ in range(2)]
        for j in range(DIN // TILE):
            cols = slice(j * TILE, (j + 1) * TILE)
            g = gate[0, :, cols].astype(f32)
            sg = gate_of(g)
            sl = g * sg
            grad_gated = inv * ss[:, cols] - gs[:, cols] * corr
            dy = grad_gated * sl
            yn = ys[:, cols]
            x = xb[0, :, cols].astype(f32)
            y = yn + skip[:, cols] * x
            low = (grad_gated * y * (sg + sl * (1.0 - sg))).astype(bf16)
            ggate[0, :, cols] = low
            gg_s[span(s), cols] = low
            dyb = dy.astype(bf16)
            dyout[0, :, cols] = dyb
            dy_s[s, :, cols] = dyb
            gskip[:, cols] += jnp.sum(dy * x, axis=0, keepdims=True)
            acc = acc + gather_heads(dy * yn, sel[:HALF, cols])
            dye = (dy * einx[:, cols]).astype(bf16)
            d0 = mm(cct[:, :HALF], dye[:HALF])
            d1 = mm(cct[:, HALF:], dye[HALF:])
            dir1[0, :, cols] = d1.astype(bf16)
            ex.buf[s, 0, :, cols] = (d0 + tot0x[:, cols] * d1).astype(bf16)
            for q in range(2):
                dc[q] = dc[q] + mm_nt(dye[both(q)], s_in[q, :, cols])
        wred[0] = acc
        for q in range(2):
            dcs[s, both(q)] = dc[q]

    @pl.when(i >= seqs)
    def _():
        s = i - seqs
        causal, low_lanes = masks()
        cum = cumin[0]
        for q in range(2):
            cum_t[q] = jnp.transpose(cum[both(q)])
        einx[...] = spread(softplus(vin[0]), sel)
        bb = xb[0, :, DIN : DIN + NSTATE]
        cc = xb[0, :, DIN + NSTATE :]
        for q in range(2):
            g_s[q] = mm_nt(cc[both(q)], bb[both(q)])
        dg_s[...] = jnp.zeros_like(dg_s)

        def pair_step(p):
            cols = pl.ds(pl.multiple_of(p * HALF, HALF), HALF)
            decays = pair_decays(cum, cum_t, p, causal)
            for q in range(2):
                rows = both(q)
                xsb = (xb[0, rows, cols].astype(f32) * einx[rows, cols]).astype(bf16)
                dyb = dy_s[s, rows, cols]
                dyf = dyb.astype(f32)
                grads = []
                for a in range(2):
                    m = (decays[2 * q + a] * g_s[q]).astype(bf16)
                    grads.append(mm_tn(m, dyb))
                    mine = low_lanes if a == 0 else jnp.logical_not(low_lanes)
                    dm = mm_nt(jnp.where(mine, dyf, 0.0).astype(bf16), xsb)
                    dg_s[q] += dm * decays[2 * q + a]
                dxs[0, rows, cols] = jnp.where(low_lanes, grads[0], grads[1]).astype(bf16)

        @pl.when(s == 0)
        def _():
            for k in range(gates.chunks):
                cols = slice(k * GATE_CHUNK, (k + 1) * GATE_CHUNK)
                pgate[:, cols] = mm(nt[...], gg_s[:, cols]).astype(bf16)
                gates.m_start(k)

        @pl.when(s == 1)
        def _():
            loop(0, outs.chunks, outs.m_done)

        def two_pairs(pp):
            for h in range(2):
                pair_step(2 * pp + h)

        loop(0, PAIRS // 4, two_pairs)
        wave(2 * i + 1)

        @pl.when(s == 0)
        def _():
            loop(0, gates.chunks, gates.m_done)

            def out_rows(r):
                rows = pl.ds(pl.multiple_of(r * TILE, TILE), TILE)
                pout[rows, :] = mm_tn(ml_s[:, rows], dr_s[...]).astype(bf16)

            loop(0, DIN // TILE, out_rows)
            loop(0, outs.chunks, outs.m_start)

        loop(PAIRS // 4, PAIRS // 2, two_pairs)
        for q in range(2):
            rows = both(q)
            dg = dg_s[q].astype(bf16)
            dbc[0, rows, :NSTATE] = mm_tn(dg, cc[rows])
            dbc[0, rows, NSTATE:] = mm(dg, bb[rows]) + dcs[s, rows]
        live = live_rows(lengths, s)
        for j in range(D // TILE):
            cols = slice(j * TILE, (j + 1) * TILE)
            mixed[0, :, cols] = (live * (tok[0, :, cols].astype(f32) + mm(ml_s[span(s), :], wout[:, cols]))).astype(bf16)

    @pl.when(i == 2 * seqs - 1)
    def _():
        loop(4 * seqs, max(2 * seqs + BACK_LAGS[2] - 1, 2 * seqs + 3 + gates.chunks + outs.chunks), wave)
        loop(0, seqs, ex.finish)
        for r in (gates, outs):
            loop(0, r.chunks, r.drain_group)


def back_kernel(
    lengths, dl, skip_in, tok, cot, rhalo, gain, ggate, w_any, wd, cin, xb, spb, bc, dy, dxs, dir1, later, sin, loc,
    vin, cumin, wred, dbc, cw, nt, nth, xgate, xout, gskip, gggain,
    gtok, rzx, rout, small_out, ggain_out,
    sel, skip, wfull, w_sem, dt_cat, eo_cat, tots, db_s, qacc, ends, gp, gz_s, gzh_s, pconv, gcw, gcb, gdb, gdl, ggain,
    rim_out, rim_in, rim_send, rim_recv, *comm,
):
    i = pl.program_id(0)
    seqs = rhalo.shape[0]
    count = lax.axis_size("ctx")
    me = lax.axis_index("ctx")
    members = lax.axis_size("group")
    gates = Reducer(None, rzx, D // members, GATE_CHUNK, False, None, (xgate,) + comm[0:5])
    outs = Reducer(None, rout, DIN // members, OUT_CHUNK, True, None, (xout,) + comm[5:10])
    convs = Reducer(pconv, rzx, D // members, CONV_CHUNK, False, comm[10:13], comm[13:19])
    convs.base = DIN
    load_w = pltpu.make_async_copy(w_any, wfull, w_sem.at[0])
    little, least = Small(*comm[19:23]), Small(*comm[23:27])
    bc_step = TILES

    last_conv = 2 * bc_step + 5

    def conv_at(t):
        k = lax.div(t - 7, 4)
        even = jnp.logical_and(t >= 7, jnp.logical_and(lax.rem(t - 7, 4) == 0, k < convs.chunks - 1))
        last = t == last_conv
        return jnp.where(last, convs.chunks - 1, k), jnp.logical_or(even, last)

    def wave(t):
        for r, at in ((gates, 2), (outs, 2 + gates.chunks)):
            r.wave(t - at, [r.y_done, r.z_done, r.b_done, r.f_done], r.each)
        convs.wave(t, [convs.x_done, convs.y_done, convs.z_done, convs.b_done, convs.f_done], conv_at, CONV_LAG)

    def rim_copy(q):
        return remote(rim_out.at[q], rim_in.at[q], rim_send.at[q], rim_recv.at[q], ctx=lax.rem(me + count - 1, count))

    def span(s):
        return pl.ds(pl.multiple_of(s * SPAN, SPAN), SPAN)

    def edge(s):
        return pl.ds(pl.multiple_of(s * RIM, RIM), RIM)

    def back(rows, grad):
        rows, inv, _ = normalized(rows, row_of(gain))
        ggain[...] += jnp.sum(grad * rows * inv, axis=0, keepdims=True)
        gained = row_of(gain) * grad
        mean = jnp.mean(gained * rows, axis=-1, keepdims=True)
        return inv * gained - rows * (inv * inv * inv * mean)

    @pl.when(i == 0)
    def _():
        meet(("ctx", "group"))
        for r in (gates, outs):
            loop(0, r.chunks, r.y_start)
        load_w.start()
        sel[...] = head_map()
        skip[...] = spread(rows_of(lane_row(skip_in)), sel)[0:1]
        for acc in (db_s, qacc, ends, gcw, gcb, gdb, gdl, ggain):
            acc[...] = jnp.zeros_like(acc)
        for slot in range(2):
            gp[slot, 0:RIM] = jnp.zeros((RIM, TILE), f32)
            gp[slot, RIM + SPAN :] = jnp.zeros((8, TILE), f32)
        pconv[:, CONVW + HALF :] = jnp.zeros((D, GZW - CONVW - HALF), bf16)

        def setup(s):
            dt = softplus(vin[s])
            _, e_out, _, tot1, total = local_decays(cumin[s])
            dt_cat[s] = jnp.concatenate(halves(dt), axis=1)
            eo_cat[s] = jnp.concatenate(halves(e_out), axis=1)
            both_rows = jnp.concatenate([rows_of(tot1), rows_of(total)], axis=0)
            tots[s] = spread(both_rows, sel)

        loop(0, seqs, setup)

    def conv_back(s, dact, cols, slot=0):
        gco = dact * spb[s].astype(f32)
        gp[slot, RIM : RIM + SPAN] = gco
        gcb[:, cols] += jnp.sum(gco, axis=0, keepdims=True)
        own = cin[s, RIM:].astype(f32)
        before = cin[s, :RIM].astype(f32)
        main = jnp.zeros((SPAN, TILE), f32)
        rim = jnp.zeros((RIM, TILE), f32)
        for k in range(KCONV):
            ahead = KCONV - 1 - k
            moved = gco if ahead == 0 else gp[slot, RIM + ahead : RIM + ahead + SPAN]
            early = gp[slot, ahead : ahead + RIM]
            main = main + cw[k : k + 1, cols] * moved
            rim = rim + cw[k : k + 1, cols] * early
            gcw[k : k + 1, cols] += jnp.sum(own * moved, axis=0, keepdims=True) + jnp.sum(
                before * early, axis=0, keepdims=True
            )
        gz_s[span(s), cols] = main.astype(bf16)
        gzh_s[edge(s), cols] = rim.astype(bf16)

    def partial(cols):
        pconv[:, cols] = (mm(nt[...], gz_s[:, cols]) + mm(nth[...], gzh_s[:, cols])).astype(bf16)

    wave(2 * i)

    @pl.when(i < bc_step)
    def _():
        cols = pl.ds(pl.multiple_of(i * TILE, TILE), TILE)

        def x_tile(s, slot):
            dte = mm(dt_cat[s], sel[:, cols])
            eo = mm(eo_cat[s], sel[:, cols])
            near = later[s]
            near32 = near.astype(f32)
            tot = tots[s, :, cols]
            reach = [(dir1[s].astype(f32) + tot[0:1] * near32).astype(bf16), near]
            fed = jnp.concatenate(
                [mm(bc[s, both(q), :NSTATE], reach[q]) for q in range(2)], axis=0
            )
            x = xb[s].astype(f32)
            dx_s = dxs[s].astype(f32) + eo * fed
            qacc[s] += gather_heads(x * dx_s, sel[:HALF, cols])
            xw = (x * dte * eo).astype(bf16)
            for q in range(2):
                db_s[s, both(q)] += mm_nt(xw[both(q)], reach[q])
            held = near32 * (tot[8:9] * sin[s].astype(f32) + loc[s].astype(f32))
            ends[s] += gather_heads(rows_of(jnp.sum(held, axis=0, keepdims=True)), sel[:HALF, cols])
            conv_back(s, dte * dx_s + skip[:, cols] * dy[s].astype(f32), cols, slot)

        def two_seqs(h):
            for slot in range(2):
                x_tile(2 * h + slot, slot)

        loop(0, seqs // 4, two_seqs)

        @pl.when(jnp.logical_and(lax.rem(i, 2) == 0, i >= 2))
        def _():
            convs.m_done(lax.div(i, 2) - 1)

        wave(2 * i + 1)
        loop(seqs // 4, seqs // 2, two_seqs)
        partial(cols)

        @pl.when(lax.rem(i, 2) == 1)
        def _():
            convs.m_start(lax.div(i, 2))

    @pl.when(i == bc_step)
    def _():
        cols = slice(DIN, CONVW)
        rate = jnp.exp(lane_row(dl))

        def bc_tile(s):
            conv_back(s, jnp.concatenate([dbc[s, :, :NSTATE] + db_s[s], dbc[s, :, NSTATE:]], axis=1), cols)
            v = vin[s]
            dt = softplus(v)
            q = qacc[s]
            at_end = lax.broadcasted_iota(jnp.int32, (SPAN, 1), 0) == SPAN - 1
            dcum = wred[s] - dt * q + jnp.where(at_end, ends[s][0:1], 0.0)
            glog = running_sum(dcum, False)
            gpd = (q - rate * glog) * sigmoid(v)
            lanes = lax.broadcasted_iota(jnp.int32, (SPAN, HALF), 1) < HEADS
            gpd = jnp.where(lanes, gpd, 0.0)
            gz_s[span(s), CONVW : CONVW + HALF] = gpd.astype(bf16)
            gdb[...] += jnp.sum(gpd, axis=0, keepdims=True)
            gdl[...] += -rate * jnp.sum(dt * glog, axis=0, keepdims=True)

        loop(0, seqs, bc_tile)
        convs.m_done(convs.chunks - 2)
        wave(2 * i + 1)
        partial(cols)
        pconv[:, CONVW : CONVW + HALF] = mm(nt[...], gz_s[:, CONVW : CONVW + HALF]).astype(bf16)
        convs.m_start(convs.chunks - 1)
        rows = [gcw[k : k + 1, j * HALF : (j + 1) * HALF] for k in range(KCONV) for j in range(CONVW // HALF)]
        rows += [gcb[:, j * HALF : (j + 1) * HALF] for j in range(CONVW // HALF)]
        rows += [gdb[...], gdl[...]]
        rows += [gather_heads(rows_of(gskip[...]), sel[:HALF])[0:1]]
        rows += [gggain[:, j * HALF : (j + 1) * HALF] for j in range(PAIRS)]
        little.held[0, SMALL_ROWS - 8 :] = jnp.zeros((8, HALF), f32)
        for r, row in enumerate(rows):
            little.held[0, r : r + 1, :] = row
        little.start(0)
        load_w.wait()
        edges = mm_nt(gzh_s[...], wfull[:, DIN:ZXW])
        for q in range(seqs):
            rim_out[q] = back(rhalo[q], edges[q * RIM : (q + 1) * RIM]).astype(bf16)
            pl.when(me > 0)(lambda q=q: rim_copy(q).start())

        @pl.when(me == count - 1)
        def _():
            rim_in[...] = jnp.zeros_like(rim_in)

    @pl.when(i == bc_step + 2)
    def _():
        little.done(0)
        little.start(1)

    @pl.when(i > bc_step)
    def _():
        s = i - bc_step - 1
        grad = mm_nt(gz_s[span(s), :CONVW], wfull[:, DIN:]) + mm_nt(ggate[0], wfull[:, :DIN])
        grad = grad + mm_nt(gz_s[span(s), CONVW:], wd[...])

        @pl.when(s == 0)
        def _():
            convs.m_done(convs.chunks - 1)

        wave(2 * i + 1)
        live = live_rows(lengths, s)
        out = live * cot[0].astype(f32) + back(tok[0], grad)
        gtok[0, : SPAN - RIM] = out[: SPAN - RIM].astype(bf16)
        pl.when(me < count - 1)(lambda: rim_copy(s).wait_recv())
        gtok[0, SPAN - RIM :] = (out[SPAN - RIM :] + rim_in[s].astype(f32)).astype(bf16)

    @pl.when(i == bc_step + seqs)
    def _():
        least.held[0] = jnp.zeros_like(least.held[0])
        for j in range(D // HALF):
            least.held[0, j : j + 1, :] = ggain[:, j * HALF : (j + 1) * HALF]
        least.start(0)
        little.done(1)
        small_out[...] = little.held[2]
        ends_at = max(last_conv + 4 * CONV_LAG, 1 + gates.chunks + outs.chunks + 3 * STAGE_LAG) + 1
        here = 2 * (bc_step + seqs) + 2
        loop(here, min(here + 2, ends_at), wave)
        least.done(0)
        least.start(1)
        loop(here + 2, ends_at, wave)
        for r in (gates, outs, convs):
            loop(0, r.chunks, r.drain_ctx)
        loop(0, convs.chunks, convs.drain_group)
        little.drain()
        for q in range(seqs):
            pl.when(me > 0)(lambda q=q: rim_copy(q).wait_send())
        least.done(1)
        ggain_out[...] = least.held[2]
        least.drain()


def done_kernel(
    rzx, rdelta, rout, small, gain_sum,
    g_gain, g_zx, g_delta, g_out, g_cw, g_cb, g_db, g_dl, g_skip, g_gated,
):
    @pl.when(pl.program_id(0) == 0)
    def _():
        tiles = CONVW // HALF
        for k in range(KCONV):
            for j in range(tiles):
                g_cw[k : k + 1, j * HALF : (j + 1) * HALF] = small[k * tiles + j : k * tiles + j + 1, :]
        at = KCONV * tiles
        for j in range(tiles):
            g_cb[j * HALF : (j + 1) * HALF] = small[at + j, :]
        at += tiles
        for ref in (g_db, g_dl, g_skip):
            ref[...] = small[at, :][:HEADS]
            at += 1
        for j in range(PAIRS):
            g_gated[j * HALF : (j + 1) * HALF] = small[at + j, :]
        for j in range(D // HALF):
            g_gain[j * HALF : (j + 1) * HALF] = gain_sum[j, :]
        g_delta[...] = jnp.transpose(rdelta[...].astype(f32))[:HEADS]

    g_zx[...] = rzx[:, :ZXW].astype(f32)
    g_out[...] = rout[...].astype(f32)


def whole(shape):
    zeros = (0,) * len(shape)
    return pl.BlockSpec(shape, lambda s: zeros, pipeline_mode=pl.Buffered(1))


def summed(shape):
    zeros = (0,) * len(shape)
    return pl.BlockSpec(shape, lambda s: zeros)


def per_seq(*shape):
    zeros = (0,) * len(shape)
    return pl.BlockSpec((1,) + shape, lambda s: (s,) + zeros)


SMEM = pl.BlockSpec(memory_space=pltpu.SMEM)
ANY = pl.BlockSpec(memory_space=pl.ANY)


def staged(seqs, phase, *shape):
    zeros = (0,) * len(shape)
    if phase == 0:
        return pl.BlockSpec((1,) + shape, lambda i: (jnp.minimum(i, seqs - 1),) + zeros)
    if phase == 1:
        return pl.BlockSpec((1,) + shape, lambda i: (jnp.maximum(i - seqs, 0),) + zeros)
    return pl.BlockSpec((1,) + shape, lambda i: (lax.rem(i, seqs),) + zeros)


def call(kernel, steps, in_specs, outs, scratch, name, collective=None):
    params = dict(vmem_limit_bytes=VMEM_LIMIT)
    if collective is not None:
        params.update(collective_id=collective, has_side_effects=True)
    return pl.pallas_call(
        kernel,
        grid=(steps,),
        in_specs=in_specs,
        out_specs=[o[0] for o in outs],
        out_shape=[jax.ShapeDtypeStruct(o[1], o[2]) for o in outs],
        scratch_shapes=[pltpu.VMEM(*sc) if isinstance(sc, tuple) else sc for sc in scratch],
        compiler_params=pltpu.CompilerParams(**params),
        name=name,
    )


def local(
    tokens_in, seq_lengths, norm_gain, w_zx, w_delta, w_out, conv_weight, conv_bias,
    delta_bias, decay_log, skip_gain, gated_gain, cotangent,
):
    seqs = tokens_in.shape[0]
    count = lax.axis_size("ctx")
    group = lax.axis_size("group")
    chips = max(group // 2, 1)
    w_delta = jnp.pad(w_delta, ((0, 0), (0, HALF - HEADS)))
    dma = pltpu.SemaphoreType.DMA
    at0 = lambda *shape: staged(seqs, 0, *shape)
    at1 = lambda *shape: staged(seqs, 1, *shape)
    at01 = lambda *shape: staged(seqs, 2, *shape)

    def tiled(rows, first, lead=None):
        def index(i):
            u = jnp.clip(i - first, 0, TILES - 1)
            return (0, 0, u if lead is None else jnp.where(i == 0, lead, u))

        return pl.BlockSpec((seqs, rows, TILE), index)

    state = (seqs, NSTATE, DIN)
    nt, nth, rhalo, cin, xb, spb, vraw, cum, st0, loc, ylocal, gate, decs, wfull, wdfull, wofull, state_in = call(
        front_kernel,
        PIECES,
        [whole((seqs, SPAN, D)), ANY, ANY, ANY, ANY, whole((D,)), whole((KCONV, CONVW)), whole((CONVW,)), SMEM, SMEM],
        [
            (summed((D, seqs * SPAN)), (D, seqs * SPAN), bf16),
            (summed((D, seqs * RIM)), (D, seqs * RIM), bf16),
            (summed((seqs, RIM, D)), (seqs, RIM, D), bf16),
            (tiled(RIM + SPAN, 1, TILES), (seqs, RIM + SPAN, CONVW), bf16),
            (tiled(SPAN, 1, TILES), (seqs, SPAN, CONVW), bf16),
            (tiled(SPAN, 1, TILES), (seqs, SPAN, CONVW), bf16),
            (summed((seqs, SPAN, HALF)), (seqs, SPAN, HALF), f32),
            (summed((seqs, SPAN, HALF)), (seqs, SPAN, HALF), f32),
            (tiled(NSTATE, 1), state, bf16),
            (tiled(NSTATE, 1), state, bf16),
            (tiled(SPAN, TILES + 1), (seqs, SPAN, DIN), bf16),
            (tiled(SPAN, TILES + 1), (seqs, SPAN, DIN), bf16),
            (summed((seqs, count * 8, HALF)), (seqs, count * 8, HALF), f32),
            (ANY, (D, ZXW), bf16),
            (ANY, (D, HALF), bf16),
            (ANY, (DIN, D), bf16),
            (ANY, state, bf16),
        ],
        [((2 * HALF, DIN), bf16), ((seqs, RIM, D), bf16), ((seqs * RIM, D), f32), ((seqs, RIM + SPAN, D), bf16), ((D, ZXW), bf16),
         ((D, HALF), bf16), ((1, CONVW), f32),
         ((seqs, RIM + SPAN, TILE), f32), ((seqs, SPAN, DIN), bf16), ((seqs, NSTATE, SPAN), bf16),
         ((seqs, 2, HALF, HALF), f32), ((seqs, SPAN, 2 * HALF), bf16), ((seqs, SPAN, 2 * HALF), bf16),
         ((seqs, 2, HALF, HALF), f32), ((seqs, 8, DIN), f32), ((seqs, count * 8, HALF), f32)]
        + [dma((2,))] + [dma((PIECES + 2, chips))] * 4 + [dma((3,)), dma((2,)), dma((count,)), dma((count,))]
        + Exchange.scratch(TILES, seqs, TILE, count),
        "front",
        0,
    )(tokens_in, tokens_in, w_zx, w_delta, w_out, norm_gain, conv_weight, conv_bias, delta_bias, decay_log)

    x_gate_shape = (DIN // GATE_CHUNK, D // group, GATE_CHUNK)
    x_out_shape = (D // OUT_CHUNK, DIN // group, OUT_CHUNK)
    mixed_out, dy, ggate, wred, dir1, gskip, gggain, dxs, dbc, x_gate, x_out, later = call(
        middle_kernel,
        2 * seqs,
        [SMEM, SMEM, at1(SPAN, D), at0(SPAN, D), at0(SPAN, DIN), at0(SPAN, DIN), at01(SPAN, CONVW), at01(SPAN, HALF),
         at01(SPAN, HALF), at0(NSTATE, DIN), at0(NSTATE, DIN), whole((seqs, count * 8, HALF)), whole((DIN, D)),
         whole((DIN,)), whole((D, seqs * SPAN))],
        [
            (at1(SPAN, D), (seqs, SPAN, D), bf16),
            (at0(SPAN, DIN), (seqs, SPAN, DIN), bf16),
            (at0(SPAN, DIN), (seqs, SPAN, DIN), bf16),
            (at0(SPAN, HALF), (seqs, SPAN, HALF), f32),
            (at0(NSTATE, DIN), (seqs, NSTATE, DIN), bf16),
            (summed((1, DIN)), (1, DIN), f32),
            (summed((1, DIN)), (1, DIN), f32),
            (at1(SPAN, DIN), (seqs, SPAN, DIN), bf16),
            (at1(SPAN, 2 * NSTATE), (seqs, SPAN, 2 * NSTATE), f32),
            (summed(x_gate_shape), x_gate_shape, bf16),
            (summed(x_out_shape), x_out_shape, bf16),
            (ANY, (seqs, NSTATE, DIN), bf16),
        ],
        [((2 * HALF, DIN), bf16), ((1, DIN), f32), ((1, DIN), f32), ((2, HALF, HALF), f32), ((SPAN, DIN), f32), ((SPAN, DIN), f32), ((SPAN, DIN), f32),
         ((SPAN, DIN), f32), ((2, NSTATE, DIN), bf16), ((seqs, SPAN, HALF), f32), ((seqs, SPAN, DIN), bf16),
         ((seqs * SPAN, DIN), bf16), ((seqs * SPAN, DIN), bf16), ((seqs * SPAN, D), bf16), ((D, DIN), bf16), ((DIN, D), bf16),
         ((2, HALF, HALF), f32), ((2, HALF, HALF), f32)]
        + Exchange.scratch(seqs, 1, DIN, count)
        + Reducer.group_scratch(*x_gate_shape, group)
        + Reducer.group_scratch(*x_out_shape, group),
        "middle",
        1,
    )(seq_lengths, skip_gain, tokens_in, cotangent, ylocal, gate, xb, vraw, cum, st0, state_in, decs, wofull, gated_gain, nt)

    def tile_in(rows, tiles):
        return pl.BlockSpec((seqs, rows, TILE), lambda i: (0, 0, jnp.minimum(i, tiles - 1)))

    def late(*shape):
        zeros = (0,) * len(shape)
        return pl.BlockSpec((1,) + shape, lambda i: (jnp.clip(i - TILES - 1, 0, seqs - 1),) + zeros)

    bc_spec = pl.BlockSpec((seqs, SPAN, TILE), lambda i: (0, 0, TILES), pipeline_mode=pl.Buffered(1))
    height = SMALL_ROWS
    x_conv_shape = (GZW // CONV_CHUNK, D // group, CONV_CHUNK)
    gtok, r_zx, r_out, small, gain_sum = call(
        back_kernel,
        TILES + 1 + seqs,
        [SMEM, SMEM, SMEM, late(SPAN, D), late(SPAN, D), whole((seqs, RIM, D)), whole((D,)), late(SPAN, DIN), ANY, whole((D, HALF)),
         tile_in(RIM + SPAN, TILES + 1), tile_in(SPAN, TILES + 1), tile_in(SPAN, TILES + 1), bc_spec, tile_in(SPAN, TILES),
         tile_in(SPAN, TILES), tile_in(NSTATE, TILES), tile_in(NSTATE, TILES), tile_in(NSTATE, TILES), tile_in(NSTATE, TILES),
         whole((seqs, SPAN, HALF)), whole((seqs, SPAN, HALF)), whole((seqs, SPAN, HALF)), whole((seqs, SPAN, 2 * NSTATE)),
         whole((KCONV, CONVW)), whole((D, seqs * SPAN)), whole((D, seqs * RIM)),
         whole(x_gate_shape), whole(x_out_shape), whole((1, DIN)), whole((1, DIN))],
        [
            (late(SPAN, D), (seqs, SPAN, D), bf16),
            (summed((D // group, DIN + GZW)), (D // group, DIN + GZW), bf16),
            (summed((DIN // group, D)), (DIN // group, D), bf16),
            (summed((height, HALF)), (height, HALF), f32),
            (summed((8, HALF)), (8, HALF), f32),
        ],
        [((2 * HALF, DIN), bf16), ((1, DIN), f32), ((D, ZXW), bf16), dma((1,)), ((seqs, SPAN, 2 * HALF), bf16),
         ((seqs, SPAN, 2 * HALF), bf16), ((seqs, 16, DIN), f32),
         ((seqs, SPAN, NSTATE), f32), ((seqs, SPAN, HALF), f32), ((seqs, 8, HALF), f32), ((2, RIM + SPAN + 8, TILE), f32),
         ((seqs * SPAN, CONVW + HALF), bf16), ((seqs * RIM, CONVW), bf16), ((D, GZW), bf16), ((KCONV, CONVW), f32),
         ((1, CONVW), f32), ((1, HALF), f32), ((1, HALF), f32), ((1, D), f32), ((seqs, RIM, D), bf16), ((seqs, RIM, D), bf16),
         dma((seqs,)), dma((seqs,))]
        + Reducer.ctx_scratch(*x_gate_shape, False, count)
        + Reducer.ctx_scratch(*x_out_shape, True, count)
        + Reducer.group_scratch(*x_conv_shape, group)
        + [(x_conv_shape, bf16)]
        + Reducer.ctx_scratch(*x_conv_shape, False, count)
        + Small.scratch(height, group, count)
        + Small.scratch(8, group, count),
        "back",
        2,
    )(seq_lengths, decay_log, skip_gain, tokens_in, cotangent, rhalo, norm_gain, ggate, wfull, wdfull, cin, xb, spb, xb, dy, dxs, dir1, later, state_in, loc,
      vraw, cum, wred, dbc, conv_weight, nt, nth, x_gate, x_out, gskip, gggain)

    zx_rows, out_rows = D // group, DIN // group
    turns = 2
    halved = lambda rows, cols: pl.BlockSpec((rows // turns, cols), lambda i: (i, 0))
    grad = lambda *shape: (summed(shape), jax.ShapeDtypeStruct(shape, f32))
    specs, shapes = zip(
        grad(D), (halved(zx_rows, ZXW), jax.ShapeDtypeStruct((zx_rows, ZXW), f32)),
        grad(HEADS, zx_rows), (halved(out_rows, D), jax.ShapeDtypeStruct((out_rows, D), f32)), grad(KCONV, CONVW), grad(CONVW),
        grad(HEADS), grad(HEADS), grad(HEADS), grad(DIN),
    )
    results = pl.pallas_call(
        done_kernel,
        grid=(turns,),
        in_specs=[halved(zx_rows, DIN + GZW), pl.BlockSpec((zx_rows, HALF), lambda i: (0, ZXW // HALF)), halved(out_rows, D),
                  whole((SMALL_ROWS, HALF)), whole((8, HALF))],
        out_specs=specs,
        out_shape=shapes,
        name="done",
    )(r_zx, r_zx, r_out, small, gain_sum)
    return (mixed_out, gtok, *results[:2], results[2].T, *results[3:])


def solution(mesh):
    rows = P("group", "ctx", None)
    own = P("group", None)
    in_specs = (rows, P("group"), P(), own, own, own, P(), P(), P(), P(), P(), P(), rows)
    out_specs = (rows, rows, P(), own, own, own, P(), P(), P(), P(), P(), P())
    return jax.shard_map(local, mesh=mesh, in_specs=in_specs, out_specs=out_specs, check_vma=False)
```

```python
import jax
import jax.numpy as jnp
from jax import lax
from jax.experimental import pallas as pl
from jax.experimental.pallas import tpu as pltpu
from jax.sharding import PartitionSpec as P

D = 768
HEADS = 24
HEADDIM = 64
NSTATE = 128
KCONV = 4
SPAN = 256
DIN = 1536
CONVW = 1792
ZXW = 3328
RIM = 16
HALF = 128
TILE = 256
PAIRS = 12
EPS = 1e-05

f32 = jnp.float32
bf16 = jnp.bfloat16
NT = (((1,), (1,)), ((), ()))
TN = (((0,), (0,)), ((), ()))
VMEM_LIMIT = 63 * 1024 * 1024
GATE_CHUNK = 512
OUT_CHUNK = 256
CONV_CHUNK = 512
BACK_LAGS = (4, 7, 9)
STAGE_LAG = 4
CONV_LAG = 3
MIDDLE_LAG = 2
SCAN_LAG = 4
HOPS = ("group", "ctx")
SMALL_ROWS = 88
CLOSE_LAG = 6
GZW = 2048


def mm(a, b):
    return jnp.dot(a, b, preferred_element_type=f32)


def mm_nt(a, b):
    return lax.dot_general(a, b, NT, preferred_element_type=f32)


def mm_tn(a, b):
    return lax.dot_general(a, b, TN, preferred_element_type=f32)


def halves(v):
    high = v.astype(bf16)
    return high, (v - high.astype(f32)).astype(bf16)


def head_map():
    rows = lax.broadcasted_iota(jnp.int32, (2 * HALF, DIN), 0) % HALF
    cols = lax.broadcasted_iota(jnp.int32, (2 * HALF, DIN), 1) // HEADDIM
    return jnp.where(rows == cols, 1.0, 0.0).astype(bf16)


def spread(v, sel):
    return mm(jnp.concatenate(halves(v), axis=1), sel[...])


def gather_heads(v, sel_part):
    high, low = halves(v)
    return mm_nt(high, sel_part) + mm_nt(low, sel_part)


def triangle(size, lower):
    rows = lax.broadcasted_iota(jnp.int32, (size, size), 0)
    cols = lax.broadcasted_iota(jnp.int32, (size, size), 1)
    keep = rows >= cols if lower else rows <= cols
    return jnp.where(keep, 1.0, 0.0).astype(f32)


def running_sum(v, lower):
    rest, terms = v, []
    for _ in range(3):
        high = rest.astype(bf16)
        rest = rest - high.astype(f32)
        terms.append(high)
    tri = triangle(v.shape[0], lower).astype(bf16)
    return mm(tri, terms[0]) + (mm(tri, terms[1]) + mm(tri, terms[2]))


def softplus(v):
    return jnp.maximum(v, 0.0) + jnp.log1p(jnp.exp(-jnp.abs(v)))


def sigmoid(v):
    return 1.0 / (1.0 + jnp.exp(-v))


def gate_of(v):
    return 0.5 * jnp.tanh(0.5 * v) + 0.5


def local_decays(cum):
    mid, end = cum[HALF - 1 : HALF], cum[SPAN - 1 : SPAN]
    rows = lax.broadcasted_iota(jnp.int32, (SPAN, 1), 0)
    first = rows < HALF
    start = jnp.where(first, 0.0, mid)
    stop = jnp.where(first, mid, end)
    return jnp.exp(cum - start), jnp.exp(stop - cum), jnp.exp(mid), jnp.exp(end - mid), jnp.exp(end)


def rows_of(v):
    return jnp.broadcast_to(v, (8, v.shape[1]))


def lane_row(ref):
    lanes = lax.broadcasted_iota(jnp.int32, (1, HALF), 1)
    row = jnp.zeros((1, HALF), f32)
    for h in range(HEADS):
        row = jnp.where(lanes == h, ref[h], row)
    return row


def row_of(ref):
    return ref[...].reshape(1, ref.shape[0])


def live_rows(lengths, s):
    start = lax.axis_index("ctx") * SPAN
    return (lax.broadcasted_iota(jnp.int32, (SPAN, 1), 0) + start < lengths[s]).astype(f32)


def normalized(rows, gain):
    rows = rows.astype(f32)
    inv = lax.rsqrt(jnp.mean(rows * rows, axis=-1, keepdims=True) + EPS)
    return rows, inv, (rows * inv * gain).astype(bf16)


def remote(src, dst, send_sem, recv_sem, **where):
    return pltpu.make_async_remote_copy(
        src_ref=src, dst_ref=dst, send_sem=send_sem, recv_sem=recv_sem,
        device_id=where, device_id_type=pl.DeviceIdType.MESH,
    )


def loop(start, stop, body):
    def step(i, c):
        body(i)
        return c

    lax.fori_loop(start, stop, step, 0)


def greet(axes):
    barrier = pltpu.get_barrier_semaphore()
    for axis in axes:
        size = lax.axis_size(axis)
        me = lax.axis_index(axis)

        def signal(d, axis=axis, size=size, me=me):
            pl.semaphore_signal(
                barrier, inc=1, device_id={axis: lax.rem(me + d, size)}, device_id_type=pl.DeviceIdType.MESH
            )

        loop(1, size, signal)


def settle(axes):
    pl.semaphore_wait(pltpu.get_barrier_semaphore(), sum(lax.axis_size(axis) - 1 for axis in axes))


def meet(axes):
    greet(axes)
    settle(axes)


class Exchange:
    def __init__(self, reverse, out_at, bufs, sems):
        self.reverse, self.out_at, self.sems = reverse, out_at, sems
        self.buf, self.y_buf, self.z_src, self.z_buf, self.z_back, self.p_buf, self.mine_buf, self.their_buf, self.decx = bufs
        self.depth = self.buf.shape[1]
        ctx = lax.axis_index("ctx")
        self.ctx = ctx
        self.outer = lax.axis_size("ctx") // 2
        self.owners = min(self.outer, 4)
        self.stride = self.outer // self.owners
        self.inner = lax.rem(ctx, 2)
        self.line = ctx // 2
        self.mine = self.line // self.stride
        self.half = NSTATE // 2
        self.rows = self.half // self.owners

    def half_rows(self, inner):
        return pl.ds(pl.multiple_of(inner * self.half, self.half), self.half)

    def part(self, j):
        return pl.ds(pl.multiple_of(j * self.rows, self.rows), self.rows)

    def other_owners(self, body):
        if self.stride == 1:
            loop(1, self.owners, lambda d: body(lax.rem(self.mine + d, self.owners)))
        else:
            loop(0, self.owners, lambda j: pl.when(j * self.stride != self.line)(lambda: body(j)))

    def other_lines(self, body):
        loop(1, self.outer, lambda d: body(lax.rem(self.line + d, self.outer)))

    def if_owner(self, body):
        if self.stride == 1:
            body()
        else:
            pl.when(self.mine * self.stride == self.line)(body)

    def y_copy(self, u):
        return remote(
            self.buf.at[u, :, self.half_rows(1 - self.inner)], self.y_buf.at[u], self.sems.at[0, u, 0], self.sems.at[1, u, 0],
            ctx=self.ctx + 1 - 2 * self.inner,
        )

    def z_copy(self, u, j, sender):
        return remote(
            self.z_src.at[u, :, self.part(j)], self.z_buf.at[u, sender], self.sems.at[2, u, j], self.sems.at[3, u, sender],
            ctx=j * self.stride * 2 + self.inner,
        )

    def b_copy(self, u, line, j):
        return remote(
            self.z_back.at[u, line], self.p_buf.at[u, :, self.part(j)], self.sems.at[4, u, line], self.sems.at[5, u, j],
            ctx=line * 2 + self.inner,
        )

    def f_copy(self, u, inner):
        return remote(
            self.their_buf.at[u], self.out_at(u, self.half_rows(inner)), self.sems.at[6, u, 0], self.sems.at[7, u, 0],
            ctx=self.ctx + 1 - 2 * self.inner,
        )

    def keep(self, u):
        return pltpu.make_async_copy(self.mine_buf.at[u], self.out_at(u, self.half_rows(self.inner)), self.sems.at[8, u, 0])

    def decay(self, a, block):
        return self.decx[a, pl.ds(pl.multiple_of(block * 8, 8), 8), :][0:1]

    def pair(self, u, a):
        own = self.buf[u, a, self.half_rows(self.inner), :].astype(f32)
        other = self.y_buf[u, a].astype(f32)
        first = self.inner == 0
        return jnp.where(first, own, other), jnp.where(first, other, own)

    def start(self, u):
        self.y_copy(u).start()

    def middle(self, u):
        self.y_copy(u).wait_recv()
        for a in range(self.depth):
            s0, s1 = self.pair(u, a)
            if self.reverse:
                total = s0 + self.decay(a, 2 * self.line) * s1
            else:
                total = self.decay(a, 2 * self.line + 1) * s0 + s1
            self.z_src[u, a] = total.astype(bf16)
        self.other_owners(lambda j: self.z_copy(u, j, self.line).start())

    def scan(self, u):
        def run():
            self.other_lines(lambda line: self.z_copy(u, self.mine, line).wait_recv())
            self.z_buf[u, self.line] = self.z_src[u, :, self.part(self.mine), :]
            for a in range(self.depth):

                def step(k, carry):
                    line = self.outer - 1 - k if self.reverse else k
                    self.z_back[u, line, a] = carry.astype(bf16)
                    both_decays = self.decay(a, 2 * line) * self.decay(a, 2 * line + 1)
                    return both_decays * carry + self.z_buf[u, line, a].astype(f32)

                lax.fori_loop(0, self.outer, step, jnp.zeros(self.z_buf.shape[3:], f32))
            self.other_lines(lambda line: self.b_copy(u, line, self.mine).start())
            self.p_buf[u, :, self.part(self.mine), :] = self.z_back[u, self.line]

        self.if_owner(run)

    def close(self, u):
        self.other_owners(lambda j: self.b_copy(u, self.line, j).wait_recv())
        for a in range(self.depth):
            s0, s1 = self.pair(u, a)
            near = self.p_buf[u, a].astype(f32)
            if self.reverse:
                far = s1 + self.decay(a, 2 * self.line + 1) * near
            else:
                far = s0 + self.decay(a, 2 * self.line) * near
            keeps_near = self.inner == (1 if self.reverse else 0)
            self.mine_buf[u, a] = jnp.where(keeps_near, near, far).astype(bf16)
            self.their_buf[u, a] = jnp.where(keeps_near, far, near).astype(bf16)
        self.f_copy(u, self.inner).start()
        self.keep(u).start()

    def finish(self, u):
        self.f_copy(u, 1 - self.inner).wait_recv()
        self.keep(u).wait()
        self.y_copy(u).wait_send()
        self.other_owners(lambda j: self.z_copy(u, j, self.line).wait_send())
        self.if_owner(lambda: self.other_lines(lambda line: self.b_copy(u, line, self.mine).wait_send()))
        self.f_copy(u, self.inner).wait_send()

    @staticmethod
    def scratch(units, depth, lanes, count):
        outer = count // 2
        half = NSTATE // 2
        rows = half // min(outer, 4)
        bufs = [(units, depth, NSTATE, lanes), (units, depth, half, lanes), (units, depth, half, lanes),
                (units, outer, depth, rows, lanes), (units, outer, depth, rows, lanes), (units, depth, half, lanes),
                (units, depth, half, lanes), (units, depth, half, lanes)]
        return (
            [(b, bf16) for b in bufs]
            + [((depth, count * 8, lanes), f32)]
            + [pltpu.SemaphoreType.DMA((9, units, max(outer, 4)))]
        )


class Spread:
    def __init__(self, shard, full, sems):
        self.shard, self.full = shard, full
        self.x_send, self.x_recv, self.m_send, self.m_recv, self.own = sems
        size = lax.axis_size("group")
        self.cores = 2 if size % 2 == 0 else 1
        self.chips = size // self.cores
        self.me = lax.axis_index("group")
        self.core = lax.rem(self.me, self.cores)
        self.chip = self.me // self.cores
        self.rows = shard.shape[0]

    def place(self, member, cols):
        return self.full.at[pl.ds(pl.multiple_of(member * self.rows, 32), self.rows), cols]

    def across(self, p, cols, d):
        peer = lax.rem(self.chip + d, self.chips) * self.cores + self.core
        return remote(
            self.shard.at[:, cols], self.place(self.me, cols), self.x_send.at[p, d], self.x_recv.at[p, d], group=peer
        )

    def mate(self, p, cols, d):
        member = lax.rem(self.chip + self.chips - d, self.chips) * self.cores + self.core
        src = self.shard.at[:, cols] if d == 0 else self.place(member, cols)
        return remote(
            src, self.place(member, cols), self.m_send.at[p, d], self.m_recv.at[p, d],
            group=self.me + 1 - 2 * self.core,
        )

    def keep(self, p):
        return pltpu.make_async_copy(self.shard, self.place(self.me, slice(None)), self.own.at[p])

    def start_chip(self, p):
        if self.cores == 2:
            self.mate(p, slice(None), 0).start()
        self.keep(p).start()

    def finish_chip(self, p):
        if self.cores == 2:
            self.mate(p, slice(None), 0).wait_recv()
        self.keep(p).wait()

    def start(self, p, cols):
        for d in range(1, self.chips):
            self.across(p, cols, d).start()

    def forward(self, p, cols):
        for d in range(1, self.chips):
            self.across(p, cols, d).wait_recv()
            if self.cores == 2:
                self.mate(p, cols, d).start()

    def finish(self, p, cols):
        if self.cores == 2:
            for d in range(1, self.chips):
                self.mate(p, cols, d).wait_recv()

    def drain(self, p, cols):
        for d in range(1, self.chips):
            self.across(p, cols, d).wait_send()
            if self.cores == 2:
                self.mate(p, cols, d).wait_send()

    def drain_chip(self, p):
        if self.cores == 2:
            self.mate(p, slice(None), 0).wait_send()


def owner_count(rows, width, by_rows, outer):
    fits = lambda n: (rows // 2) % (16 * n) == 0 if by_rows else width % (128 * n) == 0
    return max(n for n in (1, 2, 4) if outer % n == 0 and fits(n))


class Reducer:
    def __init__(self, part, out, rows, width, by_rows, group_bufs, ctx_bufs):
        self.part, self.out, self.rows, self.width, self.by_rows = part, out, rows, width, by_rows
        if group_bufs is not None:
            self.m_buf, self.x_buf, self.g_sems = group_bufs
        self.ships = ctx_bufs is not None
        if self.ships:
            self.y_src, self.y_buf, self.z_src, self.z_buf, self.full, self.c_sems = ctx_bufs
        else:
            self.y_src = out
        self.chunks = self.y_src.shape[0]
        self.base = 0
        self.group = lax.axis_index("group")
        self.cores = 2
        self.chips = lax.axis_size("group") // 2
        self.core = lax.rem(self.group, 2)
        self.chip = self.group // 2
        self.ctx = lax.axis_index("ctx")
        self.outer = lax.axis_size("ctx") // 2
        self.owners = owner_count(rows, width, by_rows, self.outer)
        self.stride = self.outer // self.owners
        self.inner = lax.rem(self.ctx, 2)
        self.line = self.ctx // 2
        self.mine = self.line // self.stride
        self.half = rows // 2

    def cols(self, k):
        return pl.ds(pl.multiple_of(k * self.width, self.width), self.width)

    def member(self, chip, core):
        return pl.ds(pl.multiple_of((chip * 2 + core) * self.rows, 64), self.rows)

    def half_rows(self, inner):
        return pl.ds(pl.multiple_of(inner * self.half, 16), self.half)

    def piece(self, j, base):
        if self.by_rows:
            n = self.half // self.owners
            return pl.ds(pl.multiple_of(base + j * n, 16), n), pl.ds(0, self.width)
        n = self.width // self.owners
        return pl.ds(pl.multiple_of(base, 16), self.half), pl.ds(pl.multiple_of(j * n, 128), n)

    def m_copy(self, k, chip):
        return remote(
            self.part.at[self.member(chip, 1 - self.core), self.cols(k)], self.m_buf.at[k, chip],
            self.g_sems.at[0, k, chip], self.g_sems.at[1, k, chip], group=self.group + 1 - 2 * self.core,
        )

    def x_copy(self, k, chip, sender):
        return remote(
            self.m_buf.at[k, chip], self.x_buf.at[k, sender], self.g_sems.at[2, k, chip], self.g_sems.at[3, k, sender],
            group=chip * 2 + self.core,
        )

    def y_copy(self, k):
        return remote(
            self.y_src.at[k, self.half_rows(1 - self.inner)], self.y_buf.at[k], self.c_sems.at[0, k, 0], self.c_sems.at[1, k, 0],
            ctx=self.ctx + 1 - 2 * self.inner,
        )

    def z_copy(self, k, j, sender):
        rows, cols = self.piece(j, 0)
        return remote(
            self.z_src.at[k, rows, cols], self.z_buf.at[k, sender], self.c_sems.at[2, k, j], self.c_sems.at[3, k, sender],
            ctx=j * self.stride * 2 + self.inner,
        )

    def b_copy(self, k, line, j):
        rows, cols = self.piece(j, self.inner * self.half)
        return remote(
            self.full.at[k, rows, cols], self.full.at[k, rows, cols], self.c_sems.at[4, k, line], self.c_sems.at[5, k, j],
            ctx=line * 2 + self.inner,
        )

    def f_copy(self, k, inner):
        rows = self.half_rows(inner)
        return remote(
            self.full.at[k, rows], self.full.at[k, rows], self.c_sems.at[6, k, 0], self.c_sems.at[7, k, 0],
            ctx=self.ctx + 1 - 2 * self.inner,
        )

    def other_chips(self, body):
        for d in range(1, self.chips):
            body(lax.rem(self.chip + d, self.chips))

    def other_owners(self, body):
        if self.stride == 1:
            for d in range(1, self.owners):
                body(lax.rem(self.mine + d, self.owners))
        else:
            for j in range(self.owners):
                pl.when(j * self.stride != self.line)(lambda j=j: body(j))

    def other_lines(self, body):
        loop(1, self.outer, lambda d: body(lax.rem(self.line + d, self.outer)))

    def if_owner(self, body):
        if self.stride == 1:
            body()
        else:
            pl.when(self.mine * self.stride == self.line)(body)

    def m_start(self, k):
        for chip in range(self.chips):
            self.m_copy(k, chip).start()

    def m_done(self, k):
        for chip in range(self.chips):
            self.m_copy(k, chip).wait_recv()
            own = self.part[self.member(chip, self.core), self.cols(k)].astype(f32)
            self.m_buf[k, chip] = (own + self.m_buf[k, chip].astype(f32)).astype(bf16)
        self.other_chips(lambda chip: self.x_copy(k, chip, self.chip).start())

    def x_done(self, k):
        total = self.m_buf[k, self.chip].astype(f32)
        for d in range(1, self.chips):
            chip = lax.rem(self.chip + d, self.chips)
            self.x_copy(k, chip, chip).wait_recv()
            total = total + self.x_buf[k, chip].astype(f32)
        self.y_src[k] = total.astype(bf16)
        if self.ships:
            self.y_start(k)

    def y_start(self, k):
        self.y_copy(k).start()

    def y_done(self, k):
        self.y_copy(k).wait_recv()
        own = self.y_src[k, self.half_rows(self.inner), :].astype(f32)
        self.z_src[k] = (own + self.y_buf[k].astype(f32)).astype(bf16)
        self.other_owners(lambda j: self.z_copy(k, j, self.line).start())

    def z_done(self, k):
        def run():
            rows, cols = self.piece(self.mine, 0)
            self.other_lines(lambda line: self.z_copy(k, self.mine, line).wait_recv())
            self.z_buf[k, self.line] = self.z_src[k, rows, cols]
            total = self.z_buf[k, 0].astype(f32)
            for line in range(1, self.outer):
                total = total + self.z_buf[k, line].astype(f32)
            rows, cols = self.piece(self.mine, self.inner * self.half)
            self.full[k, rows, cols] = total.astype(bf16)
            self.other_lines(lambda line: self.b_copy(k, line, self.mine).start())

        self.if_owner(run)

    def b_done(self, k):
        self.other_owners(lambda j: self.b_copy(k, self.line, j).wait_recv())
        self.f_copy(k, self.inner).start()

    def f_done(self, k):
        self.f_copy(k, 1 - self.inner).wait_recv()
        self.out[:, pl.ds(pl.multiple_of(self.base + k * self.width, 128), self.width)] = self.full[k]

    def drain_group(self, k):
        for chip in range(self.chips):
            self.m_copy(k, chip).wait_send()
        self.other_chips(lambda chip: self.x_copy(k, chip, self.chip).wait_send())

    def drain_ctx(self, k):
        self.y_copy(k).wait_send()
        self.other_owners(lambda j: self.z_copy(k, j, self.line).wait_send())
        self.if_owner(lambda: self.other_lines(lambda line: self.b_copy(k, line, self.mine).wait_send()))
        self.f_copy(k, self.inner).wait_send()

    def wave(self, t, acts, chunk_at, lag=STAGE_LAG):
        for order, act in reversed(list(enumerate(acts))):
            k, is_due = chunk_at(t - order * lag)
            pl.when(is_due)(lambda k=k, act=act: act(k))

    def each(self, t):
        return t, jnp.logical_and(t >= 0, t < self.chunks)

    @staticmethod
    def group_scratch(chunks, rows, width, group):
        chips = group // 2
        buf = ((chunks, chips, rows, width), bf16)
        return [buf, buf, pltpu.SemaphoreType.DMA((4, chunks, max(chips, 2)))]

    @staticmethod
    def ctx_scratch(chunks, rows, width, by_rows, count):
        outer = count // 2
        owners = owner_count(rows, width, by_rows, outer)
        half = rows // 2
        piece = (half // owners, width) if by_rows else (half, width // owners)
        bufs = [(chunks, half, width), (chunks, half, width), (chunks, outer) + piece, (chunks, rows, width)]
        return [(b, bf16) for b in bufs] + [pltpu.SemaphoreType.DMA((8, chunks, max(outer, 2)))]


class Small:
    def __init__(self, held, got, sends, recvs):
        self.held, self.got, self.sends, self.recvs = held, got, sends, recvs

    def copy(self, h, j, sender):
        return remote(
            self.held.at[h], self.got.at[h, sender], self.sends.at[h, j], self.recvs.at[h, sender], **{HOPS[h]: j}
        )

    def others(self, h, body):
        size, mine = lax.axis_size(HOPS[h]), lax.axis_index(HOPS[h])
        loop(1, size, lambda d: body(lax.rem(mine + d, size)))

    def start(self, h):
        mine = lax.axis_index(HOPS[h])
        self.others(h, lambda j: self.copy(h, j, mine).start())

    def done(self, h):
        self.others(h, lambda j: self.copy(h, j, j).wait_recv())
        self.got[h, lax.axis_index(HOPS[h])] = self.held[h]
        total = self.got[h, 0]
        for j in range(1, lax.axis_size(HOPS[h])):
            total = total + self.got[h, j]
        self.held[h + 1] = total

    def drain(self):
        for h in range(2):
            mine = lax.axis_index(HOPS[h])
            self.others(h, lambda j: self.copy(h, j, mine).wait_send())

    @staticmethod
    def scratch(height, group, count):
        widest = max(group, count)
        dma = pltpu.SemaphoreType.DMA
        return [((3, height, HALF), f32), ((2, widest, height, HALF), f32), dma((2, widest)), dma((2, widest))]


def masks():
    rows = lax.broadcasted_iota(jnp.int32, (HALF, HALF), 0)
    cols = lax.broadcasted_iota(jnp.int32, (HALF, HALF), 1)
    return rows >= cols, cols < HEADDIM


def both(q):
    return slice(q * HALF, (q + 1) * HALF)


def pair_decays(cum, cum_t, p, causal):
    rolled = pltpu.roll(cum, lax.rem(HALF - 2 * p, HALF), 1)
    out = []
    for q in range(2):
        for a in range(2):
            gaps = rolled[both(q), a : a + 1] - cum_t[q, pl.ds(2 * p + a, 1), :]
            out.append(jnp.exp(jnp.where(causal, gaps, -jnp.inf)))
    return out


TILES = DIN // TILE
PIECES = 2 * TILES + 1
DT0 = DIN + CONVW - 2 * NSTATE
AHEAD = 5


def front_kernel(
    tok, tok_any, wzx, wdl, wout, gain, cw, cb_in, db, dl,
    nt, nth, rhalo, cin, xb, spb, vout, cumout, st0, loc, ylocal, gate, decs_out, wfull, wdfull, wofull, sin,
    sel, halo, nh_s, ext, w, wd, cb, cin_s, xs_s, bt, scores, out_cat, dt_cat, cum_t, tot1x, decs,
    halo_sem, x_send, x_recv, m_send, m_recv, w_own, w_store, dec_send, dec_recv, *exchange,
):
    i = pl.program_id(0)
    seqs = tok.shape[0]
    count = lax.axis_size("ctx")
    me = lax.axis_index("ctx")
    sems = (x_send, x_recv, m_send, m_recv, w_own)
    zx, wo, de = Spread(wzx, w, sems), Spread(wout, wofull, sems), Spread(wdl, wd, sems)
    last, small_piece = PIECES, PIECES + 1

    def unit_cols(u):
        return pl.ds(pl.multiple_of(u * TILE, TILE), TILE)

    def piece(p):
        at = jnp.where(p <= TILES, DIN + (p - 1) * TILE, (p - 1 - TILES) * TILE)
        return pl.ds(pl.multiple_of(at, TILE), TILE)

    first_piece = pl.ds(DT0, 2 * NSTATE)
    ex = Exchange(False, lambda u, rows: sin.at[:, rows, unit_cols(u)], exchange[:9], exchange[9])
    halo_copy = remote(
        tok_any.at[:, pl.ds(SPAN - RIM, RIM), :], halo, halo_sem.at[0], halo_sem.at[1], ctx=lax.rem(me + 1, count)
    )
    keep_w = pltpu.make_async_copy(w, wfull, w_store.at[0])
    keep_d = pltpu.make_async_copy(wd, wdfull, w_store.at[1])

    def dec_copy(block, sender):
        rows = pl.ds(pl.multiple_of(sender * 8, 8), 8)
        return remote(decs.at[:, rows, :], decs.at[:, rows, :], dec_send.at[block], dec_recv.at[sender], ctx=block)

    def other_blocks(body):
        loop(1, count, lambda d: body(lax.rem(me + d, count)))

    def conv_tile(s, cols_w, cols_c):
        cin_s[s] = mm(ext[s], w[:, cols_w])
        cin[s] = cin_s[s].astype(bf16)
        o = cb[:, cols_c]
        for k in range(KCONV):
            o = o + cw[k : k + 1, cols_c] * cin_s[s, RIM - KCONV + 1 + k : RIM - KCONV + 1 + k + SPAN, :]
        sg = gate_of(o)
        a = o * sg
        xb[s] = a.astype(bf16)
        spb[s] = (sg + a * (1.0 - sg)).astype(bf16)
        return a

    def unit_decays(u):
        for s in range(seqs):
            ex.decx[s] = spread(decs[s], sel.at[:, unit_cols(u)])

    @pl.when(i == 0)
    def _():
        meet(("ctx", "group"))
        pl.when(me < count - 1)(lambda: halo_copy.start())
        de.start(small_piece, slice(None))
        zx.start(0, first_piece)
        de.start_chip(2)
        zx.start_chip(0)
        cb[...] = row_of(cb_in)
        for p in range(1, AHEAD):
            zx.start(p, piece(p))
        wo.start_chip(1)
        sel[...] = head_map()

        @pl.when(me == 0)
        def _():
            halo[...] = jnp.zeros_like(halo)

        def norm_main(s):
            nm = normalized(tok[s], row_of(gain))[2]
            ext[s, RIM:] = nm
            nt[:, pl.ds(pl.multiple_of(s * SPAN, SPAN), SPAN)] = jnp.transpose(nm.astype(f32)).astype(bf16)

        loop(0, seqs, norm_main)

        @pl.when(me > 0)
        def _():
            halo_copy.wait_recv()

        def norm_halo(s):
            nh = normalized(halo[s], row_of(gain))[2]
            ext[s, 0:RIM] = nh
            nh_s[pl.ds(pl.multiple_of(s * RIM, RIM), RIM), :] = nh.astype(f32)
            rhalo[s] = halo[s]

        loop(0, seqs, norm_halo)
        nth[...] = jnp.transpose(nh_s[...]).astype(bf16)
        de.forward(small_piece, slice(None))
        zx.forward(0, first_piece)
        zx.finish_chip(0)
        de.finish_chip(2)

    @pl.when(i + 1 < PIECES)
    def _():
        zx.forward(i + 1, piece(i + 1))

    @pl.when(i + AHEAD < PIECES)
    def _():
        zx.start(i + AHEAD, piece(i + AHEAD))

    @pl.when(i + AHEAD == PIECES)
    def _():
        wo.start(last, slice(None))

    @pl.when(i == 0)
    def _():
        zx.finish(0, first_piece)
        de.finish(small_piece, slice(None))
        shift, rate = lane_row(db), jnp.exp(lane_row(dl))

        def delta(s):
            a = conv_tile(s, slice(DT0, DT0 + TILE), slice(DIN, DIN + TILE))
            bb, cc = a[:, :NSTATE].astype(bf16), a[:, NSTATE:].astype(bf16)
            bt[s] = jnp.transpose(a[:, :NSTATE]).astype(bf16)
            for q in range(2):
                scores[s, q] = mm_nt(cc[both(q)], bb[both(q)])
            v = mm(ext[s, RIM:], wd[...]) + shift
            vout[s] = v
            dt = softplus(v)
            cum = running_sum(-rate * dt, True)
            cumout[s] = cum
            for q in range(2):
                cum_t[s, q] = jnp.transpose(cum[both(q)])
            e_in, e_out, tot0, tot1, total = local_decays(cum)
            decs[s, pl.ds(pl.multiple_of(me * 8, 8), 8), :] = rows_of(total)
            out_cat[s] = jnp.concatenate(halves(dt * e_out), axis=1)
            dt_cat[s] = jnp.concatenate(halves(dt), axis=1)
            tot1x[s] = spread(rows_of(tot1), sel)

        loop(0, seqs, delta)
        other_blocks(lambda b: dec_copy(b, me).start())

    @pl.when(jnp.logical_and(i >= 1, i < PIECES))
    def _():
        zx.finish(i, piece(i))

    def act_at(t, lag, act):
        u = t - 1 - lag
        pl.when(jnp.logical_and(u >= 0, u < TILES))(lambda: act(u))

    def close(u):
        unit_decays(u)
        ex.close(u)

    def scan(u):
        unit_decays(u)
        ex.scan(u)

    def middle(u):
        unit_decays(u)
        ex.middle(u)

    @pl.when(i == 3)
    def _():
        other_blocks(lambda b: dec_copy(b, b).wait_recv())

    def wave(t):
        act_at(t, CLOSE_LAG, close)
        act_at(t, SCAN_LAG, scan)
        act_at(t, MIDDLE_LAG, middle)

    wave(i)

    @pl.when(jnp.logical_and(i >= 1, i <= TILES))
    def _():
        u = i - 1
        cols = unit_cols(u)

        def x_tile(s):
            a = conv_tile(s, piece(i), cols)
            xs_s[s, :, cols] = a.astype(bf16)
            xw = (a * mm(out_cat[s], sel[:, cols])).astype(bf16)
            s0 = mm(bt[s, :, :HALF], xw[:HALF])
            s1 = mm(bt[s, :, HALF:], xw[HALF:])
            st0[s] = s0.astype(bf16)
            low = (tot1x[s, :, cols][0:1] * s0 + s1).astype(bf16)
            loc[s] = low
            ex.buf[u, s] = low

        loop(0, seqs, x_tile)
        ex.start(u)

    @pl.when(i > TILES)
    def _():
        u = i - 1 - TILES
        causal, low_lanes = masks()

        def intra(s):
            cum = cumout[s]
            dtx = mm(dt_cat[s], sel[:, unit_cols(u)])
            for h in range(2):
                p = 2 * u + h
                lanes = slice(h * HALF, (h + 1) * HALF)
                decays = pair_decays(cum, cum_t.at[s], p, causal)
                for q in range(2):
                    rows = both(q)
                    m = jnp.concatenate([(decays[2 * q + a] * scores[s, q]).astype(bf16) for a in range(2)], axis=1)
                    x = xs_s[s, rows, pl.ds(pl.multiple_of(p * HALF, HALF), HALF)].astype(f32) * dtx[rows, lanes]
                    x = jnp.concatenate([jnp.where(low_lanes, x, 0.0), jnp.where(low_lanes, 0.0, x)], axis=0)
                    ylocal[s, rows, lanes] = mm(m, x.astype(bf16)).astype(bf16)
            gate[s] = mm(ext[s, RIM:], w[:, piece(i)]).astype(bf16)

        def two_intra(h):
            for b in range(2):
                intra(2 * h + b)

        loop(0, seqs // 2, two_intra)

    @pl.when(i == PIECES - 1)
    def _():
        keep_w.start()
        keep_d.start()
        decs_out[...] = decs[...]
        wo.forward(last, slice(None))
        loop(PIECES, TILES + CLOSE_LAG + 1, wave)
        loop(0, TILES, ex.finish)
        wo.finish(last, slice(None))
        wo.finish_chip(1)
        zx.drain_chip(0)
        wo.drain_chip(1)
        de.drain_chip(2)
        de.drain(small_piece, slice(None))
        zx.drain(0, first_piece)
        loop(1, PIECES, lambda p: zx.drain(p, piece(p)))
        wo.drain(last, slice(None))
        other_blocks(lambda b: dec_copy(b, me).wait_send())
        pl.when(me < count - 1)(lambda: halo_copy.wait_send())
        keep_w.wait()
        keep_d.wait()


def middle_kernel(
    lengths, skip_in, tok, cot, ylocal, gate, xb, vin, cumin, st0, sin, decs, wout, ggain_in, nt,
    mixed, dyout, ggate, wred, dir1, gskip, gggain, dxs, dbc, xgate, xout, later,
    sel, skip, ggain, cum_t, einx, ys, gs, ss, s_in, dcs, dy_s, ml_s, gg_s, dr_s, pgate, pout, g_s, dg_s, *exchange,
):
    i = pl.program_id(0)
    seqs = dy_s.shape[0]
    ex = Exchange(True, lambda u, rows: later.at[pl.ds(u, 1), rows, :], exchange[:9], exchange[9])
    members = lax.axis_size("group")
    gates = Reducer(pgate, xgate, D // members, GATE_CHUNK, False, exchange[10:13], None)
    outs = Reducer(pout, xout, DIN // members, OUT_CHUNK, True, exchange[13:16], None)

    def span(s):
        return pl.ds(pl.multiple_of(s * SPAN, SPAN), SPAN)

    def group_wave(t):
        gates.wave(t - 2 * seqs - 3, [gates.x_done], gates.each)
        outs.wave(t - 2 * seqs - 3 - gates.chunks, [outs.x_done], outs.each)

    def wave(t):
        group_wave(t)

        def act_at(lag, act):
            u = lax.div(t - lag, 2)

            def run():
                ex.decx[0] = spread(decs[u], sel)
                act(u)

            pl.when(jnp.logical_and(t >= lag, jnp.logical_and(2 * u + lag == t, u < seqs)))(run)

        act_at(BACK_LAGS[2], ex.close)
        act_at(BACK_LAGS[1], ex.scan)
        act_at(BACK_LAGS[0], ex.middle)

    @pl.when(i == 0)
    def _():
        greet(("ctx", "group"))
        sel[...] = head_map()
        skip[...] = spread(rows_of(lane_row(skip_in)), sel)[0:1]
        ggain[...] = row_of(ggain_in)
        gskip[...] = jnp.zeros_like(gskip)
        gggain[...] = jnp.zeros_like(gggain)

    @pl.when(i == 1)
    def _():
        settle(("ctx", "group"))

    @pl.when(jnp.logical_and(i >= 1, i <= seqs))
    def _():
        ex.start(i - 1)

    wave(2 * i)

    @pl.when(i < seqs)
    def _():
        s = i
        cum = cumin[0]
        e_in, e_out, tot0, tot1, total = local_decays(cum)
        einx[...] = spread(e_in, sel)
        tot0x = spread(rows_of(tot0), sel)[0:1]
        s_in[0] = sin[0]
        s_in[1] = (tot0x * sin[0].astype(f32) + st0[0].astype(f32)).astype(bf16)
        cc = xb[0, :, DIN + NSTATE :]

        def gate_step(j, total_sq):
            cols = pl.ds(pl.multiple_of(j * TILE, TILE), TILE)
            for q in range(2):
                rows = both(q)
                ys[rows, cols] = ylocal[0, rows, cols].astype(f32) + einx[rows, cols] * mm(cc[rows], s_in[q, :, cols])
            y = ys[:, cols] + skip[:, cols] * xb[0, :, cols].astype(f32)
            g = gate[0, :, cols].astype(f32)
            gated = y * (g * gate_of(g))
            gs[:, cols] = gated
            sq = gated * gated
            return total_sq + sq[:, :HALF] + sq[:, HALF:]

        wave(2 * i + 1)
        sq = lax.fori_loop(0, DIN // TILE, gate_step, jnp.zeros((SPAN, HALF), f32))
        inv = lax.rsqrt(jnp.sum(sq, axis=1, keepdims=True) * (1.0 / DIN) + EPS)
        live = live_rows(lengths, s)
        drive = (live * cot[0].astype(f32)).astype(bf16)
        dr_s[span(s), :] = drive

        def back_step(j, acc):
            cols = pl.ds(pl.multiple_of(j * TILE, TILE), TILE)
            gm = mm_nt(drive, wout[cols, :])
            gated = gs[:, cols]
            unit = gated * inv
            ml_s[span(s), cols] = (unit * ggain[:, cols]).astype(bf16)
            gggain[:, cols] += jnp.sum(gm * unit, axis=0, keepdims=True)
            scaled = gm * ggain[:, cols]
            ss[:, cols] = scaled
            prod = scaled * gated
            return acc + prod[:, :HALF] + prod[:, HALF:]

        dots = lax.fori_loop(0, DIN // TILE, back_step, jnp.zeros((SPAN, HALF), f32))
        dots = jnp.sum(dots, axis=1, keepdims=True) * (1.0 / DIN)
        corr = inv * inv * inv * dots
        cct = jnp.transpose(cc.astype(f32)).astype(bf16)
        acc = jnp.zeros((SPAN, HALF), f32)
        dc = [jnp.zeros((HALF, HALF), f32) for _ in range(2)]
        for j in range(DIN // TILE):
            cols = slice(j * TILE, (j + 1) * TILE)
            g = gate[0, :, cols].astype(f32)
            sg = gate_of(g)
            sl = g * sg
            grad_gated = inv * ss[:, cols] - gs[:, cols] * corr
            dy = grad_gated * sl
            yn = ys[:, cols]
            x = xb[0, :, cols].astype(f32)
            y = yn + skip[:, cols] * x
            low = (grad_gated * y * (sg + sl * (1.0 - sg))).astype(bf16)
            ggate[0, :, cols] = low
            gg_s[span(s), cols] = low
            dyb = dy.astype(bf16)
            dyout[0, :, cols] = dyb
            dy_s[s, :, cols] = dyb
            gskip[:, cols] += jnp.sum(dy * x, axis=0, keepdims=True)
            acc = acc + gather_heads(dy * yn, sel[:HALF, cols])
            dye = (dy * einx[:, cols]).astype(bf16)
            d0 = mm(cct[:, :HALF], dye[:HALF])
            d1 = mm(cct[:, HALF:], dye[HALF:])
            dir1[0, :, cols] = d1.astype(bf16)
            ex.buf[s, 0, :, cols] = (d0 + tot0x[:, cols] * d1).astype(bf16)
            for q in range(2):
                dc[q] = dc[q] + mm_nt(dye[both(q)], s_in[q, :, cols])
        wred[0] = acc
        for q in range(2):
            dcs[s, both(q)] = dc[q]

    @pl.when(i >= seqs)
    def _():
        s = i - seqs
        causal, low_lanes = masks()
        cum = cumin[0]
        for q in range(2):
            cum_t[q] = jnp.transpose(cum[both(q)])
        einx[...] = spread(softplus(vin[0]), sel)
        bb = xb[0, :, DIN : DIN + NSTATE]
        cc = xb[0, :, DIN + NSTATE :]
        for q in range(2):
            g_s[q] = mm_nt(cc[both(q)], bb[both(q)])
        dg_s[...] = jnp.zeros_like(dg_s)

        def pair_step(p):
            cols = pl.ds(pl.multiple_of(p * HALF, HALF), HALF)
            decays = pair_decays(cum, cum_t, p, causal)
            for q in range(2):
                rows = both(q)
                xsb = (xb[0, rows, cols].astype(f32) * einx[rows, cols]).astype(bf16)
                dyb = dy_s[s, rows, cols]
                dyf = dyb.astype(f32)
                grads = []
                for a in range(2):
                    m = (decays[2 * q + a] * g_s[q]).astype(bf16)
                    grads.append(mm_tn(m, dyb))
                    mine = low_lanes if a == 0 else jnp.logical_not(low_lanes)
                    dm = mm_nt(jnp.where(mine, dyf, 0.0).astype(bf16), xsb)
                    dg_s[q] += dm * decays[2 * q + a]
                dxs[0, rows, cols] = jnp.where(low_lanes, grads[0], grads[1]).astype(bf16)

        @pl.when(s == 0)
        def _():
            for k in range(gates.chunks):
                cols = slice(k * GATE_CHUNK, (k + 1) * GATE_CHUNK)
                pgate[:, cols] = mm(nt[...], gg_s[:, cols]).astype(bf16)
                gates.m_start(k)

        @pl.when(s == 1)
        def _():
            loop(0, outs.chunks, outs.m_done)

        def two_pairs(pp):
            for h in range(2):
                pair_step(2 * pp + h)

        loop(0, PAIRS // 4, two_pairs)
        wave(2 * i + 1)

        @pl.when(s == 0)
        def _():
            loop(0, gates.chunks, gates.m_done)

            def out_rows(r):
                rows = pl.ds(pl.multiple_of(r * TILE, TILE), TILE)
                pout[rows, :] = mm_tn(ml_s[:, rows], dr_s[...]).astype(bf16)

            loop(0, DIN // TILE, out_rows)
            loop(0, outs.chunks, outs.m_start)

        loop(PAIRS // 4, PAIRS // 2, two_pairs)
        for q in range(2):
            rows = both(q)
            dg = dg_s[q].astype(bf16)
            dbc[0, rows, :NSTATE] = mm_tn(dg, cc[rows])
            dbc[0, rows, NSTATE:] = mm(dg, bb[rows]) + dcs[s, rows]
        live = live_rows(lengths, s)
        for j in range(D // TILE):
            cols = slice(j * TILE, (j + 1) * TILE)
            mixed[0, :, cols] = (live * (tok[0, :, cols].astype(f32) + mm(ml_s[span(s), :], wout[:, cols]))).astype(bf16)

    @pl.when(i == 2 * seqs - 1)
    def _():
        loop(4 * seqs, max(2 * seqs + BACK_LAGS[2] - 1, 2 * seqs + 3 + gates.chunks + outs.chunks), wave)
        loop(0, seqs, ex.finish)
        for r in (gates, outs):
            loop(0, r.chunks, r.drain_group)


def back_kernel(
    lengths, dl, skip_in, tok, cot, rhalo, gain, ggate, w_any, wd, cin, xb, spb, bc, dy, dxs, dir1, later, sin, loc,
    vin, cumin, wred, dbc, cw, nt, nth, xgate, xout, gskip, gggain,
    gtok, rzx, rout, small_out, ggain_out,
    sel, skip, wfull, w_sem, dt_cat, eo_cat, tots, db_s, qacc, ends, gp, gz_s, gzh_s, pconv, gcw, gcb, gdb, gdl, ggain,
    rim_out, rim_in, rim_send, rim_recv, *comm,
):
    i = pl.program_id(0)
    seqs = rhalo.shape[0]
    count = lax.axis_size("ctx")
    me = lax.axis_index("ctx")
    members = lax.axis_size("group")
    gates = Reducer(None, rzx, D // members, GATE_CHUNK, False, None, (xgate,) + comm[0:5])
    outs = Reducer(None, rout, DIN // members, OUT_CHUNK, True, None, (xout,) + comm[5:10])
    convs = Reducer(pconv, rzx, D // members, CONV_CHUNK, False, comm[10:13], comm[13:19])
    convs.base = DIN
    load_w = pltpu.make_async_copy(w_any, wfull, w_sem.at[0])
    little, least = Small(*comm[19:23]), Small(*comm[23:27])
    bc_step = TILES

    last_conv = 2 * bc_step + 5

    def conv_at(t):
        k = lax.div(t - 7, 4)
        even = jnp.logical_and(t >= 7, jnp.logical_and(lax.rem(t - 7, 4) == 0, k < convs.chunks - 1))
        last = t == last_conv
        return jnp.where(last, convs.chunks - 1, k), jnp.logical_or(even, last)

    def wave(t):
        for r, at in ((gates, 2), (outs, 2 + gates.chunks)):
            r.wave(t - at, [r.y_done, r.z_done, r.b_done, r.f_done], r.each)
        convs.wave(t, [convs.x_done, convs.y_done, convs.z_done, convs.b_done, convs.f_done], conv_at, CONV_LAG)

    def rim_copy(q):
        return remote(rim_out.at[q], rim_in.at[q], rim_send.at[q], rim_recv.at[q], ctx=lax.rem(me + count - 1, count))

    def span(s):
        return pl.ds(pl.multiple_of(s * SPAN, SPAN), SPAN)

    def edge(s):
        return pl.ds(pl.multiple_of(s * RIM, RIM), RIM)

    def back(rows, grad):
        rows, inv, _ = normalized(rows, row_of(gain))
        ggain[...] += jnp.sum(grad * rows * inv, axis=0, keepdims=True)
        gained = row_of(gain) * grad
        mean = jnp.mean(gained * rows, axis=-1, keepdims=True)
        return inv * gained - rows * (inv * inv * inv * mean)

    @pl.when(i == 0)
    def _():
        meet(("ctx", "group"))
        for r in (gates, outs):
            loop(0, r.chunks, r.y_start)
        load_w.start()
        sel[...] = head_map()
        skip[...] = spread(rows_of(lane_row(skip_in)), sel)[0:1]
        for acc in (db_s, qacc, ends, gcw, gcb, gdb, gdl, ggain):
            acc[...] = jnp.zeros_like(acc)
        for slot in range(2):
            gp[slot, 0:RIM] = jnp.zeros((RIM, TILE), f32)
            gp[slot, RIM + SPAN :] = jnp.zeros((8, TILE), f32)
        pconv[:, CONVW + HALF :] = jnp.zeros((D, GZW - CONVW - HALF), bf16)

        def setup(s):
            dt = softplus(vin[s])
            _, e_out, _, tot1, total = local_decays(cumin[s])
            dt_cat[s] = jnp.concatenate(halves(dt), axis=1)
            eo_cat[s] = jnp.concatenate(halves(e_out), axis=1)
            both_rows = jnp.concatenate([rows_of(tot1), rows_of(total)], axis=0)
            tots[s] = spread(both_rows, sel)

        loop(0, seqs, setup)

    def conv_back(s, dact, cols, slot=0):
        gco = dact * spb[s].astype(f32)
        gp[slot, RIM : RIM + SPAN] = gco
        gcb[:, cols] += jnp.sum(gco, axis=0, keepdims=True)
        own = cin[s, RIM:].astype(f32)
        before = cin[s, :RIM].astype(f32)
        main = jnp.zeros((SPAN, TILE), f32)
        rim = jnp.zeros((RIM, TILE), f32)
        for k in range(KCONV):
            ahead = KCONV - 1 - k
            moved = gco if ahead == 0 else gp[slot, RIM + ahead : RIM + ahead + SPAN]
            early = gp[slot, ahead : ahead + RIM]
            main = main + cw[k : k + 1, cols] * moved
            rim = rim + cw[k : k + 1, cols] * early
            gcw[k : k + 1, cols] += jnp.sum(own * moved, axis=0, keepdims=True) + jnp.sum(
                before * early, axis=0, keepdims=True
            )
        gz_s[span(s), cols] = main.astype(bf16)
        gzh_s[edge(s), cols] = rim.astype(bf16)

    def partial(cols):
        pconv[:, cols] = (mm(nt[...], gz_s[:, cols]) + mm(nth[...], gzh_s[:, cols])).astype(bf16)

    wave(2 * i)

    @pl.when(i < bc_step)
    def _():
        cols = pl.ds(pl.multiple_of(i * TILE, TILE), TILE)

        def x_tile(s, slot):
            dte = mm(dt_cat[s], sel[:, cols])
            eo = mm(eo_cat[s], sel[:, cols])
            near = later[s]
            near32 = near.astype(f32)
            tot = tots[s, :, cols]
            reach = [(dir1[s].astype(f32) + tot[0:1] * near32).astype(bf16), near]
            fed = jnp.concatenate(
                [mm(bc[s, both(q), :NSTATE], reach[q]) for q in range(2)], axis=0
            )
            x = xb[s].astype(f32)
            dx_s = dxs[s].astype(f32) + eo * fed
            qacc[s] += gather_heads(x * dx_s, sel[:HALF, cols])
            xw = (x * dte * eo).astype(bf16)
            for q in range(2):
                db_s[s, both(q)] += mm_nt(xw[both(q)], reach[q])
            held = near32 * (tot[8:9] * sin[s].astype(f32) + loc[s].astype(f32))
            ends[s] += gather_heads(rows_of(jnp.sum(held, axis=0, keepdims=True)), sel[:HALF, cols])
            conv_back(s, dte * dx_s + skip[:, cols] * dy[s].astype(f32), cols, slot)

        def two_seqs(h):
            for slot in range(2):
                x_tile(2 * h + slot, slot)

        loop(0, seqs // 4, two_seqs)

        @pl.when(jnp.logical_and(lax.rem(i, 2) == 0, i >= 2))
        def _():
            convs.m_done(lax.div(i, 2) - 1)

        wave(2 * i + 1)
        loop(seqs // 4, seqs // 2, two_seqs)
        partial(cols)

        @pl.when(lax.rem(i, 2) == 1)
        def _():
            convs.m_start(lax.div(i, 2))

    @pl.when(i == bc_step)
    def _():
        cols = slice(DIN, CONVW)
        rate = jnp.exp(lane_row(dl))

        def bc_tile(s, slot):
            conv_back(s, jnp.concatenate([dbc[s, :, :NSTATE] + db_s[s], dbc[s, :, NSTATE:]], axis=1), cols, slot)
            v = vin[s]
            dt = softplus(v)
            q = qacc[s]
            at_end = lax.broadcasted_iota(jnp.int32, (SPAN, 1), 0) == SPAN - 1
            dcum = wred[s] - dt * q + jnp.where(at_end, ends[s][0:1], 0.0)
            glog = running_sum(dcum, False)
            gpd = (q - rate * glog) * sigmoid(v)
            lanes = lax.broadcasted_iota(jnp.int32, (SPAN, HALF), 1) < HEADS
            gpd = jnp.where(lanes, gpd, 0.0)
            gz_s[span(s), CONVW : CONVW + HALF] = gpd.astype(bf16)
            gdb[...] += jnp.sum(gpd, axis=0, keepdims=True)
            gdl[...] += -rate * jnp.sum(dt * glog, axis=0, keepdims=True)

        def two_bc(h):
            for slot in range(2):
                bc_tile(2 * h + slot, slot)

        loop(0, seqs // 2, two_bc)
        convs.m_done(convs.chunks - 2)
        wave(2 * i + 1)
        partial(cols)
        pconv[:, CONVW : CONVW + HALF] = mm(nt[...], gz_s[:, CONVW : CONVW + HALF]).astype(bf16)
        convs.m_start(convs.chunks - 1)
        rows = [gcw[k : k + 1, j * HALF : (j + 1) * HALF] for k in range(KCONV) for j in range(CONVW // HALF)]
        rows += [gcb[:, j * HALF : (j + 1) * HALF] for j in range(CONVW // HALF)]
        rows += [gdb[...], gdl[...]]
        rows += [gather_heads(rows_of(gskip[...]), sel[:HALF])[0:1]]
        rows += [gggain[:, j * HALF : (j + 1) * HALF] for j in range(PAIRS)]
        little.held[0, SMALL_ROWS - 8 :] = jnp.zeros((8, HALF), f32)
        for r, row in enumerate(rows):
            little.held[0, r : r + 1, :] = row
        little.start(0)
        load_w.wait()
        edges = mm_nt(gzh_s[...], wfull[:, DIN:ZXW])
        for q in range(seqs):
            rim_out[q] = back(rhalo[q], edges[q * RIM : (q + 1) * RIM]).astype(bf16)
            pl.when(me > 0)(lambda q=q: rim_copy(q).start())

        @pl.when(me == count - 1)
        def _():
            rim_in[...] = jnp.zeros_like(rim_in)

    @pl.when(i == bc_step + 2)
    def _():
        little.done(0)
        little.start(1)

    @pl.when(i > bc_step)
    def _():
        s = i - bc_step - 1
        grad = mm_nt(gz_s[span(s), :CONVW], wfull[:, DIN:]) + mm_nt(ggate[0], wfull[:, :DIN])
        grad = grad + mm_nt(gz_s[span(s), CONVW:], wd[...])

        @pl.when(s == 0)
        def _():
            convs.m_done(convs.chunks - 1)

        wave(2 * i + 1)
        live = live_rows(lengths, s)
        out = live * cot[0].astype(f32) + back(tok[0], grad)
        gtok[0, : SPAN - RIM] = out[: SPAN - RIM].astype(bf16)
        pl.when(me < count - 1)(lambda: rim_copy(s).wait_recv())
        gtok[0, SPAN - RIM :] = (out[SPAN - RIM :] + rim_in[s].astype(f32)).astype(bf16)

    @pl.when(i == bc_step + seqs)
    def _():
        least.held[0] = jnp.zeros_like(least.held[0])
        for j in range(D // HALF):
            least.held[0, j : j + 1, :] = ggain[:, j * HALF : (j + 1) * HALF]
        least.start(0)
        little.done(1)
        small_out[...] = little.held[2]
        ends_at = max(last_conv + 4 * CONV_LAG, 1 + gates.chunks + outs.chunks + 3 * STAGE_LAG) + 1
        here = 2 * (bc_step + seqs) + 2
        loop(here, min(here + 2, ends_at), wave)
        least.done(0)
        least.start(1)
        loop(here + 2, ends_at, wave)
        for r in (gates, outs, convs):
            loop(0, r.chunks, r.drain_ctx)
        loop(0, convs.chunks, convs.drain_group)
        little.drain()
        for q in range(seqs):
            pl.when(me > 0)(lambda q=q: rim_copy(q).wait_send())
        least.done(1)
        ggain_out[...] = least.held[2]
        least.drain()


def done_kernel(
    rzx, rdelta, rout, small, gain_sum,
    g_gain, g_zx, g_delta, g_out, g_cw, g_cb, g_db, g_dl, g_skip, g_gated,
):
    @pl.when(pl.program_id(0) == 0)
    def _():
        tiles = CONVW // HALF
        for k in range(KCONV):
            for j in range(tiles):
                g_cw[k : k + 1, j * HALF : (j + 1) * HALF] = small[k * tiles + j : k * tiles + j + 1, :]
        at = KCONV * tiles
        for j in range(tiles):
            g_cb[j * HALF : (j + 1) * HALF] = small[at + j, :]
        at += tiles
        for ref in (g_db, g_dl, g_skip):
            ref[...] = small[at, :][:HEADS]
            at += 1
        for j in range(PAIRS):
            g_gated[j * HALF : (j + 1) * HALF] = small[at + j, :]
        for j in range(D // HALF):
            g_gain[j * HALF : (j + 1) * HALF] = gain_sum[j, :]
        g_delta[...] = jnp.transpose(rdelta[...].astype(f32))[:HEADS]

    g_zx[...] = rzx[:, :ZXW].astype(f32)
    g_out[...] = rout[...].astype(f32)


def whole(shape):
    zeros = (0,) * len(shape)
    return pl.BlockSpec(shape, lambda s: zeros, pipeline_mode=pl.Buffered(1))


def summed(shape):
    zeros = (0,) * len(shape)
    return pl.BlockSpec(shape, lambda s: zeros)


def per_seq(*shape):
    zeros = (0,) * len(shape)
    return pl.BlockSpec((1,) + shape, lambda s: (s,) + zeros)


SMEM = pl.BlockSpec(memory_space=pltpu.SMEM)
ANY = pl.BlockSpec(memory_space=pl.ANY)


def staged(seqs, phase, *shape):
    zeros = (0,) * len(shape)
    if phase == 0:
        return pl.BlockSpec((1,) + shape, lambda i: (jnp.minimum(i, seqs - 1),) + zeros)
    if phase == 1:
        return pl.BlockSpec((1,) + shape, lambda i: (jnp.maximum(i - seqs, 0),) + zeros)
    return pl.BlockSpec((1,) + shape, lambda i: (lax.rem(i, seqs),) + zeros)


def call(kernel, steps, in_specs, outs, scratch, name, collective=None):
    params = dict(vmem_limit_bytes=VMEM_LIMIT)
    if collective is not None:
        params.update(collective_id=collective, has_side_effects=True)
    return pl.pallas_call(
        kernel,
        grid=(steps,),
        in_specs=in_specs,
        out_specs=[o[0] for o in outs],
        out_shape=[jax.ShapeDtypeStruct(o[1], o[2]) for o in outs],
        scratch_shapes=[pltpu.VMEM(*sc) if isinstance(sc, tuple) else sc for sc in scratch],
        compiler_params=pltpu.CompilerParams(**params),
        name=name,
    )


def local(
    tokens_in, seq_lengths, norm_gain, w_zx, w_delta, w_out, conv_weight, conv_bias,
    delta_bias, decay_log, skip_gain, gated_gain, cotangent,
):
    seqs = tokens_in.shape[0]
    count = lax.axis_size("ctx")
    group = lax.axis_size("group")
    chips = max(group // 2, 1)
    w_delta = jnp.pad(w_delta, ((0, 0), (0, HALF - HEADS)))
    dma = pltpu.SemaphoreType.DMA
    at0 = lambda *shape: staged(seqs, 0, *shape)
    at1 = lambda *shape: staged(seqs, 1, *shape)
    at01 = lambda *shape: staged(seqs, 2, *shape)

    def tiled(rows, first, lead=None):
        def index(i):
            u = jnp.clip(i - first, 0, TILES - 1)
            return (0, 0, u if lead is None else jnp.where(i == 0, lead, u))

        return pl.BlockSpec((seqs, rows, TILE), index)

    state = (seqs, NSTATE, DIN)
    nt, nth, rhalo, cin, xb, spb, vraw, cum, st0, loc, ylocal, gate, decs, wfull, wdfull, wofull, state_in = call(
        front_kernel,
        PIECES,
        [whole((seqs, SPAN, D)), ANY, ANY, ANY, ANY, whole((D,)), whole((KCONV, CONVW)), whole((CONVW,)), SMEM, SMEM],
        [
            (summed((D, seqs * SPAN)), (D, seqs * SPAN), bf16),
            (summed((D, seqs * RIM)), (D, seqs * RIM), bf16),
            (summed((seqs, RIM, D)), (seqs, RIM, D), bf16),
            (tiled(RIM + SPAN, 1, TILES), (seqs, RIM + SPAN, CONVW), bf16),
            (tiled(SPAN, 1, TILES), (seqs, SPAN, CONVW), bf16),
            (tiled(SPAN, 1, TILES), (seqs, SPAN, CONVW), bf16),
            (summed((seqs, SPAN, HALF)), (seqs, SPAN, HALF), f32),
            (summed((seqs, SPAN, HALF)), (seqs, SPAN, HALF), f32),
            (tiled(NSTATE, 1), state, bf16),
            (tiled(NSTATE, 1), state, bf16),
            (tiled(SPAN, TILES + 1), (seqs, SPAN, DIN), bf16),
            (tiled(SPAN, TILES + 1), (seqs, SPAN, DIN), bf16),
            (summed((seqs, count * 8, HALF)), (seqs, count * 8, HALF), f32),
            (ANY, (D, ZXW), bf16),
            (ANY, (D, HALF), bf16),
            (ANY, (DIN, D), bf16),
            (ANY, state, bf16),
        ],
        [((2 * HALF, DIN), bf16), ((seqs, RIM, D), bf16), ((seqs * RIM, D), f32), ((seqs, RIM + SPAN, D), bf16), ((D, ZXW), bf16),
         ((D, HALF), bf16), ((1, CONVW), f32),
         ((seqs, RIM + SPAN, TILE), f32), ((seqs, SPAN, DIN), bf16), ((seqs, NSTATE, SPAN), bf16),
         ((seqs, 2, HALF, HALF), f32), ((seqs, SPAN, 2 * HALF), bf16), ((seqs, SPAN, 2 * HALF), bf16),
         ((seqs, 2, HALF, HALF), f32), ((seqs, 8, DIN), f32), ((seqs, count * 8, HALF), f32)]
        + [dma((2,))] + [dma((PIECES + 2, chips))] * 4 + [dma((3,)), dma((2,)), dma((count,)), dma((count,))]
        + Exchange.scratch(TILES, seqs, TILE, count),
        "front",
        0,
    )(tokens_in, tokens_in, w_zx, w_delta, w_out, norm_gain, conv_weight, conv_bias, delta_bias, decay_log)

    x_gate_shape = (DIN // GATE_CHUNK, D // group, GATE_CHUNK)
    x_out_shape = (D // OUT_CHUNK, DIN // group, OUT_CHUNK)
    mixed_out, dy, ggate, wred, dir1, gskip, gggain, dxs, dbc, x_gate, x_out, later = call(
        middle_kernel,
        2 * seqs,
        [SMEM, SMEM, at1(SPAN, D), at0(SPAN, D), at0(SPAN, DIN), at0(SPAN, DIN), at01(SPAN, CONVW), at01(SPAN, HALF),
         at01(SPAN, HALF), at0(NSTATE, DIN), at0(NSTATE, DIN), whole((seqs, count * 8, HALF)), whole((DIN, D)),
         whole((DIN,)), whole((D, seqs * SPAN))],
        [
            (at1(SPAN, D), (seqs, SPAN, D), bf16),
            (at0(SPAN, DIN), (seqs, SPAN, DIN), bf16),
            (at0(SPAN, DIN), (seqs, SPAN, DIN), bf16),
            (at0(SPAN, HALF), (seqs, SPAN, HALF), f32),
            (at0(NSTATE, DIN), (seqs, NSTATE, DIN), bf16),
            (summed((1, DIN)), (1, DIN), f32),
            (summed((1, DIN)), (1, DIN), f32),
            (at1(SPAN, DIN), (seqs, SPAN, DIN), bf16),
            (at1(SPAN, 2 * NSTATE), (seqs, SPAN, 2 * NSTATE), f32),
            (summed(x_gate_shape), x_gate_shape, bf16),
            (summed(x_out_shape), x_out_shape, bf16),
            (ANY, (seqs, NSTATE, DIN), bf16),
        ],
        [((2 * HALF, DIN), bf16), ((1, DIN), f32), ((1, DIN), f32), ((2, HALF, HALF), f32), ((SPAN, DIN), f32), ((SPAN, DIN), f32), ((SPAN, DIN), f32),
         ((SPAN, DIN), f32), ((2, NSTATE, DIN), bf16), ((seqs, SPAN, HALF), f32), ((seqs, SPAN, DIN), bf16),
         ((seqs * SPAN, DIN), bf16), ((seqs * SPAN, DIN), bf16), ((seqs * SPAN, D), bf16), ((D, DIN), bf16), ((DIN, D), bf16),
         ((2, HALF, HALF), f32), ((2, HALF, HALF), f32)]
        + Exchange.scratch(seqs, 1, DIN, count)
        + Reducer.group_scratch(*x_gate_shape, group)
        + Reducer.group_scratch(*x_out_shape, group),
        "middle",
        1,
    )(seq_lengths, skip_gain, tokens_in, cotangent, ylocal, gate, xb, vraw, cum, st0, state_in, decs, wofull, gated_gain, nt)

    def tile_in(rows, tiles):
        return pl.BlockSpec((seqs, rows, TILE), lambda i: (0, 0, jnp.minimum(i, tiles - 1)))

    def late(*shape):
        zeros = (0,) * len(shape)
        return pl.BlockSpec((1,) + shape, lambda i: (jnp.clip(i - TILES - 1, 0, seqs - 1),) + zeros)

    bc_spec = pl.BlockSpec((seqs, SPAN, TILE), lambda i: (0, 0, TILES), pipeline_mode=pl.Buffered(1))
    height = SMALL_ROWS
    x_conv_shape = (GZW // CONV_CHUNK, D // group, CONV_CHUNK)
    gtok, r_zx, r_out, small, gain_sum = call(
        back_kernel,
        TILES + 1 + seqs,
        [SMEM, SMEM, SMEM, late(SPAN, D), late(SPAN, D), whole((seqs, RIM, D)), whole((D,)), late(SPAN, DIN), ANY, whole((D, HALF)),
         tile_in(RIM + SPAN, TILES + 1), tile_in(SPAN, TILES + 1), tile_in(SPAN, TILES + 1), bc_spec, tile_in(SPAN, TILES),
         tile_in(SPAN, TILES), tile_in(NSTATE, TILES), tile_in(NSTATE, TILES), tile_in(NSTATE, TILES), tile_in(NSTATE, TILES),
         whole((seqs, SPAN, HALF)), whole((seqs, SPAN, HALF)), whole((seqs, SPAN, HALF)), whole((seqs, SPAN, 2 * NSTATE)),
         whole((KCONV, CONVW)), whole((D, seqs * SPAN)), whole((D, seqs * RIM)),
         whole(x_gate_shape), whole(x_out_shape), whole((1, DIN)), whole((1, DIN))],
        [
            (late(SPAN, D), (seqs, SPAN, D), bf16),
            (summed((D // group, DIN + GZW)), (D // group, DIN + GZW), bf16),
            (summed((DIN // group, D)), (DIN // group, D), bf16),
            (summed((height, HALF)), (height, HALF), f32),
            (summed((8, HALF)), (8, HALF), f32),
        ],
        [((2 * HALF, DIN), bf16), ((1, DIN), f32), ((D, ZXW), bf16), dma((1,)), ((seqs, SPAN, 2 * HALF), bf16),
         ((seqs, SPAN, 2 * HALF), bf16), ((seqs, 16, DIN), f32),
         ((seqs, SPAN, NSTATE), f32), ((seqs, SPAN, HALF), f32), ((seqs, 8, HALF), f32), ((2, RIM + SPAN + 8, TILE), f32),
         ((seqs * SPAN, CONVW + HALF), bf16), ((seqs * RIM, CONVW), bf16), ((D, GZW), bf16), ((KCONV, CONVW), f32),
         ((1, CONVW), f32), ((1, HALF), f32), ((1, HALF), f32), ((1, D), f32), ((seqs, RIM, D), bf16), ((seqs, RIM, D), bf16),
         dma((seqs,)), dma((seqs,))]
        + Reducer.ctx_scratch(*x_gate_shape, False, count)
        + Reducer.ctx_scratch(*x_out_shape, True, count)
        + Reducer.group_scratch(*x_conv_shape, group)
        + [(x_conv_shape, bf16)]
        + Reducer.ctx_scratch(*x_conv_shape, False, count)
        + Small.scratch(height, group, count)
        + Small.scratch(8, group, count),
        "back",
        2,
    )(seq_lengths, decay_log, skip_gain, tokens_in, cotangent, rhalo, norm_gain, ggate, wfull, wdfull, cin, xb, spb, xb, dy, dxs, dir1, later, state_in, loc,
      vraw, cum, wred, dbc, conv_weight, nt, nth, x_gate, x_out, gskip, gggain)

    zx_rows, out_rows = D // group, DIN // group
    turns = 2
    halved = lambda rows, cols: pl.BlockSpec((rows // turns, cols), lambda i: (i, 0))
    grad = lambda *shape: (summed(shape), jax.ShapeDtypeStruct(shape, f32))
    specs, shapes = zip(
        grad(D), (halved(zx_rows, ZXW), jax.ShapeDtypeStruct((zx_rows, ZXW), f32)),
        grad(HEADS, zx_rows), (halved(out_rows, D), jax.ShapeDtypeStruct((out_rows, D), f32)), grad(KCONV, CONVW), grad(CONVW),
        grad(HEADS), grad(HEADS), grad(HEADS), grad(DIN),
    )
    results = pl.pallas_call(
        done_kernel,
        grid=(turns,),
        in_specs=[halved(zx_rows, DIN + GZW), pl.BlockSpec((zx_rows, HALF), lambda i: (0, ZXW // HALF)), halved(out_rows, D),
                  whole((SMALL_ROWS, HALF)), whole((8, HALF))],
        out_specs=specs,
        out_shape=shapes,
        name="done",
    )(r_zx, r_zx, r_out, small, gain_sum)
    return (mixed_out, gtok, *results[:2], results[2].T, *results[3:])


def solution(mesh):
    rows = P("group", "ctx", None)
    own = P("group", None)
    in_specs = (rows, P("group"), P(), own, own, own, P(), P(), P(), P(), P(), P(), rows)
    out_specs = (rows, rows, P(), own, own, own, P(), P(), P(), P(), P(), P())
    return jax.shard_map(local, mesh=mesh, in_specs=in_specs, out_specs=out_specs, check_vma=False)
```
